32 devices in a mesh: dp: 4 (over x, core), fsdp: 8 (over z, y).
Axes of the slice: x: 2, y: 2, z: 4, core: 2. Of those that a mesh axis runs over, the one named last changes fastest.
Arguments:
- tokens: bfloat16 [32768, 768], P(('dp', 'fsdp')), may hold values from -6 to 6
- doc_lengths: int32 [32, 8], P(('dp', 'fsdp')), may hold values from 1 to 512, 1024 in all within a row
- cotangent: bfloat16 [32768, 768], P(('dp', 'fsdp')), may hold values from -6 to 6
- w_qkv: bfloat16 [768, 2304], P(('dp', 'fsdp')), may hold values from -0.21875 to 0.21875
- w_out: bfloat16 [768, 768], P(('dp', 'fsdp')), may hold values from -0.21875 to 0.21875
- w_up: bfloat16 [768, 3072], P(('dp', 'fsdp')), may hold values from -0.21875 to 0.21875
- w_down: bfloat16 [3072, 768], P(('dp', 'fsdp')), may hold values from -0.109375 to 0.109375
- gain_attn: bfloat16 [768], P(('dp', 'fsdp')), may hold values from 0.5 to 1.5
- gain_inner: bfloat16 [768], P(('dp', 'fsdp')), may hold values from 0.5 to 1.5
- gain_ffn: bfloat16 [768], P(('dp', 'fsdp')), may hold values from 0.5 to 1.5
- gain_mid: bfloat16 [3072], P(('dp', 'fsdp')), may hold values from 0.5 to 1.5
Outputs:
- result: bfloat16 [32768, 768], P(('dp', 'fsdp'))
- grad_tokens: float32 [32768, 768], P(('dp', 'fsdp'))
- grad_w_qkv: float32 [768, 2304], P(('dp', 'fsdp'))
- grad_w_out: float32 [768, 768], P(('dp', 'fsdp'))
- grad_w_up: float32 [768, 3072], P(('dp', 'fsdp'))
- grad_w_down: float32 [3072, 768], P(('dp', 'fsdp'))
- grad_gain_attn: float32 [768], P(('dp', 'fsdp'))
- grad_gain_inner: float32 [768], P(('dp', 'fsdp'))
- grad_gain_ffn: float32 [768], P(('dp', 'fsdp'))
- grad_gain_mid: float32 [3072], P(('dp', 'fsdp'))
The draws below stay inside these ranges and needn't reach their ends.
Inputs may be any that keep to these rules, and one draw needn't show every extreme that they name: `doc_lengths`: each row's 8 lengths sum to 1024; its last document is padding at the row's end, and some document of each row has exactly 512 tokens.
All inputs are finite; a program needn't handle non-finite values.
Results may differ from the reference program's by a relative error of at most 0.013.
Values may be sent and summed in bfloat16 or wider, within the bound.
No kernel may reach another device: no remote copies, remote signals or barrier semaphores. Data moves between devices by JAX's collectives and lax.ppermute only.
A program may use at most 192 MiB of HBM per device.

```python
import math
import jax
import jax.numpy as jnp
import numpy as np
from jax import lax

D = 768
HEADS = 12
HEAD_DIM = 64
FF = 3072
SEQ = 1024
DOCS = 8
MOST = 512
ROWS = 32
TOKENS = 32768


def raised(array, rng, source, target, shards_of, factor):
    def block_of(dim):
        return (jnp.arange(array.shape[dim]) // (array.shape[dim] // shards_of)).reshape((-1,) + (1,) * (array.ndim - 1 - dim))

    first = jax.random.permutation(rng, shards_of)[block_of(target)]
    other_side = (block_of(target) + shards_of // 2) % shards_of
    return jnp.where((block_of(source) == first) | (block_of(source) == other_side), factor * array, array)


def block_scale(stream_key, shape, split, low, top_value):
    loudness = 1.0
    for dim, blocks in split:
        draws = jax.random.uniform(jax.random.fold_in(jax.random.fold_in(stream_key, 6), dim), (blocks,), jnp.float32, low / len(split), top_value / len(split))
        loudness = loudness * jnp.repeat(jnp.exp(draws), shape[dim] // blocks).reshape((-1,) + (1,) * (len(shape) - 1 - dim))
    return loudness


def length_profile(number_of, total, limit, skew):
    portions = [(1 << 20) // math.isqrt(grade ** skew) + 1 for grade in range(2, number_of + 1)]
    surplus, holding = total - limit - (number_of - 1), [1] * (number_of - 1)
    while surplus > 0:
        free = [i for i in range(number_of - 1) if holding[i] < limit]
        mass, remaining = sum([portions[i] for i in free]), surplus
        for i in free:
            extra = min(limit - holding[i], max(1, remaining * portions[i] // mass), surplus)
            holding[i] = holding[i] + extra
            surplus = surplus - extra
    return np.array([limit] + holding)


def ragged(rng, count, total, reach, skew):
    if count == 2:
        one = jax.random.randint(rng, (), max(1, total - reach), min(reach, total - 1) + 1)
        return jnp.stack([one, total - one])
    tallies = jnp.asarray(length_profile(count, total, reach, skew), jnp.int32)
    couples = (count - 1) // 2
    source_of, receiver = tallies[1:1 + 2 * couples:2], tallies[2:2 + 2 * couples:2]
    margin = jnp.minimum(source_of - 1, reach - receiver)
    moved = jax.random.randint(jax.random.fold_in(rng, 1), (couples,), 0, 1 << 20) % (margin + 1)
    tallies = tallies.at[1:1 + 2 * couples:2].set(source_of - moved).at[2:2 + 2 * couples:2].set(receiver + moved)
    return tallies[jax.random.permutation(jax.random.fold_in(rng, 2), count)]


def bell_draw(rng, dims, scale, bound, shards=(), kind=jnp.bfloat16):
    level = block_scale(rng, dims, shards, -0.22, 0.18) if shards else 1.0
    drawn = jax.random.normal(rng, dims, jnp.float32) * scale * level
    return jnp.minimum(jnp.maximum(drawn, -bound), bound).astype(kind)


def bell_draw_with(stream_key, extent, scale, bound, shards, heavy, held_as=jnp.bfloat16):
    values = scale * jax.random.normal(stream_key, extent, jnp.float32)
    if shards:
        values = values * block_scale(stream_key, extent, shards, -0.22, 0.18)
    return jnp.clip(raised(values, jax.random.fold_in(stream_key, 3), *heavy), -bound, bound).astype(held_as)


def setup_inputs(seed: int = 0) -> dict:
    key_of = jax.random.split(jax.random.key(seed), 12)
    return {
        "tokens": bell_draw_with(key_of[0], (TOKENS, D), 1.0, 6.0, ((0, 32),), (0, 1, 32, 2.75)),
        "doc_lengths": jax.vmap(lambda own: ragged(own, DOCS, SEQ, MOST, 2))(jax.random.split(key_of[1], ROWS)).reshape((ROWS, DOCS)).astype(jnp.int32),
        "cotangent": bell_draw(key_of[2], (TOKENS, D), 1.0, 6.0, ((0, 32),)),
        "w_qkv": bell_draw(key_of[3], (D, 3 * D), D ** -0.5, 0.21875, ((0, 32),)),
        "w_out": bell_draw(key_of[4], (D, D), D ** -0.5, 0.21875, ((0, 32),)),
        "w_up": bell_draw(key_of[5], (D, FF), D ** -0.5, 0.21875, ((0, 32),)),
        "w_down": bell_draw(key_of[6], (FF, D), FF ** -0.5, 0.109375, ((0, 32),)),
        "gain_attn": jnp.clip(1.0 + 0.1 * jax.random.normal(key_of[7], (D,), jnp.float32), 0.5, 1.5).astype(jnp.bfloat16),
        "gain_inner": jnp.clip(1.0 + 0.1 * jax.random.normal(key_of[8], (D,), jnp.float32), 0.5, 1.5).astype(jnp.bfloat16),
        "gain_ffn": jnp.clip(1.0 + 0.1 * jax.random.normal(key_of[9], (D,), jnp.float32), 0.5, 1.5).astype(jnp.bfloat16),
        "gain_mid": jnp.clip(1.0 + 0.1 * jax.random.normal(key_of[10], (FF,), jnp.float32), 0.5, 1.5).astype(jnp.bfloat16),
    }


EXACT = lax.Precision.HIGHEST

@jax.custom_vjp
def low(v):
    return lax.optimization_barrier(v.astype(jnp.bfloat16)).astype(jnp.float32)

@jax.custom_vjp
def low_back(v):
    return v

def low_keep(v):
    return (low(v), None)

def low_pass(kept, grad):
    return (grad,)

def back_keep(v):
    return (v, None)

def back_low(kept, grad):
    return (low(grad),)
low.defvjp(low_keep, low_pass)
low_back.defvjp(back_keep, back_low)

def doc_layout(doc_lengths, seq_len):
    doc_ends = jnp.cumsum(doc_lengths, axis=-1).astype(jnp.int32)
    doc_starts = (doc_ends - doc_lengths).astype(jnp.int32)
    places = jnp.arange(seq_len, dtype=jnp.int32)
    passed = (places[None, :, None] >= doc_ends[:, None, :]).astype(jnp.int32)
    segment = lax.optimization_barrier(jnp.sum(passed, axis=-1)).astype(jnp.int32)
    doc_count = doc_lengths.shape[-1]
    member = segment[:, :, None] == jnp.arange(doc_count, dtype=jnp.int32)[None, None, :]
    offset = lax.optimization_barrier(jnp.sum(jnp.where(member, doc_starts[:, None, :], 0), axis=-1)).astype(jnp.int32)
    position = places[None, :] - offset
    valid_mask = segment < doc_count - 1
    return (segment, position, valid_mask)

def rotary_tables(position, head_dim):
    half_dim = head_dim // 2
    frequency = jnp.exp(jnp.arange(half_dim, dtype=jnp.float32) * (-2.0 * math.log(10000.0) / head_dim))
    angles = position.astype(jnp.float32)[..., None] * frequency
    return (jnp.cos(angles), jnp.sin(angles))

def rotate(values_in, cosine_table, sine_table):
    half_dim = values_in.shape[-1] // 2
    first_half = values_in[..., :half_dim]
    second_half = values_in[..., half_dim:]
    cos_wide = cosine_table[:, :, None, :]
    sin_wide = sine_table[:, :, None, :]
    return jnp.concatenate([first_half * cos_wide - second_half * sin_wide, second_half * cos_wide + first_half * sin_wide], axis=-1)

def layer_norm(values_in, gain_vec):
    mean_val = lax.optimization_barrier(jnp.mean(values_in, axis=-1, keepdims=True))
    centered = values_in - mean_val
    variance = lax.optimization_barrier(jnp.mean(centered * centered, axis=-1, keepdims=True))
    return centered * lax.rsqrt(variance + 1e-05) * gain_vec

def attend_row(pieces):
    queries, key_rows, value_rows, segment = pieces
    seq_len = queries.shape[0]
    places = jnp.arange(seq_len, dtype=jnp.int32)
    allowed = (segment[:, None] == segment[None, :]) & (places[None, :] <= places[:, None])
    scaling = 1.0 / math.sqrt(HEAD_DIM)
    scores = low_back(jnp.einsum('qhd,khd->hqk', queries, key_rows, precision=EXACT) * scaling)
    scores = jnp.where(allowed[None, :, :], scores, -1e+30)
    row_max = lax.optimization_barrier(jnp.max(scores, axis=-1, keepdims=True))
    powers = jnp.exp(scores - row_max)
    attn_probs = low(powers / lax.optimization_barrier(jnp.sum(powers, axis=-1, keepdims=True)))
    return jnp.einsum('hqk,khd->qhd', attn_probs, value_rows, precision=EXACT)

def layer(inputs_f, w_qkv, w_out, w_up, w_down, gain_attn, gain_inner, gain_ffn, gain_mid, segment, cosine_table, sine_table):
    row_count, seq_len, model_width = inputs_f.shape
    head_shape = (row_count, seq_len, HEADS, HEAD_DIM)
    normed_one = low(layer_norm(inputs_f, gain_attn))
    qkv = low_back(jnp.einsum('rsd,de->rse', normed_one, w_qkv, precision=EXACT))
    queries = low(rotate(qkv[..., :model_width].reshape(head_shape), cosine_table, sine_table))
    key_heads = low(rotate(qkv[..., model_width:2 * model_width].reshape(head_shape), cosine_table, sine_table))
    value_heads = low(qkv[..., 2 * model_width:].reshape(head_shape))
    mixed_out = lax.map(jax.checkpoint(attend_row), (queries, key_heads, value_heads, segment))
    mixed_out = low_back(mixed_out.reshape(row_count, seq_len, model_width))
    inner_low = low(layer_norm(mixed_out, gain_inner))
    after_attn = inputs_f + low_back(jnp.einsum('rsd,de->rse', inner_low, w_out, precision=EXACT))
    normed_two = low(layer_norm(after_attn, gain_ffn))
    hidden = low_back(jnp.einsum('rsd,df->rsf', normed_two, w_up, precision=EXACT))
    middle = low(layer_norm(jax.nn.gelu(hidden, approximate=False), gain_mid))
    return after_attn + low_back(jnp.einsum('rsf,fd->rsd', middle, w_down, precision=EXACT))

def reference(tokens, doc_lengths, cotangent, w_qkv, w_out, w_up, w_down, gain_attn, gain_inner, gain_ffn, gain_mid):
    row_count = doc_lengths.shape[0]
    seq_len = tokens.shape[0] // row_count
    model_width = tokens.shape[1]
    group_rows = 4 if row_count % 4 == 0 else 2 if row_count % 2 == 0 else 1
    group_count = row_count // group_rows
    segment, position, valid_mask = doc_layout(doc_lengths, seq_len)
    cosine_table, sine_table = rotary_tables(position, HEAD_DIM)
    weights = tuple((item_w.astype(jnp.float32) for item_w in (w_qkv, w_out, w_up, w_down, gain_attn, gain_inner, gain_ffn, gain_mid)))
    inputs_f = tokens.astype(jnp.float32).reshape(group_count, group_rows, seq_len, model_width)
    grad_out = cotangent.astype(jnp.float32).reshape(row_count, seq_len, model_width) * valid_mask[..., None].astype(jnp.float32)
    grad_out = grad_out.reshape(group_count, group_rows, seq_len, model_width)
    seg_groups = segment.reshape(group_count, group_rows, seq_len)
    half_dim = HEAD_DIM // 2
    cos_groups = cosine_table.reshape(group_count, group_rows, seq_len, half_dim)
    sin_groups = sine_table.reshape(group_count, group_rows, seq_len, half_dim)

    def group_step(totals, pieces):
        x_group, g_group, s_group, c_group, n_group = pieces

        def forward_fn(x_value, *weight_values):
            return layer(x_value, *weight_values, s_group, c_group, n_group)
        outputs, pull_back = jax.vjp(forward_fn, x_group, *weights)
        gradients = pull_back(g_group)
        totals = tuple((total_g + new_g for total_g, new_g in zip(totals, gradients[1:])))
        return (totals, (outputs, gradients[0]))
    zeros_init = tuple((jnp.zeros_like(item_w) for item_w in weights))
    totals, (outputs, grad_x) = lax.scan(group_step, zeros_init, (inputs_f, grad_out, seg_groups, cos_groups, sin_groups))
    result = outputs.reshape(row_count * seq_len, model_width).astype(jnp.bfloat16)
    grad_tokens = grad_x.reshape(row_count * seq_len, model_width)
    return (result, grad_tokens, totals[0], totals[1], totals[2], totals[3], totals[4], totals[5], totals[6], totals[7])
```

```python
import functools
import math

import jax
import jax.numpy as jnp
from jax import lax
from jax.experimental import pallas as pl
from jax.experimental.pallas import tpu as pltpu
from jax.sharding import PartitionSpec as P

HEADS = 12
HEAD_DIM = 64
PAIR = 2 * HEAD_DIM
PAIRS = HEADS // 2
EPSILON = 1e-05
MASKED_SCORE = -1e30
ROOT_HALF = 0.7071067811865476
INV_ROOT_TAU = 0.3989422804014327
BF = jnp.bfloat16
F32 = jnp.float32
MIB = 1 << 20
AXES = ("dp", "fsdp")
BLOCK = 256


def dot(a, b, dims=((1,), (0,))):
    return lax.dot_general(a, b, (dims, ((), ())), preferred_element_type=F32)


def params(mib):
    return pltpu.CompilerParams(vmem_limit_bytes=mib * MIB)


def swap_halves(x):
    lane = lax.broadcasted_iota(jnp.int32, x.shape, 1)
    low = lax.rem(lane, HEAD_DIM) < HEAD_DIM // 2
    half = HEAD_DIM // 2
    return jnp.where(low, pltpu.roll(x, PAIR - half, 1), pltpu.roll(x, half, 1))


def unit_norm(x):
    mean = jnp.mean(x, axis=-1, keepdims=True)
    centred = x - mean
    inv = lax.rsqrt(jnp.mean(centred * centred, axis=-1, keepdims=True) + EPSILON)
    return centred * inv, inv


def norm_back(grad, gain, unit, inv):
    d_unit = grad * gain
    return inv * (
        d_unit
        - jnp.mean(d_unit, axis=-1, keepdims=True)
        - unit * jnp.mean(d_unit * unit, axis=-1, keepdims=True)
    )


def whole(shape):
    return pl.BlockSpec(shape, lambda *_: (0,) * len(shape), pipeline_mode=pl.Buffered(1))


def rows(width, block=BLOCK):
    return pl.BlockSpec((block, width), lambda i: (i, 0))


def shaped(shape, dtype):
    return jax.ShapeDtypeStruct(shape, dtype)


def qkv_kernel(x_ref, w_ref, gain_ref, cos_ref, sin_ref, h_ref, qkv_ref):
    unit, _ = unit_norm(x_ref[...].astype(F32))
    h = (unit * gain_ref[...]).astype(BF)
    h_ref[...] = h
    cos, sin = cos_ref[...], sin_ref[...]
    width = h.shape[1]
    for part in range(3):
        y = dot(h, w_ref[:, part * width : (part + 1) * width])
        for c in range(width // PAIR):
            z = y[:, c * PAIR : (c + 1) * PAIR]
            if part < 2:
                z = z * cos + swap_halves(z) * sin
            if part == 0:
                z = z * (1.0 / math.sqrt(HEAD_DIM))
            at = part * width + c * PAIR
            qkv_ref[:, at : at + PAIR] = z.astype(BF)


def qkv_forward(tokens, w_qkv, gain, cos, sin):
    t, d = tokens.shape
    n = w_qkv.shape[1]
    return pl.pallas_call(
        qkv_kernel,
        grid=(t // BLOCK,),
        in_specs=[rows(d), whole((d, n)), whole((1, d)), rows(PAIR), rows(PAIR)],
        out_specs=[rows(d), rows(n)],
        out_shape=[shaped((t, d), BF), shaped((t, n), BF)],
        compiler_params=params(48),
        cost_estimate=pl.CostEstimate(
            flops=2 * t * d * n, transcendentals=0, bytes_accessed=2 * d * n + 12 * t * d
        ),
        name="qkv_forward",
    )(tokens, w_qkv, gain, cos, sin)


def window(i, n):
    return slice((i - n + 1) * BLOCK, (i + 1) * BLOCK)


def head_masks(shape):
    lane = lax.broadcasted_iota(jnp.int32, shape, 1)
    return lane < HEAD_DIM


def attention_forward_kernel(wide, reach, q_ref, k_ref, v_ref, start_ref, o_ref, lse_ref, bias):
    row, pair = pl.program_id(0), pl.program_id(1)
    seq = q_ref.shape[0]
    blocks = seq // BLOCK

    @pl.when(pair == 0)
    def _():
        for i in range(blocks):
            at = slice(i * BLOCK, (i + 1) * BLOCK)
            shape = (BLOCK, wide * BLOCK)
            key = (i - wide + 1) * BLOCK + lax.broadcasted_iota(jnp.int32, shape, 1)
            query = i * BLOCK + lax.broadcasted_iota(jnp.int32, shape, 0)
            keep = (key >= start_ref[at, :]) & (key <= query)
            bias[at, :] = jnp.where(keep, 0.0, MASKED_SCORE)

    first = head_masks((BLOCK, PAIR))
    for i in range(blocks):
        at = slice(i * BLOCK, (i + 1) * BLOCK)
        most = min(wide, i + 1)
        for n in range(1, most + 1):

            @pl.when(reach[row * blocks + i] == n)
            def _():
                q = q_ref[at, :]
                w = window(i, n)
                k, v = k_ref[w, :], v_ref[w, :]
                b = bias[at, (wide - n) * BLOCK :]
                mask = head_masks(k.shape)
                zero = jnp.zeros_like(k)
                total, lses = None, []
                scale = None
                for h in range(2):
                    pick = mask if h == 0 else jnp.logical_not(mask)
                    s = dot(q, jnp.where(pick, k, zero), ((1,), (1,))) + b
                    top = jnp.max(s, axis=-1, keepdims=True)
                    p = jnp.exp(s - top)
                    den = jnp.sum(p, axis=-1, keepdims=True)
                    probs = (p * (1.0 / den)).astype(BF)
                    part = dot(probs, jnp.where(pick, v, zero))
                    total = part if total is None else total + part
                    lses.append(top + jnp.log(den))
                o_ref[at, :] = total
                both = jnp.where(first, lses[0], lses[1]).T
                lse_ref[0, 0:1, at] = both[0:1, :]
                lse_ref[0, 1:2, at] = both[HEAD_DIM : HEAD_DIM + 1, :]


def attention_forward(reach, qkv, start, row_count, wide):
    t = qkv.shape[0]
    seq = t // row_count
    d = qkv.shape[1] // 3

    def columns(part):
        return pl.BlockSpec((seq, PAIR), lambda r, p, *_: (r, part * PAIRS + p))

    return pl.pallas_call(
        functools.partial(attention_forward_kernel, wide),
        grid_spec=pltpu.PrefetchScalarGridSpec(
            num_scalar_prefetch=1,
            grid=(row_count, PAIRS),
            in_specs=[
                columns(0),
                columns(1),
                columns(2),
                pl.BlockSpec((seq, 1), lambda r, p, *_: (r, 0)),
            ],
            out_specs=[
                pl.BlockSpec((seq, PAIR), lambda r, p, *_: (r, p)),
                pl.BlockSpec((1, 8, seq), lambda r, p, *_: (r * PAIRS + p, 0, 0)),
            ],
            scratch_shapes=[pltpu.VMEM((seq, wide * BLOCK), F32)],
        ),
        out_shape=[shaped((t, d), F32), shaped((row_count * PAIRS, 8, seq), F32)],
        compiler_params=params(32),
        cost_estimate=pl.CostEstimate(
            flops=8 * t * d * BLOCK, transcendentals=t * HEADS * 512, bytes_accessed=12 * t * d
        ),
        name="attention_forward",
    )(reach, qkv, qkv, qkv, start)


def attention_backward_kernel(
    wide, reach, q_ref, k_ref, v_ref, do_ref, o_ref, lse_ref, start_ref, cos_ref, sin_ref,
    dq_ref, dk_ref, dv_ref, bias, ks, vs, qs, dos, dk_acc, dv_acc, dq_acc,
):
    row, pair = pl.program_id(0), pl.program_id(1)
    seq = q_ref.shape[0]
    blocks = seq // BLOCK

    @pl.when(pair == 0)
    def _():
        for i in range(blocks):
            at = slice(i * BLOCK, (i + 1) * BLOCK)
            shape = (wide * BLOCK, BLOCK)
            key = (i - wide + 1) * BLOCK + lax.broadcasted_iota(jnp.int32, shape, 0)
            query = i * BLOCK + lax.broadcasted_iota(jnp.int32, shape, 1)
            keep = (key >= start_ref[0:1, at]) & (key <= query)
            bias[:, at] = jnp.where(keep, 0.0, MASKED_SCORE)

    mask = head_masks((seq, PAIR))
    for src, dst in ((k_ref, ks), (v_ref, vs), (q_ref, qs), (do_ref, dos)):
        x = src[...]
        zero = jnp.zeros_like(x)
        dst[0] = jnp.where(mask, x, zero)
        dst[1] = jnp.where(mask, zero, x)
    dk_acc[...] = jnp.zeros_like(dk_acc)
    dv_acc[...] = jnp.zeros_like(dv_acc)
    lane8 = lax.broadcasted_iota(jnp.int32, (8, PAIR), 1) // HEAD_DIM
    row8 = lax.broadcasted_iota(jnp.int32, (8, PAIR), 0)
    picks = (lane8 == row8).astype(F32)
    delta = lax.dot_general(
        picks, do_ref[...].astype(F32) * o_ref[...], (((1,), (1,)), ((), ())),
        precision=lax.Precision.HIGHEST, preferred_element_type=F32,
    )
    for i in range(blocks):
        at = slice(i * BLOCK, (i + 1) * BLOCK)
        most = min(wide, i + 1)
        for n in range(1, most + 1):

            @pl.when(reach[row * blocks + i] == n)
            def _():
                w = window(i, n)
                b = bias[(wide - n) * BLOCK :, at]
                q, do = q_ref[at, :], do_ref[at, :]
                ps, dss = [], []
                for h in range(2):
                    s = dot(ks[h, w, :], q, ((1,), (1,))) + b
                    p = jnp.exp(s - lse_ref[0, h : h + 1, at])
                    dp = dot(vs[h, w, :], do, ((1,), (1,)))
                    ds = (p * (dp - delta[h : h + 1, at])).astype(BF)
                    ps.append(p.astype(BF))
                    dss.append(ds)
                dv_acc[w, :] += dot(ps[0], dos[0, at, :]) + dot(ps[1], dos[1, at, :])
                dk_acc[w, :] += dot(dss[0], qs[0, at, :]) + dot(dss[1], qs[1, at, :])
                dq_acc[at, :] = dot(dss[0], ks[0, w, :], ((0,), (0,))) + dot(
                    dss[1], ks[1, w, :], ((0,), (0,))
                )

    cos, sin = cos_ref[...], sin_ref[...]
    dq = dq_acc[...] * (1.0 / math.sqrt(HEAD_DIM))
    dk = dk_acc[...]
    dq_ref[...] = (dq * cos - swap_halves(dq) * sin).astype(BF)
    dk_ref[...] = (dk * cos - swap_halves(dk) * sin).astype(BF)
    dv_ref[...] = dv_acc[...].astype(BF)


def attention_backward(reach, qkv, d_mixed, mixed, lse, start_row, cos, sin, row_count, wide):
    t = qkv.shape[0]
    seq = t // row_count
    d = qkv.shape[1] // 3

    def columns(part):
        return pl.BlockSpec((seq, PAIR), lambda r, p, *_: (r, part * PAIRS + p))

    table = pl.BlockSpec((seq, PAIR), lambda r, p, *_: (r, 0))
    return pl.pallas_call(
        functools.partial(attention_backward_kernel, wide),
        grid_spec=pltpu.PrefetchScalarGridSpec(
            num_scalar_prefetch=1,
            grid=(row_count, PAIRS),
            in_specs=[
                columns(0), columns(1), columns(2), columns(0), columns(0),
                pl.BlockSpec((1, 8, seq), lambda r, p, *_: (r * PAIRS + p, 0, 0)),
                pl.BlockSpec((8, seq), lambda r, p, *_: (r, 0)),
                table, table,
            ],
            out_specs=[columns(0)] * 3,
            scratch_shapes=[
                pltpu.VMEM((wide * BLOCK, seq), F32),
                pltpu.VMEM((2, seq, PAIR), BF),
                pltpu.VMEM((2, seq, PAIR), BF),
                pltpu.VMEM((2, seq, PAIR), BF),
                pltpu.VMEM((2, seq, PAIR), BF),
                pltpu.VMEM((seq, PAIR), F32),
                pltpu.VMEM((seq, PAIR), F32),
                pltpu.VMEM((seq, PAIR), F32),
            ],
        ),
        out_shape=[shaped((t, d), BF)] * 3,
        compiler_params=params(40),
        cost_estimate=pl.CostEstimate(
            flops=20 * t * d * BLOCK, transcendentals=t * HEADS * 512, bytes_accessed=20 * t * d
        ),
        name="attention_backward",
    )(reach, qkv, qkv, qkv, d_mixed, mixed, lse, start_row, cos, sin)


def up_kernel(o_ref, x_ref, wo_ref, wu_ref, gi_ref, gf_ref, gm_ref,
              a_ref, x1_ref, h2_ref, m_ref, slope_ref, inv_ref):
    unit, _ = unit_norm(o_ref[...])
    a = (unit * gi_ref[...]).astype(BF)
    a_ref[...] = a
    x1 = x_ref[...].astype(F32) + dot(a, wo_ref[...])
    x1_ref[...] = x1
    unit, _ = unit_norm(x1)
    h2 = (unit * gf_ref[...]).astype(BF)
    h2_ref[...] = h2
    hidden = dot(h2, wu_ref[...])
    cdf = 0.5 + 0.5 * lax.erf(hidden * ROOT_HALF)
    slope = cdf + hidden * (jnp.exp(-0.5 * hidden * hidden) * INV_ROOT_TAU)
    slope_ref[...] = slope.astype(BF)
    unit, inv = unit_norm(hidden * cdf)
    m_ref[...] = (unit * gm_ref[...]).astype(BF)
    inv_ref[...] = jnp.broadcast_to(inv, inv_ref.shape)


def up_forward(mixed, tokens, w_out, w_up, gain_inner, gain_ffn, gain_mid):
    t, d = tokens.shape
    f = w_up.shape[1]
    return pl.pallas_call(
        up_kernel,
        grid=(t // BLOCK,),
        in_specs=[rows(d), rows(d), whole((d, d)), whole((d, f)), whole((1, d)), whole((1, d)), whole((1, f))],
        out_specs=[rows(d), rows(d), rows(d), rows(f), rows(f), rows(PAIR)],
        out_shape=[
            shaped((t, d), BF), shaped((t, d), F32), shaped((t, d), BF),
            shaped((t, f), BF), shaped((t, f), BF), shaped((t, PAIR), F32),
        ],
        compiler_params=params(56),
        cost_estimate=pl.CostEstimate(
            flops=2 * t * d * (d + f), transcendentals=2 * t * f, bytes_accessed=2 * d * (d + f) + 4 * t * f + 14 * t * d
        ),
        name="up_forward",
    )(mixed, tokens, w_out, w_up, gain_inner, gain_ffn, gain_mid)


def down_kernel(m_ref, slope_ref, inv_ref, x1_ref, ct_ref, valid_ref, wd_ref, gm_ref,
                y_ref, dpre_ref, gwd_ref, gg_ref):
    step = pl.program_id(0)
    m = m_ref[...]
    y_ref[...] = (x1_ref[...] + dot(m, wd_ref[...])).astype(BF)
    gy = jnp.where(valid_ref[...] > 0, ct_ref[...], jnp.zeros_like(ct_ref))
    part = dot(m, gy, ((0,), (0,)))
    dm = dot(gy, wd_ref[...], ((1,), (1,)))
    gain = gm_ref[...]
    mf = m.astype(F32)
    prod = dm * mf
    d_unit = dm * gain
    d_act = inv_ref[:, 0:1] * (
        d_unit
        - jnp.mean(d_unit, axis=-1, keepdims=True)
        - (mf * (1.0 / gain)) * jnp.mean(prod, axis=-1, keepdims=True)
    )
    dpre_ref[...] = (d_act * slope_ref[...].astype(F32)).astype(BF)
    gain_part = jnp.sum(prod, axis=0, keepdims=True) * (1.0 / gain)

    @pl.when(step == 0)
    def _():
        gwd_ref[...] = part
        gg_ref[...] = gain_part

    @pl.when(step > 0)
    def _():
        gwd_ref[...] += part
        gg_ref[...] += gain_part


def down_both(m, slope, inv, x1, cotangent, valid, w_down, gain_mid):
    t, d = x1.shape
    f = m.shape[1]
    return pl.pallas_call(
        down_kernel,
        grid=(t // BLOCK,),
        in_specs=[rows(f), rows(f), rows(PAIR), rows(d), rows(d), rows(1), whole((f, d)), whole((1, f))],
        out_specs=[rows(d), rows(f), whole((f, d)), whole((1, f))],
        out_shape=[shaped((t, d), BF), shaped((t, f), BF), shaped((f, d), F32), shaped((1, f), F32)],
        compiler_params=params(60),
        cost_estimate=pl.CostEstimate(
            flops=6 * t * d * f, transcendentals=0, bytes_accessed=6 * d * f + 6 * t * f + 8 * t * d
        ),
        name="down_both",
    )(m, slope, inv, x1, cotangent, valid, w_down, gain_mid)


def up_back_kernel(dpre_ref, h2_ref, x1_ref, ct_ref, valid_ref, a_ref, o_ref, wu_ref, wo_ref, gf_ref, gi_ref,
                   dx1_ref, do_ref, gwu_ref, gwo_ref, ggf_ref, ggi_ref):
    step = pl.program_id(0)
    dpre = dpre_ref[...]
    part_up = dot(h2_ref[...], dpre, ((0,), (0,)))
    dh2 = dot(dpre, wu_ref[...], ((1,), (1,)))
    unit, inv = unit_norm(x1_ref[...])
    ffn_part = jnp.sum(dh2 * unit, axis=0, keepdims=True)
    gy = jnp.where(valid_ref[...] > 0, ct_ref[...].astype(F32), 0.0)
    dx1 = gy + norm_back(dh2, gf_ref[...], unit, inv)
    dx1_ref[...] = dx1
    low = dx1.astype(BF)
    part_out = dot(a_ref[...], low, ((0,), (0,)))
    da = dot(low, wo_ref[...], ((1,), (1,)))
    unit, inv = unit_norm(o_ref[...])
    inner_part = jnp.sum(da * unit, axis=0, keepdims=True)
    do_ref[...] = norm_back(da, gi_ref[...], unit, inv).astype(BF)

    @pl.when(step == 0)
    def _():
        gwu_ref[...] = part_up
        gwo_ref[...] = part_out
        ggf_ref[...] = ffn_part
        ggi_ref[...] = inner_part

    @pl.when(step > 0)
    def _():
        gwu_ref[...] += part_up
        gwo_ref[...] += part_out
        ggf_ref[...] += ffn_part
        ggi_ref[...] += inner_part


def up_backward(dpre, h2, x1, cotangent, valid, a, mixed, w_up, w_out, gain_ffn, gain_inner):
    t, d = x1.shape
    f = dpre.shape[1]
    return pl.pallas_call(
        up_back_kernel,
        grid=(t // BLOCK,),
        in_specs=[rows(f), rows(d), rows(d), rows(d), rows(1), rows(d), rows(d),
                  whole((d, f)), whole((d, d)), whole((1, d)), whole((1, d))],
        out_specs=[rows(d), rows(d), whole((d, f)), whole((d, d)), whole((1, d)), whole((1, d))],
        out_shape=[shaped((t, d), F32), shaped((t, d), BF), shaped((d, f), F32), shaped((d, d), F32),
                   shaped((1, d), F32), shaped((1, d), F32)],
        compiler_params=params(60),
        cost_estimate=pl.CostEstimate(
            flops=4 * t * d * (d + f), transcendentals=0, bytes_accessed=6 * d * (d + f) + 2 * t * f + 24 * t * d
        ),
        name="up_backward",
    )(dpre, h2, x1, cotangent, valid, a, mixed, w_up, w_out, gain_ffn, gain_inner)


def qkv_grad_kernel(h_ref, dq_ref, dk_ref, dv_ref, g_ref):
    step = pl.program_id(0)
    h = h_ref[...]
    d = h.shape[1]
    for c, ref in enumerate((dq_ref, dk_ref, dv_ref)):
        part = dot(h, ref[...], ((0,), (0,)))
        cols = slice(c * d, (c + 1) * d)

        @pl.when(step == 0)
        def _():
            g_ref[:, cols] = part

        @pl.when(step > 0)
        def _():
            g_ref[:, cols] += part


def qkv_weight_grad(h, dq, dk, dv):
    t, d = h.shape
    return pl.pallas_call(
        qkv_grad_kernel,
        grid=(t // BLOCK,),
        in_specs=[rows(d)] * 4,
        out_specs=whole((d, 3 * d)),
        out_shape=shaped((d, 3 * d), F32),
        compiler_params=params(40),
        cost_estimate=pl.CostEstimate(flops=6 * t * d * d, transcendentals=0, bytes_accessed=12 * d * d + 8 * t * d),
        name="qkv_weight_grad",
    )(h, dq, dk, dv)


def qkv_back_kernel(dq_ref, dk_ref, dv_ref, x_ref, dx1_ref, w_ref, gain_ref, dx_ref, gg_ref):
    step = pl.program_id(0)
    d = x_ref.shape[1]
    dh = None
    for c, ref in enumerate((dq_ref, dk_ref, dv_ref)):
        part = dot(ref[...], w_ref[:, c * d : (c + 1) * d], ((1,), (1,)))
        dh = part if dh is None else dh + part
    unit, inv = unit_norm(x_ref[...].astype(F32))
    gain_part = jnp.sum(dh * unit, axis=0, keepdims=True)
    dx_ref[...] = dx1_ref[...] + norm_back(dh, gain_ref[...], unit, inv)

    @pl.when(step == 0)
    def _():
        gg_ref[...] = gain_part

    @pl.when(step > 0)
    def _():
        gg_ref[...] += gain_part


def qkv_backward(dq, dk, dv, tokens, dx1, w_qkv, gain):
    t, d = tokens.shape
    return pl.pallas_call(
        qkv_back_kernel,
        grid=(t // BLOCK,),
        in_specs=[rows(d)] * 5 + [whole((d, 3 * d)), whole((1, d))],
        out_specs=[rows(d), whole((1, d))],
        out_shape=[shaped((t, d), F32), shaped((1, d), F32)],
        compiler_params=params(48),
        cost_estimate=pl.CostEstimate(flops=6 * t * d * d, transcendentals=0, bytes_accessed=6 * d * d + 16 * t * d),
        name="qkv_backward",
    )(dq, dk, dv, tokens, dx1, w_qkv, gain)


def layout(doc_lengths, seq):
    docs = doc_lengths.shape[-1]
    upto = jnp.arange(docs)[:, None] <= jnp.arange(docs)[None, :]
    ends = jnp.sum(jnp.where(upto[None], doc_lengths[:, :, None], 0), axis=1)
    places = jnp.arange(seq, dtype=jnp.int32)
    passed = places[None, :, None] >= ends[:, None, :]
    start = jnp.sum(jnp.where(passed, doc_lengths[:, None, :], 0), axis=-1)
    valid = places[None, :] < ends[:, docs - 2 : docs - 1]
    return start.astype(jnp.int32), places[None, :] - start, valid


def tables(position):
    half = HEAD_DIM // 2
    lane = jnp.arange(PAIR)
    frequency = jnp.exp((lane % half).astype(F32) * (-2.0 * math.log(10000.0) / HEAD_DIM))
    angles = position.reshape(-1, 1).astype(F32) * frequency[None, :]
    sign = jnp.where(lane % HEAD_DIM < half, -1.0, 1.0)
    return jnp.cos(angles), jnp.sin(angles) * sign[None, :]


def gather(x):
    return lax.all_gather(x, AXES, axis=0, tiled=True)


def scatter(g):
    return lax.psum_scatter(g, AXES, scatter_dimension=0, tiled=True)


def local(tokens, doc_lengths, cotangent, w_qkv, w_out, w_up, w_down,
          gain_attn, gain_inner, gain_ffn, gain_mid):
    row_count = doc_lengths.shape[0]
    seq = tokens.shape[0] // row_count
    wide = min(seq, 512) // BLOCK + 1
    blocks = seq // BLOCK
    start, position, valid = layout(doc_lengths, seq)
    cos, sin = tables(position)
    firsts = start[:, ::BLOCK] // BLOCK
    reach = (jnp.arange(blocks, dtype=jnp.int32)[None, :] - firsts + 1).reshape(-1)
    start_col = start.reshape(-1, 1)
    start_row = jnp.repeat(start, 8, axis=0)
    valid_col = valid.astype(jnp.int32).reshape(-1, 1)

    f_qkv, f_out, f_up, f_down = (gather(w) for w in (w_qkv, w_out, w_up, w_down))
    g_attn, g_inner, g_ffn, g_mid = (
        gather(g).astype(F32).reshape(1, -1) for g in (gain_attn, gain_inner, gain_ffn, gain_mid)
    )
    h1, qkv = qkv_forward(tokens, f_qkv, g_attn, cos, sin)
    mixed, lse = attention_forward(reach, qkv, start_col, row_count, wide)
    a, x1, h2, m, slope, inv = up_forward(mixed, tokens, f_out, f_up, g_inner, g_ffn, g_mid)
    result, dpre, grad_down, grad_mid = down_both(m, slope, inv, x1, cotangent, valid_col, f_down, g_mid)
    dx1, d_mixed, grad_up, grad_out, grad_ffn, grad_inner = up_backward(
        dpre, h2, x1, cotangent, valid_col, a, mixed, f_up, f_out, g_ffn, g_inner
    )
    dq, dk, dv = attention_backward(reach, qkv, d_mixed, mixed, lse, start_row, cos, sin, row_count, wide)
    grad_qkv = qkv_weight_grad(h1, dq, dk, dv)
    grad_tokens, grad_attn = qkv_backward(dq, dk, dv, tokens, dx1, f_qkv, g_attn)
    weights = tuple(scatter(g.astype(BF)).astype(F32) for g in (grad_qkv, grad_out, grad_up, grad_down))
    gains = tuple(scatter(g.reshape(-1)) for g in (grad_attn, grad_inner, grad_ffn, grad_mid))
    return (result, grad_tokens) + weights + gains


def solution(mesh):
    matrix, vector = P(AXES, None), P(AXES)
    return jax.shard_map(
        local,
        mesh=mesh,
        in_specs=(matrix,) * 7 + (vector,) * 4,
        out_specs=(matrix,) * 6 + (vector,) * 4,
        check_vma=False,
    )
```

```python
import functools
import math

import jax
import jax.numpy as jnp
from jax import lax
from jax.experimental import pallas as pl
from jax.experimental.pallas import tpu as pltpu
from jax.sharding import PartitionSpec as P

HEADS = 12
HEAD_DIM = 64
PAIR = 2 * HEAD_DIM
PAIRS = HEADS // 2
EPSILON = 1e-05
MASKED_SCORE = -1e30
ROOT_HALF = 0.7071067811865476
INV_ROOT_TAU = 0.3989422804014327
BF = jnp.bfloat16
F32 = jnp.float32
MIB = 1 << 20
AXES = ("dp", "fsdp")
BLOCK = 256
LANES = 768


def dot(a, b, dims=((1,), (0,))):
    return lax.dot_general(a, b, (dims, ((), ())), preferred_element_type=F32)


def params(mib):
    return pltpu.CompilerParams(vmem_limit_bytes=mib * MIB)


def swap_halves(x):
    lane = lax.broadcasted_iota(jnp.int32, x.shape, 1)
    low = lax.rem(lane, HEAD_DIM) < HEAD_DIM // 2
    half = HEAD_DIM // 2
    return jnp.where(low, pltpu.roll(x, PAIR - half, 1), pltpu.roll(x, half, 1))


def unit_norm(x):
    mean = jnp.mean(x, axis=-1, keepdims=True)
    centred = x - mean
    inv = lax.rsqrt(jnp.mean(centred * centred, axis=-1, keepdims=True) + EPSILON)
    return centred * inv, inv


def norm_back(grad, gain, unit, inv):
    d_unit = grad * gain
    return inv * (
        d_unit
        - jnp.mean(d_unit, axis=-1, keepdims=True)
        - unit * jnp.mean(d_unit * unit, axis=-1, keepdims=True)
    )


def whole(shape):
    return pl.BlockSpec(shape, lambda *_: (0,) * len(shape), pipeline_mode=pl.Buffered(1))


def rows(width, block=BLOCK):
    return pl.BlockSpec((block, width), lambda i: (i, 0))


def shaped(shape, dtype):
    return jax.ShapeDtypeStruct(shape, dtype)


def hbm():
    return pl.BlockSpec(memory_space=pl.ANY)


def fetch(order, parts, places, sem):
    if order is None:
        for part, (_, _, buffer, _) in zip(parts, places):
            pltpu.make_async_copy(part, buffer, sem).start()
        return
    count = parts[0].shape[0]
    for p, part in enumerate(parts):
        for b in range(count):
            owner = order[p * count + b]
            for first, size, buffer, column in places:
                pltpu.make_async_copy(
                    part.at[b, pl.ds(first, size), :],
                    buffer.at[pl.ds(pl.multiple_of(owner * size, 8), size), pl.ds(column, LANES)],
                    sem,
                ).start()


def arrive(buffers, sem):
    for buffer in buffers:
        pltpu.make_async_copy(buffer, buffer, sem).wait()


def deal(order, total, keep_ref, send_ref, places):
    half = keep_ref.shape[0]

    def one(j, target, at):
        owner = order[at]
        for first, size, buffer, column in places:
            block = buffer[pl.ds(pl.multiple_of(owner * size, 8), size), column : column + LANES]
            target[j, first : first + size, :] = block.astype(target.dtype)

    @pl.loop(0, half)
    def _(j):
        one(j, keep_ref, j)
        one(j, send_ref, j + half)


def slabs(first, size, buffer, width):
    return [(first + s * size, size, buffer, s * LANES) for s in range(width // LANES)]


def spread(rows_in, offset, count, owners):
    lanes = rows_in.shape[1]
    wide = owners * count
    lane = lax.broadcasted_iota(jnp.int32, (lanes, wide), 0)
    column = lax.broadcasted_iota(jnp.int32, (lanes, wide), 1)
    pick = (lane - offset == lax.rem(column, count)).astype(F32).astype(BF)
    full = dot(rows_in, pick)
    owner = lax.broadcasted_iota(jnp.int32, (owners, wide), 0)
    column = lax.broadcasted_iota(jnp.int32, (owners, wide), 1)
    own = (column >= owner * count) & (column < owner * count + count)
    return jnp.sum(jnp.where(own, full, 0.0), axis=0, keepdims=True)


def qkv_kernel(split, sizes, *refs):
    if split:
        order, x_ref, cos_ref, sin_ref, *refs = refs
        parts, refs = refs[:8], refs[8:]
        h_ref, qkv_ref, w_ref, ga_ref, gi_ref, gf_ref, gm_ref, gains, sem, gain_sem = refs
    else:
        order, x_ref, cos_ref, sin_ref, ga_ref, *refs = refs
        parts, refs = refs[:1], refs[1:]
        h_ref, qkv_ref, w_ref, sem = refs
    width = x_ref.shape[1]
    step = pl.program_id(0)
    if split:
        size = width // 32
        weight = slabs(0, size, w_ref, 3 * width)

        @pl.when(step == 0)
        def _():
            fetch(order, parts, [(3 * size, 8, gains, 0)], gain_sem)
            fetch(order, parts, weight, sem)
            arrive([gains], gain_sem)
            owner = lax.broadcasted_iota(jnp.int32, (32, 256), 0)
            lane = lax.broadcasted_iota(jnp.int32, (32, 256), 1)
            pick = (lane == owner * 8).astype(F32).astype(BF)
            per_owner = dot(pick, gains[:, :256]).astype(BF)
            at = 0
            for ref, count in zip((ga_ref, gi_ref, gf_ref, gm_ref), sizes):
                ref[...] = spread(per_owner, at, count, 32)
                at += count
            arrive([w_ref], sem)
    else:

        @pl.when(step == 0)
        def _():
            fetch(None, parts, [(0, 0, w_ref, 0)], sem)
            arrive([w_ref], sem)

    unit, _ = unit_norm(x_ref[...].astype(F32))
    h = (unit * ga_ref[...]).astype(BF)
    h_ref[...] = h
    cos, sin = cos_ref[...], sin_ref[...]
    for part in range(3):
        y = dot(h, w_ref[:, part * width : (part + 1) * width])
        for c in range(width // PAIR):
            z = y[:, c * PAIR : (c + 1) * PAIR]
            if part < 2:
                z = z * cos + swap_halves(z) * sin
            if part == 0:
                z = z * (1.0 / math.sqrt(HEAD_DIM))
            at = part * width + c * PAIR
            qkv_ref[:, at : at + PAIR] = z.astype(BF)


def prefetched(kernel, order, inputs, in_specs, out_specs, out_shape, scratch, grid, mib, name, flops, data):
    return pl.pallas_call(
        kernel,
        grid_spec=pltpu.PrefetchScalarGridSpec(
            num_scalar_prefetch=1,
            grid=grid,
            in_specs=in_specs,
            out_specs=out_specs,
            scratch_shapes=scratch,
        ),
        out_shape=out_shape,
        compiler_params=params(mib),
        cost_estimate=pl.CostEstimate(flops=flops, transcendentals=0, bytes_accessed=data),
        name=name,
    )(order, *inputs)


def rows(width, block=BLOCK):
    return pl.BlockSpec((block, width), lambda i, *_: (i, 0))


def whole(shape):
    return pl.BlockSpec(shape, lambda *_: (0,) * len(shape), pipeline_mode=pl.Buffered(1))


def qkv_forward(split, order, tokens, cos, sin, parts, gain, sizes):
    t, d = tokens.shape
    n = 3 * d
    inputs = [tokens, cos, sin]
    in_specs = [rows(d), rows(PAIR), rows(PAIR)]
    out_specs = [rows(d), rows(n), whole((d, n))]
    out_shape = [shaped((t, d), BF), shaped((t, n), BF), shaped((d, n), BF)]
    scratch = [pltpu.SemaphoreType.DMA]
    if split:
        widths = [32 * s for s in sizes]
        out_specs += [whole((1, w)) for w in widths]
        out_shape += [shaped((1, w), F32) for w in widths]
        scratch = [pltpu.VMEM((32 * 8, LANES), BF), pltpu.SemaphoreType.DMA, pltpu.SemaphoreType.DMA]
    else:
        inputs.append(gain)
        in_specs.append(whole((1, d)))
    return prefetched(
        functools.partial(qkv_kernel, split, sizes), order, inputs + list(parts), in_specs + [hbm()] * len(parts),
        out_specs, out_shape, scratch, (t // BLOCK,), 40, "qkv_forward",
        2 * t * d * n, 4 * d * n + 12 * t * d,
    )


def window(i, n):
    return slice((i - n + 1) * BLOCK, (i + 1) * BLOCK)


def head_masks(shape):
    lane = lax.broadcasted_iota(jnp.int32, shape, 1)
    return lane < HEAD_DIM


def attention_forward_kernel(wide, reach, q_ref, k_ref, v_ref, start_ref, o_ref, lse_ref, bias):
    row, pair = pl.program_id(0), pl.program_id(1)
    seq = q_ref.shape[0]
    blocks = seq // BLOCK

    @pl.when(pair == 0)
    def _():
        for i in range(blocks):
            at = slice(i * BLOCK, (i + 1) * BLOCK)
            shape = (BLOCK, wide * BLOCK)
            key = (i - wide + 1) * BLOCK + lax.broadcasted_iota(jnp.int32, shape, 1)
            query = i * BLOCK + lax.broadcasted_iota(jnp.int32, shape, 0)
            keep = (key >= start_ref[at, :]) & (key <= query)
            bias[at, :] = jnp.where(keep, 0.0, MASKED_SCORE)

    first = head_masks((BLOCK, PAIR))
    for i in range(blocks):
        at = slice(i * BLOCK, (i + 1) * BLOCK)
        most = min(wide, i + 1)
        for n in range(1, most + 1):

            @pl.when(reach[row * blocks + i] == n)
            def _():
                q = q_ref[at, :]
                w = window(i, n)
                k, v = k_ref[w, :], v_ref[w, :]
                b = bias[at, (wide - n) * BLOCK :]
                mask = head_masks(k.shape)
                zero = jnp.zeros_like(k)
                total, lses = None, []
                scale = None
                for h in range(2):
                    pick = mask if h == 0 else jnp.logical_not(mask)
                    s = dot(q, jnp.where(pick, k, zero), ((1,), (1,))) + b
                    top = jnp.max(s, axis=-1, keepdims=True)
                    p = jnp.exp(s - top)
                    den = jnp.sum(p, axis=-1, keepdims=True)
                    probs = (p * (1.0 / den)).astype(BF)
                    part = dot(probs, jnp.where(pick, v, zero))
                    total = part if total is None else total + part
                    lses.append(top + jnp.log(den))
                o_ref[at, :] = total
                both = jnp.where(first, lses[0], lses[1]).T
                lse_ref[0, 0:1, at] = both[0:1, :]
                lse_ref[0, 1:2, at] = both[HEAD_DIM : HEAD_DIM + 1, :]


def attention_forward(reach, qkv, start, row_count, wide):
    t = qkv.shape[0]
    seq = t // row_count
    d = qkv.shape[1] // 3

    def columns(part):
        return pl.BlockSpec((seq, PAIR), lambda r, p, *_: (r, part * PAIRS + p))

    return pl.pallas_call(
        functools.partial(attention_forward_kernel, wide),
        grid_spec=pltpu.PrefetchScalarGridSpec(
            num_scalar_prefetch=1,
            grid=(row_count, PAIRS),
            in_specs=[
                columns(0),
                columns(1),
                columns(2),
                pl.BlockSpec((seq, 1), lambda r, p, *_: (r, 0)),
            ],
            out_specs=[
                pl.BlockSpec((seq, PAIR), lambda r, p, *_: (r, p)),
                pl.BlockSpec((1, 8, seq), lambda r, p, *_: (r * PAIRS + p, 0, 0)),
            ],
            scratch_shapes=[pltpu.VMEM((seq, wide * BLOCK), F32)],
        ),
        out_shape=[shaped((t, d), F32), shaped((row_count * PAIRS, 8, seq), F32)],
        compiler_params=params(32),
        cost_estimate=pl.CostEstimate(
            flops=8 * t * d * BLOCK, transcendentals=t * HEADS * 512, bytes_accessed=12 * t * d
        ),
        name="attention_forward",
    )(reach, qkv, qkv, qkv, start)


def attention_backward_kernel(
    wide, reach, q_ref, k_ref, v_ref, do_ref, o_ref, lse_ref, start_ref, cos_ref, sin_ref,
    dq_ref, dk_ref, dv_ref, bias, ks, vs, qs, dos, dk_acc, dv_acc, dq_acc,
):
    row, pair = pl.program_id(0), pl.program_id(1)
    seq = q_ref.shape[0]
    blocks = seq // BLOCK

    @pl.when(pair == 0)
    def _():
        for i in range(blocks):
            at = slice(i * BLOCK, (i + 1) * BLOCK)
            shape = (wide * BLOCK, BLOCK)
            key = (i - wide + 1) * BLOCK + lax.broadcasted_iota(jnp.int32, shape, 0)
            query = i * BLOCK + lax.broadcasted_iota(jnp.int32, shape, 1)
            keep = (key >= start_ref[0:1, at]) & (key <= query)
            bias[:, at] = jnp.where(keep, 0.0, MASKED_SCORE)

    mask = head_masks((seq, PAIR))
    for src, dst in ((k_ref, ks), (v_ref, vs), (q_ref, qs), (do_ref, dos)):
        x = src[...]
        zero = jnp.zeros_like(x)
        dst[0] = jnp.where(mask, x, zero)
        dst[1] = jnp.where(mask, zero, x)
    dk_acc[...] = jnp.zeros_like(dk_acc)
    dv_acc[...] = jnp.zeros_like(dv_acc)
    lane8 = lax.broadcasted_iota(jnp.int32, (8, PAIR), 1) // HEAD_DIM
    row8 = lax.broadcasted_iota(jnp.int32, (8, PAIR), 0)
    picks = (lane8 == row8).astype(F32)
    delta = lax.dot_general(
        picks, do_ref[...].astype(F32) * o_ref[...], (((1,), (1,)), ((), ())),
        precision=lax.Precision.HIGHEST, preferred_element_type=F32,
    )
    for i in range(blocks):
        at = slice(i * BLOCK, (i + 1) * BLOCK)
        most = min(wide, i + 1)
        for n in range(1, most + 1):

            @pl.when(reach[row * blocks + i] == n)
            def _():
                w = window(i, n)
                b = bias[(wide - n) * BLOCK :, at]
                q, do = q_ref[at, :], do_ref[at, :]
                ps, dss = [], []
                for h in range(2):
                    s = dot(ks[h, w, :], q, ((1,), (1,))) + b
                    p = jnp.exp(s - lse_ref[0, h : h + 1, at])
                    dp = dot(vs[h, w, :], do, ((1,), (1,)))
                    ds = (p * (dp - delta[h : h + 1, at])).astype(BF)
                    ps.append(p.astype(BF))
                    dss.append(ds)
                dv_acc[w, :] += dot(ps[0], dos[0, at, :]) + dot(ps[1], dos[1, at, :])
                dk_acc[w, :] += dot(dss[0], qs[0, at, :]) + dot(dss[1], qs[1, at, :])
                dq_acc[at, :] = dot(dss[0], ks[0, w, :], ((0,), (0,))) + dot(
                    dss[1], ks[1, w, :], ((0,), (0,))
                )

    cos, sin = cos_ref[...], sin_ref[...]
    dq = dq_acc[...] * (1.0 / math.sqrt(HEAD_DIM))
    dk = dk_acc[...]
    dq_ref[...] = (dq * cos - swap_halves(dq) * sin).astype(BF)
    dk_ref[...] = (dk * cos - swap_halves(dk) * sin).astype(BF)
    dv_ref[...] = dv_acc[...].astype(BF)


def attention_backward(reach, qkv, d_mixed, mixed, lse, start_row, cos, sin, row_count, wide):
    t = qkv.shape[0]
    seq = t // row_count
    d = qkv.shape[1] // 3

    def columns(part):
        return pl.BlockSpec((seq, PAIR), lambda r, p, *_: (r, part * PAIRS + p))

    table = pl.BlockSpec((seq, PAIR), lambda r, p, *_: (r, 0))
    return pl.pallas_call(
        functools.partial(attention_backward_kernel, wide),
        grid_spec=pltpu.PrefetchScalarGridSpec(
            num_scalar_prefetch=1,
            grid=(row_count, PAIRS),
            in_specs=[
                columns(0), columns(1), columns(2), columns(0), columns(0),
                pl.BlockSpec((1, 8, seq), lambda r, p, *_: (r * PAIRS + p, 0, 0)),
                pl.BlockSpec((8, seq), lambda r, p, *_: (r, 0)),
                table, table,
            ],
            out_specs=[columns(0)] * 3,
            scratch_shapes=[
                pltpu.VMEM((wide * BLOCK, seq), F32),
                pltpu.VMEM((2, seq, PAIR), BF),
                pltpu.VMEM((2, seq, PAIR), BF),
                pltpu.VMEM((2, seq, PAIR), BF),
                pltpu.VMEM((2, seq, PAIR), BF),
                pltpu.VMEM((seq, PAIR), F32),
                pltpu.VMEM((seq, PAIR), F32),
                pltpu.VMEM((seq, PAIR), F32),
            ],
        ),
        out_shape=[shaped((t, d), BF)] * 3,
        compiler_params=params(40),
        cost_estimate=pl.CostEstimate(
            flops=20 * t * d * BLOCK, transcendentals=t * HEADS * 512, bytes_accessed=20 * t * d
        ),
        name="attention_backward",
    )(reach, qkv, qkv, qkv, d_mixed, mixed, lse, start_row, cos, sin)


def up_kernel(split, *refs):
    order, o_ref, x_ref, gi_ref, gf_ref, gm_ref, *refs = refs
    count = 8 if split else 2
    parts, refs = refs[:count], refs[count:]
    a_ref, x1_ref, h2_ref, m_ref, slope_ref, inv_ref, wo_ref, wu_ref, sem = refs
    d, f = wu_ref.shape
    size = d // 32
    places = [(0, size, wo_ref, 0)] + slabs(size, size, wu_ref, f) if split else [(0, 0, wo_ref, 0), (0, 0, wu_ref, 0)]

    @pl.when(pl.program_id(0) == 0)
    def _():
        fetch(order if split else None, parts, places, sem)

    unit, _ = unit_norm(o_ref[...])
    a = (unit * gi_ref[...]).astype(BF)
    a_ref[...] = a

    @pl.when(pl.program_id(0) == 0)
    def _():
        arrive([wo_ref, wu_ref], sem)

    x1 = x_ref[...].astype(F32) + dot(a, wo_ref[...])
    x1_ref[...] = x1
    unit, _ = unit_norm(x1)
    h2 = (unit * gf_ref[...]).astype(BF)
    h2_ref[...] = h2
    hidden = dot(h2, wu_ref[...])
    cdf = 0.5 + 0.5 * lax.erf(hidden * ROOT_HALF)
    slope = cdf + hidden * (jnp.exp(-0.5 * hidden * hidden) * INV_ROOT_TAU)
    slope_ref[...] = slope.astype(BF)
    unit, inv = unit_norm(hidden * cdf)
    m_ref[...] = (unit * gm_ref[...]).astype(BF)
    inv_ref[...] = jnp.broadcast_to(inv, inv_ref.shape)


def up_forward(split, order, mixed, tokens, gain_inner, gain_ffn, gain_mid, parts):
    t, d = tokens.shape
    f = gain_mid.shape[1]
    return prefetched(
        functools.partial(up_kernel, split), order,
        [mixed, tokens, gain_inner, gain_ffn, gain_mid, *parts],
        [rows(d), rows(d), whole((1, d)), whole((1, d)), whole((1, f))] + [hbm()] * len(parts),
        [rows(d), rows(d), rows(d), rows(f), rows(f), rows(PAIR), whole((d, d)), whole((d, f))],
        [
            shaped((t, d), BF), shaped((t, d), F32), shaped((t, d), BF),
            shaped((t, f), BF), shaped((t, f), BF), shaped((t, PAIR), F32),
            shaped((d, d), BF), shaped((d, f), BF),
        ],
        [pltpu.SemaphoreType.DMA], (t // BLOCK,), 56, "up_forward",
        2 * t * d * (d + f), 4 * d * (d + f) + 4 * t * f + 14 * t * d,
    )


def down_kernel(split, *refs):
    order, back, m_ref, slope_ref, inv_ref, x1_ref, ct_ref, valid_ref, gm_ref, *refs = refs
    count = 8 if split else 1
    parts, refs = refs[:count], refs[count:]
    y_ref, dpre_ref, gg_ref, *refs = refs
    if split:
        keep_ref, send_ref, wd_ref, total, sem = refs
    else:
        total, wd_ref, sem = refs
    f, d = wd_ref.shape
    step = pl.program_id(0)

    @pl.when(step == 0)
    def _():
        fetch(order if split else None, parts, [(0, f // 32, wd_ref, 0)], sem)

    m = m_ref[...]
    gy = jnp.where(valid_ref[...] > 0, ct_ref[...], jnp.zeros_like(ct_ref))
    part = dot(m, gy, ((0,), (0,)))

    @pl.when(step == 0)
    def _():
        total[...] = part
        arrive([wd_ref], sem)

    @pl.when(step > 0)
    def _():
        total[...] += part

    dm = dot(gy, wd_ref[...], ((1,), (1,)))
    gain = gm_ref[...]
    mf = m.astype(F32)
    prod = dm * mf
    d_unit = dm * gain
    d_act = inv_ref[:, 0:1] * (
        d_unit
        - jnp.mean(d_unit, axis=-1, keepdims=True)
        - (mf * (1.0 / gain)) * jnp.mean(prod, axis=-1, keepdims=True)
    )
    dpre_ref[...] = (d_act * slope_ref[...].astype(F32)).astype(BF)
    y_ref[...] = (x1_ref[...] + dot(m, wd_ref[...])).astype(BF)
    gain_part = jnp.sum(prod, axis=0, keepdims=True) * (1.0 / gain)

    @pl.when(step == 0)
    def _():
        gg_ref[...] = gain_part

    @pl.when(step > 0)
    def _():
        gg_ref[...] += gain_part

    if split:

        @pl.when(step == pl.num_programs(0) - 1)
        def _():
            deal(back, total, keep_ref, send_ref, [(0, f // 32, total, 0)])


def dealt(split, size, shapes):
    if split:
        half = (16, size, LANES)
        return [whole(half)] * 2, [shaped(half, F32), shaped(half, BF)], [pltpu.VMEM(s, F32) for s in shapes]
    return [whole(s) for s in shapes], [shaped(s, F32) for s in shapes], []


def prefetched2(kernel, order, back, inputs, in_specs, out_specs, out_shape, scratch, grid, mib, name, flops, data):
    return pl.pallas_call(
        kernel,
        grid_spec=pltpu.PrefetchScalarGridSpec(
            num_scalar_prefetch=2, grid=grid, in_specs=in_specs, out_specs=out_specs, scratch_shapes=scratch,
        ),
        out_shape=out_shape,
        compiler_params=params(mib),
        cost_estimate=pl.CostEstimate(flops=flops, transcendentals=0, bytes_accessed=data),
        name=name,
    )(order, back, *inputs)


def down_both(split, order, back, m, slope, inv, x1, cotangent, valid, gain_mid, parts):
    t, d = x1.shape
    f = m.shape[1]
    out_specs, out_shape, scratch = dealt(split, f // 32, [(f, d)])
    weight = [pltpu.VMEM((f, d), BF)]
    return prefetched2(
        functools.partial(down_kernel, split), order, back,
        [m, slope, inv, x1, cotangent, valid, gain_mid, *parts],
        [rows(f), rows(f), rows(PAIR), rows(d), rows(d), rows(1), whole((1, f))] + [hbm()] * len(parts),
        [rows(d), rows(f), whole((1, f))] + out_specs,
        [shaped((t, d), BF), shaped((t, f), BF), shaped((1, f), F32)] + out_shape,
        weight + scratch + [pltpu.SemaphoreType.DMA], (t // BLOCK,), 60, "down_both",
        6 * t * d * f, 6 * d * f + 6 * t * f + 8 * t * d,
    )


def up_back_kernel(split, *refs):
    order, back, dpre_ref, h2_ref, x1_ref, ct_ref, valid_ref, a_ref, o_ref, wu_ref, wo_ref, gf_ref, gi_ref, *refs = refs
    dx1_ref, do_ref, ggf_ref, ggi_ref, *refs = refs
    if split:
        keep_ref, send_ref, gwo_ref, gwu_ref = refs
    else:
        gwo_ref, gwu_ref = refs
    step = pl.program_id(0)
    dpre = dpre_ref[...]
    part_up = dot(h2_ref[...], dpre, ((0,), (0,)))
    dh2 = dot(dpre, wu_ref[...], ((1,), (1,)))
    unit, inv = unit_norm(x1_ref[...])
    ffn_part = jnp.sum(dh2 * unit, axis=0, keepdims=True)
    gy = jnp.where(valid_ref[...] > 0, ct_ref[...].astype(F32), 0.0)
    dx1 = gy + norm_back(dh2, gf_ref[...], unit, inv)
    dx1_ref[...] = dx1
    low = dx1.astype(BF)
    part_out = dot(a_ref[...], low, ((0,), (0,)))
    da = dot(low, wo_ref[...], ((1,), (1,)))
    unit, inv = unit_norm(o_ref[...])
    inner_part = jnp.sum(da * unit, axis=0, keepdims=True)
    do_ref[...] = norm_back(da, gi_ref[...], unit, inv).astype(BF)

    @pl.when(step == 0)
    def _():
        gwu_ref[...] = part_up
        gwo_ref[...] = part_out
        ggf_ref[...] = ffn_part
        ggi_ref[...] = inner_part

    @pl.when(step > 0)
    def _():
        gwu_ref[...] += part_up
        gwo_ref[...] += part_out
        ggf_ref[...] += ffn_part
        ggi_ref[...] += inner_part

    if split:
        d, f = gwu_ref.shape
        size = d // 32

        @pl.when(step == pl.num_programs(0) - 1)
        def _():
            deal(back, None, keep_ref, send_ref, [(0, size, gwo_ref, 0)] + slabs(size, size, gwu_ref, f))


def up_backward(split, order, back, dpre, h2, x1, cotangent, valid, a, mixed, w_up, w_out, gain_ffn, gain_inner):
    t, d = x1.shape
    f = dpre.shape[1]
    out_specs, out_shape, scratch = dealt(split, (d + f) // 32, [(d, d), (d, f)])
    return prefetched2(
        functools.partial(up_back_kernel, split), order, back,
        [dpre, h2, x1, cotangent, valid, a, mixed, w_up, w_out, gain_ffn, gain_inner],
        [rows(f), rows(d), rows(d), rows(d), rows(1), rows(d), rows(d),
         whole((d, f)), whole((d, d)), whole((1, d)), whole((1, d))],
        [rows(d), rows(d), whole((1, d)), whole((1, d))] + out_specs,
        [shaped((t, d), F32), shaped((t, d), BF), shaped((1, d), F32), shaped((1, d), F32)] + out_shape,
        scratch, (t // BLOCK,), 60, "up_backward",
        4 * t * d * (d + f), 6 * d * (d + f) + 2 * t * f + 24 * t * d,
    )


def qkv_grad_kernel(split, *refs):
    order, back, h_ref, dq_ref, dk_ref, dv_ref, *refs = refs
    if split:
        keep_ref, send_ref, g_ref = refs
    else:
        (g_ref,) = refs
    step = pl.program_id(0)
    h = h_ref[...]
    d = h.shape[1]
    for c, ref in enumerate((dq_ref, dk_ref, dv_ref)):
        part = dot(h, ref[...], ((0,), (0,)))
        cols = slice(c * d, (c + 1) * d)

        @pl.when(step == 0)
        def _():
            g_ref[:, cols] = part

        @pl.when(step > 0)
        def _():
            g_ref[:, cols] += part

    if split:

        @pl.when(step == pl.num_programs(0) - 1)
        def _():
            deal(back, None, keep_ref, send_ref, slabs(0, d // 32, g_ref, 3 * d))


def qkv_weight_grad(split, order, back, h, dq, dk, dv):
    t, d = h.shape
    out_specs, out_shape, scratch = dealt(split, 3 * d // 32, [(d, 3 * d)])
    return prefetched2(
        functools.partial(qkv_grad_kernel, split), order, back,
        [h, dq, dk, dv], [rows(d)] * 4, out_specs, out_shape, scratch,
        (t // BLOCK,), 40, "qkv_weight_grad", 6 * t * d * d, 12 * d * d + 8 * t * d,
    )


def qkv_back_kernel(dq_ref, dk_ref, dv_ref, x_ref, dx1_ref, w_ref, gain_ref, dx_ref, gg_ref):
    step = pl.program_id(0)
    d = x_ref.shape[1]
    dh = None
    for c, ref in enumerate((dq_ref, dk_ref, dv_ref)):
        part = dot(ref[...], w_ref[:, c * d : (c + 1) * d], ((1,), (1,)))
        dh = part if dh is None else dh + part
    unit, inv = unit_norm(x_ref[...].astype(F32))
    gain_part = jnp.sum(dh * unit, axis=0, keepdims=True)
    dx_ref[...] = dx1_ref[...] + norm_back(dh, gain_ref[...], unit, inv)

    @pl.when(step == 0)
    def _():
        gg_ref[...] = gain_part

    @pl.when(step > 0)
    def _():
        gg_ref[...] += gain_part


def qkv_backward(dq, dk, dv, tokens, dx1, w_qkv, gain):
    t, d = tokens.shape
    return pl.pallas_call(
        qkv_back_kernel,
        grid=(t // BLOCK,),
        in_specs=[rows(d)] * 5 + [whole((d, 3 * d)), whole((1, d))],
        out_specs=[rows(d), whole((1, d))],
        out_shape=[shaped((t, d), F32), shaped((1, d), F32)],
        compiler_params=params(48),
        cost_estimate=pl.CostEstimate(flops=6 * t * d * d, transcendentals=0, bytes_accessed=6 * d * d + 16 * t * d),
        name="qkv_backward",
    )(dq, dk, dv, tokens, dx1, w_qkv, gain)


def layout(doc_lengths, seq):
    docs = doc_lengths.shape[-1]
    upto = jnp.arange(docs)[:, None] <= jnp.arange(docs)[None, :]
    ends = jnp.sum(jnp.where(upto[None], doc_lengths[:, :, None], 0), axis=1)
    places = jnp.arange(seq, dtype=jnp.int32)
    passed = places[None, :, None] >= ends[:, None, :]
    start = jnp.sum(jnp.where(passed, doc_lengths[:, None, :], 0), axis=-1)
    valid = places[None, :] < ends[:, docs - 2 : docs - 1]
    return start.astype(jnp.int32), places[None, :] - start, valid


def tables(position):
    half = HEAD_DIM // 2
    lane = jnp.arange(PAIR)
    frequency = jnp.exp((lane % half).astype(F32) * (-2.0 * math.log(10000.0) / HEAD_DIM))
    angles = position.reshape(-1, 1).astype(F32) * frequency[None, :]
    sign = jnp.where(lane % HEAD_DIM < half, -1.0, 1.0)
    return jnp.cos(angles), jnp.sin(angles) * sign[None, :]


Z = 4
GROUPS = ((0, 2), (1, 3))


def index(x, core, z, y):
    return ((x * 2 + core) * Z + z) * 2 + y


def permute(value, move):
    places = [(x, c, z, y) for x in range(2) for c in range(2) for z in range(Z) for y in range(2)]
    return lax.ppermute(value, AXES, [(index(*p), index(*move(*p))) for p in places])


def over_x(v):
    return permute(v, lambda x, c, z, y: (1 - x, c, z, y))


def over_y(v):
    return permute(v, lambda x, c, z, y: (x, c, z, 1 - y))


def over_core(v):
    return permute(v, lambda x, c, z, y: (x, 1 - c, z, y))


def over_z(v, shift):
    return permute(v, lambda x, c, z, y: (x, c, (z + shift) % Z, y))


def across_z(v, bit):
    return permute(v, lambda x, c, z, y: (x, c, z ^ bit, y))


def place():
    dp, fs = lax.axis_index("dp"), lax.axis_index("fsdp")
    return dp // 2, dp % 2, fs // 2, fs % 2


def gather_order():
    x, c, z, y = place()
    order = []
    for core in range(2):
        for group, first in zip(GROUPS, ("x", "y")):
            for second in range(2):
                for one in range(2):
                    dx, dy = (one, second) if first == "x" else (second, one)
                    for shift in group:
                        order.append(index(x ^ dx, c ^ core, (z - shift) % Z, y ^ dy))
    return jnp.stack(order).astype(jnp.int32)


def scatter_order():
    x, c, z, y = place()
    order = []
    for core in range(2):
        for group, first in zip(GROUPS, ("y", "x")):
            for one in (1, 0):
                for second in (1, 0):
                    dx, dy = (second, one) if first == "y" else (one, second)
                    for shift in group:
                        order.append(index(x ^ dx, c ^ core, (z + shift) % Z, y ^ dy))
    return jnp.stack(order).astype(jnp.int32)


def tie(value, other):
    return lax.optimization_barrier((value, other))[0]


def gather_z(block):
    return [block] + [over_z(block, s) for s in (1, 2, 3)]


def gather_xy(by_z):
    even = jnp.stack([by_z[s] for s in GROUPS[0]])
    odd = jnp.stack([by_z[s] for s in GROUPS[1]])
    even = jnp.concatenate([even, over_x(even)])
    odd = jnp.concatenate([odd, over_y(odd)])
    return [even, over_y(even), odd, over_x(odd)]


def gather_core(parts):
    return parts + [over_core(p) for p in parts]


def reduce_blocks(keep, send):
    total = keep + over_core(send).astype(F32)
    a, b = total[:8], total[8:]
    a = a[4:] + over_y(a[:4].astype(BF)).astype(F32)
    b = b[4:] + over_x(b[:4].astype(BF)).astype(F32)
    a = a[2:] + over_x(a[:2].astype(BF)).astype(F32)
    b = b[2:] + over_y(b[:2].astype(BF)).astype(F32)
    r1, r2, r3 = over_z(b[0].astype(BF), 1), over_z(a[1].astype(BF), 2), over_z(b[1].astype(BF), 3)
    return a[0] + r1.astype(F32) + r2.astype(F32) + r3.astype(F32)


def unslab(block, width):
    size = block.shape[0] * LANES // width
    return jnp.concatenate([block[s * size : (s + 1) * size] for s in range(width // LANES)], axis=1)


def slab(block):
    return [block[:, s * LANES : (s + 1) * LANES] for s in range(block.shape[1] // LANES)]


def local(fast, tokens, doc_lengths, cotangent, w_qkv, w_out, w_up, w_down,
          gain_attn, gain_inner, gain_ffn, gain_mid):
    row_count = doc_lengths.shape[0]
    seq = tokens.shape[0] // row_count
    wide = min(seq, 512) // BLOCK + 1
    blocks = seq // BLOCK
    shards = (gain_attn, gain_inner, gain_ffn, gain_mid)
    sizes = [g.shape[0] for g in shards]
    if fast:
        order, back = gather_order(), scatter_order()
        gains_row = jnp.pad(jnp.concatenate(shards)[None], ((0, 7), (0, LANES - sum(sizes))))
        first = gather_z(jnp.concatenate(slab(w_qkv) + [gains_row]))
        mine = tie(jnp.concatenate([w_out] + slab(w_up)), first[1:])
        second = gather_z(mine)
        third = gather_z(tie(w_down, second[1:]))
        parts_qkv = gather_xy(first)
        parts_up = gather_xy([tie(second[0], parts_qkv)] + second[1:])
        parts_down = gather_xy([tie(third[0], parts_up)] + third[1:])
        parts_qkv, parts_up, parts_down = (gather_core(p) for p in (parts_qkv, parts_up, parts_down))
        gains = None
    else:
        order = back = jnp.zeros((8,), jnp.int32)

        def gather(v):
            return lax.all_gather(v, AXES, axis=0, tiled=True)

        parts_qkv, parts_up, parts_down = [gather(w_qkv)], [gather(w_out), gather(w_up)], [gather(w_down)]
        gains = [gather(g).astype(F32).reshape(1, -1) for g in shards]

    start, position, valid = layout(doc_lengths, seq)
    cos, sin = tables(position)
    firsts = start[:, ::BLOCK] // BLOCK
    reach = (jnp.arange(blocks, dtype=jnp.int32)[None, :] - firsts + 1).reshape(-1)
    start_col = start.reshape(-1, 1)
    start_row = jnp.repeat(start, 8, axis=0)
    valid_col = valid.astype(jnp.int32).reshape(-1, 1)

    h1, qkv, full_qkv, *rest = qkv_forward(
        fast, order, tokens, cos, sin, parts_qkv, None if fast else gains[0], sizes
    )
    g_attn, g_inner, g_ffn, g_mid = rest if fast else gains
    mixed, lse = attention_forward(reach, qkv, start_col, row_count, wide)
    a, x1, h2, m, slope, inv, full_out, full_up = up_forward(
        fast, order, mixed, tokens, g_inner, g_ffn, g_mid, parts_up
    )
    result, dpre, grad_mid, *grad_down = down_both(
        fast, order, back, m, slope, inv, x1, cotangent, valid_col, g_mid, parts_down
    )
    dx1, d_mixed, grad_ffn, grad_inner, *grad_up = up_backward(
        fast, order, back, dpre, h2, x1, cotangent, valid_col, a, mixed, full_up, full_out, g_ffn, g_inner
    )
    dq, dk, dv = attention_backward(reach, qkv, d_mixed, mixed, lse, start_row, cos, sin, row_count, wide)
    grad_qkv = qkv_weight_grad(fast, order, back, h1, dq, dk, dv)
    grad_tokens, grad_attn = qkv_backward(dq, dk, dv, tokens, dx1, full_qkv, g_attn)
    gain_grads = (grad_attn, grad_inner, grad_ffn, grad_mid)
    if fast:
        own_down = reduce_blocks(*grad_down)
        own_up = reduce_blocks(*grad_up)
        own_qkv = reduce_blocks(*grad_qkv)
        cut = w_out.shape[0]
        weights = (unslab(own_qkv, w_qkv.shape[1]), own_up[:cut], unslab(own_up[cut:], w_up.shape[1]), own_down)
        packed = jnp.concatenate([g.reshape(-1, LANES) for g in gain_grads])
        packed = jnp.pad(packed, ((0, -packed.shape[0] % 8), (0, 0)))
        for move in (over_core, over_x, over_y, lambda v: across_z(v, 1), lambda v: across_z(v, 2)):
            packed = packed + move(packed)
        me = index(*place())
        summed, at = [], 0
        for size, full in zip(sizes, gain_grads):
            flat = packed[at : at + full.size // LANES].reshape(-1)
            summed.append(lax.dynamic_slice(flat, (me * size,), (size,)))
            at += full.size // LANES
        return (result, grad_tokens) + weights + tuple(summed)

    def scatter(g):
        return lax.psum_scatter(g, AXES, scatter_dimension=0, tiled=True)

    order_of = (grad_qkv[0], grad_up[0], grad_up[1], grad_down[0])
    weights = tuple(scatter(g.astype(BF)).astype(F32) for g in order_of)
    return (result, grad_tokens) + weights + tuple(scatter(g.reshape(-1)) for g in gain_grads)


def solution(mesh):
    matrix, vector = P(AXES, None), P(AXES)
    fast = mesh.shape["dp"] == 4 and mesh.shape["fsdp"] == 2 * Z
    return jax.shard_map(
        functools.partial(local, fast),
        mesh=mesh,
        in_specs=(matrix,) * 7 + (vector,) * 4,
        out_specs=(matrix,) * 6 + (vector,) * 4,
        check_vma=False,
    )
```

```python
import functools
import math

import jax
import jax.numpy as jnp
from jax import lax
from jax.experimental import pallas as pl
from jax.experimental.pallas import tpu as pltpu
from jax.sharding import PartitionSpec as P

HEADS = 12
HEAD_DIM = 64
PAIR = 2 * HEAD_DIM
PAIRS = HEADS // 2
EPSILON = 1e-05
MASKED_SCORE = -1e30
ROOT_HALF = 0.7071067811865476
INV_ROOT_TAU = 0.3989422804014327
BF = jnp.bfloat16
F32 = jnp.float32
MIB = 1 << 20
AXES = ("dp", "fsdp")
BLOCK = 256
LANES = 768


def dot(a, b, dims=((1,), (0,))):
    return lax.dot_general(a, b, (dims, ((), ())), preferred_element_type=F32)


def params(mib):
    return pltpu.CompilerParams(vmem_limit_bytes=mib * MIB)


def swap_halves(x):
    lane = lax.broadcasted_iota(jnp.int32, x.shape, 1)
    low = lax.rem(lane, HEAD_DIM) < HEAD_DIM // 2
    half = HEAD_DIM // 2
    return jnp.where(low, pltpu.roll(x, PAIR - half, 1), pltpu.roll(x, half, 1))


def unit_norm(x):
    mean = jnp.mean(x, axis=-1, keepdims=True)
    centred = x - mean
    inv = lax.rsqrt(jnp.mean(centred * centred, axis=-1, keepdims=True) + EPSILON)
    return centred * inv, inv


def norm_back(grad, gain, unit, inv):
    d_unit = grad * gain
    return inv * (
        d_unit
        - jnp.mean(d_unit, axis=-1, keepdims=True)
        - unit * jnp.mean(d_unit * unit, axis=-1, keepdims=True)
    )


def whole(shape):
    return pl.BlockSpec(shape, lambda *_: (0,) * len(shape), pipeline_mode=pl.Buffered(1))


def rows(width, block=BLOCK):
    return pl.BlockSpec((block, width), lambda i: (i, 0))


def shaped(shape, dtype):
    return jax.ShapeDtypeStruct(shape, dtype)


def hbm():
    return pl.BlockSpec(memory_space=pl.ANY)


def fetch(order, parts, places, sem):
    if order is None:
        for part, (_, _, buffer, _) in zip(parts, places):
            pltpu.make_async_copy(part, buffer, sem).start()
        return
    count = parts[0].shape[0]
    for p, part in enumerate(parts):
        for b in range(count):
            owner = order[p * count + b]
            for first, size, buffer, column in places:
                pltpu.make_async_copy(
                    part.at[b, pl.ds(first, size), :],
                    buffer.at[pl.ds(pl.multiple_of(owner * size, 8), size), pl.ds(column, LANES)],
                    sem,
                ).start()


def arrive(buffers, sem):
    for buffer in buffers:
        pltpu.make_async_copy(buffer, buffer, sem).wait()


def deal(order, keep_ref, send_ref, places):
    half = keep_ref.shape[0]

    def one(j, target, at):
        owner = order[at]
        for first, size, buffer, column in places:
            block = buffer[pl.ds(pl.multiple_of(owner * size, 8), size), column : column + LANES]
            target[j, first : first + size, :] = block.astype(target.dtype)

    @pl.loop(0, half)
    def _(j):
        one(j, keep_ref, j)
        one(j, send_ref, j + half)


def slabs(first, size, buffer, width):
    return [(first + s * size, size, buffer, s * LANES) for s in range(width // LANES)]


def spread(rows_in, offset, count, owners):
    lanes = rows_in.shape[1]
    wide = owners * count
    lane = lax.broadcasted_iota(jnp.int32, (lanes, wide), 0)
    column = lax.broadcasted_iota(jnp.int32, (lanes, wide), 1)
    pick = (lane - offset == lax.rem(column, count)).astype(F32).astype(BF)
    full = dot(rows_in, pick)
    owner = lax.broadcasted_iota(jnp.int32, (owners, wide), 0)
    column = lax.broadcasted_iota(jnp.int32, (owners, wide), 1)
    own = (column >= owner * count) & (column < owner * count + count)
    return jnp.sum(jnp.where(own, full, 0.0), axis=0, keepdims=True)


def qkv_kernel(split, sizes, *refs):
    if split:
        order, x_ref, cos_ref, sin_ref, *refs = refs
        parts, refs = refs[:8], refs[8:]
        h_ref, qkv_ref, w_ref, ga_ref, gi_ref, gf_ref, gm_ref, gains, sem, gain_sem = refs
    else:
        order, x_ref, cos_ref, sin_ref, ga_ref, *refs = refs
        parts, refs = refs[:1], refs[1:]
        h_ref, qkv_ref, w_ref, sem = refs
    width = x_ref.shape[1]
    step = pl.program_id(0)
    if split:
        size = width // 32
        weight = slabs(0, size, w_ref, 3 * width)

        @pl.when(step == 0)
        def _():
            fetch(order, parts, [(3 * size, 8, gains, 0)], gain_sem)
            fetch(order, parts, weight, sem)
            arrive([gains], gain_sem)
            owner = lax.broadcasted_iota(jnp.int32, (32, 256), 0)
            lane = lax.broadcasted_iota(jnp.int32, (32, 256), 1)
            pick = (lane == owner * 8).astype(F32).astype(BF)
            per_owner = dot(pick, gains[:, :256]).astype(BF)
            at = 0
            for ref, count in zip((ga_ref, gi_ref, gf_ref, gm_ref), sizes):
                ref[...] = spread(per_owner, at, count, 32)
                at += count
            arrive([w_ref], sem)
    else:

        @pl.when(step == 0)
        def _():
            fetch(None, parts, [(0, 0, w_ref, 0)], sem)
            arrive([w_ref], sem)

    unit, _ = unit_norm(x_ref[...].astype(F32))
    h = (unit * ga_ref[...]).astype(BF)
    h_ref[...] = h
    cos, sin = cos_ref[...], sin_ref[...]
    for part in range(3):
        y = dot(h, w_ref[:, part * width : (part + 1) * width])
        for c in range(width // PAIR):
            z = y[:, c * PAIR : (c + 1) * PAIR]
            if part < 2:
                z = z * cos + swap_halves(z) * sin
            if part == 0:
                z = z * (1.0 / math.sqrt(HEAD_DIM))
            at = part * width + c * PAIR
            qkv_ref[:, at : at + PAIR] = z.astype(BF)


def prefetched(kernel, order, inputs, in_specs, out_specs, out_shape, scratch, grid, mib, name, flops, data):
    return pl.pallas_call(
        kernel,
        grid_spec=pltpu.PrefetchScalarGridSpec(
            num_scalar_prefetch=1,
            grid=grid,
            in_specs=in_specs,
            out_specs=out_specs,
            scratch_shapes=scratch,
        ),
        out_shape=out_shape,
        compiler_params=params(mib),
        cost_estimate=pl.CostEstimate(flops=flops, transcendentals=0, bytes_accessed=data),
        name=name,
    )(order, *inputs)


def rows(width, block=BLOCK):
    return pl.BlockSpec((block, width), lambda i, *_: (i, 0))


def whole(shape):
    return pl.BlockSpec(shape, lambda *_: (0,) * len(shape), pipeline_mode=pl.Buffered(1))


def qkv_forward(split, order, tokens, cos, sin, parts, gain, sizes):
    t, d = tokens.shape
    n = 3 * d
    inputs = [tokens, cos, sin]
    in_specs = [rows(d), rows(PAIR), rows(PAIR)]
    out_specs = [rows(d), rows(n), whole((d, n))]
    out_shape = [shaped((t, d), BF), shaped((t, n), BF), shaped((d, n), BF)]
    scratch = [pltpu.SemaphoreType.DMA]
    if split:
        widths = [32 * s for s in sizes]
        out_specs += [whole((1, w)) for w in widths]
        out_shape += [shaped((1, w), F32) for w in widths]
        scratch = [pltpu.VMEM((32 * 8, LANES), BF), pltpu.SemaphoreType.DMA, pltpu.SemaphoreType.DMA]
    else:
        inputs.append(gain)
        in_specs.append(whole((1, d)))
    return prefetched(
        functools.partial(qkv_kernel, split, sizes), order, inputs + list(parts), in_specs + [hbm()] * len(parts),
        out_specs, out_shape, scratch, (t // BLOCK,), 40, "qkv_forward",
        2 * t * d * n, 4 * d * n + 12 * t * d,
    )


def window(i, n):
    return slice((i - n + 1) * BLOCK, (i + 1) * BLOCK)


def head_masks(shape):
    lane = lax.broadcasted_iota(jnp.int32, shape, 1)
    return lane < HEAD_DIM


def attention_forward_kernel(wide, reach, q_ref, k_ref, v_ref, start_ref, o_ref, lse_ref, bias):
    row, pair = pl.program_id(0), pl.program_id(1)
    seq = q_ref.shape[0]
    blocks = seq // BLOCK

    @pl.when(pair == 0)
    def _():
        for i in range(blocks):
            at = slice(i * BLOCK, (i + 1) * BLOCK)
            shape = (BLOCK, wide * BLOCK)
            key = (i - wide + 1) * BLOCK + lax.broadcasted_iota(jnp.int32, shape, 1)
            query = i * BLOCK + lax.broadcasted_iota(jnp.int32, shape, 0)
            keep = (key >= start_ref[at, :]) & (key <= query)
            bias[at, :] = jnp.where(keep, 0.0, MASKED_SCORE)

    first = head_masks((BLOCK, PAIR))
    for i in range(blocks):
        at = slice(i * BLOCK, (i + 1) * BLOCK)
        most = min(wide, i + 1)
        for n in range(1, most + 1):

            @pl.when(reach[row * blocks + i] == n)
            def _():
                q = q_ref[at, :]
                w = window(i, n)
                k, v = k_ref[w, :], v_ref[w, :]
                b = bias[at, (wide - n) * BLOCK :]
                mask = head_masks(k.shape)
                zero = jnp.zeros_like(k)
                total, lses = None, []
                scale = None
                for h in range(2):
                    pick = mask if h == 0 else jnp.logical_not(mask)
                    s = dot(q, jnp.where(pick, k, zero), ((1,), (1,))) + b
                    top = jnp.max(s, axis=-1, keepdims=True)
                    p = jnp.exp(s - top)
                    den = jnp.sum(p, axis=-1, keepdims=True)
                    probs = (p * (1.0 / den)).astype(BF)
                    part = dot(probs, jnp.where(pick, v, zero))
                    total = part if total is None else total + part
                    lses.append(top + jnp.log(den))
                o_ref[at, :] = total
                both = jnp.where(first, lses[0], lses[1]).T
                lse_ref[0, 0:1, at] = both[0:1, :]
                lse_ref[0, 1:2, at] = both[HEAD_DIM : HEAD_DIM + 1, :]


def attention_forward(reach, qkv, start, row_count, wide):
    t = qkv.shape[0]
    seq = t // row_count
    d = qkv.shape[1] // 3

    def columns(part):
        return pl.BlockSpec((seq, PAIR), lambda r, p, *_: (r, part * PAIRS + p))

    return pl.pallas_call(
        functools.partial(attention_forward_kernel, wide),
        grid_spec=pltpu.PrefetchScalarGridSpec(
            num_scalar_prefetch=1,
            grid=(row_count, PAIRS),
            in_specs=[
                columns(0),
                columns(1),
                columns(2),
                pl.BlockSpec((seq, 1), lambda r, p, *_: (r, 0)),
            ],
            out_specs=[
                pl.BlockSpec((seq, PAIR), lambda r, p, *_: (r, p)),
                pl.BlockSpec((1, 8, seq), lambda r, p, *_: (r * PAIRS + p, 0, 0)),
            ],
            scratch_shapes=[pltpu.VMEM((seq, wide * BLOCK), F32)],
        ),
        out_shape=[shaped((t, d), F32), shaped((row_count * PAIRS, 8, seq), F32)],
        compiler_params=params(32),
        cost_estimate=pl.CostEstimate(
            flops=8 * t * d * BLOCK, transcendentals=t * HEADS * 512, bytes_accessed=12 * t * d
        ),
        name="attention_forward",
    )(reach, qkv, qkv, qkv, start)


def attention_backward_kernel(
    wide, reach, q_ref, k_ref, v_ref, do_ref, o_ref, lse_ref, start_ref, cos_ref, sin_ref,
    dq_ref, dk_ref, dv_ref, bias, ks, vs, qs, dos, dk_acc, dv_acc, dq_acc,
):
    row, pair = pl.program_id(0), pl.program_id(1)
    seq = q_ref.shape[0]
    blocks = seq // BLOCK

    @pl.when(pair == 0)
    def _():
        for i in range(blocks):
            at = slice(i * BLOCK, (i + 1) * BLOCK)
            shape = (wide * BLOCK, BLOCK)
            key = (i - wide + 1) * BLOCK + lax.broadcasted_iota(jnp.int32, shape, 0)
            query = i * BLOCK + lax.broadcasted_iota(jnp.int32, shape, 1)
            keep = (key >= start_ref[0:1, at]) & (key <= query)
            bias[:, at] = jnp.where(keep, 0.0, MASKED_SCORE)

    mask = head_masks((seq, PAIR))
    for src, dst in ((k_ref, ks), (v_ref, vs), (q_ref, qs), (do_ref, dos)):
        x = src[...]
        zero = jnp.zeros_like(x)
        dst[0] = jnp.where(mask, x, zero)
        dst[1] = jnp.where(mask, zero, x)
    dk_acc[...] = jnp.zeros_like(dk_acc)
    dv_acc[...] = jnp.zeros_like(dv_acc)
    lane8 = lax.broadcasted_iota(jnp.int32, (8, PAIR), 1) // HEAD_DIM
    row8 = lax.broadcasted_iota(jnp.int32, (8, PAIR), 0)
    picks = (lane8 == row8).astype(F32)
    delta = lax.dot_general(
        picks, do_ref[...].astype(F32) * o_ref[...], (((1,), (1,)), ((), ())),
        precision=lax.Precision.HIGHEST, preferred_element_type=F32,
    )
    for i in range(blocks):
        at = slice(i * BLOCK, (i + 1) * BLOCK)
        most = min(wide, i + 1)
        for n in range(1, most + 1):

            @pl.when(reach[row * blocks + i] == n)
            def _():
                w = window(i, n)
                b = bias[(wide - n) * BLOCK :, at]
                q, do = q_ref[at, :], do_ref[at, :]
                ps, dss = [], []
                for h in range(2):
                    s = dot(ks[h, w, :], q, ((1,), (1,))) + b
                    p = jnp.exp(s - lse_ref[0, h : h + 1, at])
                    dp = dot(vs[h, w, :], do, ((1,), (1,)))
                    ds = (p * (dp - delta[h : h + 1, at])).astype(BF)
                    ps.append(p.astype(BF))
                    dss.append(ds)
                dv_acc[w, :] += dot(ps[0], dos[0, at, :]) + dot(ps[1], dos[1, at, :])
                dk_acc[w, :] += dot(dss[0], qs[0, at, :]) + dot(dss[1], qs[1, at, :])
                dq_acc[at, :] = dot(dss[0], ks[0, w, :], ((0,), (0,))) + dot(
                    dss[1], ks[1, w, :], ((0,), (0,))
                )

    cos, sin = cos_ref[...], sin_ref[...]
    dq = dq_acc[...] * (1.0 / math.sqrt(HEAD_DIM))
    dk = dk_acc[...]
    dq_ref[...] = (dq * cos - swap_halves(dq) * sin).astype(BF)
    dk_ref[...] = (dk * cos - swap_halves(dk) * sin).astype(BF)
    dv_ref[...] = dv_acc[...].astype(BF)


def attention_backward(reach, qkv, d_mixed, mixed, lse, start_row, cos, sin, row_count, wide, base, pairs):
    t = qkv.shape[0]
    seq = t // row_count
    d = pairs * PAIR

    def columns(part):
        return pl.BlockSpec((seq, PAIR), lambda r, p, *_: (r, part * PAIRS + base + p))

    table = pl.BlockSpec((seq, PAIR), lambda r, p, *_: (r, 0))
    return pl.pallas_call(
        functools.partial(attention_backward_kernel, wide),
        grid_spec=pltpu.PrefetchScalarGridSpec(
            num_scalar_prefetch=1,
            grid=(row_count, pairs),
            in_specs=[
                columns(0), columns(1), columns(2), columns(0), columns(0),
                pl.BlockSpec((1, 8, seq), lambda r, p, *_: (r * PAIRS + base + p, 0, 0)),
                pl.BlockSpec((8, seq), lambda r, p, *_: (r, 0)),
                table, table,
            ],
            out_specs=[pl.BlockSpec((seq, PAIR), lambda r, p, *_: (r, p))] * 3,
            scratch_shapes=[
                pltpu.VMEM((wide * BLOCK, seq), F32),
                pltpu.VMEM((2, seq, PAIR), BF),
                pltpu.VMEM((2, seq, PAIR), BF),
                pltpu.VMEM((2, seq, PAIR), BF),
                pltpu.VMEM((2, seq, PAIR), BF),
                pltpu.VMEM((seq, PAIR), F32),
                pltpu.VMEM((seq, PAIR), F32),
                pltpu.VMEM((seq, PAIR), F32),
            ],
        ),
        out_shape=[shaped((t, d), BF)] * 3,
        compiler_params=params(40),
        cost_estimate=pl.CostEstimate(
            flops=20 * t * d * BLOCK, transcendentals=t * HEADS * 512, bytes_accessed=20 * t * d
        ),
        name="attention_backward",
    )(reach, qkv, qkv, qkv, d_mixed, mixed, lse, start_row, cos, sin)


def up_kernel(split, *refs):
    order, o_ref, x_ref, gi_ref, gf_ref, gm_ref, *refs = refs
    count = 8 if split else 2
    parts, refs = refs[:count], refs[count:]
    a_ref, x1_ref, h2_ref, m_ref, slope_ref, inv_ref, wo_ref, wu_ref, sem = refs
    d, f = wu_ref.shape
    size = d // 32
    places = [(0, size, wo_ref, 0)] + slabs(size, size, wu_ref, f) if split else [(0, 0, wo_ref, 0), (0, 0, wu_ref, 0)]

    @pl.when(pl.program_id(0) == 0)
    def _():
        fetch(order if split else None, parts, places, sem)

    unit, _ = unit_norm(o_ref[...])
    a = (unit * gi_ref[...]).astype(BF)
    a_ref[...] = a

    @pl.when(pl.program_id(0) == 0)
    def _():
        arrive([wo_ref, wu_ref], sem)

    x1 = x_ref[...].astype(F32) + dot(a, wo_ref[...])
    x1_ref[...] = x1
    unit, _ = unit_norm(x1)
    h2 = (unit * gf_ref[...]).astype(BF)
    h2_ref[...] = h2
    hidden = dot(h2, wu_ref[...])
    cdf = 0.5 + 0.5 * lax.erf(hidden * ROOT_HALF)
    slope = cdf + hidden * (jnp.exp(-0.5 * hidden * hidden) * INV_ROOT_TAU)
    slope_ref[...] = slope.astype(BF)
    unit, inv = unit_norm(hidden * cdf)
    m_ref[...] = (unit * gm_ref[...]).astype(BF)
    inv_ref[...] = jnp.broadcast_to(inv, inv_ref.shape)


def up_forward(split, order, mixed, tokens, gain_inner, gain_ffn, gain_mid, parts):
    t, d = tokens.shape
    f = gain_mid.shape[1]
    return prefetched(
        functools.partial(up_kernel, split), order,
        [mixed, tokens, gain_inner, gain_ffn, gain_mid, *parts],
        [rows(d), rows(d), whole((1, d)), whole((1, d)), whole((1, f))] + [hbm()] * len(parts),
        [rows(d), rows(d), rows(d), rows(f), rows(f), rows(PAIR), whole((d, d)), whole((d, f))],
        [
            shaped((t, d), BF), shaped((t, d), F32), shaped((t, d), BF),
            shaped((t, f), BF), shaped((t, f), BF), shaped((t, PAIR), F32),
            shaped((d, d), BF), shaped((d, f), BF),
        ],
        [pltpu.SemaphoreType.DMA], (t // BLOCK,), 56, "up_forward",
        2 * t * d * (d + f), 4 * d * (d + f) + 4 * t * f + 14 * t * d,
    )


def down_kernel(split, *refs):
    order, back, m_ref, slope_ref, inv_ref, x1_ref, ct_ref, valid_ref, gm_ref, *refs = refs
    count = 8 if split else 1
    parts, refs = refs[:count], refs[count:]
    y_ref, dpre_ref, gg_ref, *refs = refs
    if split:
        keep_ref, send_ref, wd_ref, total, sem = refs
    else:
        total, wd_ref, sem = refs
    f, d = wd_ref.shape
    step = pl.program_id(0)

    @pl.when(step == 0)
    def _():
        fetch(order if split else None, parts, [(0, f // 32, wd_ref, 0)], sem)

    m = m_ref[...]
    gy = jnp.where(valid_ref[...] > 0, ct_ref[...], jnp.zeros_like(ct_ref))
    part = dot(m, gy, ((0,), (0,)))

    @pl.when(step == 0)
    def _():
        total[...] = part
        arrive([wd_ref], sem)

    @pl.when(step > 0)
    def _():
        total[...] += part

    dm = dot(gy, wd_ref[...], ((1,), (1,)))
    gain = gm_ref[...]
    mf = m.astype(F32)
    prod = dm * mf
    d_unit = dm * gain
    d_act = inv_ref[:, 0:1] * (
        d_unit
        - jnp.mean(d_unit, axis=-1, keepdims=True)
        - (mf * (1.0 / gain)) * jnp.mean(prod, axis=-1, keepdims=True)
    )
    dpre_ref[...] = (d_act * slope_ref[...].astype(F32)).astype(BF)
    y_ref[...] = (x1_ref[...] + dot(m, wd_ref[...])).astype(BF)
    gain_part = jnp.sum(prod, axis=0, keepdims=True) * (1.0 / gain)

    @pl.when(step == 0)
    def _():
        gg_ref[...] = gain_part

    @pl.when(step > 0)
    def _():
        gg_ref[...] += gain_part

    if split:

        @pl.when(step == pl.num_programs(0) - 1)
        def _():
            deal(back, keep_ref, send_ref, [(0, f // 32, total, 0)])


def dealt(split, size, shapes):
    if split:
        half = (16, size, LANES)
        return [whole(half)] * 2, [shaped(half, F32), shaped(half, BF)], [pltpu.VMEM(s, F32) for s in shapes]
    return [whole(s) for s in shapes], [shaped(s, F32) for s in shapes], []


def prefetched2(kernel, order, back, inputs, in_specs, out_specs, out_shape, scratch, grid, mib, name, flops, data):
    return pl.pallas_call(
        kernel,
        grid_spec=pltpu.PrefetchScalarGridSpec(
            num_scalar_prefetch=2, grid=grid, in_specs=in_specs, out_specs=out_specs, scratch_shapes=scratch,
        ),
        out_shape=out_shape,
        compiler_params=params(mib),
        cost_estimate=pl.CostEstimate(flops=flops, transcendentals=0, bytes_accessed=data),
        name=name,
    )(order, back, *inputs)


def down_both(split, order, back, m, slope, inv, x1, cotangent, valid, gain_mid, parts):
    t, d = x1.shape
    f = m.shape[1]
    out_specs, out_shape, scratch = dealt(split, f // 32, [(f, d)])
    weight = [pltpu.VMEM((f, d), BF)]
    return prefetched2(
        functools.partial(down_kernel, split), order, back,
        [m, slope, inv, x1, cotangent, valid, gain_mid, *parts],
        [rows(f), rows(f), rows(PAIR), rows(d), rows(d), rows(1), whole((1, f))] + [hbm()] * len(parts),
        [rows(d), rows(f), whole((1, f))] + out_specs,
        [shaped((t, d), BF), shaped((t, f), BF), shaped((1, f), F32)] + out_shape,
        weight + scratch + [pltpu.SemaphoreType.DMA], (t // BLOCK,), 60, "down_both",
        6 * t * d * f, 6 * d * f + 6 * t * f + 8 * t * d,
    )


def up_back_kernel(dpre_ref, x1_ref, ct_ref, valid_ref, o_ref, wu_ref, wo_ref, gf_ref, gi_ref,
                   dx1_ref, low_ref, do_ref, ggf_ref, ggi_ref):
    step = pl.program_id(0)
    dh2 = dot(dpre_ref[...], wu_ref[...], ((1,), (1,)))
    unit, inv = unit_norm(x1_ref[...])
    ffn_part = jnp.sum(dh2 * unit, axis=0, keepdims=True)
    gy = jnp.where(valid_ref[...] > 0, ct_ref[...].astype(F32), 0.0)
    dx1 = gy + norm_back(dh2, gf_ref[...], unit, inv)
    dx1_ref[...] = dx1
    low = dx1.astype(BF)
    low_ref[...] = low
    da = dot(low, wo_ref[...], ((1,), (1,)))
    unit, inv = unit_norm(o_ref[...])
    inner_part = jnp.sum(da * unit, axis=0, keepdims=True)
    do_ref[...] = norm_back(da, gi_ref[...], unit, inv).astype(BF)

    @pl.when(step == 0)
    def _():
        ggf_ref[...] = ffn_part
        ggi_ref[...] = inner_part

    @pl.when(step > 0)
    def _():
        ggf_ref[...] += ffn_part
        ggi_ref[...] += inner_part


def up_backward(dpre, x1, cotangent, valid, mixed, w_up, w_out, gain_ffn, gain_inner):
    t, d = x1.shape
    f = dpre.shape[1]
    return pl.pallas_call(
        up_back_kernel,
        grid=(t // BLOCK,),
        in_specs=[rows(f), rows(d), rows(d), rows(1), rows(d),
                  whole((d, f)), whole((d, d)), whole((1, d)), whole((1, d))],
        out_specs=[rows(d), rows(d), rows(d), whole((1, d)), whole((1, d))],
        out_shape=[shaped((t, d), F32), shaped((t, d), BF), shaped((t, d), BF), shaped((1, d), F32), shaped((1, d), F32)],
        compiler_params=params(40),
        cost_estimate=pl.CostEstimate(
            flops=2 * t * d * (d + f), transcendentals=0, bytes_accessed=2 * d * (d + f) + 2 * t * f + 24 * t * d
        ),
        name="up_backward",
    )(dpre, x1, cotangent, valid, mixed, w_up, w_out, gain_ffn, gain_inner)


def up_grad_kernel(split, *refs):
    back, h2_ref, dpre_ref, a_ref, low_ref, *refs = refs
    if split:
        keep_ref, send_ref, gwo_ref, gwu_ref = refs
    else:
        gwo_ref, gwu_ref = refs
    step = pl.program_id(0)
    part_up = dot(h2_ref[...], dpre_ref[...], ((0,), (0,)))
    part_out = dot(a_ref[...], low_ref[...], ((0,), (0,)))

    @pl.when(step == 0)
    def _():
        gwu_ref[...] = part_up
        gwo_ref[...] = part_out

    @pl.when(step > 0)
    def _():
        gwu_ref[...] += part_up
        gwo_ref[...] += part_out

    if split:
        d, f = gwu_ref.shape
        size = d // 32

        @pl.when(step == pl.num_programs(0) - 1)
        def _():
            deal(back, keep_ref, send_ref, [(0, size, gwo_ref, 0)] + slabs(size, size, gwu_ref, f))


def up_weight_grad(split, back, h2, dpre, a, low):
    t, d = h2.shape
    f = dpre.shape[1]
    out_specs, out_shape, scratch = dealt(split, (d + f) // 32, [(d, d), (d, f)])
    return prefetched(
        functools.partial(up_grad_kernel, split), back, [h2, dpre, a, low],
        [rows(d), rows(f), rows(d), rows(d)], out_specs, out_shape, scratch, (t // BLOCK,), 56, "up_weight_grad",
        2 * t * d * (d + f), 6 * d * (d + f) + 2 * t * f + 6 * t * d,
    )


def qkv_grad_kernel(split, *refs):
    back, h_ref, *refs = refs
    count = len(refs) - 3 if split else len(refs) - 1
    ins, refs = refs[:count], refs[count:]
    if split:
        keep_ref, send_ref, g_ref = refs
    else:
        (g_ref,) = refs
    step = pl.program_id(0)
    h = h_ref[...]
    at = 0
    for ref in ins:
        part = dot(h, ref[...], ((0,), (0,)))
        cols = slice(at, at + ref.shape[1])
        at += ref.shape[1]

        @pl.when(step == 0)
        def _():
            g_ref[:, cols] = part

        @pl.when(step > 0)
        def _():
            g_ref[:, cols] += part

    if split:
        d, n = g_ref.shape

        @pl.when(step == pl.num_programs(0) - 1)
        def _():
            deal(back, keep_ref, send_ref, slabs(0, d // 32, g_ref, n))


def qkv_weight_grad(split, back, h, pieces):
    t, d = h.shape
    n = sum(p.shape[1] for p in pieces)
    out_specs, out_shape, scratch = dealt(split, n // 32, [(d, n)])
    return prefetched(
        functools.partial(qkv_grad_kernel, split), back, [h, *pieces],
        [rows(d)] + [rows(p.shape[1]) for p in pieces], out_specs, out_shape, scratch,
        (t // BLOCK,), 40, "qkv_weight_grad", 2 * t * d * n, 4 * d * n + 2 * t * (d + n),
    )


def qkv_back_kernel(starts, *refs):
    count = len(starts)
    pieces, refs = refs[:count], refs[count:]
    x_ref, dx1_ref, w_ref, gain_ref, dx_ref, gg_ref = refs
    step = pl.program_id(0)
    dh = None
    for at, ref in zip(starts, pieces):
        part = dot(ref[...], w_ref[:, at : at + ref.shape[1]], ((1,), (1,)))
        dh = part if dh is None else dh + part
    unit, inv = unit_norm(x_ref[...].astype(F32))
    gain_part = jnp.sum(dh * unit, axis=0, keepdims=True)
    dx_ref[...] = dx1_ref[...] + norm_back(dh, gain_ref[...], unit, inv)

    @pl.when(step == 0)
    def _():
        gg_ref[...] = gain_part

    @pl.when(step > 0)
    def _():
        gg_ref[...] += gain_part


def qkv_backward(pieces, starts, tokens, dx1, w_qkv, gain):
    t, d = tokens.shape
    return pl.pallas_call(
        functools.partial(qkv_back_kernel, starts),
        grid=(t // BLOCK,),
        in_specs=[rows(p.shape[1]) for p in pieces] + [rows(d)] * 2 + [whole((d, 3 * d)), whole((1, d))],
        out_specs=[rows(d), whole((1, d))],
        out_shape=[shaped((t, d), F32), shaped((1, d), F32)],
        compiler_params=params(48),
        cost_estimate=pl.CostEstimate(flops=6 * t * d * d, transcendentals=0, bytes_accessed=6 * d * d + 16 * t * d),
        name="qkv_backward",
    )(*pieces, tokens, dx1, w_qkv, gain)


def layout(doc_lengths, seq):
    docs = doc_lengths.shape[-1]
    upto = jnp.arange(docs)[:, None] <= jnp.arange(docs)[None, :]
    ends = jnp.sum(jnp.where(upto[None], doc_lengths[:, :, None], 0), axis=1)
    places = jnp.arange(seq, dtype=jnp.int32)
    passed = places[None, :, None] >= ends[:, None, :]
    start = jnp.sum(jnp.where(passed, doc_lengths[:, None, :], 0), axis=-1)
    valid = places[None, :] < ends[:, docs - 2 : docs - 1]
    return start.astype(jnp.int32), places[None, :] - start, valid


def tables(position):
    half = HEAD_DIM // 2
    lane = jnp.arange(PAIR)
    frequency = jnp.exp((lane % half).astype(F32) * (-2.0 * math.log(10000.0) / HEAD_DIM))
    angles = position.reshape(-1, 1).astype(F32) * frequency[None, :]
    sign = jnp.where(lane % HEAD_DIM < half, -1.0, 1.0)
    return jnp.cos(angles), jnp.sin(angles) * sign[None, :]


Z = 4
GROUPS = ((0, 2), (1, 3))


def index(x, core, z, y):
    return ((x * 2 + core) * Z + z) * 2 + y


def permute(value, move):
    places = [(x, c, z, y) for x in range(2) for c in range(2) for z in range(Z) for y in range(2)]
    return lax.ppermute(value, AXES, [(index(*p), index(*move(*p))) for p in places])


def over_x(v):
    return permute(v, lambda x, c, z, y: (1 - x, c, z, y))


def over_y(v):
    return permute(v, lambda x, c, z, y: (x, c, z, 1 - y))


def over_core(v):
    return permute(v, lambda x, c, z, y: (x, 1 - c, z, y))


def over_z(v, shift):
    return permute(v, lambda x, c, z, y: (x, c, (z + shift) % Z, y))


def across_z(v, bit):
    return permute(v, lambda x, c, z, y: (x, c, z ^ bit, y))


def place():
    dp, fs = lax.axis_index("dp"), lax.axis_index("fsdp")
    return dp // 2, dp % 2, fs // 2, fs % 2


def gather_order():
    x, c, z, y = place()
    order = []
    for core in range(2):
        for group, first in zip(GROUPS, ("x", "y")):
            for second in range(2):
                for one in range(2):
                    dx, dy = (one, second) if first == "x" else (second, one)
                    for shift in group:
                        order.append(index(x ^ dx, c ^ core, (z - shift) % Z, y ^ dy))
    return jnp.stack(order).astype(jnp.int32)


def scatter_order():
    x, c, z, y = place()
    order = []
    for core in range(2):
        for group, first in zip(GROUPS, ("y", "x")):
            for one in (1, 0):
                for second in (1, 0):
                    dx, dy = (second, one) if first == "y" else (one, second)
                    for shift in group:
                        order.append(index(x ^ dx, c ^ core, (z + shift) % Z, y ^ dy))
    return jnp.stack(order).astype(jnp.int32)


def tie(value, other):
    return lax.optimization_barrier((value, other))[0]


class Gather:
    def __init__(self, block):
        self.by_z = [block]

    def z(self, after=None):
        block = self.by_z[0] if after is None else tie(self.by_z[0], after)
        self.by_z = [block] + [over_z(block, s) for s in (1, 2, 3)]
        return self.by_z[1:]

    def first(self, after=None):
        even = jnp.stack([self.by_z[s] for s in GROUPS[0]])
        odd = jnp.stack([self.by_z[s] for s in GROUPS[1]])
        if after is not None:
            even, odd = tie((even, odd), after)
        self.even = jnp.concatenate([even, over_x(even)])
        self.odd = jnp.concatenate([odd, over_y(odd)])
        return [self.even, self.odd]

    def second(self, after=None):
        even, odd = (self.even, self.odd) if after is None else tie((self.even, self.odd), after)
        self.near = [even, odd, over_core(even), over_core(odd)]
        self.far = [over_y(even), over_x(odd)]
        return self.far

    def core(self, after=None):
        far = self.far if after is None else tie(self.far, after)
        even, odd, even_core, odd_core = self.near
        return [even, far[0], odd, far[1], even_core, over_core(far[0]), odd_core, over_core(far[1])]


class Reduce:
    def __init__(self, keep, send):
        self.keep, self.send = keep, send

    def core(self, after=None):
        send = self.send if after is None else tie(self.send, after)
        self.got = self.core_got = over_core(send)
        return self.got

    def first(self, after=None):
        total = self.keep + self.got.astype(F32)
        self.a, self.b = total[:8], total[8:]
        sends = (self.a[:4].astype(BF), self.b[:4].astype(BF))
        if after is not None:
            sends = tie(sends, after)
        self.got = (over_y(sends[0]), over_x(sends[1]))
        return self.got

    def second(self, after=None):
        self.a = self.a[4:] + self.got[0].astype(F32)
        self.b = self.b[4:] + self.got[1].astype(F32)
        sends = (self.a[:2].astype(BF), self.b[:2].astype(BF))
        if after is not None:
            sends = tie(sends, after)
        self.got = (over_x(sends[0]), over_y(sends[1]))
        return self.got

    def z(self, after=None):
        self.a = self.a[2:] + self.got[0].astype(F32)
        self.b = self.b[2:] + self.got[1].astype(F32)
        sends = (self.b[0].astype(BF), self.a[1].astype(BF), self.b[1].astype(BF))
        if after is not None:
            sends = tie(sends, after)
        self.got = [over_z(s, i + 1) for i, s in enumerate(sends)]
        return self.got

    def own(self):
        return self.a[0] + sum(g.astype(F32) for g in self.got)


def unslab(block, width):
    size = block.shape[0] * LANES // width
    return jnp.concatenate([block[s * size : (s + 1) * size] for s in range(width // LANES)], axis=1)


def slab(block):
    return [block[:, s * LANES : (s + 1) * LANES] for s in range(block.shape[1] // LANES)]


def local(fast, tokens, doc_lengths, cotangent, w_qkv, w_out, w_up, w_down,
          gain_attn, gain_inner, gain_ffn, gain_mid):
    row_count = doc_lengths.shape[0]
    seq = tokens.shape[0] // row_count
    d = tokens.shape[1]
    wide = min(seq, 512) // BLOCK + 1
    blocks = seq // BLOCK
    shards = (gain_attn, gain_inner, gain_ffn, gain_mid)
    sizes = [g.shape[0] for g in shards]

    start, position, valid = layout(doc_lengths, seq)
    cos, sin = tables(position)
    firsts = start[:, ::BLOCK] // BLOCK
    reach = (jnp.arange(blocks, dtype=jnp.int32)[None, :] - firsts + 1).reshape(-1)
    start_col = start.reshape(-1, 1)
    start_row = jnp.repeat(start, 8, axis=0)
    valid_col = valid.astype(jnp.int32).reshape(-1, 1)

    if fast:
        order, back = gather_order(), scatter_order()
        gains_row = jnp.pad(jnp.concatenate(shards)[None], ((0, 7), (0, LANES - sum(sizes))))
        one = Gather(jnp.concatenate(slab(w_qkv) + [gains_row]))
        two = Gather(jnp.concatenate([w_out] + slab(w_up)))
        three = Gather(w_down)
        seen = one.z()
        seen = two.z(seen)
        one.first()
        far = one.second()
        three.z((seen, far))
        two.first(far)
        parts_qkv = one.core()
        gains = [None]
    else:
        order = back = jnp.zeros((8,), jnp.int32)

        def gather(v):
            return lax.all_gather(v, AXES, axis=0, tiled=True)

        parts_qkv, parts_up, parts_down = [gather(w_qkv)], [gather(w_out), gather(w_up)], [gather(w_down)]
        gains = [gather(g).astype(F32).reshape(1, -1) for g in shards]

    h1, qkv, full_qkv, *rest = qkv_forward(fast, order, tokens, cos, sin, parts_qkv, gains[0], sizes)
    g_attn, g_inner, g_ffn, g_mid = rest if fast else gains
    if fast:
        two.second(g_attn)
        three.first(g_attn)
    mixed, lse = attention_forward(reach, qkv, start_col, row_count, wide)
    if fast:
        parts_up = two.core(lse)
        three.second(lse)
    a, x1, h2, m, slope, inv, full_out, full_up = up_forward(
        fast, order, mixed, tokens, g_inner, g_ffn, g_mid, parts_up
    )
    if fast:
        parts_down = three.core(inv)
    result, dpre, grad_mid, *grad_down = down_both(
        fast, order, back, m, slope, inv, x1, cotangent, valid_col, g_mid, parts_down
    )
    if fast:
        red_down = Reduce(*grad_down)
        red_down.core()
    dx1, low, d_mixed, grad_ffn, grad_inner = up_backward(
        dpre, x1, cotangent, valid_col, mixed, full_up, full_out, g_ffn, g_inner
    )
    if fast:
        first = red_down.first(grad_ffn)
        low = tie(low, (grad_ffn, red_down.core_got))
    grad_up = up_weight_grad(fast, back, h2, dpre, a, low)
    if fast:
        second = red_down.second(grad_up)
        red_up = Reduce(*grad_up)
        red_up.core()
        lse = tie(lse, first)

    def attend(base, pairs, lse):
        return attention_backward(
            reach, qkv, d_mixed, mixed, lse, start_row, cos, sin, row_count, wide, base, pairs
        )

    third = PAIRS // 3
    lse = tie(lse, grad_up[-1])
    g0 = attend(0, third, lse)
    if fast:
        down_z = red_down.z(g0)
        first = red_up.first(g0)
        lse = tie(lse, (second, red_up.core_got))
    g1 = attend(third, third, tie(lse, g0))
    if fast:
        second = red_up.second(g1)
        h1 = tie(h1, first)
    grad_qkv = [qkv_weight_grad(fast, back, h1, [p for pair in zip(g0, g1) for p in pair])]
    if fast:
        red_most = Reduce(*grad_qkv[0])
        red_most.core()
        own_down = red_down.own()
        lse = tie(lse, down_z)
    g2 = attend(2 * third, third, tie(lse, grad_qkv[0][-1]))
    if fast:
        up_z = red_up.z(g2)
        first = red_most.first(g2)
        h1 = tie(h1, (second, red_most.core_got))
    grad_qkv.append(qkv_weight_grad(fast, back, h1, list(g2)))
    if fast:
        red_last = Reduce(*grad_qkv[1])
        red_last.core()
        second = red_most.second(grad_qkv[1])
        dx1 = tie(dx1, first)
    pieces, starts = [], []
    for g, group in enumerate((g0, g1, g2)):
        for part, piece in enumerate(group):
            pieces.append(piece if g or not fast else tie(piece, grad_qkv[1][-1]))
            starts.append(part * d + g * third * PAIR)
    grad_tokens, grad_attn = qkv_backward(pieces, starts, tokens, dx1, full_qkv, g_attn)
    gain_grads = (grad_attn, grad_inner, grad_ffn, grad_mid)
    cut = 2 * third * PAIR
    if fast:
        red_last.first(grad_attn)
        red_most.z(grad_attn)
        red_last.second()
        own_up = red_up.own()
        red_last.z()
        packed = jnp.concatenate([g.reshape(-1, LANES) for g in gain_grads])
        packed = jnp.pad(packed, ((0, -packed.shape[0] % 8), (0, 0)))
        packed = packed + over_core(packed)
        packed = packed + over_x(packed)
        packed = packed + over_y(packed)
        packed = packed + over_z(packed, 1) + over_z(packed, 2) + over_z(packed, 3)
        most, last = unslab(red_most.own(), 3 * cut), unslab(red_last.own(), 3 * (d - cut))
        size = w_out.shape[0]
        weights = (own_up[:size], unslab(own_up[size:], w_up.shape[1]), own_down)
        me = index(*place())
        summed, at = [], 0
        for size, full in zip(sizes, gain_grads):
            flat = packed[at : at + full.size // LANES].reshape(-1)
            summed.append(lax.dynamic_slice(flat, (me * size,), (size,)))
            at += full.size // LANES
    else:

        def scatter(g):
            return lax.psum_scatter(g, AXES, scatter_dimension=0, tiled=True)

        most, last, *weights = (
            scatter(g.astype(BF)).astype(F32)
            for g in (grad_qkv[0][0], grad_qkv[1][0], grad_up[0], grad_up[1], grad_down[0])
        )
        summed = [scatter(g.reshape(-1)) for g in gain_grads]
    columns = []
    for part in range(3):
        columns += [most[:, part * cut : (part + 1) * cut], last[:, part * (d - cut) : (part + 1) * (d - cut)]]
    return (result, grad_tokens, jnp.concatenate(columns, axis=1)) + tuple(weights) + tuple(summed)


def solution(mesh):
    matrix, vector = P(AXES, None), P(AXES)
    fast = mesh.shape["dp"] == 4 and mesh.shape["fsdp"] == 2 * Z
    return jax.shard_map(
        functools.partial(local, fast),
        mesh=mesh,
        in_specs=(matrix,) * 7 + (vector,) * 4,
        out_specs=(matrix,) * 6 + (vector,) * 4,
        check_vma=False,
    )
```

```python
import functools
import math

import jax
import jax.numpy as jnp
from jax import lax
from jax.experimental import pallas as pl
from jax.experimental.pallas import tpu as pltpu
from jax.sharding import PartitionSpec as P

HEADS = 12
HEAD_DIM = 64
PAIR = 2 * HEAD_DIM
PAIRS = HEADS // 2
EPSILON = 1e-05
MASKED_SCORE = -1e30
ROOT_HALF = 0.7071067811865476
INV_ROOT_TAU = 0.3989422804014327
BF = jnp.bfloat16
F32 = jnp.float32
MIB = 1 << 20
AXES = ("dp", "fsdp")
BLOCK = 256
LANES = 768


def dot(a, b, dims=((1,), (0,))):
    return lax.dot_general(a, b, (dims, ((), ())), preferred_element_type=F32)


def params(mib):
    return pltpu.CompilerParams(vmem_limit_bytes=mib * MIB)


def swap_halves(x):
    lane = lax.broadcasted_iota(jnp.int32, x.shape, 1)
    low = lax.rem(lane, HEAD_DIM) < HEAD_DIM // 2
    half = HEAD_DIM // 2
    return jnp.where(low, pltpu.roll(x, PAIR - half, 1), pltpu.roll(x, half, 1))


def unit_norm(x):
    mean = jnp.mean(x, axis=-1, keepdims=True)
    centred = x - mean
    inv = lax.rsqrt(jnp.mean(centred * centred, axis=-1, keepdims=True) + EPSILON)
    return centred * inv, inv


def norm_back(grad, gain, unit, inv):
    d_unit = grad * gain
    return inv * (
        d_unit
        - jnp.mean(d_unit, axis=-1, keepdims=True)
        - unit * jnp.mean(d_unit * unit, axis=-1, keepdims=True)
    )


def whole(shape):
    return pl.BlockSpec(shape, lambda *_: (0,) * len(shape), pipeline_mode=pl.Buffered(1))


def rows(width, block=BLOCK):
    return pl.BlockSpec((block, width), lambda i: (i, 0))


def shaped(shape, dtype):
    return jax.ShapeDtypeStruct(shape, dtype)


def hbm():
    return pl.BlockSpec(memory_space=pl.ANY)


def fetch(order, parts, places, sem):
    if len(parts) < 8 and parts[0].ndim == 2:
        for part, (_, _, buffer, _) in zip(parts, places):
            pltpu.make_async_copy(part, buffer, sem).start()
        return
    count = parts[0].shape[0]
    for p, part in enumerate(parts):
        for b in range(count):
            owner = b if order is None else order[p * count + b]
            for first, size, buffer, column in places:
                row = owner * size if order is None else pl.multiple_of(owner * size, 8)
                pltpu.make_async_copy(
                    part.at[b, pl.ds(first, size), :],
                    buffer.at[pl.ds(row, size), pl.ds(column, LANES)],
                    sem,
                ).start()


def arrive(buffers, sem):
    for buffer in buffers:
        pltpu.make_async_copy(buffer, buffer, sem).wait()


def deal(order, keep_ref, send_ref, places):
    half = keep_ref.shape[0]

    def one(j, target, at):
        owner = order[at]
        for first, size, buffer, column in places:
            block = buffer[pl.ds(pl.multiple_of(owner * size, 8), size), column : column + LANES]
            target[j, first : first + size, :] = block.astype(target.dtype)

    @pl.loop(0, half)
    def _(j):
        one(j, keep_ref, j)
        one(j, send_ref, j + half)


def slabs(first, size, buffer, width):
    return [(first + s * size, size, buffer, s * LANES) for s in range(width // LANES)]


def spread(rows_in, offset, count, owners):
    lanes = rows_in.shape[1]
    wide = owners * count
    lane = lax.broadcasted_iota(jnp.int32, (lanes, wide), 0)
    column = lax.broadcasted_iota(jnp.int32, (lanes, wide), 1)
    pick = (lane - offset == lax.rem(column, count)).astype(F32).astype(BF)
    full = dot(rows_in, pick)
    owner = lax.broadcasted_iota(jnp.int32, (owners, wide), 0)
    column = lax.broadcasted_iota(jnp.int32, (owners, wide), 1)
    own = (column >= owner * count) & (column < owner * count + count)
    return jnp.sum(jnp.where(own, full, 0.0), axis=0, keepdims=True)


def qkv_kernel(split, sizes, *refs):
    if split:
        order, x_ref, cos_ref, sin_ref, *refs = refs
        parts, refs = refs[:8], refs[8:]
        h_ref, qkv_ref, w_ref, ga_ref, gi_ref, gf_ref, gm_ref, gains, sem, gain_sem = refs
    else:
        order, x_ref, cos_ref, sin_ref, ga_ref, *refs = refs
        parts, refs = refs[:1], refs[1:]
        h_ref, qkv_ref, w_ref, sem = refs
    width = x_ref.shape[1]
    step = pl.program_id(0)
    if split:
        size = width // 32
        weight = slabs(0, size, w_ref, 3 * width)

        @pl.when(step == 0)
        def _():
            fetch(order, parts, [(3 * size, 8, gains, 0)], gain_sem)
            fetch(order, parts, weight, sem)
            arrive([gains], gain_sem)
            owner = lax.broadcasted_iota(jnp.int32, (32, 256), 0)
            lane = lax.broadcasted_iota(jnp.int32, (32, 256), 1)
            pick = (lane == owner * 8).astype(F32).astype(BF)
            per_owner = dot(pick, gains[:, :256]).astype(BF)
            at = 0
            for ref, count in zip((ga_ref, gi_ref, gf_ref, gm_ref), sizes):
                ref[...] = spread(per_owner, at, count, 32)
                at += count
            arrive([w_ref], sem)
    else:

        @pl.when(step == 0)
        def _():
            fetch(None, parts, [(0, 0, w_ref, 0)], sem)
            arrive([w_ref], sem)

    unit, _ = unit_norm(x_ref[...].astype(F32))
    h = (unit * ga_ref[...]).astype(BF)
    h_ref[...] = h
    cos, sin = cos_ref[...], sin_ref[...]
    for part in range(3):
        y = dot(h, w_ref[:, part * width : (part + 1) * width])
        for c in range(width // PAIR):
            z = y[:, c * PAIR : (c + 1) * PAIR]
            if part < 2:
                z = z * cos + swap_halves(z) * sin
            if part == 0:
                z = z * (1.0 / math.sqrt(HEAD_DIM))
            at = part * width + c * PAIR
            qkv_ref[:, at : at + PAIR] = z.astype(BF)


def prefetched(kernel, order, inputs, in_specs, out_specs, out_shape, scratch, grid, mib, name, flops, data):
    return pl.pallas_call(
        kernel,
        grid_spec=pltpu.PrefetchScalarGridSpec(
            num_scalar_prefetch=1,
            grid=grid,
            in_specs=in_specs,
            out_specs=out_specs,
            scratch_shapes=scratch,
        ),
        out_shape=out_shape,
        compiler_params=params(mib),
        cost_estimate=pl.CostEstimate(flops=flops, transcendentals=0, bytes_accessed=data),
        name=name,
    )(order, *inputs)


def rows(width, block=BLOCK):
    return pl.BlockSpec((block, width), lambda i, *_: (i, 0))


def whole(shape):
    return pl.BlockSpec(shape, lambda *_: (0,) * len(shape), pipeline_mode=pl.Buffered(1))


def qkv_forward(split, order, tokens, cos, sin, parts, gain, sizes):
    t, d = tokens.shape
    n = 3 * d
    inputs = [tokens, cos, sin]
    in_specs = [rows(d), rows(PAIR), rows(PAIR)]
    out_specs = [rows(d), rows(n), whole((d, n))]
    out_shape = [shaped((t, d), BF), shaped((t, n), BF), shaped((d, n), BF)]
    scratch = [pltpu.SemaphoreType.DMA]
    if split:
        widths = [32 * s for s in sizes]
        out_specs += [whole((1, w)) for w in widths]
        out_shape += [shaped((1, w), F32) for w in widths]
        scratch = [pltpu.VMEM((32 * 8, LANES), BF), pltpu.SemaphoreType.DMA, pltpu.SemaphoreType.DMA]
    else:
        inputs.append(gain)
        in_specs.append(whole((1, d)))
    return prefetched(
        functools.partial(qkv_kernel, split, sizes), order, inputs + list(parts), in_specs + [hbm()] * len(parts),
        out_specs, out_shape, scratch, (t // BLOCK,), 40, "qkv_forward",
        2 * t * d * n, 4 * d * n + 12 * t * d,
    )


def window(i, n):
    return slice((i - n + 1) * BLOCK, (i + 1) * BLOCK)


def head_masks(shape):
    lane = lax.broadcasted_iota(jnp.int32, shape, 1)
    return lane < HEAD_DIM


def attention_forward_kernel(wide, reach, q_ref, k_ref, v_ref, start_ref, o_ref, lse_ref, bias):
    row, pair = pl.program_id(0), pl.program_id(1)
    seq = q_ref.shape[0]
    blocks = seq // BLOCK

    @pl.when(pair == 0)
    def _():
        for i in range(blocks):
            at = slice(i * BLOCK, (i + 1) * BLOCK)
            shape = (BLOCK, wide * BLOCK)
            key = (i - wide + 1) * BLOCK + lax.broadcasted_iota(jnp.int32, shape, 1)
            query = i * BLOCK + lax.broadcasted_iota(jnp.int32, shape, 0)
            keep = (key >= start_ref[at, :]) & (key <= query)
            bias[at, :] = jnp.where(keep, 0.0, MASKED_SCORE)

    first = head_masks((BLOCK, PAIR))
    for i in range(blocks):
        at = slice(i * BLOCK, (i + 1) * BLOCK)
        most = min(wide, i + 1)
        for n in range(1, most + 1):

            @pl.when(reach[row * blocks + i] == n)
            def _():
                q = q_ref[at, :]
                w = window(i, n)
                k, v = k_ref[w, :], v_ref[w, :]
                b = bias[at, (wide - n) * BLOCK :]
                mask = head_masks(k.shape)
                zero = jnp.zeros_like(k)
                total, lses = None, []
                scale = None
                for h in range(2):
                    pick = mask if h == 0 else jnp.logical_not(mask)
                    s = dot(q, jnp.where(pick, k, zero), ((1,), (1,))) + b
                    top = jnp.max(s, axis=-1, keepdims=True)
                    p = jnp.exp(s - top)
                    den = jnp.sum(p, axis=-1, keepdims=True)
                    probs = (p * (1.0 / den)).astype(BF)
                    part = dot(probs, jnp.where(pick, v, zero))
                    total = part if total is None else total + part
                    lses.append(top + jnp.log(den))
                o_ref[at, :] = total
                both = jnp.where(first, lses[0], lses[1]).T
                lse_ref[0, 0:1, at] = both[0:1, :]
                lse_ref[0, 1:2, at] = both[HEAD_DIM : HEAD_DIM + 1, :]


def attention_forward(reach, qkv, start, row_count, wide):
    t = qkv.shape[0]
    seq = t // row_count
    d = qkv.shape[1] // 3

    def columns(part):
        return pl.BlockSpec((seq, PAIR), lambda r, p, *_: (r, part * PAIRS + p))

    return pl.pallas_call(
        functools.partial(attention_forward_kernel, wide),
        grid_spec=pltpu.PrefetchScalarGridSpec(
            num_scalar_prefetch=1,
            grid=(row_count, PAIRS),
            in_specs=[
                columns(0),
                columns(1),
                columns(2),
                pl.BlockSpec((seq, 1), lambda r, p, *_: (r, 0)),
            ],
            out_specs=[
                pl.BlockSpec((seq, PAIR), lambda r, p, *_: (r, p)),
                pl.BlockSpec((1, 8, seq), lambda r, p, *_: (r * PAIRS + p, 0, 0)),
            ],
            scratch_shapes=[pltpu.VMEM((seq, wide * BLOCK), F32)],
        ),
        out_shape=[shaped((t, d), F32), shaped((row_count * PAIRS, 8, seq), F32)],
        compiler_params=params(32),
        cost_estimate=pl.CostEstimate(
            flops=8 * t * d * BLOCK, transcendentals=t * HEADS * 512, bytes_accessed=12 * t * d
        ),
        name="attention_forward",
    )(reach, qkv, qkv, qkv, start)


def attention_backward_kernel(
    wide, reach, q_ref, k_ref, v_ref, do_ref, o_ref, lse_ref, start_ref, cos_ref, sin_ref,
    dq_ref, dk_ref, dv_ref, bias, ks, vs, qs, dos, dk_acc, dv_acc, dq_acc,
):
    row, pair = pl.program_id(0), pl.program_id(1)
    seq = q_ref.shape[0]
    blocks = seq // BLOCK

    @pl.when(pair == 0)
    def _():
        for i in range(blocks):
            at = slice(i * BLOCK, (i + 1) * BLOCK)
            shape = (wide * BLOCK, BLOCK)
            key = (i - wide + 1) * BLOCK + lax.broadcasted_iota(jnp.int32, shape, 0)
            query = i * BLOCK + lax.broadcasted_iota(jnp.int32, shape, 1)
            keep = (key >= start_ref[0:1, at]) & (key <= query)
            bias[:, at] = jnp.where(keep, 0.0, MASKED_SCORE)

    mask = head_masks((seq, PAIR))
    for src, dst in ((k_ref, ks), (v_ref, vs), (q_ref, qs), (do_ref, dos)):
        x = src[...]
        zero = jnp.zeros_like(x)
        dst[0] = jnp.where(mask, x, zero)
        dst[1] = jnp.where(mask, zero, x)
    dk_acc[...] = jnp.zeros_like(dk_acc)
    dv_acc[...] = jnp.zeros_like(dv_acc)
    lane8 = lax.broadcasted_iota(jnp.int32, (8, PAIR), 1) // HEAD_DIM
    row8 = lax.broadcasted_iota(jnp.int32, (8, PAIR), 0)
    picks = (lane8 == row8).astype(F32)
    delta = lax.dot_general(
        picks, do_ref[...].astype(F32) * o_ref[...], (((1,), (1,)), ((), ())),
        precision=lax.Precision.HIGHEST, preferred_element_type=F32,
    )
    for i in range(blocks):
        at = slice(i * BLOCK, (i + 1) * BLOCK)
        most = min(wide, i + 1)
        for n in range(1, most + 1):

            @pl.when(reach[row * blocks + i] == n)
            def _():
                w = window(i, n)
                b = bias[(wide - n) * BLOCK :, at]
                q, do = q_ref[at, :], do_ref[at, :]
                ps, dss = [], []
                for h in range(2):
                    s = dot(ks[h, w, :], q, ((1,), (1,))) + b
                    p = jnp.exp(s - lse_ref[0, h : h + 1, at])
                    dp = dot(vs[h, w, :], do, ((1,), (1,)))
                    ds = (p * (dp - delta[h : h + 1, at])).astype(BF)
                    ps.append(p.astype(BF))
                    dss.append(ds)
                dv_acc[w, :] += dot(ps[0], dos[0, at, :]) + dot(ps[1], dos[1, at, :])
                dk_acc[w, :] += dot(dss[0], qs[0, at, :]) + dot(dss[1], qs[1, at, :])
                dq_acc[at, :] = dot(dss[0], ks[0, w, :], ((0,), (0,))) + dot(
                    dss[1], ks[1, w, :], ((0,), (0,))
                )

    cos, sin = cos_ref[...], sin_ref[...]
    dq = dq_acc[...] * (1.0 / math.sqrt(HEAD_DIM))
    dk = dk_acc[...]
    dq_ref[...] = (dq * cos - swap_halves(dq) * sin).astype(BF)
    dk_ref[...] = (dk * cos - swap_halves(dk) * sin).astype(BF)
    dv_ref[...] = dv_acc[...].astype(BF)


def attention_backward(reach, qkv, d_mixed, mixed, lse, start_row, cos, sin, row_count, wide, base, pairs):
    t = qkv.shape[0]
    seq = t // row_count
    d = pairs * PAIR

    def columns(part):
        return pl.BlockSpec((seq, PAIR), lambda r, p, *_: (r, part * PAIRS + base + p))

    table = pl.BlockSpec((seq, PAIR), lambda r, p, *_: (r, 0))
    return pl.pallas_call(
        functools.partial(attention_backward_kernel, wide),
        grid_spec=pltpu.PrefetchScalarGridSpec(
            num_scalar_prefetch=1,
            grid=(row_count, pairs),
            in_specs=[
                columns(0), columns(1), columns(2), columns(0), columns(0),
                pl.BlockSpec((1, 8, seq), lambda r, p, *_: (r * PAIRS + base + p, 0, 0)),
                pl.BlockSpec((8, seq), lambda r, p, *_: (r, 0)),
                table, table,
            ],
            out_specs=[pl.BlockSpec((seq, PAIR), lambda r, p, *_: (r, p))] * 3,
            scratch_shapes=[
                pltpu.VMEM((wide * BLOCK, seq), F32),
                pltpu.VMEM((2, seq, PAIR), BF),
                pltpu.VMEM((2, seq, PAIR), BF),
                pltpu.VMEM((2, seq, PAIR), BF),
                pltpu.VMEM((2, seq, PAIR), BF),
                pltpu.VMEM((seq, PAIR), F32),
                pltpu.VMEM((seq, PAIR), F32),
                pltpu.VMEM((seq, PAIR), F32),
            ],
        ),
        out_shape=[shaped((t, d), BF)] * 3,
        compiler_params=params(40),
        cost_estimate=pl.CostEstimate(
            flops=20 * t * d * BLOCK, transcendentals=t * HEADS * 512, bytes_accessed=20 * t * d
        ),
        name="attention_backward",
    )(reach, qkv, qkv, qkv, d_mixed, mixed, lse, start_row, cos, sin)


def up_kernel(split, o_ref, x_ref, ct_ref, valid_ref, gi_ref, gf_ref, gm_ref, *refs):
    count = 1 if split else 2
    parts, refs = refs[:count], refs[count:]
    a_ref, x1_ref, h2_ref, m_ref, slope_ref, inv_ref, wo_ref, wu_ref, grad_ref, total, sem = refs
    d, f = wu_ref.shape
    size = d // 32
    step = pl.program_id(0)
    places = [(0, size, wo_ref, 0)] + slabs(size, size, wu_ref, f) if split else [(0, 0, wo_ref, 0), (0, 0, wu_ref, 0)]

    @pl.when(step == 0)
    def _():
        fetch(None, parts, places, sem)

    unit, _ = unit_norm(o_ref[...])
    a = (unit * gi_ref[...]).astype(BF)
    a_ref[...] = a

    @pl.when(step == 0)
    def _():
        arrive([wo_ref, wu_ref], sem)

    x1 = x_ref[...].astype(F32) + dot(a, wo_ref[...])
    x1_ref[...] = x1
    unit, _ = unit_norm(x1)
    h2 = (unit * gf_ref[...]).astype(BF)
    h2_ref[...] = h2
    hidden = dot(h2, wu_ref[...])
    cdf = 0.5 + 0.5 * lax.erf(hidden * ROOT_HALF)
    slope = cdf + hidden * (jnp.exp(-0.5 * hidden * hidden) * INV_ROOT_TAU)
    slope_ref[...] = slope.astype(BF)
    unit, inv = unit_norm(hidden * cdf)
    m = (unit * gm_ref[...]).astype(BF)
    m_ref[...] = m
    inv_ref[...] = jnp.broadcast_to(inv, inv_ref.shape)
    gy = jnp.where(valid_ref[...] > 0, ct_ref[...], jnp.zeros_like(ct_ref))
    part = dot(m, gy, ((0,), (0,)))

    @pl.when(step == 0)
    def _():
        total[...] = part

    @pl.when(step > 0)
    def _():
        total[...] += part

    @pl.when(step == pl.num_programs(0) - 1)
    def _():
        grad_ref[...] = total[...].astype(BF)


def up_forward(split, mixed, tokens, cotangent, valid, gain_inner, gain_ffn, gain_mid, parts):
    t, d = tokens.shape
    f = gain_mid.shape[1]
    return pl.pallas_call(
        functools.partial(up_kernel, split),
        grid=(t // BLOCK,),
        in_specs=[rows(d), rows(d), rows(d), rows(1), whole((1, d)), whole((1, d)), whole((1, f))] + [hbm()] * len(parts),
        out_specs=[rows(d), rows(d), rows(d), rows(f), rows(f), rows(PAIR), whole((d, d)), whole((d, f)), whole((f, d))],
        out_shape=[
            shaped((t, d), BF), shaped((t, d), F32), shaped((t, d), BF),
            shaped((t, f), BF), shaped((t, f), BF), shaped((t, PAIR), F32),
            shaped((d, d), BF), shaped((d, f), BF), shaped((f, d), BF),
        ],
        scratch_shapes=[pltpu.VMEM((f, d), F32), pltpu.SemaphoreType.DMA],
        compiler_params=params(60),
        cost_estimate=pl.CostEstimate(
            flops=2 * t * d * (d + 2 * f), transcendentals=2 * t * f,
            bytes_accessed=4 * d * (d + f) + 2 * d * f + 4 * t * f + 16 * t * d,
        ),
        name="up_forward",
    )(mixed, tokens, cotangent, valid, gain_inner, gain_ffn, gain_mid, *parts)


def down_kernel(split, m_ref, slope_ref, inv_ref, x1_ref, ct_ref, valid_ref, gm_ref, part_ref,
                y_ref, dpre_ref, gg_ref, wd_ref, sem):
    f, d = wd_ref.shape
    step = pl.program_id(0)

    @pl.when(step == 0)
    def _():
        first = part_ref.shape[1] - f // 32 if split else 0
        fetch(None, [part_ref], [(first, f // 32, wd_ref, 0)], sem)
        arrive([wd_ref], sem)

    m = m_ref[...]
    gy = jnp.where(valid_ref[...] > 0, ct_ref[...], jnp.zeros_like(ct_ref))
    dm = dot(gy, wd_ref[...], ((1,), (1,)))
    gain = gm_ref[...]
    mf = m.astype(F32)
    prod = dm * mf
    d_unit = dm * gain
    d_act = inv_ref[:, 0:1] * (
        d_unit
        - jnp.mean(d_unit, axis=-1, keepdims=True)
        - (mf * (1.0 / gain)) * jnp.mean(prod, axis=-1, keepdims=True)
    )
    dpre_ref[...] = (d_act * slope_ref[...].astype(F32)).astype(BF)
    y_ref[...] = (x1_ref[...] + dot(m, wd_ref[...])).astype(BF)
    gain_part = jnp.sum(prod, axis=0, keepdims=True) * (1.0 / gain)

    @pl.when(step == 0)
    def _():
        gg_ref[...] = gain_part

    @pl.when(step > 0)
    def _():
        gg_ref[...] += gain_part


def dealt(split, size, shapes):
    if split:
        half = (16, size, LANES)
        return [whole(half)] * 2, [shaped(half, F32), shaped(half, BF)], [pltpu.VMEM(s, F32) for s in shapes]
    return [whole(s) for s in shapes], [shaped(s, F32) for s in shapes], []


def down_both(split, m, slope, inv, x1, cotangent, valid, gain_mid, part):
    t, d = x1.shape
    f = m.shape[1]
    return pl.pallas_call(
        functools.partial(down_kernel, split),
        grid=(t // BLOCK,),
        in_specs=[rows(f), rows(f), rows(PAIR), rows(d), rows(d), rows(1), whole((1, f)), hbm()],
        out_specs=[rows(d), rows(f), whole((1, f))],
        out_shape=[shaped((t, d), BF), shaped((t, f), BF), shaped((1, f), F32)],
        scratch_shapes=[pltpu.VMEM((f, d), BF), pltpu.SemaphoreType.DMA],
        compiler_params=params(48),
        cost_estimate=pl.CostEstimate(
            flops=4 * t * d * f, transcendentals=0, bytes_accessed=2 * d * f + 6 * t * f + 8 * t * d
        ),
        name="down_both",
    )(m, slope, inv, x1, cotangent, valid, gain_mid, part)


def up_back_kernel(dpre_ref, x1_ref, ct_ref, valid_ref, o_ref, wu_ref, wo_ref, gf_ref, gi_ref,
                   dx1_ref, low_ref, do_ref, ggf_ref, ggi_ref):
    step = pl.program_id(0)
    dh2 = dot(dpre_ref[...], wu_ref[...], ((1,), (1,)))
    unit, inv = unit_norm(x1_ref[...])
    ffn_part = jnp.sum(dh2 * unit, axis=0, keepdims=True)
    gy = jnp.where(valid_ref[...] > 0, ct_ref[...].astype(F32), 0.0)
    dx1 = gy + norm_back(dh2, gf_ref[...], unit, inv)
    dx1_ref[...] = dx1
    low = dx1.astype(BF)
    low_ref[...] = low
    da = dot(low, wo_ref[...], ((1,), (1,)))
    unit, inv = unit_norm(o_ref[...])
    inner_part = jnp.sum(da * unit, axis=0, keepdims=True)
    do_ref[...] = norm_back(da, gi_ref[...], unit, inv).astype(BF)

    @pl.when(step == 0)
    def _():
        ggf_ref[...] = ffn_part
        ggi_ref[...] = inner_part

    @pl.when(step > 0)
    def _():
        ggf_ref[...] += ffn_part
        ggi_ref[...] += inner_part


def up_backward(dpre, x1, cotangent, valid, mixed, w_up, w_out, gain_ffn, gain_inner):
    t, d = x1.shape
    f = dpre.shape[1]
    return pl.pallas_call(
        up_back_kernel,
        grid=(t // BLOCK,),
        in_specs=[rows(f), rows(d), rows(d), rows(1), rows(d),
                  whole((d, f)), whole((d, d)), whole((1, d)), whole((1, d))],
        out_specs=[rows(d), rows(d), rows(d), whole((1, d)), whole((1, d))],
        out_shape=[shaped((t, d), F32), shaped((t, d), BF), shaped((t, d), BF), shaped((1, d), F32), shaped((1, d), F32)],
        compiler_params=params(40),
        cost_estimate=pl.CostEstimate(
            flops=2 * t * d * (d + f), transcendentals=0, bytes_accessed=2 * d * (d + f) + 2 * t * f + 24 * t * d
        ),
        name="up_backward",
    )(dpre, x1, cotangent, valid, mixed, w_up, w_out, gain_ffn, gain_inner)


def up_grad_kernel(split, *refs):
    back, h2_ref, dpre_ref, a_ref, low_ref, *refs = refs
    if split:
        keep_ref, send_ref, gwo_ref, gwu_ref = refs
    else:
        gwo_ref, gwu_ref = refs
    step = pl.program_id(0)
    part_up = dot(h2_ref[...], dpre_ref[...], ((0,), (0,)))
    part_out = dot(a_ref[...], low_ref[...], ((0,), (0,)))

    @pl.when(step == 0)
    def _():
        gwu_ref[...] = part_up
        gwo_ref[...] = part_out

    @pl.when(step > 0)
    def _():
        gwu_ref[...] += part_up
        gwo_ref[...] += part_out

    if split:
        d, f = gwu_ref.shape
        size = d // 32

        @pl.when(step == pl.num_programs(0) - 1)
        def _():
            deal(back, keep_ref, send_ref, [(0, size, gwo_ref, 0)] + slabs(size, size, gwu_ref, f))


def up_weight_grad(split, back, h2, dpre, a, low):
    t, d = h2.shape
    f = dpre.shape[1]
    out_specs, out_shape, scratch = dealt(split, (d + f) // 32, [(d, d), (d, f)])
    return prefetched(
        functools.partial(up_grad_kernel, split), back, [h2, dpre, a, low],
        [rows(d), rows(f), rows(d), rows(d)], out_specs, out_shape, scratch, (t // BLOCK,), 56, "up_weight_grad",
        2 * t * d * (d + f), 6 * d * (d + f) + 2 * t * f + 6 * t * d,
    )


def qkv_grad_kernel(split, *refs):
    back, h_ref, *refs = refs
    count = len(refs) - 3 if split else len(refs) - 1
    ins, refs = refs[:count], refs[count:]
    if split:
        keep_ref, send_ref, g_ref = refs
    else:
        (g_ref,) = refs
    step = pl.program_id(0)
    h = h_ref[...]
    at = 0
    for ref in ins:
        part = dot(h, ref[...], ((0,), (0,)))
        cols = slice(at, at + ref.shape[1])
        at += ref.shape[1]

        @pl.when(step == 0)
        def _():
            g_ref[:, cols] = part

        @pl.when(step > 0)
        def _():
            g_ref[:, cols] += part

    if split:
        d, n = g_ref.shape

        @pl.when(step == pl.num_programs(0) - 1)
        def _():
            deal(back, keep_ref, send_ref, slabs(0, d // 32, g_ref, n))


def qkv_weight_grad(split, back, h, pieces):
    t, d = h.shape
    n = sum(p.shape[1] for p in pieces)
    out_specs, out_shape, scratch = dealt(split, n // 32, [(d, n)])
    return prefetched(
        functools.partial(qkv_grad_kernel, split), back, [h, *pieces],
        [rows(d)] + [rows(p.shape[1]) for p in pieces], out_specs, out_shape, scratch,
        (t // BLOCK,), 40, "qkv_weight_grad", 2 * t * d * n, 4 * d * n + 2 * t * (d + n),
    )


def qkv_back_kernel(starts, *refs):
    count = len(starts)
    pieces, refs = refs[:count], refs[count:]
    x_ref, dx1_ref, w_ref, gain_ref, dx_ref, gg_ref = refs
    step = pl.program_id(0)
    dh = None
    for at, ref in zip(starts, pieces):
        part = dot(ref[...], w_ref[:, at : at + ref.shape[1]], ((1,), (1,)))
        dh = part if dh is None else dh + part
    unit, inv = unit_norm(x_ref[...].astype(F32))
    gain_part = jnp.sum(dh * unit, axis=0, keepdims=True)
    dx_ref[...] = dx1_ref[...] + norm_back(dh, gain_ref[...], unit, inv)

    @pl.when(step == 0)
    def _():
        gg_ref[...] = gain_part

    @pl.when(step > 0)
    def _():
        gg_ref[...] += gain_part


def qkv_backward(pieces, starts, tokens, dx1, w_qkv, gain):
    t, d = tokens.shape
    return pl.pallas_call(
        functools.partial(qkv_back_kernel, starts),
        grid=(t // BLOCK,),
        in_specs=[rows(p.shape[1]) for p in pieces] + [rows(d)] * 2 + [whole((d, 3 * d)), whole((1, d))],
        out_specs=[rows(d), whole((1, d))],
        out_shape=[shaped((t, d), F32), shaped((1, d), F32)],
        compiler_params=params(48),
        cost_estimate=pl.CostEstimate(flops=6 * t * d * d, transcendentals=0, bytes_accessed=6 * d * d + 16 * t * d),
        name="qkv_backward",
    )(*pieces, tokens, dx1, w_qkv, gain)


def layout(doc_lengths, seq):
    docs = doc_lengths.shape[-1]
    upto = jnp.arange(docs)[:, None] <= jnp.arange(docs)[None, :]
    ends = jnp.sum(jnp.where(upto[None], doc_lengths[:, :, None], 0), axis=1)
    places = jnp.arange(seq, dtype=jnp.int32)
    passed = places[None, :, None] >= ends[:, None, :]
    start = jnp.sum(jnp.where(passed, doc_lengths[:, None, :], 0), axis=-1)
    valid = places[None, :] < ends[:, docs - 2 : docs - 1]
    return start.astype(jnp.int32), places[None, :] - start, valid


def tables(position):
    half = HEAD_DIM // 2
    lane = jnp.arange(PAIR)
    frequency = jnp.exp((lane % half).astype(F32) * (-2.0 * math.log(10000.0) / HEAD_DIM))
    angles = position.reshape(-1, 1).astype(F32) * frequency[None, :]
    sign = jnp.where(lane % HEAD_DIM < half, -1.0, 1.0)
    return jnp.cos(angles), jnp.sin(angles) * sign[None, :]


Z = 4
GROUPS = ((0, 2), (1, 3))


def index(x, core, z, y):
    return ((x * 2 + core) * Z + z) * 2 + y


def permute(value, move):
    places = [(x, c, z, y) for x in range(2) for c in range(2) for z in range(Z) for y in range(2)]
    return lax.ppermute(value, AXES, [(index(*p), index(*move(*p))) for p in places])


def over_x(v):
    return permute(v, lambda x, c, z, y: (1 - x, c, z, y))


def over_y(v):
    return permute(v, lambda x, c, z, y: (x, c, z, 1 - y))


def over_core(v):
    return permute(v, lambda x, c, z, y: (x, 1 - c, z, y))


def over_z(v, shift):
    return permute(v, lambda x, c, z, y: (x, c, (z + shift) % Z, y))


def across_z(v, bit):
    return permute(v, lambda x, c, z, y: (x, c, z ^ bit, y))


def place():
    dp, fs = lax.axis_index("dp"), lax.axis_index("fsdp")
    return dp // 2, dp % 2, fs // 2, fs % 2


def gather_order():
    x, c, z, y = place()
    order = []
    for core in range(2):
        for group, first in zip(GROUPS, ("x", "y")):
            for second in range(2):
                for one in range(2):
                    dx, dy = (one, second) if first == "x" else (second, one)
                    for shift in group:
                        order.append(index(x ^ dx, c ^ core, (z - shift) % Z, y ^ dy))
    return jnp.stack(order).astype(jnp.int32)


def scatter_order():
    x, c, z, y = place()
    order = []
    for core in range(2):
        for group, first in zip(GROUPS, ("y", "x")):
            for one in (1, 0):
                for second in (1, 0):
                    dx, dy = (second, one) if first == "y" else (one, second)
                    for shift in group:
                        order.append(index(x ^ dx, c ^ core, (z + shift) % Z, y ^ dy))
    return jnp.stack(order).astype(jnp.int32)


def tie(value, other):
    return lax.optimization_barrier((value, other))[0]


class Gather:
    def __init__(self, block):
        self.by_z = [block]

    def z(self, after=None):
        block = self.by_z[0] if after is None else tie(self.by_z[0], after)
        self.by_z = [block] + [over_z(block, s) for s in (1, 2, 3)]
        return self.by_z[1:]

    def first(self, after=None):
        even = jnp.stack([self.by_z[s] for s in GROUPS[0]])
        odd = jnp.stack([self.by_z[s] for s in GROUPS[1]])
        if after is not None:
            even, odd = tie((even, odd), after)
        self.even = jnp.concatenate([even, over_x(even)])
        self.odd = jnp.concatenate([odd, over_y(odd)])
        return [self.even, self.odd]

    def second(self, after=None):
        even, odd = (self.even, self.odd) if after is None else tie((self.even, self.odd), after)
        self.near = [even, odd, over_core(even), over_core(odd)]
        self.far = [over_y(even), over_x(odd)]
        return self.far

    def core(self, after=None):
        far = self.far if after is None else tie(self.far, after)
        even, odd, even_core, odd_core = self.near
        return [even, far[0], odd, far[1], even_core, over_core(far[0]), odd_core, over_core(far[1])]


class Reduce:
    def __init__(self, keep, send):
        self.keep, self.send = keep, send

    def core(self, after=None):
        send = self.send if after is None else tie(self.send, after)
        self.got = self.core_got = over_core(send)
        return self.got

    def first(self, after=None):
        total = self.keep + self.got.astype(F32)
        self.a, self.b = total[:8], total[8:]
        sends = (self.a[:4].astype(BF), self.b[:4].astype(BF))
        if after is not None:
            sends = tie(sends, after)
        self.got = (over_y(sends[0]), over_x(sends[1]))
        return self.got

    def second(self, after=None):
        self.a = self.a[4:] + self.got[0].astype(F32)
        self.b = self.b[4:] + self.got[1].astype(F32)
        sends = (self.a[:2].astype(BF), self.b[:2].astype(BF))
        if after is not None:
            sends = tie(sends, after)
        self.got = (over_x(sends[0]), over_y(sends[1]))
        return self.got

    def z(self, after=None):
        self.a = self.a[2:] + self.got[0].astype(F32)
        self.b = self.b[2:] + self.got[1].astype(F32)
        sends = (self.b[0].astype(BF), self.a[1].astype(BF), self.b[1].astype(BF))
        if after is not None:
            sends = tie(sends, after)
        self.got = [over_z(s, i + 1) for i, s in enumerate(sends)]
        return self.got

    def own(self):
        return self.a[0] + sum(g.astype(F32) for g in self.got)


def unslab(block, width):
    size = block.shape[0] * LANES // width
    return jnp.concatenate([block[s * size : (s + 1) * size] for s in range(width // LANES)], axis=1)


def slab(block):
    return [block[:, s * LANES : (s + 1) * LANES] for s in range(block.shape[1] // LANES)]


def local(fast, tokens, doc_lengths, cotangent, w_qkv, w_out, w_up, w_down,
          gain_attn, gain_inner, gain_ffn, gain_mid):
    row_count = doc_lengths.shape[0]
    seq = tokens.shape[0] // row_count
    d = tokens.shape[1]
    wide = min(seq, 512) // BLOCK + 1
    blocks = seq // BLOCK
    shards = (gain_attn, gain_inner, gain_ffn, gain_mid)
    sizes = [g.shape[0] for g in shards]

    start, position, valid = layout(doc_lengths, seq)
    cos, sin = tables(position)
    firsts = start[:, ::BLOCK] // BLOCK
    reach = (jnp.arange(blocks, dtype=jnp.int32)[None, :] - firsts + 1).reshape(-1)
    start_col = start.reshape(-1, 1)
    start_row = jnp.repeat(start, 8, axis=0)
    valid_col = valid.astype(jnp.int32).reshape(-1, 1)

    def scatter(g):
        return lax.psum_scatter(g, AXES, scatter_dimension=0, tiled=True)

    def gather(v):
        return lax.all_gather(v, AXES, axis=0, tiled=True)

    if fast:
        order, back = gather_order(), scatter_order()
        gains_row = jnp.pad(jnp.concatenate(shards)[None], ((0, 7), (0, LANES - sum(sizes))))
        rest_of = jnp.concatenate([w_out] + slab(w_up) + [w_down])
        parts_up = [gather(rest_of).reshape(-1, *rest_of.shape)]
        part_down = parts_up[0]
        one = Gather(jnp.concatenate(slab(w_qkv) + [gains_row]))
        one.z()
        one.first()
        one.second()
        parts_qkv = one.core()
        gains = [None]
    else:
        order = back = jnp.zeros((8,), jnp.int32)
        parts_qkv, parts_up, part_down = [gather(w_qkv)], [gather(w_out), gather(w_up)], gather(w_down)
        gains = [gather(g).astype(F32).reshape(1, -1) for g in shards]

    h1, qkv, full_qkv, *rest = qkv_forward(fast, order, tokens, cos, sin, parts_qkv, gains[0], sizes)
    g_attn, g_inner, g_ffn, g_mid = rest if fast else gains
    mixed, lse = attention_forward(reach, qkv, start_col, row_count, wide)
    a, x1, h2, m, slope, inv, full_out, full_up, grad_down = up_forward(
        fast, mixed, tokens, cotangent, valid_col, g_inner, g_ffn, g_mid, parts_up
    )
    own_down = scatter(grad_down).astype(F32)
    result, dpre, grad_mid = down_both(fast, m, slope, inv, x1, cotangent, valid_col, g_mid, part_down)
    dx1, low, d_mixed, grad_ffn, grad_inner = up_backward(
        dpre, x1, cotangent, valid_col, mixed, full_up, full_out, g_ffn, g_inner
    )
    grad_up = up_weight_grad(fast, back, h2, dpre, a, low)
    if fast:
        red_up = Reduce(*grad_up)
        red_up.core()

    def attend(base, pairs, lse):
        return attention_backward(
            reach, qkv, d_mixed, mixed, lse, start_row, cos, sin, row_count, wide, base, pairs
        )

    third = PAIRS // 3
    lse = tie(lse, grad_up[-1])
    g0 = attend(0, third, lse)
    if fast:
        first = red_up.first(g0)
        lse = tie(lse, red_up.core_got)
    g1 = attend(third, third, tie(lse, g0))
    if fast:
        second = red_up.second(g1)
        lse = tie(lse, first)
    g2 = attend(2 * third, third, tie(lse, g1))
    if fast:
        up_z = red_up.z(g2)
        h1, own_down = tie((h1, own_down), second)
    pieces, starts = [], []
    for part in range(3):
        for g, group in enumerate((g0, g1, g2)):
            pieces.append(group[part])
            starts.append(part * d + g * third * PAIR)
    grad_qkv = qkv_weight_grad(fast, back, h1, pieces)
    if fast:
        red_qkv = Reduce(*grad_qkv)
        red_qkv.core()
        dx1 = tie(dx1, (up_z, grad_qkv[-1]))
    grad_tokens, grad_attn = qkv_backward(pieces, starts, tokens, dx1, full_qkv, g_attn)
    gain_grads = (grad_attn, grad_inner, grad_ffn, grad_mid)
    if fast:
        own_up = red_up.own()
        red_qkv.first()
        second = red_qkv.second(grad_attn)
        red_qkv.z()
        packed = jnp.concatenate([g.reshape(-1, LANES) for g in gain_grads])
        packed = jnp.pad(packed, ((0, -packed.shape[0] % 8), (0, 0)))
        packed = packed + over_core(packed)
        packed = packed + over_x(packed)
        packed = packed + over_y(packed)
        packed = packed + over_z(packed, 1) + over_z(packed, 2) + over_z(packed, 3)
        size = w_out.shape[0]
        weights = (unslab(red_qkv.own(), w_qkv.shape[1]), own_up[:size], unslab(own_up[size:], w_up.shape[1]))
        me = index(*place())
        summed, at = [], 0
        for size, full in zip(sizes, gain_grads):
            flat = packed[at : at + full.size // LANES].reshape(-1)
            summed.append(lax.dynamic_slice(flat, (me * size,), (size,)))
            at += full.size // LANES
    else:
        weights = tuple(scatter(g.astype(BF)).astype(F32) for g in (grad_qkv[0], grad_up[0], grad_up[1]))
        summed = [scatter(g.reshape(-1)) for g in gain_grads]
    return (result, grad_tokens) + weights + (own_down,) + tuple(summed)


def solution(mesh):
    matrix, vector = P(AXES, None), P(AXES)
    fast = mesh.shape["dp"] == 4 and mesh.shape["fsdp"] == 2 * Z
    return jax.shard_map(
        functools.partial(local, fast),
        mesh=mesh,
        in_specs=(matrix,) * 7 + (vector,) * 4,
        out_specs=(matrix,) * 6 + (vector,) * 4,
        check_vma=False,
    )
```

```python
import functools
import math

import jax
import jax.numpy as jnp
import numpy as np
from jax import lax
from jax.experimental import pallas as pl
from jax.experimental.pallas import tpu as pltpu
from jax.sharding import PartitionSpec as P

HEADS = 12
HEAD_DIM = 64
PAIR = 2 * HEAD_DIM
PAIRS = HEADS // 2
EPSILON = 1e-05
MASKED_SCORE = -1e30
ROOT_HALF = 0.7071067811865476
INV_ROOT_TAU = 0.3989422804014327
BF = jnp.bfloat16
F32 = jnp.float32
MIB = 1 << 20
AXES = ("dp", "fsdp")
BLOCK = 256
LANES = 768
VMEM_MIB = 60
GRAD_GROUPS = 3


def dot(a, b, dims=((1,), (0,))):
    return lax.dot_general(a, b, (dims, ((), ())), preferred_element_type=F32)


def params(mib):
    return pltpu.CompilerParams(vmem_limit_bytes=max(mib, VMEM_MIB) * MIB)


def swap_halves(x):
    lane = lax.broadcasted_iota(jnp.int32, x.shape, 1)
    low = lax.rem(lane, HEAD_DIM) < HEAD_DIM // 2
    half = HEAD_DIM // 2
    return jnp.where(low, pltpu.roll(x, PAIR - half, 1), pltpu.roll(x, half, 1))


def unit_norm(x):
    mean = jnp.mean(x, axis=-1, keepdims=True)
    centred = x - mean
    inv = lax.rsqrt(jnp.mean(centred * centred, axis=-1, keepdims=True) + EPSILON)
    return centred * inv, inv


def norm_back(grad, gain, unit, inv):
    d_unit = grad * gain
    return inv * (
        d_unit
        - jnp.mean(d_unit, axis=-1, keepdims=True)
        - unit * jnp.mean(d_unit * unit, axis=-1, keepdims=True)
    )


def whole(shape):
    return pl.BlockSpec(shape, lambda *_: (0,) * len(shape), pipeline_mode=pl.Buffered(1))


def rows(width, block=BLOCK):
    return pl.BlockSpec((block, width), lambda i: (i, 0))


def shaped(shape, dtype):
    return jax.ShapeDtypeStruct(shape, dtype)


def hbm():
    return pl.BlockSpec(memory_space=pl.ANY)


def fetch(order, parts, places, sem):
    if len(parts) < 8 and parts[0].ndim == 2:
        for part, (_, _, buffer, _) in zip(parts, places):
            pltpu.make_async_copy(part, buffer, sem).start()
        return
    count = parts[0].shape[0]
    for p, part in enumerate(parts):
        for b in range(count):
            owner = b if order is None else order[p * count + b]
            for first, size, buffer, column in places:
                row = owner * size if order is None else pl.multiple_of(owner * size, 8)
                pltpu.make_async_copy(
                    part.at[b, pl.ds(first, size), :],
                    buffer.at[pl.ds(row, size), pl.ds(column, LANES)],
                    sem,
                ).start()


def arrive(buffers, sem):
    for buffer in buffers:
        pltpu.make_async_copy(buffer, buffer, sem).wait()


def deal(back, tile, outs, row, size):
    quarter = outs[0].shape[0]
    for q, out in enumerate(outs):

        @pl.loop(0, quarter)
        def _(j):
            block = tile[pl.ds(pl.multiple_of(back[q * quarter + j] * size, 8), size), :]
            out[j, pl.ds(row, size), :] = block.astype(out.dtype)


def slabs(first, size, buffer, width):
    return [(first + s * size, size, buffer, s * LANES) for s in range(width // LANES)]


def spread(rows_in, offset, count, owners):
    lanes = rows_in.shape[1]
    wide = owners * count
    lane = lax.broadcasted_iota(jnp.int32, (lanes, wide), 0)
    column = lax.broadcasted_iota(jnp.int32, (lanes, wide), 1)
    pick = (lane - offset == lax.rem(column, count)).astype(F32).astype(BF)
    full = dot(rows_in, pick)
    owner = lax.broadcasted_iota(jnp.int32, (owners, wide), 0)
    column = lax.broadcasted_iota(jnp.int32, (owners, wide), 1)
    own = (column >= owner * count) & (column < owner * count + count)
    return jnp.sum(jnp.where(own, full, 0.0), axis=0, keepdims=True)


def qkv_kernel(split, sizes, *refs):
    if split:
        order, x_ref, cos_ref, sin_ref, *refs = refs
        parts, refs = refs[:8], refs[8:]
        h_ref, other_ref, qkv_ref, w_ref, ga_ref, gi_ref, gf_ref, gm_ref, gains, sem, gain_sem = refs
        h_refs = (h_ref, other_ref)
    else:
        order, x_ref, cos_ref, sin_ref, ga_ref, *refs = refs
        parts, refs = refs[:1], refs[1:]
        h_ref, qkv_ref, w_ref, sem = refs
        h_refs = (h_ref,)
    width = x_ref.shape[1]
    step = pl.program_id(0)
    if split:
        size = width // 32
        weight = slabs(0, size, w_ref, 3 * width)

        @pl.when(step == 0)
        def _():
            fetch(order, parts, [(3 * size, 8, gains, 0)], gain_sem)
            fetch(order, parts, weight, sem)
            arrive([gains], gain_sem)
            owner = lax.broadcasted_iota(jnp.int32, (32, 256), 0)
            lane = lax.broadcasted_iota(jnp.int32, (32, 256), 1)
            pick = (lane == owner * 8).astype(F32).astype(BF)
            per_owner = dot(pick, gains[:, :256]).astype(BF)
            at = 0
            for ref, count in zip((ga_ref, gi_ref, gf_ref, gm_ref), sizes):
                ref[...] = spread(per_owner, at, count, 32)
                at += count
            arrive([w_ref], sem)
    else:

        @pl.when(step == 0)
        def _():
            fetch(None, parts, [(0, 0, w_ref, 0)], sem)
            arrive([w_ref], sem)

    unit, _ = unit_norm(x_ref[...].astype(F32))
    h = (unit * ga_ref[...]).astype(BF)
    store_low(split, order[32] if split else 0, h, h_refs)
    cos, sin = cos_ref[...], sin_ref[...]
    for part in range(3):
        y = dot(h, w_ref[:, part * width : (part + 1) * width])
        for c in range(width // PAIR):
            z = y[:, c * PAIR : (c + 1) * PAIR]
            if part < 2:
                z = z * cos + swap_halves(z) * sin
            if part == 0:
                z = z * (1.0 / math.sqrt(HEAD_DIM))
            at = part * width + c * PAIR
            qkv_ref[:, at : at + PAIR] = z.astype(BF)


def prefetched(kernel, order, inputs, in_specs, out_specs, out_shape, scratch, grid, mib, name, flops, data):
    return pl.pallas_call(
        kernel,
        grid_spec=pltpu.PrefetchScalarGridSpec(
            num_scalar_prefetch=1,
            grid=grid,
            in_specs=in_specs,
            out_specs=out_specs,
            scratch_shapes=scratch,
        ),
        out_shape=out_shape,
        compiler_params=params(mib),
        cost_estimate=pl.CostEstimate(flops=flops, transcendentals=0, bytes_accessed=data),
        name=name,
    )(order, *inputs)


def rows(width, block=BLOCK):
    return pl.BlockSpec((block, width), lambda i, *_: (i, 0))


def whole(shape):
    return pl.BlockSpec(shape, lambda *_: (0,) * len(shape), pipeline_mode=pl.Buffered(1))


def qkv_forward(split, order, tokens, cos, sin, parts, gain, sizes):
    t, d = tokens.shape
    n = 3 * d
    inputs = [tokens, cos, sin]
    in_specs = [rows(d), rows(PAIR), rows(PAIR)]
    out_specs, out_shape = low_specs(split, t, d)
    lows = len(out_specs)
    out_specs = out_specs + [rows(n), whole((d, n))]
    out_shape = out_shape + [shaped((t, n), BF), shaped((d, n), BF)]
    scratch = [pltpu.SemaphoreType.DMA]
    if split:
        widths = [32 * s for s in sizes]
        out_specs += [whole((1, w)) for w in widths]
        out_shape += [shaped((1, w), F32) for w in widths]
        scratch = [pltpu.VMEM((32 * 8, LANES), BF), pltpu.SemaphoreType.DMA, pltpu.SemaphoreType.DMA]
    else:
        inputs.append(gain)
        in_specs.append(whole((1, d)))
    outs = prefetched(
        functools.partial(qkv_kernel, split, sizes), order, inputs + list(parts), in_specs + [hbm()] * len(parts),
        out_specs, out_shape, scratch, (t // BLOCK,), 40, "qkv_forward",
        2 * t * d * n, 4 * d * n + 12 * t * d,
    )
    return (outs[:lows], *outs[lows:])


def window(i, n):
    return slice((i - n + 1) * BLOCK, (i + 1) * BLOCK)


def head_masks(shape):
    lane = lax.broadcasted_iota(jnp.int32, shape, 1)
    return lane < HEAD_DIM


def attention_forward_kernel(wide, reach, q_ref, k_ref, v_ref, start_ref, o_ref, lse_ref, bias):
    row, pair = pl.program_id(0), pl.program_id(1)
    seq = q_ref.shape[0]
    blocks = seq // BLOCK

    @pl.when(pair == 0)
    def _():
        for i in range(blocks):
            at = slice(i * BLOCK, (i + 1) * BLOCK)
            shape = (BLOCK, wide * BLOCK)
            key = (i - wide + 1) * BLOCK + lax.broadcasted_iota(jnp.int32, shape, 1)
            query = i * BLOCK + lax.broadcasted_iota(jnp.int32, shape, 0)
            keep = (key >= start_ref[at, :]) & (key <= query)
            bias[at, :] = jnp.where(keep, 0.0, MASKED_SCORE)

    first = head_masks((BLOCK, PAIR))
    for i in range(blocks):
        at = slice(i * BLOCK, (i + 1) * BLOCK)
        most = min(wide, i + 1)
        for n in range(1, most + 1):

            @pl.when(reach[row * blocks + i] == n)
            def _():
                q = q_ref[at, :]
                w = window(i, n)
                k, v = k_ref[w, :], v_ref[w, :]
                b = bias[at, (wide - n) * BLOCK :]
                mask = head_masks(k.shape)
                zero = jnp.zeros_like(k)
                total, lses = None, []
                scale = None
                for h in range(2):
                    pick = mask if h == 0 else jnp.logical_not(mask)
                    s = dot(q, jnp.where(pick, k, zero), ((1,), (1,))) + b
                    top = jnp.max(s, axis=-1, keepdims=True)
                    p = jnp.exp(s - top)
                    den = jnp.sum(p, axis=-1, keepdims=True)
                    probs = (p * (1.0 / den)).astype(BF)
                    part = dot(probs, jnp.where(pick, v, zero))
                    total = part if total is None else total + part
                    lses.append(top + jnp.log(den))
                o_ref[at, :] = total
                both = jnp.where(first, lses[0], lses[1]).T
                lse_ref[0, 0:1, at] = both[0:1, :]
                lse_ref[0, 1:2, at] = both[HEAD_DIM : HEAD_DIM + 1, :]


def attention_forward(reach, qkv, start, row_count, wide):
    t = qkv.shape[0]
    seq = t // row_count
    d = qkv.shape[1] // 3

    def columns(part):
        return pl.BlockSpec((seq, PAIR), lambda r, p, *_: (r, part * PAIRS + p))

    return pl.pallas_call(
        functools.partial(attention_forward_kernel, wide),
        grid_spec=pltpu.PrefetchScalarGridSpec(
            num_scalar_prefetch=1,
            grid=(row_count, PAIRS),
            in_specs=[
                columns(0),
                columns(1),
                columns(2),
                pl.BlockSpec((seq, 1), lambda r, p, *_: (r, 0)),
            ],
            out_specs=[
                pl.BlockSpec((seq, PAIR), lambda r, p, *_: (r, p)),
                pl.BlockSpec((1, 8, seq), lambda r, p, *_: (r * PAIRS + p, 0, 0)),
            ],
            scratch_shapes=[pltpu.VMEM((seq, wide * BLOCK), F32)],
        ),
        out_shape=[shaped((t, d), F32), shaped((row_count * PAIRS, 8, seq), F32)],
        compiler_params=params(32),
        cost_estimate=pl.CostEstimate(
            flops=8 * t * d * BLOCK, transcendentals=t * HEADS * 512, bytes_accessed=12 * t * d
        ),
        name="attention_forward",
    )(reach, qkv, qkv, qkv, start)


def attention_backward_kernel(wide, reach, q_ref, k_ref, v_ref, do_ref, o_ref, lse_ref, start_ref, cos_ref, sin_ref, *refs):
    grad_ref, bias, ks, vs, qs, dos, dk_acc, dv_acc, dq_acc = refs[-9:]
    row, pair = pl.program_id(0), pl.program_id(1)
    seq = q_ref.shape[0]
    blocks = seq // BLOCK

    @pl.when(pair == 0)
    def _():
        for i in range(blocks):
            at = slice(i * BLOCK, (i + 1) * BLOCK)
            shape = (wide * BLOCK, BLOCK)
            key = (i - wide + 1) * BLOCK + lax.broadcasted_iota(jnp.int32, shape, 0)
            query = i * BLOCK + lax.broadcasted_iota(jnp.int32, shape, 1)
            keep = (key >= start_ref[0:1, at]) & (key <= query)
            bias[:, at] = jnp.where(keep, 0.0, MASKED_SCORE)

    mask = head_masks((seq, PAIR))
    for src, dst in ((k_ref, ks), (v_ref, vs), (q_ref, qs), (do_ref, dos)):
        x = src[...]
        zero = jnp.zeros_like(x)
        dst[0] = jnp.where(mask, x, zero)
        dst[1] = jnp.where(mask, zero, x)
    dk_acc[...] = jnp.zeros_like(dk_acc)
    dv_acc[...] = jnp.zeros_like(dv_acc)
    lane8 = lax.broadcasted_iota(jnp.int32, (8, PAIR), 1) // HEAD_DIM
    row8 = lax.broadcasted_iota(jnp.int32, (8, PAIR), 0)
    picks = (lane8 == row8).astype(F32)
    delta = lax.dot_general(
        picks, do_ref[...].astype(F32) * o_ref[...], (((1,), (1,)), ((), ())),
        precision=lax.Precision.HIGHEST, preferred_element_type=F32,
    )
    for i in range(blocks):
        at = slice(i * BLOCK, (i + 1) * BLOCK)
        most = min(wide, i + 1)
        for n in range(1, most + 1):

            @pl.when(reach[row * blocks + i] == n)
            def _():
                w = window(i, n)
                b = bias[(wide - n) * BLOCK :, at]
                q, do = q_ref[at, :], do_ref[at, :]
                ps, dss = [], []
                for h in range(2):
                    s = dot(ks[h, w, :], q, ((1,), (1,))) + b
                    p = jnp.exp(s - lse_ref[0, h : h + 1, at])
                    dp = dot(vs[h, w, :], do, ((1,), (1,)))
                    ds = (p * (dp - delta[h : h + 1, at])).astype(BF)
                    ps.append(p.astype(BF))
                    dss.append(ds)
                dv_acc[w, :] += dot(ps[0], dos[0, at, :]) + dot(ps[1], dos[1, at, :])
                dk_acc[w, :] += dot(dss[0], qs[0, at, :]) + dot(dss[1], qs[1, at, :])
                dq_acc[at, :] = dot(dss[0], ks[0, w, :], ((0,), (0,))) + dot(
                    dss[1], ks[1, w, :], ((0,), (0,))
                )

    cos, sin = cos_ref[...], sin_ref[...]
    dq = dq_acc[...] * (1.0 / math.sqrt(HEAD_DIM))
    dk = dk_acc[...]
    span = grad_ref.shape[2] // 3
    grads = (dq * cos - swap_halves(dq) * sin, dk * cos - swap_halves(dk) * sin, dv_acc[...])
    for part, value in enumerate(grads):
        grad_ref[0, :, pl.ds(pl.multiple_of(part * span + pair * PAIR, PAIR), PAIR)] = value.astype(BF)


def attention_backward(reach, qkv, d_mixed, mixed, lse, start_row, cos, sin, row_count, wide, group, pairs, so_far):
    t = qkv.shape[0]
    seq = t // row_count
    base = group * pairs
    span = 3 * pairs * PAIR

    def columns(part):
        return pl.BlockSpec((seq, PAIR), lambda r, p, *_: (r, part * PAIRS + base + p))

    table = pl.BlockSpec((seq, PAIR), lambda r, p, *_: (r, 0))
    inputs = [reach, qkv, qkv, qkv, d_mixed, mixed, lse, start_row, cos, sin]
    in_specs = [
        columns(0), columns(1), columns(2), columns(0), columns(0),
        pl.BlockSpec((1, 8, seq), lambda r, p, *_: (r * PAIRS + base + p, 0, 0)),
        pl.BlockSpec((8, seq), lambda r, p, *_: (r, 0)),
        table, table,
    ]
    aliases = {}
    if so_far is not None:
        aliases = {len(inputs): 0}
        inputs.append(so_far)
        in_specs.append(hbm())
    return pl.pallas_call(
        functools.partial(attention_backward_kernel, wide),
        grid_spec=pltpu.PrefetchScalarGridSpec(
            num_scalar_prefetch=1,
            grid=(row_count, pairs),
            in_specs=in_specs,
            out_specs=pl.BlockSpec((1, seq, span), lambda r, p, *_: (group, r, 0)),
            scratch_shapes=[
                pltpu.VMEM((wide * BLOCK, seq), F32),
                pltpu.VMEM((2, seq, PAIR), BF),
                pltpu.VMEM((2, seq, PAIR), BF),
                pltpu.VMEM((2, seq, PAIR), BF),
                pltpu.VMEM((2, seq, PAIR), BF),
                pltpu.VMEM((seq, PAIR), F32),
                pltpu.VMEM((seq, PAIR), F32),
                pltpu.VMEM((seq, PAIR), F32),
            ],
        ),
        out_shape=shaped((PAIRS // pairs, t, span), BF),
        input_output_aliases=aliases,
        compiler_params=params(40),
        cost_estimate=pl.CostEstimate(
            flops=20 * t * span * BLOCK // 3, transcendentals=t * HEADS * 128, bytes_accessed=20 * t * span // 3
        ),
        name="attention_backward",
    )(*inputs)


def halves(x):
    quarter = x.shape[1] // 4
    piece = [x[:, i * quarter : (i + 1) * quarter] for i in range(4)]
    return jnp.concatenate(piece[0::2], axis=1), jnp.concatenate(piece[1::2], axis=1)


def store_low(split, core, x, refs):
    if not split:
        refs[0][...] = x
        return
    pair = halves(x)
    for c in range(2):

        @pl.when(core == c)
        def _():
            refs[0][...] = pair[c]
            refs[1][...] = pair[1 - c]


def low_specs(split, t, d):
    if split:
        return [rows(d // 2)] * 2, [shaped((t, d // 2), BF)] * 2
    return [rows(d)], [shaped((t, d), BF)]


def up_kernel(split, *refs):
    core, o_ref, x_ref, gi_ref, gf_ref, gm_ref, *refs = refs
    count = 1 if split else 2
    lows = 3 - count
    parts, refs = refs[:count], refs[count:]
    a_refs, h2_refs, refs = refs[:lows], refs[lows : 2 * lows], refs[2 * lows :]
    x1_ref, m_ref, slope_ref, inv_ref, wo_ref, wu_ref, *refs = refs
    sem = refs[-1]
    d, f = wu_ref.shape
    size = d // 32
    step = pl.program_id(0)
    places = [(0, size, wo_ref, 0)] + slabs(size, size, wu_ref, f) if split else [(0, 0, wo_ref, 0), (0, 0, wu_ref, 0)]

    @pl.when(step == 0)
    def _():
        fetch(None, parts, places, sem)

    unit, _ = unit_norm(o_ref[...])
    a = (unit * gi_ref[...]).astype(BF)
    store_low(split, core[0], a, a_refs)

    @pl.when(step == 0)
    def _():
        arrive([wo_ref, wu_ref], sem)

    x1 = x_ref[...].astype(F32) + dot(a, wo_ref[...])
    x1_ref[...] = x1
    unit, _ = unit_norm(x1)
    h2 = (unit * gf_ref[...]).astype(BF)
    store_low(split, core[0], h2, h2_refs)
    hidden = dot(h2, wu_ref[...])
    cdf = 0.5 + 0.5 * lax.erf(hidden * ROOT_HALF)
    slope = cdf + hidden * (jnp.exp(-0.5 * hidden * hidden) * INV_ROOT_TAU)
    slope_ref[...] = slope.astype(BF)
    unit, inv = unit_norm(hidden * cdf)
    m_ref[...] = (unit * gm_ref[...]).astype(BF)
    inv_ref[...] = jnp.broadcast_to(inv, inv_ref.shape)
    if split:
        quarter = f // 4
        for j in range(2):
            at = pl.multiple_of((2 * j + 1 - core[0]) * quarter, PAIR)
            refs[0][:, j * quarter : (j + 1) * quarter] = m_ref[:, pl.ds(at, quarter)]


def up_forward(split, core, mixed, tokens, gain_inner, gain_ffn, gain_mid, parts):
    t, d = tokens.shape
    f = gain_mid.shape[1]
    low_out, low_shape = low_specs(split, t, d)
    more = [(rows(f // 2), shaped((t, f // 2), BF))] * split
    outs = prefetched(
        functools.partial(up_kernel, split), core, [mixed, tokens, gain_inner, gain_ffn, gain_mid, *parts],
        [rows(d), rows(d), whole((1, d)), whole((1, d)), whole((1, f))] + [hbm()] * len(parts),
        low_out * 2 + [rows(d), rows(f), rows(f), rows(PAIR), whole((d, d)), whole((d, f))] + [m[0] for m in more],
        low_shape * 2 + [
            shaped((t, d), F32), shaped((t, f), BF), shaped((t, f), BF), shaped((t, PAIR), F32),
            shaped((d, d), BF), shaped((d, f), BF),
        ] + [m[1] for m in more],
        [pltpu.SemaphoreType.DMA], (t // BLOCK,), 60, "up_forward",
        2 * t * d * (d + f), 4 * d * (d + f) + 4 * t * f + 16 * t * d,
    )
    lows = len(low_out)
    return (outs[:lows], outs[lows : 2 * lows], *outs[2 * lows :])


def slab_rows(values, first, width):
    count = values.shape[1] // width
    line = lax.broadcasted_iota(jnp.int32, (8, width), 0)
    total = jnp.zeros((8, width), F32)
    for i in range(count):
        total = jnp.where(line == first + i, values[:, i * width : (i + 1) * width], total)
    return total


def down_kernel(split, m_ref, slope_ref, inv_ref, x1_ref, gy_ref, gm_ref, part_ref,
                y_ref, dpre_ref, gg_ref, wd_ref, sem):
    f, d = wd_ref.shape
    step = pl.program_id(0)

    @pl.when(step == 0)
    def _():
        first = part_ref.shape[1] - f // 32 if split else 0
        fetch(None, [part_ref], [(first, f // 32, wd_ref, 0)], sem)
        arrive([wd_ref], sem)

    m = m_ref[...]
    dm = dot(gy_ref[...], wd_ref[...], ((1,), (1,)))
    gain = gm_ref[...]
    mf = m.astype(F32)
    prod = dm * mf
    d_unit = dm * gain
    d_act = inv_ref[:, 0:1] * (
        d_unit
        - jnp.mean(d_unit, axis=-1, keepdims=True)
        - (mf * (1.0 / gain)) * jnp.mean(prod, axis=-1, keepdims=True)
    )
    dpre_ref[...] = (d_act * slope_ref[...].astype(F32)).astype(BF)
    y_ref[...] = (x1_ref[...] + dot(m, wd_ref[...])).astype(BF)
    part = slab_rows(jnp.sum(prod, axis=0, keepdims=True) * (1.0 / gain), 3, d)

    @pl.when(step == 0)
    def _():
        gg_ref[...] = part

    @pl.when(step > 0)
    def _():
        gg_ref[...] += part


def down_both(split, m, slope, inv, x1, gy, gain_mid, part):
    t, d = x1.shape
    f = m.shape[1]
    return pl.pallas_call(
        functools.partial(down_kernel, split),
        grid=(t // BLOCK,),
        in_specs=[rows(f), rows(f), rows(PAIR), rows(d), rows(d), whole((1, f)), hbm()],
        out_specs=[rows(d), rows(f), whole((8, d))],
        out_shape=[shaped((t, d), BF), shaped((t, f), BF), shaped((8, d), F32)],
        scratch_shapes=[pltpu.VMEM((f, d), BF), pltpu.SemaphoreType.DMA],
        compiler_params=params(48),
        cost_estimate=pl.CostEstimate(
            flops=4 * t * d * f, transcendentals=0, bytes_accessed=2 * d * f + 6 * t * f + 8 * t * d
        ),
        name="down_both",
    )(m, slope, inv, x1, gy, gain_mid, part)


def up_back_kernel(dpre_ref, x1_ref, gy_ref, o_ref, wu_ref, wo_ref, gf_ref, gi_ref,
                   dx1_ref, low_ref, do_ref, gg_ref):
    step = pl.program_id(0)
    d = x1_ref.shape[1]
    dh2 = dot(dpre_ref[...], wu_ref[...], ((1,), (1,)))
    unit, inv = unit_norm(x1_ref[...])
    part = slab_rows(jnp.sum(dh2 * unit, axis=0, keepdims=True), 2, d)
    dx1 = gy_ref[...].astype(F32) + norm_back(dh2, gf_ref[...], unit, inv)
    dx1_ref[...] = dx1
    low = dx1.astype(BF)
    low_ref[...] = low
    da = dot(low, wo_ref[...], ((1,), (1,)))
    unit, inv = unit_norm(o_ref[...])
    part = part + slab_rows(jnp.sum(da * unit, axis=0, keepdims=True), 1, d)
    do_ref[...] = norm_back(da, gi_ref[...], unit, inv).astype(BF)

    @pl.when(step == 0)
    def _():
        gg_ref[...] = part

    @pl.when(step > 0)
    def _():
        gg_ref[...] += part


def up_backward(dpre, x1, gy, mixed, w_up, w_out, gain_ffn, gain_inner):
    t, d = x1.shape
    f = dpre.shape[1]
    return pl.pallas_call(
        up_back_kernel,
        grid=(t // BLOCK,),
        in_specs=[rows(f), rows(d), rows(d), rows(d),
                  whole((d, f)), whole((d, d)), whole((1, d)), whole((1, d))],
        out_specs=[rows(d), rows(d), rows(d), whole((8, d))],
        out_shape=[shaped((t, d), F32), shaped((t, d), BF), shaped((t, d), BF), shaped((8, d), F32)],
        compiler_params=params(40),
        cost_estimate=pl.CostEstimate(
            flops=2 * t * d * (d + f), transcendentals=0, bytes_accessed=2 * d * (d + f) + 2 * t * f + 24 * t * d
        ),
        name="up_backward",
    )(dpre, x1, gy, mixed, w_up, w_out, gain_ffn, gain_inner)


def grads_kernel(split, products, *refs):
    back, *refs = refs
    count = 2 if split else 1
    left, refs = refs[: len(products) * count], refs[len(products) * count :]
    right, refs = refs[: len(products) * count], refs[len(products) * count :]
    outs, refs = refs[: 4 if split else len(products)], refs[4 if split else len(products) :]
    tile, turned = refs[0], refs[1:]
    step = pl.program_id(0)
    first, row = 0, 0
    for n, (by_left, tiles, size) in enumerate(products):
        mine = [left[n * count + c] for c in range(count)]
        value = [right[n * count + c] for c in range(count)]

        if not by_left:

            @pl.when(step == first)
            def _():
                t = mine[0].shape[0]
                for c in range(count):
                    turned[0][:, c * t : (c + 1) * t] = mine[c][...].T

        @pl.when((step >= first) & (step < first + tiles))
        def _():
            total = None
            for c in range(count):
                v = value[c][...] if len(value[c].shape) == 2 else value[c][0]
                t = v.shape[0]
                if by_left:
                    part = dot(mine[c][...], v, ((0,), (0,)))
                else:
                    part = dot(turned[0][:, c * t : (c + 1) * t], v)
                total = part if total is None else total + part
            if not split:
                outs[n][...] = total
            else:
                tile[...] = total
                if by_left:
                    owners = tile.shape[0] // size
                    for e in range(owners):
                        at = back[16 + (step - first) * owners + e]
                        for q in range(4):

                            @pl.when(at // 4 == q)
                            def _():
                                block = tile[e * size : (e + 1) * size, :]
                                outs[q][at - 4 * q, row : row + size, :] = block.astype(outs[q].dtype)
                else:
                    deal(back, tile, outs, row + pl.multiple_of((step - first) * size, 8), size)

        first += tiles
        row += size if by_left else tiles * size


def weight_grads(split, back, products):
    count = 2 if split else 1
    t = products[0][0][0].shape[0]
    left_specs, right_specs, lefts, rights, plan = [], [], [], [], []
    out_specs, out_shape = [], []
    at = row = 0
    for left, right, tiles, by_left in products:
        width = 0
        for c in range(count):
            a, b = left[c], right[c]

            if by_left and c == 0:
                tiles = tiles // count
                width = a.shape[1] // (tiles * count)

            def step(i, at=at, tiles=tiles):
                return jnp.clip(i - at, 0, tiles - 1)

            if by_left:
                per = tiles // 2
                if split and c == 0:
                    left_specs.append(pl.BlockSpec(
                        (t, width), lambda i, back, step=step, per=per: (0, (2 * (step(i) // per) + back[32]) * per + step(i) % per)
                    ))
                else:
                    left_specs.append(pl.BlockSpec((t, width), lambda i, *_, step=step: (0, step(i))))
                right_specs.append(whole(b.shape))
            else:
                width = a.shape[1]
                left_specs.append(whole(a.shape))
                if b.ndim == 3:
                    right_specs.append(pl.BlockSpec((1, t, LANES), lambda i, *_, step=step: (step(i), 0, 0)))
                else:
                    right_specs.append(pl.BlockSpec((t, LANES), lambda i, *_, step=step: (0, step(i))))
            lefts.append(a)
            rights.append(b)
        size = (width * tiles if by_left else width) // 16
        if not split:
            shape = (width * tiles, LANES) if by_left else (width, tiles * LANES)
            block = (width, LANES)
            out_specs.append(pl.BlockSpec(
                block, (lambda i, *_, step=step: (step(i), 0)) if by_left else (lambda i, *_, step=step: (0, step(i)))
            ))
            out_shape.append(shaped(shape, F32))
        plan.append((by_left, tiles, size))
        at += tiles
        row += size if by_left else tiles * size
    narrow = next(p[0][0].shape[1] for p in products if not p[3])
    if split:
        out_specs = [whole((4, row, LANES))] * 4
        out_shape = [shaped((4, row, LANES), dtype) for dtype in (BF, F32, BF, F32)]
    flops = 2 * count * t * narrow * at * LANES
    return prefetched(
        functools.partial(grads_kernel, split, tuple(plan)), back, lefts + rights, left_specs + right_specs,
        out_specs, out_shape, [pltpu.VMEM((narrow, LANES), F32), pltpu.VMEM((narrow, count * t), BF)],
        (at,), 60, "weight_grads", flops, flops // 256,
    )


def qkv_back_kernel(d_ref, x_ref, dx1_ref, w_ref, gain_ref, dx_ref, gg_ref):
    step = pl.program_id(0)
    d = x_ref.shape[1]
    groups, _, span = d_ref.shape
    span //= 3
    dh = None
    for part in range(3):
        for g in range(groups):
            at = part * d + g * span
            piece = dot(d_ref[g, :, part * span : (part + 1) * span], w_ref[:, at : at + span], ((1,), (1,)))
            dh = piece if dh is None else dh + piece
    unit, inv = unit_norm(x_ref[...].astype(F32))
    gain_part = slab_rows(jnp.sum(dh * unit, axis=0, keepdims=True), 0, d)
    dx_ref[...] = dx1_ref[...] + norm_back(dh, gain_ref[...], unit, inv)

    @pl.when(step == 0)
    def _():
        gg_ref[...] = gain_part

    @pl.when(step > 0)
    def _():
        gg_ref[...] += gain_part


def qkv_backward(d_qkv, tokens, dx1, w_qkv, gain):
    t, d = tokens.shape
    groups, _, span = d_qkv.shape
    return pl.pallas_call(
        qkv_back_kernel,
        grid=(t // BLOCK,),
        in_specs=[pl.BlockSpec((groups, BLOCK, span), lambda i: (0, i, 0))] + [rows(d)] * 2
        + [whole((d, 3 * d)), whole((1, d))],
        out_specs=[rows(d), whole((8, d))],
        out_shape=[shaped((t, d), F32), shaped((8, d), F32)],
        compiler_params=params(48),
        cost_estimate=pl.CostEstimate(flops=6 * t * d * d, transcendentals=0, bytes_accessed=6 * d * d + 16 * t * d),
        name="qkv_backward",
    )(d_qkv, tokens, dx1, w_qkv, gain)


def layout(doc_lengths, seq):
    docs = doc_lengths.shape[-1]
    upto = jnp.arange(docs)[:, None] <= jnp.arange(docs)[None, :]
    ends = jnp.sum(jnp.where(upto[None], doc_lengths[:, :, None], 0), axis=1)
    places = jnp.arange(seq, dtype=jnp.int32)
    passed = places[None, :, None] >= ends[:, None, :]
    start = jnp.sum(jnp.where(passed, doc_lengths[:, None, :], 0), axis=-1)
    valid = places[None, :] < ends[:, docs - 2 : docs - 1]
    return start.astype(jnp.int32), places[None, :] - start, valid


def tables(position):
    half = HEAD_DIM // 2
    lane = jnp.arange(PAIR)
    frequency = jnp.exp((lane % half).astype(F32) * (-2.0 * math.log(10000.0) / HEAD_DIM))
    angles = position.reshape(-1, 1).astype(F32) * frequency[None, :]
    sign = jnp.where(lane % HEAD_DIM < half, -1.0, 1.0)
    return jnp.cos(angles), jnp.sin(angles) * sign[None, :]


Z = 4
GROUPS = ((0, 2), (1, 3))


def index(x, core, z, y):
    return ((x * 2 + core) * Z + z) * 2 + y


def permute(value, move):
    places = [(x, c, z, y) for x in range(2) for c in range(2) for z in range(Z) for y in range(2)]
    return lax.ppermute(value, AXES, [(index(*p), index(*move(*p))) for p in places])


def over_x(v):
    return permute(v, lambda x, c, z, y: (1 - x, c, z, y))


def over_y(v):
    return permute(v, lambda x, c, z, y: (x, c, z, 1 - y))


def over_core(v):
    return permute(v, lambda x, c, z, y: (x, 1 - c, z, y))


def over_z(v, shift):
    return permute(v, lambda x, c, z, y: (x, c, (z + shift) % Z, y))


def place():
    dp, fs = lax.axis_index("dp"), lax.axis_index("fsdp")
    return dp >> 1, dp & 1, fs >> 1, fs & 1


def gather_order():
    rows_of = []
    for core in range(2):
        for group, first in zip(GROUPS, ("x", "y")):
            for second in range(2):
                for one in range(2):
                    dx, dy = (one, second) if first == "x" else (second, one)
                    rows_of += [(dx, core, Z - shift, dy) for shift in group]
    dx, dc, dz, dy = np.array(rows_of, np.int32).T
    x, c, z, y = place()
    order = index(x ^ dx, c ^ dc, (z + dz) & (Z - 1), y ^ dy)
    return jnp.concatenate([order, c[None]]).astype(jnp.int32)


def scatter_order():
    rows_of = []
    for group, first in zip(GROUPS, ("y", "x")):
        for one in (1, 0):
            for second in (1, 0):
                dx, dy = (second, one) if first == "y" else (one, second)
                rows_of += [(dx, shift, dy) for shift in group]
    dx, dz, dy = np.array(rows_of, np.int32).T
    x, c, z, y = place()
    order = ((x ^ dx) * Z + ((z + dz) & (Z - 1))) * 2 + (y ^ dy)
    spots = jnp.arange(len(rows_of), dtype=jnp.int32)
    where = jnp.sum(jnp.where(order[None, :] == spots[:, None], spots[None, :], 0), axis=1)
    return jnp.concatenate([order, where, c[None]]).astype(jnp.int32)


def tie(value, other):
    return lax.optimization_barrier((value, other))[0]


class Gather:
    def __init__(self, block):
        self.by_z = [block]

    def z(self, after=None):
        block = self.by_z[0] if after is None else tie(self.by_z[0], after)
        self.by_z = [block] + [over_z(block, s) for s in (1, 2, 3)]
        return self.by_z[1:]

    def first(self, after=None):
        even = jnp.stack([self.by_z[s] for s in GROUPS[0]])
        odd = jnp.stack([self.by_z[s] for s in GROUPS[1]])
        if after is not None:
            even, odd = tie((even, odd), after)
        self.even = jnp.concatenate([even, over_x(even)])
        self.odd = jnp.concatenate([odd, over_y(odd)])
        return [self.even, self.odd]

    def second(self, after=None):
        even, odd = (self.even, self.odd) if after is None else tie((self.even, self.odd), after)
        self.near = [even, odd, over_core(even), over_core(odd)]
        self.far = [over_y(even), over_x(odd)]
        return self.far

    def core(self, after=None):
        far = self.far if after is None else tie(self.far, after)
        even, odd, even_core, odd_core = self.near
        return [even, far[0], odd, far[1], even_core, over_core(far[0]), odd_core, over_core(far[1])]


class Reduce:
    def __init__(self, send_a, keep_a, send_b, keep_b):
        self.sends, self.a, self.b = (send_a, send_b), keep_a, keep_b

    def first(self, after=None):
        sends = self.sends if after is None else tie(self.sends, after)
        self.got = (over_y(sends[0]), over_x(sends[1]))
        return self.got

    def second(self, after=None):
        self.a = self.a + self.got[0].astype(F32)
        self.b = self.b + self.got[1].astype(F32)
        sends = (self.a[:2].astype(BF), self.b[:2].astype(BF))
        if after is not None:
            sends = tie(sends, after)
        self.got = (over_x(sends[0]), over_y(sends[1]))
        return self.got

    def z(self, after=None):
        self.a = self.a[2:] + self.got[0].astype(F32)
        self.b = self.b[2:] + self.got[1].astype(F32)
        sends = (self.b[0].astype(BF), self.a[1].astype(BF), self.b[1].astype(BF))
        if after is not None:
            sends = tie(sends, after)
        self.got = [over_z(s, i + 1) for i, s in enumerate(sends)]
        return self.got

    def own(self):
        return self.a[0] + sum(g.astype(F32) for g in self.got)


def unslab(block, width):
    size = block.shape[0] * LANES // width
    return jnp.concatenate([block[s * size : (s + 1) * size] for s in range(width // LANES)], axis=1)


def slab(block):
    return [block[:, s * LANES : (s + 1) * LANES] for s in range(block.shape[1] // LANES)]


def local(fast, tokens, doc_lengths, cotangent, w_qkv, w_out, w_up, w_down,
          gain_attn, gain_inner, gain_ffn, gain_mid):
    row_count = doc_lengths.shape[0]
    seq = tokens.shape[0] // row_count
    d = tokens.shape[1]
    wide = min(seq, 512) // BLOCK + 1
    blocks = seq // BLOCK
    shards = (gain_attn, gain_inner, gain_ffn, gain_mid)
    sizes = [g.shape[0] for g in shards]

    start, position, valid = layout(doc_lengths, seq)
    cos, sin = tables(position)
    firsts = start[:, ::BLOCK] // BLOCK
    reach = (jnp.arange(blocks, dtype=jnp.int32)[None, :] - firsts + 1).reshape(-1)
    start_col = start.reshape(-1, 1)
    start_row = jnp.repeat(start, 8, axis=0)
    gy = jnp.where(valid.reshape(-1, 1), cotangent, jnp.zeros_like(cotangent))

    def scatter(g):
        return lax.psum_scatter(g, AXES, scatter_dimension=0, tiled=True)

    def gather(v):
        return lax.all_gather(v, AXES, axis=0, tiled=True)

    if fast:
        order, back = gather_order(), scatter_order()
        gains_row = jnp.pad(jnp.concatenate(shards)[None], ((0, 7), (0, LANES - sum(sizes))))
        rest_of = jnp.concatenate([w_out] + slab(w_up) + [w_down])
        parts_up = [gather(rest_of).reshape(-1, *rest_of.shape)]
        part_down = parts_up[0]
        one = Gather(jnp.concatenate(slab(w_qkv) + [gains_row]))
        one.z()
        one.first()
        one.second()
        parts_qkv = one.core()
        gains = [None]
    else:
        order = back = jnp.zeros((8,), jnp.int32)
        parts_qkv, parts_up, part_down = [gather(w_qkv)], [gather(w_out), gather(w_up)], gather(w_down)
        gains = [gather(g).astype(F32).reshape(1, -1) for g in shards]

    h1, qkv, full_qkv, *rest = qkv_forward(fast, order, tokens, cos, sin, parts_qkv, gains[0], sizes)
    g_attn, g_inner, g_ffn, g_mid = rest if fast else gains
    core = order[32:] if fast else order
    mixed, lse = attention_forward(reach, qkv, start_col, row_count, wide)
    a, h2, x1, m, slope, inv, full_out, full_up, *m_other = up_forward(
        fast, core, mixed, tokens, g_inner, g_ffn, g_mid, parts_up
    )
    result, dpre, gg_down = down_both(fast, m, slope, inv, x1, gy, g_mid, part_down)
    dx1, low, d_mixed, gg_up = up_backward(dpre, x1, gy, mixed, full_up, full_out, g_ffn, g_inner)

    def shared(value):
        return (value, over_core(value)) if fast else (value,)

    def split_low(pair):
        return (pair[0], over_core(pair[1])) if fast else tuple(pair)

    m = (m, over_core(m_other[0])) if fast else (m,)
    a, h2, low, dpre = split_low(a), split_low(h2), shared(low), shared(dpre)

    def attend(group, lse, so_far):
        return attention_backward(
            reach, qkv, d_mixed, mixed, lse, start_row, cos, sin, row_count, wide, group, PAIRS // GRAD_GROUPS, so_far
        )

    f = w_up.shape[1]
    grads = weight_grads(
        fast, back, [(m, shared(gy), f // 384, True), (a, low, d // LANES, False), (h2, dpre, f // LANES, False)]
    )
    if fast:
        red = Reduce(*grads)
        first = red.first()
    d_qkv = attend(0, tie(lse, grads[-1]), None)
    if fast:
        second = red.second(d_qkv)
        lse = tie(lse, first)
    d_qkv = attend(1, lse, d_qkv)
    d_qkv = attend(2, lse, d_qkv)
    if fast:
        red_z = red.z(d_qkv)
        dx1 = tie(dx1, second)
    d_both = (d_qkv, over_core(tie(d_qkv, second))) if fast else (d_qkv,)
    grad_tokens, gg_attn = qkv_backward(d_qkv, tokens, dx1, full_qkv, g_attn)
    if fast:
        h1 = tie(split_low(h1), gg_attn)
    grad_qkv = weight_grads(fast, back, [(h1, d_both, 3 * d // LANES, False)])
    gain_rows = gg_attn + gg_up + gg_down
    if fast:
        red_qkv = Reduce(*grad_qkv)
        first = red_qkv.first(red_z)
        own = red.own()
        second = red_qkv.second()
        red_qkv.z()
        total = tie(gain_rows, first)
        total = total + over_core(total)
        total = total + over_x(total)
        total = total + over_y(total)
        total = total + over_z(total, 1) + over_z(total, 2) + over_z(total, 3)
        g_qkv = red_qkv.own()
        cuts = (w_down.shape[0], w_down.shape[0] + w_out.shape[0])
        own_down, grad_out, grad_up = own[: cuts[0]], own[cuts[0] : cuts[1]], unslab(own[cuts[1] :], f)
        me = index(*place())
        per_row = LANES // sizes[3]
        summed = [lax.dynamic_slice(total, (i, me * size), (1, size)).reshape(-1) for i, size in enumerate(sizes[:3])]
        summed.append(
            lax.dynamic_slice(total, (3 + lax.div(me, per_row), lax.rem(me, per_row) * sizes[3]), (1, sizes[3])).reshape(-1)
        )
    else:
        own_down, grad_out, grad_up, g_qkv = (scatter(g.astype(BF)).astype(F32) for g in (*grads, *grad_qkv))
        flat = gain_rows[: 3 + f // d]
        summed = [scatter(flat[i]) for i in range(3)] + [scatter(flat[3:].reshape(-1))]
        g_qkv = jnp.concatenate(slab(g_qkv))
    size = w_qkv.shape[0]
    span = LANES // 3
    g_qkv = jnp.concatenate(
        [g_qkv[g * size : (g + 1) * size, p * span : (p + 1) * span] for p in range(3) for g in range(GRAD_GROUPS)], axis=1
    )
    return (result, grad_tokens, g_qkv, grad_out, grad_up, own_down) + tuple(summed)


def solution(mesh):
    matrix, vector = P(AXES, None), P(AXES)
    fast = mesh.shape["dp"] == 4 and mesh.shape["fsdp"] == 2 * Z
    return jax.shard_map(
        functools.partial(local, fast),
        mesh=mesh,
        in_specs=(matrix,) * 7 + (vector,) * 4,
        out_specs=(matrix,) * 6 + (vector,) * 4,
        check_vma=False,
    )
```

```python
import functools
import math

import jax
import jax.numpy as jnp
import numpy as np
from jax import lax
from jax.experimental import pallas as pl
from jax.experimental.pallas import tpu as pltpu
from jax.sharding import PartitionSpec as P

HEADS = 12
HEAD_DIM = 64
PAIR = 2 * HEAD_DIM
PAIRS = HEADS // 2
EPSILON = 1e-05
MASKED_SCORE = -1e30
ROOT_HALF = 0.7071067811865476
INV_ROOT_TAU = 0.3989422804014327
BF = jnp.bfloat16
F32 = jnp.float32
MIB = 1 << 20
AXES = ("dp", "fsdp")
BLOCK = 256
LANES = 768
VMEM_MIB = 60
GRAD_GROUPS = 3


def dot(a, b, dims=((1,), (0,))):
    return lax.dot_general(a, b, (dims, ((), ())), preferred_element_type=F32)


def params(mib):
    return pltpu.CompilerParams(vmem_limit_bytes=max(mib, VMEM_MIB) * MIB)


def swap_halves(x):
    lane = lax.broadcasted_iota(jnp.int32, x.shape, 1)
    low = lax.rem(lane, HEAD_DIM) < HEAD_DIM // 2
    half = HEAD_DIM // 2
    return jnp.where(low, pltpu.roll(x, PAIR - half, 1), pltpu.roll(x, half, 1))


def unit_norm(x):
    mean = jnp.mean(x, axis=-1, keepdims=True)
    centred = x - mean
    inv = lax.rsqrt(jnp.mean(centred * centred, axis=-1, keepdims=True) + EPSILON)
    return centred * inv, inv


def norm_back(grad, gain, unit, inv):
    d_unit = grad * gain
    return inv * (
        d_unit
        - jnp.mean(d_unit, axis=-1, keepdims=True)
        - unit * jnp.mean(d_unit * unit, axis=-1, keepdims=True)
    )


def whole(shape):
    return pl.BlockSpec(shape, lambda *_: (0,) * len(shape), pipeline_mode=pl.Buffered(1))


def rows(width, block=BLOCK):
    return pl.BlockSpec((block, width), lambda i: (i, 0))


def shaped(shape, dtype):
    return jax.ShapeDtypeStruct(shape, dtype)


def hbm():
    return pl.BlockSpec(memory_space=pl.ANY)


def fetch(order, parts, places, sem):
    if len(parts) < 8 and parts[0].ndim == 2:
        for part, (_, _, buffer, _) in zip(parts, places):
            pltpu.make_async_copy(part, buffer, sem).start()
        return
    count = parts[0].shape[0]
    for p, part in enumerate(parts):
        for b in range(count):
            owner = b if order is None else order[p * count + b]
            for first, size, buffer, column in places:
                row = owner * size if order is None else pl.multiple_of(owner * size, 8)
                pltpu.make_async_copy(
                    part.at[b, pl.ds(first, size), :],
                    buffer.at[pl.ds(row, size), pl.ds(column, LANES)],
                    sem,
                ).start()


def arrive(buffers, sem):
    for buffer in buffers:
        pltpu.make_async_copy(buffer, buffer, sem).wait()


def deal(back, tile, outs, row, size):
    quarter = outs[0].shape[0]
    for q, out in enumerate(outs):

        @pl.loop(0, quarter)
        def _(j):
            block = tile[pl.ds(pl.multiple_of(back[q * quarter + j] * size, 8), size), :]
            out[j, pl.ds(row, size), :] = block.astype(out.dtype)


def slabs(first, size, buffer, width):
    return [(first + s * size, size, buffer, s * LANES) for s in range(width // LANES)]


def pack_kernel(wq_ref, wo_ref, wu_ref, wd_ref, gains_ref, one_ref, two_ref):
    row = 0
    for c in range(wq_ref.shape[1] // LANES):
        one_ref[row : row + wq_ref.shape[0], :] = wq_ref[:, c * LANES : (c + 1) * LANES]
        row += wq_ref.shape[0]
    one_ref[row:, :] = gains_ref[...]
    row = 0
    for ref in (wd_ref, wo_ref, wu_ref):
        for c in range(ref.shape[1] // LANES):
            two_ref[row : row + ref.shape[0], :] = ref[:, c * LANES : (c + 1) * LANES]
            row += ref.shape[0]


def pack(w_qkv, w_out, w_up, w_down, gains):
    first = w_qkv.size // LANES + gains.shape[0]
    second = (w_out.size + w_up.size + w_down.size) // LANES
    return pl.pallas_call(
        pack_kernel, out_shape=[shaped((first, LANES), BF), shaped((second, LANES), BF)], name="pack"
    )(w_qkv, w_out, w_up, w_down, gains)


def spread(rows_in, offset, count, owners):
    lanes = rows_in.shape[1]
    wide = owners * count
    lane = lax.broadcasted_iota(jnp.int32, (lanes, wide), 0)
    column = lax.broadcasted_iota(jnp.int32, (lanes, wide), 1)
    pick = (lane - offset == lax.rem(column, count)).astype(F32).astype(BF)
    full = dot(rows_in, pick)
    owner = lax.broadcasted_iota(jnp.int32, (owners, wide), 0)
    column = lax.broadcasted_iota(jnp.int32, (owners, wide), 1)
    own = (column >= owner * count) & (column < owner * count + count)
    return jnp.sum(jnp.where(own, full, 0.0), axis=0, keepdims=True)


def qkv_kernel(split, sizes, *refs):
    if split:
        order, x_ref, cos_ref, sin_ref, *refs = refs
        parts, refs = refs[:8], refs[8:]
        h_ref, other_ref, qkv_ref, w_ref, ga_ref, gi_ref, gf_ref, gm_ref, gains, sem, gain_sem = refs
        h_refs = (h_ref, other_ref)
    else:
        order, x_ref, cos_ref, sin_ref, ga_ref, *refs = refs
        parts, refs = refs[:1], refs[1:]
        h_ref, qkv_ref, w_ref, sem = refs
        h_refs = (h_ref,)
    width = x_ref.shape[1]
    step = pl.program_id(0)
    if split:
        size = width // 32
        weight = slabs(0, size, w_ref, 3 * width)

        @pl.when(step == 0)
        def _():
            fetch(order, parts, [(3 * size, 8, gains, 0)], gain_sem)
            fetch(order, parts, weight, sem)
            arrive([gains], gain_sem)
            owner = lax.broadcasted_iota(jnp.int32, (32, 256), 0)
            lane = lax.broadcasted_iota(jnp.int32, (32, 256), 1)
            pick = (lane == owner * 8).astype(F32).astype(BF)
            per_owner = dot(pick, gains[:, :256]).astype(BF)
            at = 0
            for ref, count in zip((ga_ref, gi_ref, gf_ref, gm_ref), sizes):
                ref[...] = spread(per_owner, at, count, 32)
                at += count
            arrive([w_ref], sem)
    else:

        @pl.when(step == 0)
        def _():
            fetch(None, parts, [(0, 0, w_ref, 0)], sem)
            arrive([w_ref], sem)

    unit, _ = unit_norm(x_ref[...].astype(F32))
    h = (unit * ga_ref[...]).astype(BF)
    store_low(split, order[32] if split else 0, h, h_refs)
    cos, sin = cos_ref[...], sin_ref[...]
    for part in range(3):
        y = dot(h, w_ref[:, part * width : (part + 1) * width])
        for c in range(width // PAIR):
            z = y[:, c * PAIR : (c + 1) * PAIR]
            if part < 2:
                z = z * cos + swap_halves(z) * sin
            if part == 0:
                z = z * (1.0 / math.sqrt(HEAD_DIM))
            at = part * width + c * PAIR
            qkv_ref[:, at : at + PAIR] = z.astype(BF)


def prefetched(kernel, order, inputs, in_specs, out_specs, out_shape, scratch, grid, mib, name, flops, data):
    return pl.pallas_call(
        kernel,
        grid_spec=pltpu.PrefetchScalarGridSpec(
            num_scalar_prefetch=1,
            grid=grid,
            in_specs=in_specs,
            out_specs=out_specs,
            scratch_shapes=scratch,
        ),
        out_shape=out_shape,
        compiler_params=params(mib),
        cost_estimate=pl.CostEstimate(flops=flops, transcendentals=0, bytes_accessed=data),
        name=name,
    )(order, *inputs)


def rows(width, block=BLOCK):
    return pl.BlockSpec((block, width), lambda i, *_: (i, 0))


def whole(shape):
    return pl.BlockSpec(shape, lambda *_: (0,) * len(shape), pipeline_mode=pl.Buffered(1))


def qkv_forward(split, order, tokens, cos, sin, parts, gain, sizes):
    t, d = tokens.shape
    n = 3 * d
    inputs = [tokens, cos, sin]
    in_specs = [rows(d), rows(PAIR), rows(PAIR)]
    out_specs, out_shape = low_specs(split, t, d)
    lows = len(out_specs)
    out_specs = out_specs + [rows(n), whole((d, n))]
    out_shape = out_shape + [shaped((t, n), BF), shaped((d, n), BF)]
    scratch = [pltpu.SemaphoreType.DMA]
    if split:
        widths = [32 * s for s in sizes]
        out_specs += [whole((1, w)) for w in widths]
        out_shape += [shaped((1, w), F32) for w in widths]
        scratch = [pltpu.VMEM((32 * 8, LANES), BF), pltpu.SemaphoreType.DMA, pltpu.SemaphoreType.DMA]
    else:
        inputs.append(gain)
        in_specs.append(whole((1, d)))
    outs = prefetched(
        functools.partial(qkv_kernel, split, sizes), order, inputs + list(parts), in_specs + [hbm()] * len(parts),
        out_specs, out_shape, scratch, (t // BLOCK,), 40, "qkv_forward",
        2 * t * d * n, 4 * d * n + 12 * t * d,
    )
    return (outs[:lows], *outs[lows:])


def window(i, n):
    return slice((i - n + 1) * BLOCK, (i + 1) * BLOCK)


def head_masks(shape):
    lane = lax.broadcasted_iota(jnp.int32, shape, 1)
    return lane < HEAD_DIM


def attention_forward_kernel(wide, reach, q_ref, k_ref, v_ref, start_ref, o_ref, lse_ref, bias):
    row, pair = pl.program_id(0), pl.program_id(1)
    seq = q_ref.shape[0]
    blocks = seq // BLOCK

    @pl.when(pair == 0)
    def _():
        for i in range(blocks):
            at = slice(i * BLOCK, (i + 1) * BLOCK)
            shape = (BLOCK, wide * BLOCK)
            key = (i - wide + 1) * BLOCK + lax.broadcasted_iota(jnp.int32, shape, 1)
            query = i * BLOCK + lax.broadcasted_iota(jnp.int32, shape, 0)
            keep = (key >= start_ref[at, :]) & (key <= query)
            bias[at, :] = jnp.where(keep, 0.0, MASKED_SCORE)

    first = head_masks((BLOCK, PAIR))
    for i in range(blocks):
        at = slice(i * BLOCK, (i + 1) * BLOCK)
        most = min(wide, i + 1)
        for n in range(1, most + 1):

            @pl.when(reach[row * blocks + i] == n)
            def _():
                q = q_ref[at, :]
                w = window(i, n)
                k, v = k_ref[w, :], v_ref[w, :]
                b = bias[at, (wide - n) * BLOCK :]
                mask = head_masks(k.shape)
                zero = jnp.zeros_like(k)
                total, lses = None, []
                scale = None
                for h in range(2):
                    pick = mask if h == 0 else jnp.logical_not(mask)
                    s = dot(q, jnp.where(pick, k, zero), ((1,), (1,))) + b
                    top = jnp.max(s, axis=-1, keepdims=True)
                    p = jnp.exp(s - top)
                    den = jnp.sum(p, axis=-1, keepdims=True)
                    probs = (p * (1.0 / den)).astype(BF)
                    part = dot(probs, jnp.where(pick, v, zero))
                    total = part if total is None else total + part
                    lses.append(top + jnp.log(den))
                o_ref[at, :] = total
                both = jnp.where(first, lses[0], lses[1]).T
                lse_ref[0, 0:1, at] = both[0:1, :]
                lse_ref[0, 1:2, at] = both[HEAD_DIM : HEAD_DIM + 1, :]


def attention_forward(reach, qkv, start, row_count, wide):
    t = qkv.shape[0]
    seq = t // row_count
    d = qkv.shape[1] // 3

    def columns(part):
        return pl.BlockSpec((seq, PAIR), lambda r, p, *_: (r, part * PAIRS + p))

    return pl.pallas_call(
        functools.partial(attention_forward_kernel, wide),
        grid_spec=pltpu.PrefetchScalarGridSpec(
            num_scalar_prefetch=1,
            grid=(row_count, PAIRS),
            in_specs=[
                columns(0),
                columns(1),
                columns(2),
                pl.BlockSpec((seq, 1), lambda r, p, *_: (r, 0)),
            ],
            out_specs=[
                pl.BlockSpec((seq, PAIR), lambda r, p, *_: (r, p)),
                pl.BlockSpec((1, 8, seq), lambda r, p, *_: (r * PAIRS + p, 0, 0)),
            ],
            scratch_shapes=[pltpu.VMEM((seq, wide * BLOCK), F32)],
        ),
        out_shape=[shaped((t, d), F32), shaped((row_count * PAIRS, 8, seq), F32)],
        compiler_params=params(32),
        cost_estimate=pl.CostEstimate(
            flops=8 * t * d * BLOCK, transcendentals=t * HEADS * 512, bytes_accessed=12 * t * d
        ),
        name="attention_forward",
    )(reach, qkv, qkv, qkv, start)


def attention_backward_kernel(wide, reach, q_ref, k_ref, v_ref, do_ref, o_ref, lse_ref, start_ref, cos_ref, sin_ref, *refs):
    grad_ref, bias, ks, vs, qs, dos, dk_acc, dv_acc, dq_acc = refs[-9:]
    row, pair = pl.program_id(0), pl.program_id(1)
    seq = q_ref.shape[0]
    blocks = seq // BLOCK

    @pl.when(pair == 0)
    def _():
        for i in range(blocks):
            at = slice(i * BLOCK, (i + 1) * BLOCK)
            shape = (wide * BLOCK, BLOCK)
            key = (i - wide + 1) * BLOCK + lax.broadcasted_iota(jnp.int32, shape, 0)
            query = i * BLOCK + lax.broadcasted_iota(jnp.int32, shape, 1)
            keep = (key >= start_ref[0:1, at]) & (key <= query)
            bias[:, at] = jnp.where(keep, 0.0, MASKED_SCORE)

    mask = head_masks((seq, PAIR))
    for src, dst in ((k_ref, ks), (v_ref, vs), (q_ref, qs), (do_ref, dos)):
        x = src[...]
        zero = jnp.zeros_like(x)
        dst[0] = jnp.where(mask, x, zero)
        dst[1] = jnp.where(mask, zero, x)
    dk_acc[...] = jnp.zeros_like(dk_acc)
    dv_acc[...] = jnp.zeros_like(dv_acc)
    lane8 = lax.broadcasted_iota(jnp.int32, (8, PAIR), 1) // HEAD_DIM
    row8 = lax.broadcasted_iota(jnp.int32, (8, PAIR), 0)
    picks = (lane8 == row8).astype(F32)
    delta = lax.dot_general(
        picks, do_ref[...].astype(F32) * o_ref[...], (((1,), (1,)), ((), ())),
        precision=lax.Precision.HIGHEST, preferred_element_type=F32,
    )
    for i in range(blocks):
        at = slice(i * BLOCK, (i + 1) * BLOCK)
        most = min(wide, i + 1)
        for n in range(1, most + 1):

            @pl.when(reach[row * blocks + i] == n)
            def _():
                w = window(i, n)
                b = bias[(wide - n) * BLOCK :, at]
                q, do = q_ref[at, :], do_ref[at, :]
                ps, dss = [], []
                for h in range(2):
                    s = dot(ks[h, w, :], q, ((1,), (1,))) + b
                    p = jnp.exp(s - lse_ref[0, h : h + 1, at])
                    dp = dot(vs[h, w, :], do, ((1,), (1,)))
                    ds = (p * (dp - delta[h : h + 1, at])).astype(BF)
                    ps.append(p.astype(BF))
                    dss.append(ds)
                dv_acc[w, :] += dot(ps[0], dos[0, at, :]) + dot(ps[1], dos[1, at, :])
                dk_acc[w, :] += dot(dss[0], qs[0, at, :]) + dot(dss[1], qs[1, at, :])
                dq_acc[at, :] = dot(dss[0], ks[0, w, :], ((0,), (0,))) + dot(
                    dss[1], ks[1, w, :], ((0,), (0,))
                )

    cos, sin = cos_ref[...], sin_ref[...]
    dq = dq_acc[...] * (1.0 / math.sqrt(HEAD_DIM))
    dk = dk_acc[...]
    span = grad_ref.shape[2] // 3
    slot = lax.rem(pair, span // PAIR)
    grads = (dq * cos - swap_halves(dq) * sin, dk * cos - swap_halves(dk) * sin, dv_acc[...])
    for part, value in enumerate(grads):
        grad_ref[0, :, pl.ds(pl.multiple_of(part * span + slot * PAIR, PAIR), PAIR)] = value.astype(BF)


def attention_backward(reach, qkv, d_mixed, mixed, lse, start_row, cos, sin, row_count, wide, group, groups, so_far):
    pairs = PAIRS // GRAD_GROUPS
    t = qkv.shape[0]
    seq = t // row_count
    base = group * pairs
    span = 3 * pairs * PAIR

    def columns(part):
        return pl.BlockSpec((seq, PAIR), lambda r, p, *_: (r, part * PAIRS + base + p))

    table = pl.BlockSpec((seq, PAIR), lambda r, p, *_: (r, 0))
    inputs = [reach, qkv, qkv, qkv, d_mixed, mixed, lse, start_row, cos, sin]
    in_specs = [
        columns(0), columns(1), columns(2), columns(0), columns(0),
        pl.BlockSpec((1, 8, seq), lambda r, p, *_: (r * PAIRS + base + p, 0, 0)),
        pl.BlockSpec((8, seq), lambda r, p, *_: (r, 0)),
        table, table,
    ]
    aliases = {}
    if so_far is not None:
        aliases = {len(inputs): 0}
        inputs.append(so_far)
        in_specs.append(hbm())
    return pl.pallas_call(
        functools.partial(attention_backward_kernel, wide),
        grid_spec=pltpu.PrefetchScalarGridSpec(
            num_scalar_prefetch=1,
            grid=(row_count, pairs * groups),
            in_specs=in_specs,
            out_specs=pl.BlockSpec((1, seq, span), lambda r, p, *_: (group + p // pairs, r, 0)),
            scratch_shapes=[
                pltpu.VMEM((wide * BLOCK, seq), F32),
                pltpu.VMEM((2, seq, PAIR), BF),
                pltpu.VMEM((2, seq, PAIR), BF),
                pltpu.VMEM((2, seq, PAIR), BF),
                pltpu.VMEM((2, seq, PAIR), BF),
                pltpu.VMEM((seq, PAIR), F32),
                pltpu.VMEM((seq, PAIR), F32),
                pltpu.VMEM((seq, PAIR), F32),
            ],
        ),
        out_shape=shaped((GRAD_GROUPS, t, span), BF),
        input_output_aliases=aliases,
        compiler_params=params(40),
        cost_estimate=pl.CostEstimate(
            flops=20 * t * span * BLOCK // 3 * groups, transcendentals=t * HEADS * 128 * groups,
            bytes_accessed=20 * t * span // 3 * groups
        ),
        name="attention_backward",
    )(*inputs)


def halves(x):
    quarter = x.shape[1] // 4
    piece = [x[:, i * quarter : (i + 1) * quarter] for i in range(4)]
    return jnp.concatenate(piece[0::2], axis=1), jnp.concatenate(piece[1::2], axis=1)


def store_low(split, core, x, refs):
    if not split:
        refs[0][...] = x
        return
    pair = halves(x)
    for c in range(2):

        @pl.when(core == c)
        def _():
            refs[0][...] = pair[c]
            refs[1][...] = pair[1 - c]


def low_specs(split, t, d):
    if split:
        return [rows(d // 2)] * 2, [shaped((t, d // 2), BF)] * 2
    return [rows(d)], [shaped((t, d), BF)]


def up_kernel(split, *refs):
    order, o_ref, x_ref, gi_ref, gf_ref, gm_ref, *refs = refs
    count = 8 if split else 2
    lows = 2 if split else 1
    parts, refs = refs[:count], refs[count:]
    a_refs, h2_refs, refs = refs[:lows], refs[lows : 2 * lows], refs[2 * lows :]
    x1_ref, m_ref, slope_ref, inv_ref, wo_ref, wu_ref, *refs = refs
    sem = refs[-1]
    d, f = wu_ref.shape
    size = d // 32
    step = pl.program_id(0)
    skip = f // 32
    places = [(0, 0, wo_ref, 0), (0, 0, wu_ref, 0)]
    if split:
        places = [(skip, size, wo_ref, 0)] + slabs(skip + size, size, wu_ref, f)

    @pl.when(step == 0)
    def _():
        fetch(order, parts, places, sem)

    unit, _ = unit_norm(o_ref[...])
    a = (unit * gi_ref[...]).astype(BF)
    core = order[32] if split else 0
    store_low(split, core, a, a_refs)

    @pl.when(step == 0)
    def _():
        arrive([wo_ref, wu_ref], sem)

    x1 = x_ref[...].astype(F32) + dot(a, wo_ref[...])
    x1_ref[...] = x1
    unit, _ = unit_norm(x1)
    h2 = (unit * gf_ref[...]).astype(BF)
    store_low(split, core, h2, h2_refs)
    hidden = dot(h2, wu_ref[...])
    cdf = 0.5 + 0.5 * lax.erf(hidden * ROOT_HALF)
    slope = cdf + hidden * (jnp.exp(-0.5 * hidden * hidden) * INV_ROOT_TAU)
    slope_ref[...] = slope.astype(BF)
    unit, inv = unit_norm(hidden * cdf)
    m_ref[...] = (unit * gm_ref[...]).astype(BF)
    inv_ref[...] = jnp.broadcast_to(inv, inv_ref.shape)
    if split:
        quarter = f // 4
        for j in range(2):
            at = pl.multiple_of((2 * j + 1 - core) * quarter, PAIR)
            refs[0][:, j * quarter : (j + 1) * quarter] = m_ref[:, pl.ds(at, quarter)]


def up_forward(split, order, mixed, tokens, gain_inner, gain_ffn, gain_mid, parts):
    t, d = tokens.shape
    f = gain_mid.shape[1]
    low_out, low_shape = low_specs(split, t, d)
    more = [(rows(f // 2), shaped((t, f // 2), BF))] * split
    outs = prefetched(
        functools.partial(up_kernel, split), order, [mixed, tokens, gain_inner, gain_ffn, gain_mid, *parts],
        [rows(d), rows(d), whole((1, d)), whole((1, d)), whole((1, f))] + [hbm()] * len(parts),
        low_out * 2 + [rows(d), rows(f), rows(f), rows(PAIR), whole((d, d)), whole((d, f))] + [m[0] for m in more],
        low_shape * 2 + [
            shaped((t, d), F32), shaped((t, f), BF), shaped((t, f), BF), shaped((t, PAIR), F32),
            shaped((d, d), BF), shaped((d, f), BF),
        ] + [m[1] for m in more],
        [pltpu.SemaphoreType.DMA], (t // BLOCK,), 60, "up_forward",
        2 * t * d * (d + f), 4 * d * (d + f) + 4 * t * f + 16 * t * d,
    )
    lows = len(low_out)
    return (outs[:lows], outs[lows : 2 * lows], *outs[2 * lows :])


def slab_rows(values, first, width):
    count = values.shape[1] // width
    line = lax.broadcasted_iota(jnp.int32, (8, width), 0)
    total = jnp.zeros((8, width), F32)
    for i in range(count):
        total = jnp.where(line == first + i, values[:, i * width : (i + 1) * width], total)
    return total


def down_kernel(split, order, m_ref, slope_ref, inv_ref, gy_ref, gm_ref, *refs):
    parts, refs = refs[: 8 if split else 1], refs[8 if split else 1 :]
    dpre_ref, gg_ref, wd_ref, sem = refs
    f, d = wd_ref.shape
    step = pl.program_id(0)

    @pl.when(step == 0)
    def _():
        fetch(order, parts, [(0, f // 32, wd_ref, 0)], sem)
        arrive([wd_ref], sem)

    mf = m_ref[...].astype(F32)
    dm = dot(gy_ref[...], wd_ref[...], ((1,), (1,)))
    gain = gm_ref[...]
    prod = dm * mf
    d_unit = dm * gain
    d_act = inv_ref[:, 0:1] * (
        d_unit
        - jnp.mean(d_unit, axis=-1, keepdims=True)
        - (mf * (1.0 / gain)) * jnp.mean(prod, axis=-1, keepdims=True)
    )
    dpre_ref[...] = (d_act * slope_ref[...].astype(F32)).astype(BF)
    part = slab_rows(jnp.sum(prod, axis=0, keepdims=True) * (1.0 / gain), 3, d)

    @pl.when(step == 0)
    def _():
        gg_ref[...] = part

    @pl.when(step > 0)
    def _():
        gg_ref[...] += part


def down_backward(split, order, m, slope, inv, gy, gain_mid, parts):
    t, d = gy.shape
    f = m.shape[1]
    return prefetched(
        functools.partial(down_kernel, split), order, [m, slope, inv, gy, gain_mid, *parts],
        [rows(f), rows(f), rows(PAIR), rows(d), whole((1, f))] + [hbm()] * len(parts),
        [rows(f), whole((8, d)), whole((f, d))],
        [shaped((t, f), BF), shaped((8, d), F32), shaped((f, d), BF)],
        [pltpu.SemaphoreType.DMA], (t // BLOCK,), 48, "down_backward",
        2 * t * d * f, 2 * d * f + 6 * t * f + 8 * t * d,
    )


def result_kernel(m_ref, x1_ref, wd_ref, y_ref):
    y_ref[...] = (x1_ref[...] + dot(m_ref[...], wd_ref[...])).astype(BF)


def down_forward(m, x1, w_down):
    t, d = x1.shape
    f = m.shape[1]
    return pl.pallas_call(
        result_kernel,
        grid=(t // BLOCK,),
        in_specs=[rows(f), rows(d), whole((f, d))],
        out_specs=rows(d),
        out_shape=shaped((t, d), BF),
        compiler_params=params(48),
        cost_estimate=pl.CostEstimate(flops=2 * t * d * f, transcendentals=0, bytes_accessed=2 * d * f + 2 * t * f + 6 * t * d),
        name="down_forward",
    )(m, x1, w_down)


def up_back_kernel(dpre_ref, x1_ref, gy_ref, o_ref, wu_ref, wo_ref, gf_ref, gi_ref,
                   dx1_ref, low_ref, do_ref, gg_ref):
    step = pl.program_id(0)
    d = x1_ref.shape[1]
    dh2 = dot(dpre_ref[...], wu_ref[...], ((1,), (1,)))
    unit, inv = unit_norm(x1_ref[...])
    part = slab_rows(jnp.sum(dh2 * unit, axis=0, keepdims=True), 2, d)
    dx1 = gy_ref[...].astype(F32) + norm_back(dh2, gf_ref[...], unit, inv)
    dx1_ref[...] = dx1
    low = dx1.astype(BF)
    low_ref[...] = low
    da = dot(low, wo_ref[...], ((1,), (1,)))
    unit, inv = unit_norm(o_ref[...])
    part = part + slab_rows(jnp.sum(da * unit, axis=0, keepdims=True), 1, d)
    do_ref[...] = norm_back(da, gi_ref[...], unit, inv).astype(BF)

    @pl.when(step == 0)
    def _():
        gg_ref[...] = part

    @pl.when(step > 0)
    def _():
        gg_ref[...] += part


def up_backward(dpre, x1, gy, mixed, w_up, w_out, gain_ffn, gain_inner):
    t, d = x1.shape
    f = dpre.shape[1]
    return pl.pallas_call(
        up_back_kernel,
        grid=(t // BLOCK,),
        in_specs=[rows(f), rows(d), rows(d), rows(d),
                  whole((d, f)), whole((d, d)), whole((1, d)), whole((1, d))],
        out_specs=[rows(d), rows(d), rows(d), whole((8, d))],
        out_shape=[shaped((t, d), F32), shaped((t, d), BF), shaped((t, d), BF), shaped((8, d), F32)],
        compiler_params=params(40),
        cost_estimate=pl.CostEstimate(
            flops=2 * t * d * (d + f), transcendentals=0, bytes_accessed=2 * d * (d + f) + 2 * t * f + 24 * t * d
        ),
        name="up_backward",
    )(dpre, x1, gy, mixed, w_up, w_out, gain_ffn, gain_inner)


def take_gains(rows_of, core, sizes):
    total = jnp.zeros((16, 256), F32)
    owner = lax.broadcasted_iota(jnp.int32, (16, LANES), 0)
    column = lax.broadcasted_iota(jnp.int32, (16, LANES), 1)
    device = (owner // 8) * 16 + core * 8 + owner % 8
    line, offset = 0, 0
    for size in sizes:
        pieces = jnp.zeros((16, LANES), F32)
        for slab_at in range(32 * size // LANES):
            base = device * size - slab_at * LANES
            own = (column >= base) & (column < base + size)
            pieces = pieces + jnp.where(own, rows_of[line : line + 1, :], 0.0)
            line += 1
        source = lax.broadcasted_iota(jnp.int32, (LANES, 256), 0)
        target = lax.broadcasted_iota(jnp.int32, (LANES, 256), 1)
        pick = (lax.rem(source, size) == target - offset).astype(F32)
        total = total + lax.dot_general(
            pieces, pick, (((1,), (0,)), ((), ())), precision=lax.Precision.HIGHEST, preferred_element_type=F32
        )
        offset += size
    return total


def grads_kernel(split, products, sizes, *refs):
    back, *refs = refs
    if sizes:
        gain_refs, refs = refs[:2], refs[2:]
    count = 2 if split else 1
    left, refs = refs[: len(products) * count], refs[len(products) * count :]
    right, refs = refs[: len(products) * count], refs[len(products) * count :]
    outs, refs = refs[: 4 if split else len(products)], refs[4 if split else len(products) :]
    tile, turned = refs[0], refs[1:]
    step = pl.program_id(0)
    first, row = 0, 0
    for n, (by_left, tiles, size) in enumerate(products):
        mine = [left[n * count + c] for c in range(count)]
        value = [right[n * count + c] for c in range(count)]

        if not by_left:

            @pl.when(step == first)
            def _():
                t = mine[0].shape[0]
                for c in range(count):
                    turned[0][:, c * t : (c + 1) * t] = mine[c][...].T

        @pl.when((step >= first) & (step < first + tiles))
        def _():
            total = None
            for c in range(count):
                v = value[c][...] if len(value[c].shape) == 2 else value[c][0]
                t = v.shape[0]
                if by_left:
                    part = dot(mine[c][...], v, ((0,), (0,)))
                else:
                    part = dot(turned[0][:, c * t : (c + 1) * t], v)
                total = part if total is None else total + part
            if not split:
                outs[n][...] = total
            else:
                tile[...] = total
                if by_left:
                    owners = tile.shape[0] // size
                    for e in range(owners):
                        at = back[16 + (step - first) * owners + e]
                        for q in range(4):

                            @pl.when(at // 4 == q)
                            def _():
                                block = tile[e * size : (e + 1) * size, :]
                                outs[q][at - 4 * q, row : row + size, :] = block.astype(outs[q].dtype)
                else:
                    deal(back, tile, outs, row + pl.multiple_of((step - first) * size, 8), size)

        first += tiles
        row += size if by_left else tiles * size

    if sizes:

        @pl.when(step == first - 1)
        def _():
            pieces = take_gains(gain_refs[0][...] + gain_refs[1][...], back[32], sizes)
            tile[...] = jnp.zeros_like(tile)
            for owner in range(16):
                tile[owner * 8 : owner * 8 + 1, :256] = pieces[owner : owner + 1, :]
            deal(back, tile, outs, row, 8)


def weight_grads(split, back, products, gain_rows=(), sizes=()):
    count = 2 if split else 1
    t = products[0][0][0].shape[0]
    left_specs, right_specs, lefts, rights, plan = [], [], [], [], []
    out_specs, out_shape = [], []
    at = row = 0
    for left, right, tiles, by_left in products:
        width = 0
        for c in range(count):
            a, b = left[c], right[c]

            if by_left and c == 0:
                tiles = tiles // count
                width = a.shape[1] // (tiles * count)

            def step(i, at=at, tiles=tiles):
                return jnp.clip(i - at, 0, tiles - 1)

            if by_left:
                per = tiles // 2
                if split and c == 0:
                    left_specs.append(pl.BlockSpec(
                        (t, width), lambda i, back, step=step, per=per: (0, (2 * (step(i) // per) + back[32]) * per + step(i) % per)
                    ))
                else:
                    left_specs.append(pl.BlockSpec((t, width), lambda i, *_, step=step: (0, step(i))))
                right_specs.append(whole(b.shape))
            else:
                width = a.shape[1]
                left_specs.append(whole(a.shape))
                if b.ndim == 3:
                    right_specs.append(pl.BlockSpec((1, t, LANES), lambda i, *_, step=step: (step(i), 0, 0)))
                else:
                    right_specs.append(pl.BlockSpec((t, LANES), lambda i, *_, step=step: (0, step(i))))
            lefts.append(a)
            rights.append(b)
        size = (width * tiles if by_left else width) // 16
        if not split:
            shape = (width * tiles, LANES) if by_left else (width, tiles * LANES)
            block = (width, LANES)
            out_specs.append(pl.BlockSpec(
                block, (lambda i, *_, step=step: (step(i), 0)) if by_left else (lambda i, *_, step=step: (0, step(i)))
            ))
            out_shape.append(shaped(shape, F32))
        plan.append((by_left, tiles, size))
        at += tiles
        row += size if by_left else tiles * size
    narrow = next(p[0][0].shape[1] for p in products if not p[3])
    if split:
        row += 8 if sizes else 0
        out_specs = [whole((4, row, LANES))] * 4
        out_shape = [shaped((4, row, LANES), dtype) for dtype in (BF, F32, BF, F32)]
    flops = 2 * count * t * narrow * at * LANES
    return prefetched(
        functools.partial(grads_kernel, split, tuple(plan), tuple(sizes)), back, [*gain_rows, *lefts, *rights],
        [whole(g.shape) for g in gain_rows] + left_specs + right_specs,
        out_specs, out_shape, [pltpu.VMEM((narrow, LANES), F32), pltpu.VMEM((narrow, count * t), BF)],
        (at,), 60, "weight_grads", flops, flops // 256,
    )


def qkv_back_kernel(d_ref, x_ref, dx1_ref, w_ref, gain_ref, up_ref, down_ref, dx_ref, gg_ref):
    step = pl.program_id(0)
    d = x_ref.shape[1]
    groups, _, span = d_ref.shape
    span //= 3
    dh = None
    for part in range(3):
        for g in range(groups):
            at = part * d + g * span
            piece = dot(d_ref[g, :, part * span : (part + 1) * span], w_ref[:, at : at + span], ((1,), (1,)))
            dh = piece if dh is None else dh + piece
    unit, inv = unit_norm(x_ref[...].astype(F32))
    gain_part = slab_rows(jnp.sum(dh * unit, axis=0, keepdims=True), 0, d)
    dx_ref[...] = dx1_ref[...] + norm_back(dh, gain_ref[...], unit, inv)

    @pl.when(step == 0)
    def _():
        gg_ref[...] = gain_part + up_ref[...] + down_ref[...]

    @pl.when(step > 0)
    def _():
        gg_ref[...] += gain_part


def qkv_backward(d_qkv, tokens, dx1, w_qkv, gain, gain_rows):
    t, d = tokens.shape
    groups, _, span = d_qkv.shape
    return pl.pallas_call(
        qkv_back_kernel,
        grid=(t // BLOCK,),
        in_specs=[pl.BlockSpec((groups, BLOCK, span), lambda i: (0, i, 0))] + [rows(d)] * 2
        + [whole((d, 3 * d)), whole((1, d))] + [whole((8, d))] * 2,
        out_specs=[rows(d), whole((8, d))],
        out_shape=[shaped((t, d), F32), shaped((8, d), F32)],
        compiler_params=params(48),
        cost_estimate=pl.CostEstimate(flops=6 * t * d * d, transcendentals=0, bytes_accessed=6 * d * d + 16 * t * d),
        name="qkv_backward",
    )(d_qkv, tokens, dx1, w_qkv, gain, *gain_rows)


def layout(doc_lengths, seq):
    docs = doc_lengths.shape[-1]
    upto = jnp.arange(docs)[:, None] <= jnp.arange(docs)[None, :]
    ends = jnp.sum(jnp.where(upto[None], doc_lengths[:, :, None], 0), axis=1)
    places = jnp.arange(seq, dtype=jnp.int32)
    passed = places[None, :, None] >= ends[:, None, :]
    start = jnp.sum(jnp.where(passed, doc_lengths[:, None, :], 0), axis=-1)
    valid = places[None, :] < ends[:, docs - 2 : docs - 1]
    return start.astype(jnp.int32), places[None, :] - start, valid


def tables(position):
    half = HEAD_DIM // 2
    lane = jnp.arange(PAIR)
    frequency = jnp.exp((lane % half).astype(F32) * (-2.0 * math.log(10000.0) / HEAD_DIM))
    angles = position.reshape(-1, 1).astype(F32) * frequency[None, :]
    sign = jnp.where(lane % HEAD_DIM < half, -1.0, 1.0)
    return jnp.cos(angles), jnp.sin(angles) * sign[None, :]


Z = 4
GROUPS = ((0, 2), (1, 3))


def index(x, core, z, y):
    return ((x * 2 + core) * Z + z) * 2 + y


def permute(value, move):
    places = [(x, c, z, y) for x in range(2) for c in range(2) for z in range(Z) for y in range(2)]
    return lax.ppermute(value, AXES, [(index(*p), index(*move(*p))) for p in places])


def over_x(v):
    return permute(v, lambda x, c, z, y: (1 - x, c, z, y))


def over_y(v):
    return permute(v, lambda x, c, z, y: (x, c, z, 1 - y))


def over_core(v):
    return permute(v, lambda x, c, z, y: (x, 1 - c, z, y))


def over_z(v, bits):
    return permute(v, lambda x, c, z, y: (x, c, z ^ bits, y))


def place():
    dp, fs = lax.axis_index("dp"), lax.axis_index("fsdp")
    return dp >> 1, dp & 1, fs >> 1, fs & 1


def gather_order():
    rows_of = []
    for core in range(2):
        for group, first in zip(GROUPS, ("x", "y")):
            for second in range(2):
                for one in range(2):
                    dx, dy = (one, second) if first == "x" else (second, one)
                    rows_of += [(dx, core, dz, dy) for dz in group]
    dx, dc, dz, dy = np.array(rows_of, np.int32).T
    x, c, z, y = place()
    order = index(x ^ dx, c ^ dc, z ^ dz, y ^ dy)
    return jnp.concatenate([order, c[None]]).astype(jnp.int32)


def scatter_order():
    rows_of = []
    for group, first in zip(GROUPS, ("y", "x")):
        for one in (1, 0):
            for second in (1, 0):
                dx, dy = (second, one) if first == "y" else (one, second)
                rows_of += [(dx, dz, dy) for dz in group]
    dx, dz, dy = np.array(rows_of, np.int32).T
    x, c, z, y = place()
    order = ((x ^ dx) * Z + (z ^ dz)) * 2 + (y ^ dy)
    spots = jnp.arange(len(rows_of), dtype=jnp.int32)
    where = jnp.sum(jnp.where(order[None, :] == spots[:, None], spots[None, :], 0), axis=1)
    return jnp.concatenate([order, where, c[None]]).astype(jnp.int32)


def tie(value, other):
    return lax.optimization_barrier((value, other))[0]


class Gather:
    def __init__(self, block):
        self.block = block

    def z(self, after=None):
        block = self.block if after is None else tie(self.block, after)
        self.even = jnp.stack([block, over_z(block, 2)])
        self.odd = over_z(self.even, 1)
        return self.odd

    def first(self, after=None):
        even, odd = (self.even, self.odd) if after is None else tie((self.even, self.odd), after)
        self.even = jnp.concatenate([even, over_x(even)])
        self.odd = jnp.concatenate([odd, over_y(odd)])
        return [self.even, self.odd]

    def second(self, after=None):
        even, odd = (self.even, self.odd) if after is None else tie((self.even, self.odd), after)
        self.near = [even, odd, over_core(even), over_core(odd)]
        self.far = [over_y(even), over_x(odd)]
        return self.far

    def core(self, after=None):
        far = self.far if after is None else tie(self.far, after)
        even, odd, even_core, odd_core = self.near
        return [even, far[0], odd, far[1], even_core, over_core(far[0]), odd_core, over_core(far[1])]


class Reduce:
    def __init__(self, send_a, keep_a, send_b, keep_b):
        self.sends, self.a, self.b = (send_a, send_b), keep_a, keep_b

    def first(self, after=None):
        sends = self.sends if after is None else tie(self.sends, after)
        self.got = (over_y(sends[0]), over_x(sends[1]))
        return self.got

    def second(self, after=None):
        self.a = self.a + self.got[0].astype(F32)
        self.b = self.b + self.got[1].astype(F32)
        sends = (self.a[:2].astype(BF), self.b[:2].astype(BF))
        if after is not None:
            sends = tie(sends, after)
        self.got = (over_x(sends[0]), over_y(sends[1]))
        return self.got

    def near_z(self, after=None):
        self.a = self.a[2:] + self.got[0].astype(F32)
        send = (self.b[2:] + self.got[1].astype(F32)).astype(BF)
        self.got = over_z(send if after is None else tie(send, after), 1)
        return self.got

    def far_z(self, after=None):
        self.a = self.a + self.got.astype(F32)
        send = self.a[1].astype(BF)
        self.got = over_z(send if after is None else tie(send, after), 2)
        return self.got

    def own(self):
        return self.a[0] + self.got.astype(F32)


def unslab(block, width):
    size = block.shape[0] * LANES // width
    return jnp.concatenate([block[s * size : (s + 1) * size] for s in range(width // LANES)], axis=1)


def slab(block):
    return [block[:, s * LANES : (s + 1) * LANES] for s in range(block.shape[1] // LANES)]


def local(fast, tokens, doc_lengths, cotangent, w_qkv, w_out, w_up, w_down,
          gain_attn, gain_inner, gain_ffn, gain_mid):
    row_count = doc_lengths.shape[0]
    seq = tokens.shape[0] // row_count
    d = tokens.shape[1]
    wide = min(seq, 512) // BLOCK + 1
    blocks = seq // BLOCK
    shards = (gain_attn, gain_inner, gain_ffn, gain_mid)
    sizes = [g.shape[0] for g in shards]

    start, position, valid = layout(doc_lengths, seq)
    cos, sin = tables(position)
    firsts = start[:, ::BLOCK] // BLOCK
    reach = (jnp.arange(blocks, dtype=jnp.int32)[None, :] - firsts + 1).reshape(-1)
    start_col = start.reshape(-1, 1)
    start_row = jnp.repeat(start, 8, axis=0)
    gy = jnp.where(valid.reshape(-1, 1), cotangent, jnp.zeros_like(cotangent))

    def scatter(g):
        return lax.psum_scatter(g, AXES, scatter_dimension=0, tiled=True)

    def gather(v):
        return lax.all_gather(v, AXES, axis=0, tiled=True)

    if fast:
        order, back = gather_order(), scatter_order()
        gains_row = jnp.pad(jnp.concatenate(shards)[None], ((0, 7), (0, LANES - sum(sizes))))
        one, two = (Gather(b) for b in pack(w_qkv, w_out, w_up, w_down, gains_row))
        seen = one.z()
        two.z(seen)
        one.first()
        far = one.second()
        two.first(far)
        parts_qkv = one.core()
        gains = [None]
    else:
        order = back = jnp.zeros((8,), jnp.int32)
        parts_qkv, parts_up, parts_down = [gather(w_qkv)], [gather(w_out), gather(w_up)], [gather(w_down)]
        gains = [gather(g).astype(F32).reshape(1, -1) for g in shards]

    h1, qkv, full_qkv, *rest = qkv_forward(fast, order, tokens, cos, sin, parts_qkv, gains[0], sizes)
    g_attn, g_inner, g_ffn, g_mid = rest if fast else gains
    if fast:
        two.second(g_attn)
    mixed, lse = attention_forward(reach, qkv, start_col, row_count, wide)
    if fast:
        parts_up = parts_down = two.core(lse)
    a, h2, x1, m, slope, inv, full_out, full_up, *m_other = up_forward(
        fast, order, mixed, tokens, g_inner, g_ffn, g_mid, parts_up
    )
    dpre, gg_down, full_down = down_backward(fast, order, m, slope, inv, gy, g_mid, parts_down)
    dx1, low, d_mixed, gg_up = up_backward(dpre, x1, gy, mixed, full_up, full_out, g_ffn, g_inner)

    def shared(value):
        return (value, over_core(value)) if fast else (value,)

    def split_low(pair):
        return (pair[0], over_core(pair[1])) if fast else tuple(pair)

    m_both = (m, over_core(m_other[0])) if fast else (m,)
    a, h2, low, dpre = split_low(a), split_low(h2), shared(low), shared(dpre)

    def attend(group, groups, lse, so_far):
        return attention_backward(
            reach, qkv, d_mixed, mixed, lse, start_row, cos, sin, row_count, wide, group, groups, so_far
        )

    f = w_up.shape[1]
    grads = weight_grads(
        fast, back, [(m_both, shared(gy), f // 384, True), (a, low, d // LANES, False), (h2, dpre, f // LANES, False)]
    )
    if fast:
        red = Reduce(*grads)
        first = red.first()
    d_qkv = attend(0, 2, tie(lse, grads[-1]), None)
    if fast:
        second = red.second(d_qkv)
        lse = tie(lse, first)
    d_qkv = attend(2, 1, lse, d_qkv)
    if fast:
        near = red.near_z(d_qkv)
        dx1 = tie(dx1, second)
    d_both = (d_qkv, over_core(tie(d_qkv, second))) if fast else (d_qkv,)
    grad_tokens, gain_rows = qkv_backward(d_qkv, tokens, dx1, full_qkv, g_attn, (gg_up, gg_down))
    if fast:
        h1 = tie(split_low(h1), (gain_rows, near))
        far = red.far_z(gain_rows)
        grad_qkv = weight_grads(fast, back, [(h1, d_both, 3 * d // LANES, False)], shared(gain_rows), sizes)
        red_qkv = Reduce(*grad_qkv)
        first = red_qkv.first()
        result = down_forward(tie(m, (grad_qkv[-1], far)), x1, full_down)
        second = red_qkv.second(result)
        own = red.own()
        red_qkv.near_z()
        red_qkv.far_z()
        g_qkv = red_qkv.own()
        cuts = (w_down.shape[0], w_down.shape[0] + w_out.shape[0])
        own_down, grad_out, grad_up = own[: cuts[0]], own[cuts[0] : cuts[1]], unslab(own[cuts[1] :], f)
        flat = g_qkv[w_qkv.size // LANES]
        g_qkv = g_qkv[: w_qkv.size // LANES]
        summed, at = [], 0
        for size in sizes:
            summed.append(flat[at : at + size])
            at += size
    else:
        grad_qkv = weight_grads(fast, back, [(h1, d_both, 3 * d // LANES, False)])
        result = down_forward(m, x1, full_down)
        own_down, grad_out, grad_up, g_qkv = (scatter(g.astype(BF)).astype(F32) for g in (*grads, *grad_qkv))
        flat = gain_rows[: 3 + f // d]
        summed = [scatter(flat[i]) for i in range(3)] + [scatter(flat[3:].reshape(-1))]
        g_qkv = jnp.concatenate(slab(g_qkv))
    size = w_qkv.shape[0]
    span = LANES // 3
    g_qkv = jnp.concatenate(
        [g_qkv[g * size : (g + 1) * size, p * span : (p + 1) * span] for p in range(3) for g in range(GRAD_GROUPS)], axis=1
    )
    return (result, grad_tokens, g_qkv, grad_out, grad_up, own_down) + tuple(summed)


def solution(mesh):
    matrix, vector = P(AXES, None), P(AXES)
    fast = mesh.shape["dp"] == 4 and mesh.shape["fsdp"] == 2 * Z
    return jax.shard_map(
        functools.partial(local, fast),
        mesh=mesh,
        in_specs=(matrix,) * 7 + (vector,) * 4,
        out_specs=(matrix,) * 6 + (vector,) * 4,
        check_vma=False,
    )
```

```python
import functools
import math

import jax
import jax.numpy as jnp
import numpy as np
from jax import lax
from jax.experimental import pallas as pl
from jax.experimental.pallas import tpu as pltpu
from jax.sharding import PartitionSpec as P

HEADS = 12
HEAD_DIM = 64
PAIR = 2 * HEAD_DIM
PAIRS = HEADS // 2
EPSILON = 1e-05
MASKED_SCORE = -1e30
ROOT_HALF = 0.7071067811865476
INV_ROOT_TAU = 0.3989422804014327
BF = jnp.bfloat16
F32 = jnp.float32
MIB = 1 << 20
AXES = ("dp", "fsdp")
BLOCK = 256
ROWS = 256
LANES = 768
VMEM_MIB = 60
GRAD_GROUPS = 3


def dot(a, b, dims=((1,), (0,))):
    return lax.dot_general(a, b, (dims, ((), ())), preferred_element_type=F32)


def params(mib):
    return pltpu.CompilerParams(vmem_limit_bytes=max(mib, VMEM_MIB) * MIB)


def swap_halves(x):
    lane = lax.broadcasted_iota(jnp.int32, x.shape, 1)
    low = lax.rem(lane, HEAD_DIM) < HEAD_DIM // 2
    half = HEAD_DIM // 2
    return jnp.where(low, pltpu.roll(x, PAIR - half, 1), pltpu.roll(x, half, 1))


def unit_norm(x):
    mean = jnp.mean(x, axis=-1, keepdims=True)
    centred = x - mean
    inv = lax.rsqrt(jnp.mean(centred * centred, axis=-1, keepdims=True) + EPSILON)
    return centred * inv, inv


def norm_back(grad, gain, unit, inv):
    d_unit = grad * gain
    return inv * (
        d_unit
        - jnp.mean(d_unit, axis=-1, keepdims=True)
        - unit * jnp.mean(d_unit * unit, axis=-1, keepdims=True)
    )


def whole(shape):
    return pl.BlockSpec(shape, lambda *_: (0,) * len(shape), pipeline_mode=pl.Buffered(1))


def rows(width, block=ROWS):
    return pl.BlockSpec((block, width), lambda i: (i, 0))


def shaped(shape, dtype):
    return jax.ShapeDtypeStruct(shape, dtype)


def hbm():
    return pl.BlockSpec(memory_space=pl.ANY)


def fetch(order, parts, places, sem):
    if len(parts) < 8 and parts[0].ndim == 2:
        for part, (_, _, buffer, _) in zip(parts, places):
            pltpu.make_async_copy(part, buffer, sem).start()
        return
    count = parts[0].shape[0]
    for p, part in enumerate(parts):
        for b in range(count):
            owner = b if order is None else order[p * count + b]
            for first, size, buffer, column in places:
                row = owner * size if order is None else pl.multiple_of(owner * size, 8)
                pltpu.make_async_copy(
                    part.at[b, pl.ds(first, size), :],
                    buffer.at[pl.ds(row, size), pl.ds(column, LANES)],
                    sem,
                ).start()


def arrive(buffers, sem):
    for buffer in buffers:
        pltpu.make_async_copy(buffer, buffer, sem).wait()


def deal(back, tile, outs, row, size):
    quarter = outs[0].shape[0]
    for q, out in enumerate(outs):

        @pl.loop(0, quarter)
        def _(j):
            block = tile[pl.ds(pl.multiple_of(back[q * quarter + j] * size, 8), size), :]
            out[j, pl.ds(row, size), :] = block.astype(out.dtype)


def slabs(first, size, buffer, width):
    return [(first + s * size, size, buffer, s * LANES) for s in range(width // LANES)]


def pack_kernel(wq_ref, wo_ref, wu_ref, wd_ref, gains_ref, one_ref, two_ref):
    row = 0
    for c in range(wq_ref.shape[1] // LANES):
        one_ref[row : row + wq_ref.shape[0], :] = wq_ref[:, c * LANES : (c + 1) * LANES]
        row += wq_ref.shape[0]
    one_ref[row:, :] = gains_ref[...]
    row = 0
    for ref in (wd_ref, wo_ref, wu_ref):
        for c in range(ref.shape[1] // LANES):
            two_ref[row : row + ref.shape[0], :] = ref[:, c * LANES : (c + 1) * LANES]
            row += ref.shape[0]


def pack(w_qkv, w_out, w_up, w_down, gains):
    first = w_qkv.size // LANES + gains.shape[0]
    second = (w_out.size + w_up.size + w_down.size) // LANES
    return pl.pallas_call(
        pack_kernel, out_shape=[shaped((first, LANES), BF), shaped((second, LANES), BF)], name="pack"
    )(w_qkv, w_out, w_up, w_down, gains)


def spread(rows_in, offset, count, owners):
    lanes = rows_in.shape[1]
    wide = owners * count
    lane = lax.broadcasted_iota(jnp.int32, (lanes, wide), 0)
    column = lax.broadcasted_iota(jnp.int32, (lanes, wide), 1)
    pick = (lane - offset == lax.rem(column, count)).astype(F32).astype(BF)
    full = dot(rows_in, pick)
    owner = lax.broadcasted_iota(jnp.int32, (owners, wide), 0)
    column = lax.broadcasted_iota(jnp.int32, (owners, wide), 1)
    own = (column >= owner * count) & (column < owner * count + count)
    return jnp.sum(jnp.where(own, full, 0.0), axis=0, keepdims=True)


def qkv_kernel(split, sizes, *refs):
    if split:
        order, x_ref, cos_ref, sin_ref, *refs = refs
        parts, refs = refs[:8], refs[8:]
        h_ref, other_ref, qkv_ref, w_ref, ga_ref, gi_ref, gf_ref, gm_ref, gains, sem, gain_sem = refs
        h_refs = (h_ref, other_ref)
    else:
        order, x_ref, cos_ref, sin_ref, ga_ref, *refs = refs
        parts, refs = refs[:1], refs[1:]
        h_ref, qkv_ref, w_ref, sem = refs
        h_refs = (h_ref,)
    width = x_ref.shape[1]
    step = pl.program_id(0)
    if split:
        size = width // 32
        weight = slabs(0, size, w_ref, 3 * width)

        @pl.when(step == 0)
        def _():
            fetch(order, parts, [(3 * size, 8, gains, 0)], gain_sem)
            fetch(order, parts, weight, sem)
            arrive([gains], gain_sem)
            owner = lax.broadcasted_iota(jnp.int32, (32, 256), 0)
            lane = lax.broadcasted_iota(jnp.int32, (32, 256), 1)
            pick = (lane == owner * 8).astype(F32).astype(BF)
            per_owner = dot(pick, gains[:, :256]).astype(BF)
            at = 0
            for ref, count in zip((ga_ref, gi_ref, gf_ref, gm_ref), sizes):
                ref[...] = spread(per_owner, at, count, 32)
                at += count
            arrive([w_ref], sem)
    else:

        @pl.when(step == 0)
        def _():
            fetch(None, parts, [(0, 0, w_ref, 0)], sem)
            arrive([w_ref], sem)

    unit, _ = unit_norm(x_ref[...].astype(F32))
    h = (unit * ga_ref[...]).astype(BF)
    store_low(split, order[32] if split else 0, h, h_refs)
    cos, sin = cos_ref[...], sin_ref[...]
    for part in range(3):
        y = dot(h, w_ref[:, part * width : (part + 1) * width])
        for c in range(width // PAIR):
            z = y[:, c * PAIR : (c + 1) * PAIR]
            if part < 2:
                z = z * cos + swap_halves(z) * sin
            if part == 0:
                z = z * (1.0 / math.sqrt(HEAD_DIM))
            at = part * width + c * PAIR
            qkv_ref[:, at : at + PAIR] = z.astype(BF)


def prefetched(kernel, order, inputs, in_specs, out_specs, out_shape, scratch, grid, mib, name, flops, data):
    return pl.pallas_call(
        kernel,
        grid_spec=pltpu.PrefetchScalarGridSpec(
            num_scalar_prefetch=1,
            grid=grid,
            in_specs=in_specs,
            out_specs=out_specs,
            scratch_shapes=scratch,
        ),
        out_shape=out_shape,
        compiler_params=params(mib),
        cost_estimate=pl.CostEstimate(flops=flops, transcendentals=0, bytes_accessed=data),
        name=name,
    )(order, *inputs)


def rows(width, block=ROWS):
    return pl.BlockSpec((block, width), lambda i, *_: (i, 0))


def whole(shape):
    return pl.BlockSpec(shape, lambda *_: (0,) * len(shape), pipeline_mode=pl.Buffered(1))


def qkv_forward(split, order, tokens, cos, sin, parts, gain, sizes):
    t, d = tokens.shape
    n = 3 * d
    inputs = [tokens, cos, sin]
    in_specs = [rows(d), rows(PAIR), rows(PAIR)]
    out_specs, out_shape = low_specs(split, t, d)
    lows = len(out_specs)
    out_specs = out_specs + [rows(n), whole((d, n))]
    out_shape = out_shape + [shaped((t, n), BF), shaped((d, n), BF)]
    scratch = [pltpu.SemaphoreType.DMA]
    if split:
        widths = [32 * s for s in sizes]
        out_specs += [whole((1, w)) for w in widths]
        out_shape += [shaped((1, w), F32) for w in widths]
        scratch = [pltpu.VMEM((32 * 8, LANES), BF), pltpu.SemaphoreType.DMA, pltpu.SemaphoreType.DMA]
    else:
        inputs.append(gain)
        in_specs.append(whole((1, d)))
    outs = prefetched(
        functools.partial(qkv_kernel, split, sizes), order, inputs + list(parts), in_specs + [hbm()] * len(parts),
        out_specs, out_shape, scratch, (t // ROWS,), 40, "qkv_forward",
        2 * t * d * n, 4 * d * n + 12 * t * d,
    )
    return (outs[:lows], *outs[lows:])


def window(i, n):
    return slice((i - n + 1) * BLOCK, (i + 1) * BLOCK)


def head_masks(shape):
    lane = lax.broadcasted_iota(jnp.int32, shape, 1)
    return lane < HEAD_DIM


def attention_forward_kernel(wide, reach, q_ref, k_ref, v_ref, start_ref, o_ref, lse_ref, bias):
    row, pair = pl.program_id(0), pl.program_id(1)
    seq = q_ref.shape[0]
    blocks = seq // BLOCK

    @pl.when(pair == 0)
    def _():
        for i in range(blocks):
            at = slice(i * BLOCK, (i + 1) * BLOCK)
            shape = (BLOCK, wide * BLOCK)
            key = (i - wide + 1) * BLOCK + lax.broadcasted_iota(jnp.int32, shape, 1)
            query = i * BLOCK + lax.broadcasted_iota(jnp.int32, shape, 0)
            keep = (key >= start_ref[at, :]) & (key <= query)
            bias[at, :] = jnp.where(keep, 0.0, MASKED_SCORE)

    first = head_masks((BLOCK, PAIR))
    for i in range(blocks):
        at = slice(i * BLOCK, (i + 1) * BLOCK)
        most = min(wide, i + 1)
        for n in range(1, most + 1):

            @pl.when(reach[row * blocks + i] == n)
            def _():
                q = q_ref[at, :]
                w = window(i, n)
                k, v = k_ref[w, :], v_ref[w, :]
                b = bias[at, (wide - n) * BLOCK :]
                mask = head_masks(k.shape)
                zero = jnp.zeros_like(k)
                total, lses = None, []
                scale = None
                for h in range(2):
                    pick = mask if h == 0 else jnp.logical_not(mask)
                    s = dot(q, jnp.where(pick, k, zero), ((1,), (1,))) + b
                    top = jnp.max(s, axis=-1, keepdims=True)
                    p = jnp.exp(s - top)
                    den = jnp.sum(p, axis=-1, keepdims=True)
                    probs = (p * (1.0 / den)).astype(BF)
                    part = dot(probs, jnp.where(pick, v, zero))
                    total = part if total is None else total + part
                    lses.append(top + jnp.log(den))
                o_ref[at, :] = total
                both = jnp.where(first, lses[0], lses[1]).T
                lse_ref[0, 0:1, at] = both[0:1, :]
                lse_ref[0, 1:2, at] = both[HEAD_DIM : HEAD_DIM + 1, :]


def attention_forward(reach, qkv, start, row_count, wide):
    t = qkv.shape[0]
    seq = t // row_count
    d = qkv.shape[1] // 3

    def columns(part):
        return pl.BlockSpec((seq, PAIR), lambda r, p, *_: (r, part * PAIRS + p))

    return pl.pallas_call(
        functools.partial(attention_forward_kernel, wide),
        grid_spec=pltpu.PrefetchScalarGridSpec(
            num_scalar_prefetch=1,
            grid=(row_count, PAIRS),
            in_specs=[
                columns(0),
                columns(1),
                columns(2),
                pl.BlockSpec((seq, 1), lambda r, p, *_: (r, 0)),
            ],
            out_specs=[
                pl.BlockSpec((seq, PAIR), lambda r, p, *_: (r, p)),
                pl.BlockSpec((1, 8, seq), lambda r, p, *_: (r * PAIRS + p, 0, 0)),
            ],
            scratch_shapes=[pltpu.VMEM((seq, wide * BLOCK), F32)],
        ),
        out_shape=[shaped((t, d), F32), shaped((row_count * PAIRS, 8, seq), F32)],
        compiler_params=params(32),
        cost_estimate=pl.CostEstimate(
            flops=8 * t * d * BLOCK, transcendentals=t * HEADS * 512, bytes_accessed=12 * t * d
        ),
        name="attention_forward",
    )(reach, qkv, qkv, qkv, start)


def attention_backward_kernel(wide, reach, q_ref, k_ref, v_ref, do_ref, o_ref, lse_ref, start_ref, cos_ref, sin_ref, *refs):
    grad_ref, bias, ks, vs, qs, dos, dk_acc, dv_acc, dq_acc = refs[-9:]
    row, pair = pl.program_id(0), pl.program_id(1)
    seq = q_ref.shape[0]
    blocks = seq // BLOCK

    @pl.when(pair == 0)
    def _():
        for i in range(blocks):
            at = slice(i * BLOCK, (i + 1) * BLOCK)
            shape = (wide * BLOCK, BLOCK)
            key = (i - wide + 1) * BLOCK + lax.broadcasted_iota(jnp.int32, shape, 0)
            query = i * BLOCK + lax.broadcasted_iota(jnp.int32, shape, 1)
            keep = (key >= start_ref[0:1, at]) & (key <= query)
            bias[:, at] = jnp.where(keep, 0.0, MASKED_SCORE)

    mask = head_masks((seq, PAIR))
    for src, dst in ((k_ref, ks), (v_ref, vs), (q_ref, qs), (do_ref, dos)):
        x = src[...]
        zero = jnp.zeros_like(x)
        dst[0] = jnp.where(mask, x, zero)
        dst[1] = jnp.where(mask, zero, x)
    dk_acc[...] = jnp.zeros_like(dk_acc)
    dv_acc[...] = jnp.zeros_like(dv_acc)
    lane8 = lax.broadcasted_iota(jnp.int32, (8, PAIR), 1) // HEAD_DIM
    row8 = lax.broadcasted_iota(jnp.int32, (8, PAIR), 0)
    picks = (lane8 == row8).astype(F32)
    delta = lax.dot_general(
        picks, do_ref[...].astype(F32) * o_ref[...], (((1,), (1,)), ((), ())),
        precision=lax.Precision.HIGHEST, preferred_element_type=F32,
    )
    for i in range(blocks):
        at = slice(i * BLOCK, (i + 1) * BLOCK)
        most = min(wide, i + 1)
        for n in range(1, most + 1):

            @pl.when(reach[row * blocks + i] == n)
            def _():
                w = window(i, n)
                b = bias[(wide - n) * BLOCK :, at]
                q, do = q_ref[at, :], do_ref[at, :]
                ps, dss = [], []
                for h in range(2):
                    s = dot(ks[h, w, :], q, ((1,), (1,))) + b
                    p = jnp.exp(s - lse_ref[0, h : h + 1, at])
                    dp = dot(vs[h, w, :], do, ((1,), (1,)))
                    ds = (p * (dp - delta[h : h + 1, at])).astype(BF)
                    ps.append(p.astype(BF))
                    dss.append(ds)
                dv_acc[w, :] += dot(ps[0], dos[0, at, :]) + dot(ps[1], dos[1, at, :])
                dk_acc[w, :] += dot(dss[0], qs[0, at, :]) + dot(dss[1], qs[1, at, :])
                dq_acc[at, :] = dot(dss[0], ks[0, w, :], ((0,), (0,))) + dot(
                    dss[1], ks[1, w, :], ((0,), (0,))
                )

    cos, sin = cos_ref[...], sin_ref[...]
    dq = dq_acc[...] * (1.0 / math.sqrt(HEAD_DIM))
    dk = dk_acc[...]
    span = grad_ref.shape[2] // 3
    slot = lax.rem(pair, span // PAIR)
    grads = (dq * cos - swap_halves(dq) * sin, dk * cos - swap_halves(dk) * sin, dv_acc[...])
    for part, value in enumerate(grads):
        grad_ref[0, :, pl.ds(pl.multiple_of(part * span + slot * PAIR, PAIR), PAIR)] = value.astype(BF)


def attention_backward(reach, qkv, d_mixed, mixed, lse, start_row, cos, sin, row_count, wide, group, groups, so_far):
    pairs = PAIRS // GRAD_GROUPS
    t = qkv.shape[0]
    seq = t // row_count
    base = group * pairs
    span = 3 * pairs * PAIR

    def columns(part):
        return pl.BlockSpec((seq, PAIR), lambda r, p, *_: (r, part * PAIRS + base + p))

    table = pl.BlockSpec((seq, PAIR), lambda r, p, *_: (r, 0))
    inputs = [reach, qkv, qkv, qkv, d_mixed, mixed, lse, start_row, cos, sin]
    in_specs = [
        columns(0), columns(1), columns(2), columns(0), columns(0),
        pl.BlockSpec((1, 8, seq), lambda r, p, *_: (r * PAIRS + base + p, 0, 0)),
        pl.BlockSpec((8, seq), lambda r, p, *_: (r, 0)),
        table, table,
    ]
    aliases = {}
    if so_far is not None:
        aliases = {len(inputs): 0}
        inputs.append(so_far)
        in_specs.append(hbm())
    return pl.pallas_call(
        functools.partial(attention_backward_kernel, wide),
        grid_spec=pltpu.PrefetchScalarGridSpec(
            num_scalar_prefetch=1,
            grid=(row_count, pairs * groups),
            in_specs=in_specs,
            out_specs=pl.BlockSpec((1, seq, span), lambda r, p, *_: (group + p // pairs, r, 0)),
            scratch_shapes=[
                pltpu.VMEM((wide * BLOCK, seq), F32),
                pltpu.VMEM((2, seq, PAIR), BF),
                pltpu.VMEM((2, seq, PAIR), BF),
                pltpu.VMEM((2, seq, PAIR), BF),
                pltpu.VMEM((2, seq, PAIR), BF),
                pltpu.VMEM((seq, PAIR), F32),
                pltpu.VMEM((seq, PAIR), F32),
                pltpu.VMEM((seq, PAIR), F32),
            ],
        ),
        out_shape=shaped((GRAD_GROUPS, t, span), BF),
        input_output_aliases=aliases,
        compiler_params=params(40),
        cost_estimate=pl.CostEstimate(
            flops=20 * t * span * BLOCK // 3 * groups, transcendentals=t * HEADS * 128 * groups,
            bytes_accessed=20 * t * span // 3 * groups
        ),
        name="attention_backward",
    )(*inputs)


def halves(x):
    quarter = x.shape[1] // 4
    piece = [x[:, i * quarter : (i + 1) * quarter] for i in range(4)]
    return jnp.concatenate(piece[0::2], axis=1), jnp.concatenate(piece[1::2], axis=1)


def store_low(split, core, x, refs):
    if not split:
        refs[0][...] = x
        return
    pair = halves(x)
    for c in range(2):

        @pl.when(core == c)
        def _():
            refs[0][...] = pair[c]
            refs[1][...] = pair[1 - c]


def low_specs(split, t, d):
    if split:
        return [rows(d // 2)] * 2, [shaped((t, d // 2), BF)] * 2
    return [rows(d)], [shaped((t, d), BF)]


def ffn_kernel(split, *refs):
    order, o_ref, x_ref, gy_ref, gi_ref, gf_ref, gm_ref, *refs = refs
    count = 8 if split else 3
    lows = 2 if split else 1
    parts, refs = refs[:count], refs[count:]
    a_refs, h2_refs, refs = refs[:lows], refs[lows : 2 * lows], refs[2 * lows :]
    x1_ref, m_ref, dpre_ref, dx1_ref, low_ref, do_ref, gg_ref, wd_ref, wo_ref, wu_ref, *refs = refs
    other_ref, refs = (refs[0], refs[1:]) if split else (None, refs)
    act, slope, dm, sem, down_sem = refs
    d, f = wu_ref.shape
    size, skip = d // 32, f // 32
    step = pl.program_id(0)
    core = order[32] if split else 0
    chunks = [slice(c, c + LANES) for c in range(0, f, LANES)]

    @pl.when(step == 0)
    def _():
        if split:
            fetch(order, parts, [(skip, size, wo_ref, 0)] + slabs(skip + size, size, wu_ref, f), sem)
            fetch(order, parts, [(0, skip, wd_ref, 0)], down_sem)
        else:
            fetch(order, parts[:2], [(0, 0, wo_ref, 0), (0, 0, wu_ref, 0)], sem)
            fetch(order, parts[2:], [(0, 0, wd_ref, 0)], down_sem)

    mixed = o_ref[...]
    unit_in, inv_in = unit_norm(mixed)
    a = (unit_in * gi_ref[...]).astype(BF)
    store_low(split, core, a, a_refs)

    @pl.when(step == 0)
    def _():
        arrive([wo_ref, wu_ref], sem)
        arrive([wd_ref], down_sem)

    x1 = x_ref[...].astype(F32) + dot(a, wo_ref[...])
    x1_ref[...] = x1
    unit_two, inv_two = unit_norm(x1)
    h2 = (unit_two * gf_ref[...]).astype(BF)
    store_low(split, core, h2, h2_refs)
    gy = gy_ref[...]
    total = None
    for at in chunks:
        hidden = dot(h2, wu_ref[:, at])
        dm[:, at] = dot(gy, wd_ref[at, :], ((1,), (1,)))
        cdf = 0.5 + 0.5 * lax.erf(hidden * ROOT_HALF)
        slope[:, at] = cdf + hidden * (jnp.exp(-0.5 * hidden * hidden) * INV_ROOT_TAU)
        value = hidden * cdf
        act[:, at] = value
        part = jnp.sum(value, axis=-1, keepdims=True)
        total = part if total is None else total + part
    mean = total * (1.0 / f)
    total = None
    for at in chunks:
        centred = act[:, at] - mean
        part = jnp.sum(centred * centred, axis=-1, keepdims=True)
        total = part if total is None else total + part
    inv = lax.rsqrt(total * (1.0 / f) + EPSILON)
    first = second = None
    gains = []
    for at in chunks:
        gain = gm_ref[:, at]
        unit = (act[:, at] - mean) * inv
        act[:, at] = unit
        m_ref[:, at] = (unit * gain).astype(BF)
        grad = dm[:, at]
        d_unit = grad * gain
        prod = grad * unit
        gains.append(jnp.sum(prod, axis=0, keepdims=True))
        part = jnp.sum(d_unit, axis=-1, keepdims=True)
        first = part if first is None else first + part
        part = jnp.sum(d_unit * unit, axis=-1, keepdims=True)
        second = part if second is None else second + part
    first, second = first * (1.0 / f), second * (1.0 / f)
    dh2 = None
    for at in chunks:
        d_act = inv * (dm[:, at] * gm_ref[:, at] - first - act[:, at] * second)
        dpre = (d_act * slope[:, at]).astype(BF)
        dpre_ref[:, at] = dpre
        part = dot(dpre, wu_ref[:, at], ((1,), (1,)))
        dh2 = part if dh2 is None else dh2 + part
    line = lax.broadcasted_iota(jnp.int32, (8, d), 0)
    rows_of = jnp.where(line == 2, jnp.sum(dh2 * unit_two, axis=0, keepdims=True), 0.0)
    for at, value in enumerate(gains):
        rows_of = jnp.where(line == 3 + at, value, rows_of)
    dx1 = gy.astype(F32) + norm_back(dh2, gf_ref[...], unit_two, inv_two)
    dx1_ref[...] = dx1
    low = dx1.astype(BF)
    low_ref[...] = low
    da = dot(low, wo_ref[...], ((1,), (1,)))
    rows_of = jnp.where(line == 1, jnp.sum(da * unit_in, axis=0, keepdims=True), rows_of)
    do_ref[...] = norm_back(da, gi_ref[...], unit_in, inv_in).astype(BF)

    @pl.when(step == 0)
    def _():
        gg_ref[...] = rows_of

    @pl.when(step > 0)
    def _():
        gg_ref[...] += rows_of

    if split:
        quarter = f // 4
        for j in range(2):
            at = pl.multiple_of((2 * j + 1 - core) * quarter, PAIR)
            other_ref[:, j * quarter : (j + 1) * quarter] = m_ref[:, pl.ds(at, quarter)]


def ffn_both(split, order, mixed, tokens, gy, gain_inner, gain_ffn, gain_mid, parts):
    t, d = tokens.shape
    f = gain_mid.shape[1]
    low_out, low_shape = low_specs(split, t, d)
    more = [(rows(f // 2), shaped((t, f // 2), BF))] * split
    outs = prefetched(
        functools.partial(ffn_kernel, split), order, [mixed, tokens, gy, gain_inner, gain_ffn, gain_mid, *parts],
        [rows(d), rows(d), rows(d), whole((1, d)), whole((1, d)), whole((1, f))] + [hbm()] * len(parts),
        low_out * 2 + [rows(d), rows(f), rows(f), rows(d), rows(d), rows(d), whole((8, d)), whole((f, d))]
        + [whole((d, d)), whole((d, f))] + [m[0] for m in more],
        low_shape * 2 + [
            shaped((t, d), F32), shaped((t, f), BF), shaped((t, f), BF), shaped((t, d), F32), shaped((t, d), BF),
            shaped((t, d), BF), shaped((8, d), F32), shaped((f, d), BF), shaped((d, d), BF), shaped((d, f), BF),
        ] + [m[1] for m in more],
        [
            pltpu.VMEM((ROWS, f), F32), pltpu.VMEM((ROWS, f), F32), pltpu.VMEM((ROWS, f), F32), pltpu.SemaphoreType.DMA, pltpu.SemaphoreType.DMA,
        ],
        (t // ROWS,), 60, "ffn_both", 2 * t * d * (2 * d + 3 * f), 6 * d * f + 4 * t * f + 30 * t * d,
    )
    lows = len(low_out)
    return (outs[:lows], outs[lows : 2 * lows], *outs[2 * lows :])


def slab_rows(values, first, width):
    count = values.shape[1] // width
    line = lax.broadcasted_iota(jnp.int32, (8, width), 0)
    total = jnp.zeros((8, width), F32)
    for i in range(count):
        total = jnp.where(line == first + i, values[:, i * width : (i + 1) * width], total)
    return total


def result_kernel(m_ref, x1_ref, wd_ref, y_ref):
    y_ref[...] = (x1_ref[...] + dot(m_ref[...], wd_ref[...])).astype(BF)


def down_forward(m, x1, w_down):
    t, d = x1.shape
    f = m.shape[1]
    return pl.pallas_call(
        result_kernel,
        grid=(t // ROWS,),
        in_specs=[rows(f), rows(d), whole((f, d))],
        out_specs=rows(d),
        out_shape=shaped((t, d), BF),
        compiler_params=params(48),
        cost_estimate=pl.CostEstimate(flops=2 * t * d * f, transcendentals=0, bytes_accessed=2 * d * f + 2 * t * f + 6 * t * d),
        name="down_forward",
    )(m, x1, w_down)


def take_gains(rows_of, core, sizes):
    total = jnp.zeros((16, 256), F32)
    owner = lax.broadcasted_iota(jnp.int32, (16, LANES), 0)
    column = lax.broadcasted_iota(jnp.int32, (16, LANES), 1)
    device = (owner // 8) * 16 + core * 8 + owner % 8
    line, offset = 0, 0
    for size in sizes:
        pieces = jnp.zeros((16, LANES), F32)
        for slab_at in range(32 * size // LANES):
            base = device * size - slab_at * LANES
            own = (column >= base) & (column < base + size)
            pieces = pieces + jnp.where(own, rows_of[line : line + 1, :], 0.0)
            line += 1
        source = lax.broadcasted_iota(jnp.int32, (LANES, 256), 0)
        target = lax.broadcasted_iota(jnp.int32, (LANES, 256), 1)
        pick = (lax.rem(source, size) == target - offset).astype(F32)
        total = total + lax.dot_general(
            pieces, pick, (((1,), (0,)), ((), ())), precision=lax.Precision.HIGHEST, preferred_element_type=F32
        )
        offset += size
    return total


def grads_kernel(split, products, sizes, *refs):
    back, *refs = refs
    if sizes:
        gain_refs, refs = refs[:2], refs[2:]
    count = 2 if split else 1
    left, refs = refs[: len(products) * count], refs[len(products) * count :]
    right, refs = refs[: len(products) * count], refs[len(products) * count :]
    outs, refs = refs[: 4 if split else len(products)], refs[4 if split else len(products) :]
    tile, turned = refs[0], refs[1:]
    step = pl.program_id(0)
    first, row = 0, 0
    for n, (by_left, tiles, size) in enumerate(products):
        mine = [left[n * count + c] for c in range(count)]
        value = [right[n * count + c] for c in range(count)]

        if not by_left:

            @pl.when(step == first)
            def _():
                t = mine[0].shape[0]
                for c in range(count):
                    turned[0][:, c * t : (c + 1) * t] = mine[c][...].T

        @pl.when((step >= first) & (step < first + tiles))
        def _():
            total = None
            for c in range(count):
                v = value[c][...] if len(value[c].shape) == 2 else value[c][0]
                t = v.shape[0]
                if by_left:
                    part = dot(mine[c][...], v, ((0,), (0,)))
                else:
                    part = dot(turned[0][:, c * t : (c + 1) * t], v)
                total = part if total is None else total + part
            if not split:
                outs[n][...] = total
            else:
                tile[...] = total
                if by_left:
                    owners = tile.shape[0] // size
                    for e in range(owners):
                        at = back[16 + (step - first) * owners + e]
                        for q in range(4):

                            @pl.when(at // 4 == q)
                            def _():
                                block = tile[e * size : (e + 1) * size, :]
                                outs[q][at - 4 * q, row : row + size, :] = block.astype(outs[q].dtype)
                else:
                    deal(back, tile, outs, row + pl.multiple_of((step - first) * size, 8), size)

        first += tiles
        row += size if by_left else tiles * size

    if sizes:

        @pl.when(step == first - 1)
        def _():
            pieces = take_gains(gain_refs[0][...] + gain_refs[1][...], back[32], sizes)
            tile[...] = jnp.zeros_like(tile)
            for owner in range(16):
                tile[owner * 8 : owner * 8 + 1, :256] = pieces[owner : owner + 1, :]
            deal(back, tile, outs, row, 8)


def weight_grads(split, back, products, gain_rows=(), sizes=()):
    count = 2 if split else 1
    t = products[0][0][0].shape[0]
    left_specs, right_specs, lefts, rights, plan = [], [], [], [], []
    out_specs, out_shape = [], []
    at = row = 0
    for left, right, tiles, by_left in products:
        width = 0
        for c in range(count):
            a, b = left[c], right[c]

            if by_left and c == 0:
                tiles = tiles // count
                width = a.shape[1] // (tiles * count)

            def step(i, at=at, tiles=tiles):
                return jnp.clip(i - at, 0, tiles - 1)

            if by_left:
                per = tiles // 2
                if split and c == 0:
                    left_specs.append(pl.BlockSpec(
                        (t, width), lambda i, back, step=step, per=per: (0, (2 * (step(i) // per) + back[32]) * per + step(i) % per)
                    ))
                else:
                    left_specs.append(pl.BlockSpec((t, width), lambda i, *_, step=step: (0, step(i))))
                right_specs.append(whole(b.shape))
            else:
                width = a.shape[1]
                left_specs.append(whole(a.shape))
                if b.ndim == 3:
                    right_specs.append(pl.BlockSpec((1, t, LANES), lambda i, *_, step=step: (step(i), 0, 0)))
                else:
                    right_specs.append(pl.BlockSpec((t, LANES), lambda i, *_, step=step: (0, step(i))))
            lefts.append(a)
            rights.append(b)
        size = (width * tiles if by_left else width) // 16
        if not split:
            shape = (width * tiles, LANES) if by_left else (width, tiles * LANES)
            block = (width, LANES)
            out_specs.append(pl.BlockSpec(
                block, (lambda i, *_, step=step: (step(i), 0)) if by_left else (lambda i, *_, step=step: (0, step(i)))
            ))
            out_shape.append(shaped(shape, F32))
        plan.append((by_left, tiles, size))
        at += tiles
        row += size if by_left else tiles * size
    narrow = next(p[0][0].shape[1] for p in products if not p[3])
    if split:
        row += 8 if sizes else 0
        out_specs = [whole((4, row, LANES))] * 4
        out_shape = [shaped((4, row, LANES), BF)] * 4
    flops = 2 * count * t * narrow * at * LANES
    return prefetched(
        functools.partial(grads_kernel, split, tuple(plan), tuple(sizes)), back, [*gain_rows, *lefts, *rights],
        [whole(g.shape) for g in gain_rows] + left_specs + right_specs,
        out_specs, out_shape, [pltpu.VMEM((narrow, LANES), F32), pltpu.VMEM((narrow, count * t), BF)],
        (at,), 60, "weight_grads", flops, flops // 256,
    )


def qkv_back_kernel(d_ref, x_ref, dx1_ref, w_ref, gain_ref, rest_ref, dx_ref, gg_ref):
    step = pl.program_id(0)
    d = x_ref.shape[1]
    groups, _, span = d_ref.shape
    span //= 3
    dh = None
    for part in range(3):
        for g in range(groups):
            at = part * d + g * span
            piece = dot(d_ref[g, :, part * span : (part + 1) * span], w_ref[:, at : at + span], ((1,), (1,)))
            dh = piece if dh is None else dh + piece
    unit, inv = unit_norm(x_ref[...].astype(F32))
    gain_part = slab_rows(jnp.sum(dh * unit, axis=0, keepdims=True), 0, d)
    dx_ref[...] = dx1_ref[...] + norm_back(dh, gain_ref[...], unit, inv)

    @pl.when(step == 0)
    def _():
        gg_ref[...] = gain_part + rest_ref[...]

    @pl.when(step > 0)
    def _():
        gg_ref[...] += gain_part


def qkv_backward(d_qkv, tokens, dx1, w_qkv, gain, gain_rows):
    t, d = tokens.shape
    groups, _, span = d_qkv.shape
    return pl.pallas_call(
        qkv_back_kernel,
        grid=(t // ROWS,),
        in_specs=[pl.BlockSpec((groups, ROWS, span), lambda i: (0, i, 0))] + [rows(d)] * 2
        + [whole((d, 3 * d)), whole((1, d))] + [whole((8, d))],
        out_specs=[rows(d), whole((8, d))],
        out_shape=[shaped((t, d), F32), shaped((8, d), F32)],
        compiler_params=params(48),
        cost_estimate=pl.CostEstimate(flops=6 * t * d * d, transcendentals=0, bytes_accessed=6 * d * d + 16 * t * d),
        name="qkv_backward",
    )(d_qkv, tokens, dx1, w_qkv, gain, gain_rows)


def layout(doc_lengths, seq):
    docs = doc_lengths.shape[-1]
    upto = jnp.arange(docs)[:, None] <= jnp.arange(docs)[None, :]
    ends = jnp.sum(jnp.where(upto[None], doc_lengths[:, :, None], 0), axis=1)
    places = jnp.arange(seq, dtype=jnp.int32)
    passed = places[None, :, None] >= ends[:, None, :]
    start = jnp.sum(jnp.where(passed, doc_lengths[:, None, :], 0), axis=-1)
    valid = places[None, :] < ends[:, docs - 2 : docs - 1]
    return start.astype(jnp.int32), places[None, :] - start, valid


def tables(position):
    half = HEAD_DIM // 2
    lane = jnp.arange(PAIR)
    frequency = jnp.exp((lane % half).astype(F32) * (-2.0 * math.log(10000.0) / HEAD_DIM))
    angles = position.reshape(-1, 1).astype(F32) * frequency[None, :]
    sign = jnp.where(lane % HEAD_DIM < half, -1.0, 1.0)
    return jnp.cos(angles), jnp.sin(angles) * sign[None, :]


Z = 4
GROUPS = ((0, 2), (1, 3))


def index(x, core, z, y):
    return ((x * 2 + core) * Z + z) * 2 + y


def permute(value, move):
    places = [(x, c, z, y) for x in range(2) for c in range(2) for z in range(Z) for y in range(2)]
    return lax.ppermute(value, AXES, [(index(*p), index(*move(*p))) for p in places])


def over_x(v):
    return permute(v, lambda x, c, z, y: (1 - x, c, z, y))


def over_y(v):
    return permute(v, lambda x, c, z, y: (x, c, z, 1 - y))


def over_core(v):
    return permute(v, lambda x, c, z, y: (x, 1 - c, z, y))


def over_z(v, bits):
    return permute(v, lambda x, c, z, y: (x, c, z ^ bits, y))


def place():
    dp, fs = lax.axis_index("dp"), lax.axis_index("fsdp")
    return dp >> 1, dp & 1, fs >> 1, fs & 1


def gather_order():
    rows_of = []
    for core in range(2):
        for group, first in zip(GROUPS, ("x", "y")):
            for second in range(2):
                for one in range(2):
                    dx, dy = (one, second) if first == "x" else (second, one)
                    rows_of += [(dx, core, dz, dy) for dz in group]
    dx, dc, dz, dy = np.array(rows_of, np.int32).T
    x, c, z, y = place()
    order = index(x ^ dx, c ^ dc, z ^ dz, y ^ dy)
    return jnp.concatenate([order, c[None]]).astype(jnp.int32)


def scatter_order():
    rows_of = []
    for group, first in zip(GROUPS, ("y", "x")):
        for one in (1, 0):
            for second in (1, 0):
                dx, dy = (second, one) if first == "y" else (one, second)
                rows_of += [(dx, dz, dy) for dz in group]
    dx, dz, dy = np.array(rows_of, np.int32).T
    x, c, z, y = place()
    order = ((x ^ dx) * Z + (z ^ dz)) * 2 + (y ^ dy)
    spots = jnp.arange(len(rows_of), dtype=jnp.int32)
    where = jnp.sum(jnp.where(order[None, :] == spots[:, None], spots[None, :], 0), axis=1)
    return jnp.concatenate([order, where, c[None]]).astype(jnp.int32)


def tie(value, other):
    return lax.optimization_barrier((value, other))[0]


class Gather:
    def __init__(self, block):
        self.block = block

    def far_z(self, after=None):
        block = self.block if after is None else tie(self.block, after)
        self.even = jnp.stack([block, over_z(block, 2)])
        return self.even

    def near_z(self, after=None):
        if after is not None:
            self.even = tie(self.even, after)
        self.odd = over_z(self.even, 1)
        return self.odd

    def first(self, after=None):
        even, odd = (self.even, self.odd) if after is None else tie((self.even, self.odd), after)
        self.even = jnp.concatenate([even, over_x(even)])
        self.odd = jnp.concatenate([odd, over_y(odd)])
        return [self.even, self.odd]

    def second(self, after=None):
        even, odd = (self.even, self.odd) if after is None else tie((self.even, self.odd), after)
        self.near = [even, odd, over_core(even), over_core(odd)]
        self.far = [over_y(even), over_x(odd)]
        return self.far

    def core(self, after=None):
        far = self.far if after is None else tie(self.far, after)
        even, odd, even_core, odd_core = self.near
        return [even, far[0], odd, far[1], even_core, over_core(far[0]), odd_core, over_core(far[1])]


class Reduce:
    def __init__(self, send_a, keep_a, send_b, keep_b):
        self.sends, self.a, self.b = (send_a, send_b), keep_a.astype(F32), keep_b.astype(F32)

    def first(self, after=None):
        sends = self.sends if after is None else tie(self.sends, after)
        self.got = (over_y(sends[0]), over_x(sends[1]))
        return self.got

    def second(self, after=None):
        self.a = self.a + self.got[0].astype(F32)
        self.b = self.b + self.got[1].astype(F32)
        sends = (self.a[:2].astype(BF), self.b[:2].astype(BF))
        if after is not None:
            sends = tie(sends, after)
        self.got = (over_x(sends[0]), over_y(sends[1]))
        return self.got

    def near_z(self, after=None):
        self.a = self.a[2:] + self.got[0].astype(F32)
        send = (self.b[2:] + self.got[1].astype(F32)).astype(BF)
        self.got = over_z(send if after is None else tie(send, after), 1)
        return self.got

    def far_z(self, after=None):
        self.a = self.a + self.got.astype(F32)
        send = self.a[1].astype(BF)
        self.got = over_z(send if after is None else tie(send, after), 2)
        return self.got

    def own(self):
        return self.a[0] + self.got.astype(F32)


def unslab(block, width):
    size = block.shape[0] * LANES // width
    return jnp.concatenate([block[s * size : (s + 1) * size] for s in range(width // LANES)], axis=1)


def slab(block):
    return [block[:, s * LANES : (s + 1) * LANES] for s in range(block.shape[1] // LANES)]


def local(fast, tokens, doc_lengths, cotangent, w_qkv, w_out, w_up, w_down,
          gain_attn, gain_inner, gain_ffn, gain_mid):
    row_count = doc_lengths.shape[0]
    seq = tokens.shape[0] // row_count
    d = tokens.shape[1]
    wide = min(seq, 512) // BLOCK + 1
    blocks = seq // BLOCK
    shards = (gain_attn, gain_inner, gain_ffn, gain_mid)
    sizes = [g.shape[0] for g in shards]

    start, position, valid = layout(doc_lengths, seq)
    cos, sin = tables(position)
    firsts = start[:, ::BLOCK] // BLOCK
    reach = (jnp.arange(blocks, dtype=jnp.int32)[None, :] - firsts + 1).reshape(-1)
    start_col = start.reshape(-1, 1)
    start_row = jnp.repeat(start, 8, axis=0)
    gy = jnp.where(valid.reshape(-1, 1), cotangent, jnp.zeros_like(cotangent))

    def scatter(g):
        return lax.psum_scatter(g, AXES, scatter_dimension=0, tiled=True)

    def gather(v):
        return lax.all_gather(v, AXES, axis=0, tiled=True)

    if fast:
        order, back = gather_order(), scatter_order()
        gains_row = jnp.pad(jnp.concatenate(shards)[None], ((0, 7), (0, LANES - sum(sizes))))
        one, two = (Gather(b) for b in pack(w_qkv, w_out, w_up, w_down, gains_row))
        seen = one.far_z()
        two.far_z(seen)
        one.near_z()
        one.first()
        far = one.second(two.even)
        two.near_z()
        two.first(far)
        parts_qkv = one.core()
        cos, sin = tie((cos, sin), (gy, start_col, start_row, reach, order, back))
        gains = [None]
    else:
        order = back = jnp.zeros((8,), jnp.int32)
        parts_qkv, parts_up, parts_down = [gather(w_qkv)], [gather(w_out), gather(w_up)], [gather(w_down)]
        gains = [gather(g).astype(F32).reshape(1, -1) for g in shards]

    h1, qkv, full_qkv, *rest = qkv_forward(fast, order, tokens, cos, sin, parts_qkv, gains[0], sizes)
    g_attn, g_inner, g_ffn, g_mid = rest if fast else gains
    if fast:
        two.second(g_attn)
    mixed, lse = attention_forward(reach, qkv, start_col, row_count, wide)
    parts = two.core(lse) if fast else parts_up + parts_down
    a, h2, x1, m, dpre, dx1, low, d_mixed, gg, full_down, _, _, *m_other = ffn_both(
        fast, order, mixed, tokens, gy, g_inner, g_ffn, g_mid, parts
    )

    def shared(value):
        return (value, over_core(value)) if fast else (value,)

    def split_low(pair):
        return (pair[0], over_core(pair[1])) if fast else tuple(pair)

    gy_both = shared(gy)
    m_both = (m, over_core(m_other[0])) if fast else (m,)
    a, h2, low, dpre = split_low(a), split_low(h2), shared(low), shared(dpre)

    def attend(group, groups, lse, so_far):
        return attention_backward(
            reach, qkv, d_mixed, mixed, lse, start_row, cos, sin, row_count, wide, group, groups, so_far
        )

    f = w_up.shape[1]
    d_qkv = attend(0, 1, lse, None)
    if fast:
        a = tie(a, d_qkv)
    grads = weight_grads(
        fast, back, [(m_both, gy_both, f // 384, True), (a, low, d // LANES, False), (h2, dpre, f // LANES, False)]
    )
    if fast:
        red = Reduce(*grads)
        first = red.first()
    d_qkv = attend(1, 2, tie(lse, grads[-1]), d_qkv)
    if fast:
        second = red.second(d_qkv)
        dx1 = tie(dx1, first)
    d_both = (d_qkv, over_core(tie(d_qkv, first))) if fast else (d_qkv,)
    grad_tokens, gain_rows = qkv_backward(d_qkv, tokens, dx1, full_qkv, g_attn, gg)
    if fast:
        near = red.near_z(gain_rows)
        h1 = tie(split_low(h1), (gain_rows, second))
        grad_qkv = weight_grads(fast, back, [(h1, d_both, 3 * d // LANES, False)], shared(gain_rows), sizes)
        red_qkv = Reduce(*grad_qkv)
        first = red_qkv.first()
        far = red.far_z(grad_qkv[-1])
        result = down_forward(tie(m, (grad_qkv[-1], near)), x1, full_down)
        second = red_qkv.second((result, far))
        own = red.own()
        red_qkv.near_z()
        red_qkv.far_z()
        g_qkv = red_qkv.own()
        cuts = (w_down.shape[0], w_down.shape[0] + w_out.shape[0])
        own_down, grad_out, grad_up = own[: cuts[0]], own[cuts[0] : cuts[1]], unslab(own[cuts[1] :], f)
        flat = g_qkv[w_qkv.size // LANES]
        g_qkv = g_qkv[: w_qkv.size // LANES]
        summed, at = [], 0
        for size in sizes:
            summed.append(flat[at : at + size])
            at += size
    else:
        grad_qkv = weight_grads(fast, back, [(h1, d_both, 3 * d // LANES, False)])
        result = down_forward(m, x1, full_down)
        own_down, grad_out, grad_up, g_qkv = (scatter(g.astype(BF)).astype(F32) for g in (*grads, *grad_qkv))
        flat = gain_rows[: 3 + f // d]
        summed = [scatter(flat[i]) for i in range(3)] + [scatter(flat[3:].reshape(-1))]
        g_qkv = jnp.concatenate(slab(g_qkv))
    size = w_qkv.shape[0]
    span = LANES // 3
    g_qkv = jnp.concatenate(
        [g_qkv[g * size : (g + 1) * size, p * span : (p + 1) * span] for p in range(3) for g in range(GRAD_GROUPS)], axis=1
    )
    return (result, grad_tokens, g_qkv, grad_out, grad_up, own_down) + tuple(summed)


def solution(mesh):
    matrix, vector = P(AXES, None), P(AXES)
    fast = mesh.shape["dp"] == 4 and mesh.shape["fsdp"] == 2 * Z
    return jax.shard_map(
        functools.partial(local, fast),
        mesh=mesh,
        in_specs=(matrix,) * 7 + (vector,) * 4,
        out_specs=(matrix,) * 6 + (vector,) * 4,
        check_vma=False,
    )
```

```python
import functools
import math

import jax
import jax.numpy as jnp
import numpy as np
from jax import lax
from jax.experimental import pallas as pl
from jax.experimental.pallas import tpu as pltpu
from jax.sharding import PartitionSpec as P

HEADS = 12
HEAD_DIM = 64
PAIR = 2 * HEAD_DIM
PAIRS = HEADS // 2
EPSILON = 1e-05
MASKED_SCORE = -1e30
ROOT_HALF = 0.7071067811865476
INV_ROOT_TAU = 0.3989422804014327
BF = jnp.bfloat16
F32 = jnp.float32
MIB = 1 << 20
AXES = ("dp", "fsdp")
BLOCK = 256
ROWS = 256
LANES = 768
VMEM_MIB = 60
GRAD_GROUPS = 3


def dot(a, b, dims=((1,), (0,))):
    return lax.dot_general(a, b, (dims, ((), ())), preferred_element_type=F32)


def params(mib):
    return pltpu.CompilerParams(vmem_limit_bytes=max(mib, VMEM_MIB) * MIB)


def swap_halves(x):
    lane = lax.broadcasted_iota(jnp.int32, x.shape, 1)
    low = lax.rem(lane, HEAD_DIM) < HEAD_DIM // 2
    half = HEAD_DIM // 2
    return jnp.where(low, pltpu.roll(x, PAIR - half, 1), pltpu.roll(x, half, 1))


def unit_norm(x):
    mean = jnp.mean(x, axis=-1, keepdims=True)
    centred = x - mean
    inv = lax.rsqrt(jnp.mean(centred * centred, axis=-1, keepdims=True) + EPSILON)
    return centred * inv, inv


def norm_back(grad, gain, unit, inv):
    d_unit = grad * gain
    return inv * (
        d_unit
        - jnp.mean(d_unit, axis=-1, keepdims=True)
        - unit * jnp.mean(d_unit * unit, axis=-1, keepdims=True)
    )


def whole(shape):
    return pl.BlockSpec(shape, lambda *_: (0,) * len(shape), pipeline_mode=pl.Buffered(1))


def rows(width, block=ROWS):
    return pl.BlockSpec((block, width), lambda i: (i, 0))


def shaped(shape, dtype):
    return jax.ShapeDtypeStruct(shape, dtype)


def hbm():
    return pl.BlockSpec(memory_space=pl.ANY)


def fetch(order, parts, places, sem):
    if len(parts) < 8 and parts[0].ndim == 2:
        for part, (_, _, buffer, _) in zip(parts, places):
            pltpu.make_async_copy(part, buffer, sem).start()
        return
    count = parts[0].shape[0]
    for p, part in enumerate(parts):
        for b in range(count):
            owner = b if order is None else order[p * count + b]
            for first, size, buffer, column in places:
                row = owner * size if order is None else pl.multiple_of(owner * size, 8)
                pltpu.make_async_copy(
                    part.at[b, pl.ds(first, size), :],
                    buffer.at[pl.ds(row, size), pl.ds(column, LANES)],
                    sem,
                ).start()


def arrive(buffers, sem):
    for buffer in buffers:
        pltpu.make_async_copy(buffer, buffer, sem).wait()


def deal(back, tile, outs, row, size):
    quarter = outs[0].shape[0]
    for q, out in enumerate(outs):

        @pl.loop(0, quarter)
        def _(j):
            block = tile[pl.ds(pl.multiple_of(back[q * quarter + j] * size, 8), size), :]
            out[j, pl.ds(row, size), :] = block.astype(out.dtype)


def slabs(first, size, buffer, width):
    return [(first + s * size, size, buffer, s * LANES) for s in range(width // LANES)]


def pack_kernel(wq_ref, wo_ref, wu_ref, wd_ref, gains_ref, one_ref, two_ref):
    row = 0
    for c in range(wq_ref.shape[1] // LANES):
        one_ref[row : row + wq_ref.shape[0], :] = wq_ref[:, c * LANES : (c + 1) * LANES]
        row += wq_ref.shape[0]
    one_ref[row:, :] = gains_ref[...]
    row = 0
    for ref in (wd_ref, wo_ref, wu_ref):
        for c in range(ref.shape[1] // LANES):
            two_ref[row : row + ref.shape[0], :] = ref[:, c * LANES : (c + 1) * LANES]
            row += ref.shape[0]


def pack(w_qkv, w_out, w_up, w_down, gains):
    first = w_qkv.size // LANES + gains.shape[0]
    second = (w_out.size + w_up.size + w_down.size) // LANES
    return pl.pallas_call(
        pack_kernel, out_shape=[shaped((first, LANES), BF), shaped((second, LANES), BF)], name="pack"
    )(w_qkv, w_out, w_up, w_down, gains)


def spread(rows_in, offset, count, owners):
    lanes = rows_in.shape[1]
    wide = owners * count
    lane = lax.broadcasted_iota(jnp.int32, (lanes, wide), 0)
    column = lax.broadcasted_iota(jnp.int32, (lanes, wide), 1)
    pick = (lane - offset == lax.rem(column, count)).astype(F32).astype(BF)
    full = dot(rows_in, pick)
    owner = lax.broadcasted_iota(jnp.int32, (owners, wide), 0)
    column = lax.broadcasted_iota(jnp.int32, (owners, wide), 1)
    own = (column >= owner * count) & (column < owner * count + count)
    return jnp.sum(jnp.where(own, full, 0.0), axis=0, keepdims=True)


def qkv_kernel(split, sizes, *refs):
    if split:
        order, x_ref, cos_ref, sin_ref, *refs = refs
        parts, refs = refs[:8], refs[8:]
        h_ref, other_ref, qkv_ref, w_ref, ga_ref, gi_ref, gf_ref, gm_ref, gains, sem, gain_sem = refs
        h_refs = (h_ref, other_ref)
    else:
        order, x_ref, cos_ref, sin_ref, ga_ref, *refs = refs
        parts, refs = refs[:1], refs[1:]
        h_ref, qkv_ref, w_ref, sem = refs
        h_refs = (h_ref,)
    width = x_ref.shape[1]
    step = pl.program_id(0)
    if split:
        size = width // 32
        weight = slabs(0, size, w_ref, 3 * width)

        @pl.when(step == 0)
        def _():
            fetch(order, parts, [(3 * size, 8, gains, 0)], gain_sem)
            fetch(order, parts, weight, sem)
            arrive([gains], gain_sem)
            owner = lax.broadcasted_iota(jnp.int32, (32, 256), 0)
            lane = lax.broadcasted_iota(jnp.int32, (32, 256), 1)
            pick = (lane == owner * 8).astype(F32).astype(BF)
            per_owner = dot(pick, gains[:, :256]).astype(BF)
            at = 0
            for ref, count in zip((ga_ref, gi_ref, gf_ref, gm_ref), sizes):
                ref[...] = spread(per_owner, at, count, 32)
                at += count
            arrive([w_ref], sem)
    else:

        @pl.when(step == 0)
        def _():
            fetch(None, parts, [(0, 0, w_ref, 0)], sem)
            arrive([w_ref], sem)

    unit, _ = unit_norm(x_ref[...].astype(F32))
    h = (unit * ga_ref[...]).astype(BF)
    store_low(split, order[32] if split else 0, h, h_refs)
    cos, sin = cos_ref[...], sin_ref[...]
    for part in range(3):
        y = dot(h, w_ref[:, part * width : (part + 1) * width])
        for c in range(width // PAIR):
            z = y[:, c * PAIR : (c + 1) * PAIR]
            if part < 2:
                z = z * cos + swap_halves(z) * sin
            if part == 0:
                z = z * (1.0 / math.sqrt(HEAD_DIM))
            at = part * width + c * PAIR
            qkv_ref[:, at : at + PAIR] = z.astype(BF)


def prefetched(kernel, order, inputs, in_specs, out_specs, out_shape, scratch, grid, mib, name, flops, data):
    return pl.pallas_call(
        kernel,
        grid_spec=pltpu.PrefetchScalarGridSpec(
            num_scalar_prefetch=1,
            grid=grid,
            in_specs=in_specs,
            out_specs=out_specs,
            scratch_shapes=scratch,
        ),
        out_shape=out_shape,
        compiler_params=params(mib),
        cost_estimate=pl.CostEstimate(flops=flops, transcendentals=0, bytes_accessed=data),
        name=name,
    )(order, *inputs)


def rows(width, block=ROWS):
    return pl.BlockSpec((block, width), lambda i, *_: (i, 0))


def whole(shape):
    return pl.BlockSpec(shape, lambda *_: (0,) * len(shape), pipeline_mode=pl.Buffered(1))


def qkv_forward(split, order, tokens, cos, sin, parts, gain, sizes):
    t, d = tokens.shape
    n = 3 * d
    inputs = [tokens, cos, sin]
    in_specs = [rows(d), rows(PAIR), rows(PAIR)]
    out_specs, out_shape = low_specs(split, t, d)
    lows = len(out_specs)
    out_specs = out_specs + [rows(n), whole((d, n))]
    out_shape = out_shape + [shaped((t, n), BF), shaped((d, n), BF)]
    scratch = [pltpu.SemaphoreType.DMA]
    if split:
        widths = [32 * s for s in sizes]
        out_specs += [whole((1, w)) for w in widths]
        out_shape += [shaped((1, w), F32) for w in widths]
        scratch = [pltpu.VMEM((32 * 8, LANES), BF), pltpu.SemaphoreType.DMA, pltpu.SemaphoreType.DMA]
    else:
        inputs.append(gain)
        in_specs.append(whole((1, d)))
    outs = prefetched(
        functools.partial(qkv_kernel, split, sizes), order, inputs + list(parts), in_specs + [hbm()] * len(parts),
        out_specs, out_shape, scratch, (t // ROWS,), 40, "qkv_forward",
        2 * t * d * n, 4 * d * n + 12 * t * d,
    )
    return (outs[:lows], *outs[lows:])


def window(i, n):
    return slice((i - n + 1) * BLOCK, (i + 1) * BLOCK)


def head_masks(shape):
    lane = lax.broadcasted_iota(jnp.int32, shape, 1)
    return lane < HEAD_DIM


def attention_forward_kernel(wide, reach, q_ref, k_ref, v_ref, start_ref, o_ref, lse_ref, bias):
    row, pair = pl.program_id(0), pl.program_id(1)
    seq = q_ref.shape[0]
    blocks = seq // BLOCK

    @pl.when(pair == 0)
    def _():
        for i in range(blocks):
            at = slice(i * BLOCK, (i + 1) * BLOCK)
            shape = (BLOCK, wide * BLOCK)
            key = (i - wide + 1) * BLOCK + lax.broadcasted_iota(jnp.int32, shape, 1)
            query = i * BLOCK + lax.broadcasted_iota(jnp.int32, shape, 0)
            keep = (key >= start_ref[at, :]) & (key <= query)
            bias[at, :] = jnp.where(keep, 0.0, MASKED_SCORE)

    first = head_masks((BLOCK, PAIR))
    for i in range(blocks):
        at = slice(i * BLOCK, (i + 1) * BLOCK)
        most = min(wide, i + 1)
        for n in range(1, most + 1):

            @pl.when(reach[row * blocks + i] == n)
            def _():
                q = q_ref[at, :]
                w = window(i, n)
                k, v = k_ref[w, :], v_ref[w, :]
                b = bias[at, (wide - n) * BLOCK :]
                mask = head_masks(k.shape)
                zero = jnp.zeros_like(k)
                total, lses = None, []
                scale = None
                for h in range(2):
                    pick = mask if h == 0 else jnp.logical_not(mask)
                    s = dot(q, jnp.where(pick, k, zero), ((1,), (1,))) + b
                    top = jnp.max(s, axis=-1, keepdims=True)
                    p = jnp.exp(s - top)
                    den = jnp.sum(p, axis=-1, keepdims=True)
                    probs = (p * (1.0 / den)).astype(BF)
                    part = dot(probs, jnp.where(pick, v, zero))
                    total = part if total is None else total + part
                    lses.append(top + jnp.log(den))
                o_ref[at, :] = total
                both = jnp.where(first, lses[0], lses[1]).T
                lse_ref[0, 0:1, at] = both[0:1, :]
                lse_ref[0, 1:2, at] = both[HEAD_DIM : HEAD_DIM + 1, :]


def attention_forward(reach, qkv, start, row_count, wide):
    t = qkv.shape[0]
    seq = t // row_count
    d = qkv.shape[1] // 3

    def columns(part):
        return pl.BlockSpec((seq, PAIR), lambda r, p, *_: (r, part * PAIRS + p))

    return pl.pallas_call(
        functools.partial(attention_forward_kernel, wide),
        grid_spec=pltpu.PrefetchScalarGridSpec(
            num_scalar_prefetch=1,
            grid=(row_count, PAIRS),
            in_specs=[
                columns(0),
                columns(1),
                columns(2),
                pl.BlockSpec((seq, 1), lambda r, p, *_: (r, 0)),
            ],
            out_specs=[
                pl.BlockSpec((seq, PAIR), lambda r, p, *_: (r, p)),
                pl.BlockSpec((1, 8, seq), lambda r, p, *_: (r * PAIRS + p, 0, 0)),
            ],
            scratch_shapes=[pltpu.VMEM((seq, wide * BLOCK), F32)],
        ),
        out_shape=[shaped((t, d), F32), shaped((row_count * PAIRS, 8, seq), F32)],
        compiler_params=params(32),
        cost_estimate=pl.CostEstimate(
            flops=8 * t * d * BLOCK, transcendentals=t * HEADS * 512, bytes_accessed=12 * t * d
        ),
        name="attention_forward",
    )(reach, qkv, qkv, qkv, start)


def attention_backward_kernel(wide, reach, q_ref, k_ref, v_ref, do_ref, o_ref, lse_ref, start_ref, cos_ref, sin_ref, *refs):
    grad_ref, bias, ks, vs, qs, dos, dk_acc, dv_acc, dq_acc = refs[-9:]
    row, pair = pl.program_id(0), pl.program_id(1)
    seq = q_ref.shape[0]
    blocks = seq // BLOCK

    @pl.when(pair == 0)
    def _():
        for i in range(blocks):
            at = slice(i * BLOCK, (i + 1) * BLOCK)
            shape = (wide * BLOCK, BLOCK)
            key = (i - wide + 1) * BLOCK + lax.broadcasted_iota(jnp.int32, shape, 0)
            query = i * BLOCK + lax.broadcasted_iota(jnp.int32, shape, 1)
            keep = (key >= start_ref[0:1, at]) & (key <= query)
            bias[:, at] = jnp.where(keep, 0.0, MASKED_SCORE)

    mask = head_masks((seq, PAIR))
    for src, dst in ((k_ref, ks), (v_ref, vs), (q_ref, qs), (do_ref, dos)):
        x = src[...]
        zero = jnp.zeros_like(x)
        dst[0] = jnp.where(mask, x, zero)
        dst[1] = jnp.where(mask, zero, x)
    dk_acc[...] = jnp.zeros_like(dk_acc)
    dv_acc[...] = jnp.zeros_like(dv_acc)
    lane8 = lax.broadcasted_iota(jnp.int32, (8, PAIR), 1) // HEAD_DIM
    row8 = lax.broadcasted_iota(jnp.int32, (8, PAIR), 0)
    picks = (lane8 == row8).astype(F32)
    delta = lax.dot_general(
        picks, do_ref[...].astype(F32) * o_ref[...], (((1,), (1,)), ((), ())),
        precision=lax.Precision.HIGHEST, preferred_element_type=F32,
    )
    for i in range(blocks):
        at = slice(i * BLOCK, (i + 1) * BLOCK)
        most = min(wide, i + 1)
        for n in range(1, most + 1):

            @pl.when(reach[row * blocks + i] == n)
            def _():
                w = window(i, n)
                b = bias[(wide - n) * BLOCK :, at]
                q, do = q_ref[at, :], do_ref[at, :]
                ps, dss = [], []
                for h in range(2):
                    s = dot(ks[h, w, :], q, ((1,), (1,))) + b
                    p = jnp.exp(s - lse_ref[0, h : h + 1, at])
                    dp = dot(vs[h, w, :], do, ((1,), (1,)))
                    ds = (p * (dp - delta[h : h + 1, at])).astype(BF)
                    ps.append(p.astype(BF))
                    dss.append(ds)
                dv_acc[w, :] += dot(ps[0], dos[0, at, :]) + dot(ps[1], dos[1, at, :])
                dk_acc[w, :] += dot(dss[0], qs[0, at, :]) + dot(dss[1], qs[1, at, :])
                dq_acc[at, :] = dot(dss[0], ks[0, w, :], ((0,), (0,))) + dot(
                    dss[1], ks[1, w, :], ((0,), (0,))
                )

    cos, sin = cos_ref[...], sin_ref[...]
    dq = dq_acc[...] * (1.0 / math.sqrt(HEAD_DIM))
    dk = dk_acc[...]
    span = grad_ref.shape[2] // 3
    slot = lax.rem(pair, span // PAIR)
    grads = (dq * cos - swap_halves(dq) * sin, dk * cos - swap_halves(dk) * sin, dv_acc[...])
    for part, value in enumerate(grads):
        grad_ref[0, :, pl.ds(pl.multiple_of(part * span + slot * PAIR, PAIR), PAIR)] = value.astype(BF)


def attention_backward(reach, qkv, d_mixed, mixed, lse, start_row, cos, sin, row_count, wide, group, groups, so_far):
    pairs = PAIRS // GRAD_GROUPS
    t = qkv.shape[0]
    seq = t // row_count
    base = group * pairs
    span = 3 * pairs * PAIR

    def columns(part):
        return pl.BlockSpec((seq, PAIR), lambda r, p, *_: (r, part * PAIRS + base + p))

    table = pl.BlockSpec((seq, PAIR), lambda r, p, *_: (r, 0))
    inputs = [reach, qkv, qkv, qkv, d_mixed, mixed, lse, start_row, cos, sin]
    in_specs = [
        columns(0), columns(1), columns(2), columns(0), columns(0),
        pl.BlockSpec((1, 8, seq), lambda r, p, *_: (r * PAIRS + base + p, 0, 0)),
        pl.BlockSpec((8, seq), lambda r, p, *_: (r, 0)),
        table, table,
    ]
    aliases = {}
    if so_far is not None:
        aliases = {len(inputs): 0}
        inputs.append(so_far)
        in_specs.append(hbm())
    return pl.pallas_call(
        functools.partial(attention_backward_kernel, wide),
        grid_spec=pltpu.PrefetchScalarGridSpec(
            num_scalar_prefetch=1,
            grid=(row_count, pairs * groups),
            in_specs=in_specs,
            out_specs=pl.BlockSpec((1, seq, span), lambda r, p, *_: (group + p // pairs, r, 0)),
            scratch_shapes=[
                pltpu.VMEM((wide * BLOCK, seq), F32),
                pltpu.VMEM((2, seq, PAIR), BF),
                pltpu.VMEM((2, seq, PAIR), BF),
                pltpu.VMEM((2, seq, PAIR), BF),
                pltpu.VMEM((2, seq, PAIR), BF),
                pltpu.VMEM((seq, PAIR), F32),
                pltpu.VMEM((seq, PAIR), F32),
                pltpu.VMEM((seq, PAIR), F32),
            ],
        ),
        out_shape=shaped((GRAD_GROUPS, t, span), BF),
        input_output_aliases=aliases,
        compiler_params=params(40),
        cost_estimate=pl.CostEstimate(
            flops=20 * t * span * BLOCK // 3 * groups, transcendentals=t * HEADS * 128 * groups,
            bytes_accessed=20 * t * span // 3 * groups
        ),
        name="attention_backward",
    )(*inputs)


def halves(x):
    quarter = x.shape[1] // 4
    piece = [x[:, i * quarter : (i + 1) * quarter] for i in range(4)]
    return jnp.concatenate(piece[0::2], axis=1), jnp.concatenate(piece[1::2], axis=1)


def store_low(split, core, x, refs):
    if not split:
        refs[0][...] = x
        return
    pair = halves(x)
    for c in range(2):

        @pl.when(core == c)
        def _():
            refs[0][...] = pair[c]
            refs[1][...] = pair[1 - c]


def low_specs(split, t, d):
    if split:
        return [rows(d // 2)] * 2, [shaped((t, d // 2), BF)] * 2
    return [rows(d)], [shaped((t, d), BF)]


def ffn_kernel(split, *refs):
    order, o_ref, x_ref, gy_ref, gi_ref, gf_ref, gm_ref, *refs = refs
    count = 8 if split else 3
    parts, refs = refs[:count], refs[count:]
    a_ref, h2_ref, x1_ref, m_ref, dpre_ref, dx1_ref, low_ref, do_ref, wd_ref, wo_ref, wu_ref, *refs = refs
    theirs_ref, other_ref, *refs = refs if split else (None, None, *refs)
    act, slope, dm, sem, down_sem = refs
    d, f = wu_ref.shape
    size, skip = d // 32, f // 32
    step = pl.program_id(0)
    core = order[32] if split else 0
    chunks = [slice(c, c + LANES) for c in range(0, f, LANES)]

    @pl.when(step == 0)
    def _():
        if split:
            fetch(order, parts, [(skip, size, wo_ref, 0)] + slabs(skip + size, size, wu_ref, f), sem)
            fetch(order, parts, [(0, skip, wd_ref, 0)], down_sem)
        else:
            fetch(order, parts[:2], [(0, 0, wo_ref, 0), (0, 0, wu_ref, 0)], sem)
            fetch(order, parts[2:], [(0, 0, wd_ref, 0)], down_sem)

    mixed = o_ref[...]
    unit_in, inv_in = unit_norm(mixed)
    a = (unit_in * gi_ref[...]).astype(BF)
    store_low(split, core, a, (a_ref, theirs_ref.at[0] if split else None))

    @pl.when(step == 0)
    def _():
        arrive([wo_ref, wu_ref], sem)
        arrive([wd_ref], down_sem)

    x1 = x_ref[...].astype(F32) + dot(a, wo_ref[...])
    x1_ref[...] = x1
    unit_two, inv_two = unit_norm(x1)
    h2 = (unit_two * gf_ref[...]).astype(BF)
    store_low(split, core, h2, (h2_ref, theirs_ref.at[1] if split else None))
    gy = gy_ref[...]
    total = None
    for at in chunks:
        hidden = dot(h2, wu_ref[:, at])
        dm[:, at] = dot(gy, wd_ref[at, :], ((1,), (1,)))
        cdf = 0.5 + 0.5 * lax.erf(hidden * ROOT_HALF)
        slope[:, at] = cdf + hidden * (jnp.exp(-0.5 * hidden * hidden) * INV_ROOT_TAU)
        value = hidden * cdf
        act[:, at] = value
        part = jnp.sum(value, axis=-1, keepdims=True)
        total = part if total is None else total + part
    mean = total * (1.0 / f)
    total = None
    for at in chunks:
        centred = act[:, at] - mean
        part = jnp.sum(centred * centred, axis=-1, keepdims=True)
        total = part if total is None else total + part
    inv = lax.rsqrt(total * (1.0 / f) + EPSILON)
    first = second = None
    for at in chunks:
        gain = gm_ref[:, at]
        unit = (act[:, at] - mean) * inv
        act[:, at] = unit
        m_ref[:, at] = (unit * gain).astype(BF)
        d_unit = dm[:, at] * gain
        dm[:, at] = d_unit
        part = jnp.sum(d_unit, axis=-1, keepdims=True)
        first = part if first is None else first + part
        part = jnp.sum(d_unit * unit, axis=-1, keepdims=True)
        second = part if second is None else second + part
    first, second = first * (1.0 / f), second * (1.0 / f)
    dh2 = None
    for at in chunks:
        d_act = inv * (dm[:, at] - first - act[:, at] * second)
        dpre = (d_act * slope[:, at]).astype(BF)
        dpre_ref[:, at] = dpre
        part = dot(dpre, wu_ref[:, at], ((1,), (1,)))
        dh2 = part if dh2 is None else dh2 + part
    dx1 = gy.astype(F32) + norm_back(dh2, gf_ref[...], unit_two, inv_two)
    dx1_ref[...] = dx1
    low = dx1.astype(BF)
    low_ref[...] = low
    da = dot(low, wo_ref[...], ((1,), (1,)))
    do_ref[...] = norm_back(da, gi_ref[...], unit_in, inv_in).astype(BF)

    if split:
        quarter = f // 4
        for j in range(2):
            at = pl.multiple_of((2 * j + 1 - core) * quarter, PAIR)
            other_ref[:, j * quarter : (j + 1) * quarter] = m_ref[:, pl.ds(at, quarter)]


def ffn_both(split, order, mixed, tokens, gy, gain_inner, gain_ffn, gain_mid, parts):
    t, d = tokens.shape
    f = gain_mid.shape[1]
    width = d // 2 if split else d
    more = [(rows(f // 2), shaped((t, f // 2), BF))] * split
    if split:
        theirs = pl.BlockSpec((2, ROWS, width), lambda i, *_: (0, i, 0))
        more.insert(0, (theirs, shaped((2, t, width), BF)))
    return prefetched(
        functools.partial(ffn_kernel, split), order, [mixed, tokens, gy, gain_inner, gain_ffn, gain_mid, *parts],
        [rows(d), rows(d), rows(d), whole((1, d)), whole((1, d)), whole((1, f))] + [hbm()] * len(parts),
        [rows(width), rows(width), rows(d), rows(f), rows(f), rows(d), rows(d), rows(d), whole((f, d)), whole((d, d)),
         whole((d, f))] + [m[0] for m in more],
        [
            shaped((t, width), BF), shaped((t, width), BF), shaped((t, d), F32), shaped((t, f), BF), shaped((t, f), BF),
            shaped((t, d), F32), shaped((t, d), BF), shaped((t, d), BF), shaped((f, d), BF), shaped((d, d), BF),
            shaped((d, f), BF),
        ] + [m[1] for m in more],
        [
            pltpu.VMEM((ROWS, f), F32), pltpu.VMEM((ROWS, f), F32), pltpu.VMEM((ROWS, f), F32), pltpu.SemaphoreType.DMA,
            pltpu.SemaphoreType.DMA,
        ],
        (t // ROWS,), 60, "ffn_both", 2 * t * d * (2 * d + 3 * f), 6 * d * f + 4 * t * f + 30 * t * d,
    )


def result_kernel(m_ref, x1_ref, wd_ref, y_ref):
    y_ref[...] = (x1_ref[...] + dot(m_ref[...], wd_ref[...])).astype(BF)


def down_forward(m, x1, w_down):
    t, d = x1.shape
    f = m.shape[1]
    return pl.pallas_call(
        result_kernel,
        grid=(t // ROWS,),
        in_specs=[rows(f), rows(d), whole((f, d))],
        out_specs=rows(d),
        out_shape=shaped((t, d), BF),
        compiler_params=params(48),
        cost_estimate=pl.CostEstimate(flops=2 * t * d * f, transcendentals=0, bytes_accessed=2 * d * f + 2 * t * f + 6 * t * d),
        name="down_forward",
    )(m, x1, w_down)


def grads_kernel(split, products, *refs):
    back, *refs = refs
    count = 2 if split else 1
    left, refs = refs[: len(products) * count], refs[len(products) * count :]
    right, refs = refs[: len(products) * count], refs[len(products) * count :]
    outs, refs = refs[: 4 if split else len(products)], refs[4 if split else len(products) :]
    tile, turned = refs[0], refs[1:]
    step = pl.program_id(0)
    first, row = 0, 0
    for n, (by_left, tiles, size) in enumerate(products):
        mine = [left[n * count + c] for c in range(count)]
        value = [right[n * count + c] for c in range(count)]

        if not by_left:

            @pl.when(step == first)
            def _():
                t = mine[0].shape[0]
                for c in range(count):
                    flat = mine[c][...] if len(mine[c].shape) == 2 else mine[c][0]
                    turned[0][:, c * t : (c + 1) * t] = flat.T

        @pl.when((step >= first) & (step < first + tiles))
        def _():
            total = None
            for c in range(count):
                v = value[c][...] if len(value[c].shape) == 2 else value[c][0]
                t = v.shape[0]
                if by_left:
                    part = dot(mine[c][...], v, ((0,), (0,)))
                else:
                    part = dot(turned[0][:, c * t : (c + 1) * t], v)
                total = part if total is None else total + part
            if not split:
                outs[n][...] = total
            else:
                tile[...] = total
                if by_left:
                    owners = tile.shape[0] // size
                    for e in range(owners):
                        at = back[16 + (step - first) * owners + e]
                        for q in range(4):

                            @pl.when(at // 4 == q)
                            def _():
                                block = tile[e * size : (e + 1) * size, :]
                                outs[q][at - 4 * q, row : row + size, :] = block.astype(outs[q].dtype)
                else:
                    deal(back, tile, outs, row + pl.multiple_of((step - first) * size, 8), size)

        first += tiles
        row += size if by_left else tiles * size


def weight_grads(split, back, products):
    count = 2 if split else 1
    t = products[0][0][0].shape[0]
    left_specs, right_specs, lefts, rights, plan = [], [], [], [], []
    out_specs, out_shape = [], []
    at = row = 0
    for left, right, tiles, by_left in products:
        width = 0
        for c in range(count):
            a, b = left[c], right[c]
            a, part = a if isinstance(a, tuple) else (a, None)

            if by_left and c == 0:
                tiles = tiles // count
                width = a.shape[1] // (tiles * count)

            def step(i, at=at, tiles=tiles):
                return jnp.clip(i - at, 0, tiles - 1)

            if by_left:
                per = tiles // 2
                if split and c == 0:
                    left_specs.append(pl.BlockSpec(
                        (t, width), lambda i, back, step=step, per=per: (0, (2 * (step(i) // per) + back[32]) * per + step(i) % per)
                    ))
                else:
                    left_specs.append(pl.BlockSpec((t, width), lambda i, *_, step=step: (0, step(i))))
                right_specs.append(whole(b.shape))
            else:
                width = a.shape[-1]
                if part is None:
                    left_specs.append(whole(a.shape))
                else:
                    left_specs.append(pl.BlockSpec(
                        (1, t, width), lambda *_, part=part: (part, 0, 0), pipeline_mode=pl.Buffered(1)
                    ))
                if b.ndim == 3:
                    right_specs.append(pl.BlockSpec((1, t, LANES), lambda i, *_, step=step: (step(i), 0, 0)))
                else:
                    right_specs.append(pl.BlockSpec((t, LANES), lambda i, *_, step=step: (0, step(i))))
            lefts.append(a)
            rights.append(b)
        size = (width * tiles if by_left else width) // 16
        if not split:
            shape = (width * tiles, LANES) if by_left else (width, tiles * LANES)
            block = (width, LANES)
            out_specs.append(pl.BlockSpec(
                block, (lambda i, *_, step=step: (step(i), 0)) if by_left else (lambda i, *_, step=step: (0, step(i)))
            ))
            out_shape.append(shaped(shape, F32))
        plan.append((by_left, tiles, size))
        at += tiles
        row += size if by_left else tiles * size
    narrow = next(p[0][0].shape[1] for p in products if not p[3])
    if split:
        out_specs = [whole((4, row, LANES))] * 4
        out_shape = [shaped((4, row, LANES), BF)] * 4
    flops = 2 * count * t * narrow * at * LANES
    return prefetched(
        functools.partial(grads_kernel, split, tuple(plan)), back, lefts + rights, left_specs + right_specs,
        out_specs, out_shape, [pltpu.VMEM((narrow, LANES), F32), pltpu.VMEM((narrow, count * t), BF)],
        (at,), 60, "weight_grads", flops, flops // 256,
    )


def qkv_back_kernel(d_ref, x_ref, dx1_ref, w_ref, gain_ref, dx_ref):
    d = x_ref.shape[1]
    groups, _, span = d_ref.shape
    span //= 3
    dh = None
    for part in range(3):
        for g in range(groups):
            at = part * d + g * span
            piece = dot(d_ref[g, :, part * span : (part + 1) * span], w_ref[:, at : at + span], ((1,), (1,)))
            dh = piece if dh is None else dh + piece
    unit, inv = unit_norm(x_ref[...].astype(F32))
    dx_ref[...] = dx1_ref[...] + norm_back(dh, gain_ref[...], unit, inv)


def qkv_backward(d_qkv, tokens, dx1, w_qkv, gain):
    t, d = tokens.shape
    groups, _, span = d_qkv.shape
    return pl.pallas_call(
        qkv_back_kernel,
        grid=(t // ROWS,),
        in_specs=[pl.BlockSpec((groups, ROWS, span), lambda i: (0, i, 0))] + [rows(d)] * 2
        + [whole((d, 3 * d)), whole((1, d))],
        out_specs=rows(d),
        out_shape=shaped((t, d), F32),
        compiler_params=params(48),
        cost_estimate=pl.CostEstimate(flops=6 * t * d * d, transcendentals=0, bytes_accessed=6 * d * d + 16 * t * d),
        name="qkv_backward",
    )(d_qkv, tokens, dx1, w_qkv, gain)


def layout(doc_lengths, seq):
    docs = doc_lengths.shape[-1]
    upto = jnp.arange(docs)[:, None] <= jnp.arange(docs)[None, :]
    ends = jnp.sum(jnp.where(upto[None], doc_lengths[:, :, None], 0), axis=1)
    places = jnp.arange(seq, dtype=jnp.int32)
    passed = places[None, :, None] >= ends[:, None, :]
    start = jnp.sum(jnp.where(passed, doc_lengths[:, None, :], 0), axis=-1)
    valid = places[None, :] < ends[:, docs - 2 : docs - 1]
    return start.astype(jnp.int32), places[None, :] - start, valid


def tables(position):
    half = HEAD_DIM // 2
    lane = jnp.arange(PAIR)
    frequency = jnp.exp((lane % half).astype(F32) * (-2.0 * math.log(10000.0) / HEAD_DIM))
    angles = position.reshape(-1, 1).astype(F32) * frequency[None, :]
    sign = jnp.where(lane % HEAD_DIM < half, -1.0, 1.0)
    return jnp.cos(angles), jnp.sin(angles) * sign[None, :]


Z = 4
GROUPS = ((0, 2), (1, 3))


def index(x, core, z, y):
    return ((x * 2 + core) * Z + z) * 2 + y


def permute(value, move):
    places = [(x, c, z, y) for x in range(2) for c in range(2) for z in range(Z) for y in range(2)]
    return lax.ppermute(value, AXES, [(index(*p), index(*move(*p))) for p in places])


def over_x(v):
    return permute(v, lambda x, c, z, y: (1 - x, c, z, y))


def over_y(v):
    return permute(v, lambda x, c, z, y: (x, c, z, 1 - y))


def over_core(v):
    return permute(v, lambda x, c, z, y: (x, 1 - c, z, y))


def over_z(v, bits):
    return permute(v, lambda x, c, z, y: (x, c, z ^ bits, y))


def place():
    dp, fs = lax.axis_index("dp"), lax.axis_index("fsdp")
    return dp >> 1, dp & 1, fs >> 1, fs & 1


def gather_order():
    rows_of = []
    for core in range(2):
        for group, first in zip(GROUPS, ("x", "y")):
            for second in range(2):
                for one in range(2):
                    dx, dy = (one, second) if first == "x" else (second, one)
                    rows_of += [(dx, core, dz, dy) for dz in group]
    dx, dc, dz, dy = np.array(rows_of, np.int32).T
    x, c, z, y = place()
    order = index(x ^ dx, c ^ dc, z ^ dz, y ^ dy)
    return jnp.concatenate([order, c[None]]).astype(jnp.int32)


def scatter_order():
    rows_of = []
    for group, first in zip(GROUPS, ("y", "x")):
        for one in (1, 0):
            for second in (1, 0):
                dx, dy = (second, one) if first == "y" else (one, second)
                rows_of += [(dx, dz, dy) for dz in group]
    dx, dz, dy = np.array(rows_of, np.int32).T
    x, c, z, y = place()
    order = ((x ^ dx) * Z + (z ^ dz)) * 2 + (y ^ dy)
    spots = jnp.arange(len(rows_of), dtype=jnp.int32)
    where = jnp.sum(jnp.where(order[None, :] == spots[:, None], spots[None, :], 0), axis=1)
    return jnp.concatenate([order, where, c[None]]).astype(jnp.int32)


def tie(value, other):
    return lax.optimization_barrier((value, other))[0]


class Gather:
    def __init__(self, block):
        self.block = block

    def far_z(self, after=None):
        block = self.block if after is None else tie(self.block, after)
        self.even = jnp.stack([block, over_z(block, 2)])
        return self.even

    def near_z(self, after=None):
        if after is not None:
            self.even = tie(self.even, after)
        self.odd = over_z(self.even, 1)
        return self.odd

    def first(self, after=None):
        even, odd = (self.even, self.odd) if after is None else tie((self.even, self.odd), after)
        self.even = jnp.concatenate([even, over_x(even)])
        self.odd = jnp.concatenate([odd, over_y(odd)])
        return [self.even, self.odd]

    def second(self, after=None):
        even, odd = (self.even, self.odd) if after is None else tie((self.even, self.odd), after)
        self.near = [even, odd, over_core(even), over_core(odd)]
        self.far = [over_y(even), over_x(odd)]
        return self.far

    def core(self, after=None):
        far = self.far if after is None else tie(self.far, after)
        even, odd, even_core, odd_core = self.near
        return [even, far[0], odd, far[1], even_core, over_core(far[0]), odd_core, over_core(far[1])]


class Reduce:
    def __init__(self, send_a, keep_a, send_b, keep_b):
        self.sends, self.a, self.b = (send_a, send_b), keep_a.astype(F32), keep_b.astype(F32)

    def first(self, after=None):
        sends = self.sends if after is None else tie(self.sends, after)
        self.got = (over_y(sends[0]), over_x(sends[1]))
        return self.got

    def wait_for(self, after):
        if after is not None:
            self.got = tie(self.got, after)

    def second(self, after=None):
        self.wait_for(after)
        self.a = self.a + self.got[0].astype(F32)
        self.b = self.b + self.got[1].astype(F32)
        self.got = (over_x(self.a[:2].astype(BF)), over_y(self.b[:2].astype(BF)))
        return self.got

    def near_z(self, after=None):
        self.wait_for(after)
        self.a = self.a[2:] + self.got[0].astype(F32)
        self.got = over_z((self.b[2:] + self.got[1].astype(F32)).astype(BF), 1)
        return self.got

    def far_z(self, after=None):
        self.wait_for(after)
        self.a = self.a + self.got.astype(F32)
        self.got = over_z(self.a[1].astype(BF), 2)
        return self.got

    def own(self):
        return self.a[0] + self.got.astype(F32)


def unslab(block, width):
    size = block.shape[0] * LANES // width
    return jnp.concatenate([block[s * size : (s + 1) * size] for s in range(width // LANES)], axis=1)


def slab(block):
    return [block[:, s * LANES : (s + 1) * LANES] for s in range(block.shape[1] // LANES)]


def local(fast, tokens, doc_lengths, cotangent, w_qkv, w_out, w_up, w_down,
          gain_attn, gain_inner, gain_ffn, gain_mid):
    row_count = doc_lengths.shape[0]
    seq = tokens.shape[0] // row_count
    d, f = tokens.shape[1], w_up.shape[1]
    wide = min(seq, 512) // BLOCK + 1
    blocks = seq // BLOCK
    shards = (gain_attn, gain_inner, gain_ffn, gain_mid)
    sizes = [g.shape[0] for g in shards]

    start, position, valid = layout(doc_lengths, seq)
    cos, sin = tables(position)
    firsts = start[:, ::BLOCK] // BLOCK
    reach = (jnp.arange(blocks, dtype=jnp.int32)[None, :] - firsts + 1).reshape(-1)
    start_col = start.reshape(-1, 1)
    start_row = jnp.repeat(start, 8, axis=0)
    gy = jnp.where(valid.reshape(-1, 1), cotangent, jnp.zeros_like(cotangent))

    def scatter(g):
        return lax.psum_scatter(g, AXES, scatter_dimension=0, tiled=True)

    def gather(v):
        return lax.all_gather(v, AXES, axis=0, tiled=True)

    if fast:
        order, back = gather_order(), scatter_order()
        gains_row = jnp.pad(jnp.concatenate(shards)[None], ((0, 7), (0, LANES - sum(sizes))))
        one, two = (Gather(b) for b in pack(w_qkv, w_out, w_up, w_down, gains_row))
        seen = one.far_z()
        two.far_z(seen)
        one.near_z()
        one.first()
        far = one.second(two.even)
        two.near_z()
        two.first(far)
        parts_qkv = one.core()
        gy_both = (gy, over_core(gy))
        cos, sin = tie((cos, sin), (gy, start_col, start_row, reach, order, back))
        gains = [None]
    else:
        order = back = jnp.zeros((8,), jnp.int32)
        parts_qkv, parts_up, parts_down = [gather(w_qkv)], [gather(w_out), gather(w_up)], [gather(w_down)]
        gains = [gather(g).astype(F32).reshape(1, -1) for g in shards]

    h1, qkv, full_qkv, *rest = qkv_forward(fast, order, tokens, cos, sin, parts_qkv, gains[0], sizes)
    g_attn, g_inner, g_ffn, g_mid = rest if fast else gains
    if fast:
        two.second(g_attn)
        start_col = tie(start_col, gy_both[1])
    mixed, lse = attention_forward(reach, qkv, start_col, row_count, wide)
    parts = two.core(lse) if fast else parts_up + parts_down
    a, h2, x1, m, dpre, dx1, low, d_mixed, full_down, _, _, *other = ffn_both(
        fast, order, mixed, tokens, gy, g_inner, g_ffn, g_mid, parts
    )

    def shared(value):
        return (value, over_core(value)) if fast else (value,)

    if fast:
        m_both = (m, over_core(other[1]))
        theirs = over_core(other[0])
        a_both, h2_both = (a, (theirs, 0)), (h2, (theirs, 1))
    else:
        gy_both, m_both, a_both, h2_both = (gy,), (m,), (a,), (h2,)
    low, dpre = shared(low), shared(dpre)

    def attend(group, groups, lse, so_far):
        return attention_backward(
            reach, qkv, d_mixed, mixed, lse, start_row, cos, sin, row_count, wide, group, groups, so_far
        )

    f = w_up.shape[1]
    d_qkv = attend(0, 1, lse, None)
    if fast:
        low = tie(low, d_qkv)
    grads = weight_grads(
        fast, back,
        [(m_both, gy_both, f // 384, True), (a_both, low, d // LANES, False), (h2_both, dpre, f // LANES, False)],
    )
    if fast:
        red = Reduce(*grads)
        first = red.first()
        h1 = tie(h1, grads[-1])
    d_qkv = attend(1, 2, tie(lse, grads[-1]), d_qkv)
    if fast:
        h1 = (h1[0], over_core(h1[1]))
        d_both = (d_qkv, over_core(tie(d_qkv, (first, h1[1]))))
        second = red.second(d_qkv)
        dx1 = tie(dx1, (d_qkv, first))
    else:
        d_both = (d_qkv,)
    grad_tokens = qkv_backward(d_qkv, tokens, dx1, full_qkv, g_attn)
    if fast:
        near = red.near_z(grad_tokens)
        h1 = tie(h1, (grad_tokens, second))
    grad_qkv = weight_grads(fast, back, [(h1, d_both, 3 * d // LANES, False)])
    if fast:
        red_qkv = Reduce(*grad_qkv)
        first = red_qkv.first()
        far = red.far_z(grad_qkv[-1])
        m = tie(m, (grad_qkv[-1], near))
    result = down_forward(m, x1, full_down)
    if fast:
        red_qkv.second((result, far))
        own = red.own()
        red_qkv.near_z()
        red_qkv.far_z()
        g_qkv = red_qkv.own()
        cuts = (w_down.shape[0], w_down.shape[0] + w_out.shape[0])
        own_down, grad_out, grad_up = own[: cuts[0]], own[cuts[0] : cuts[1]], unslab(own[cuts[1] :], f)
    else:
        own_down, grad_out, grad_up, g_qkv = (scatter(g.astype(BF)).astype(F32) for g in (*grads, *grad_qkv))
        g_qkv = jnp.concatenate(slab(g_qkv))
    size = w_qkv.shape[0]
    span = LANES // 3
    g_qkv = jnp.concatenate(
        [g_qkv[g * size : (g + 1) * size, p * span : (p + 1) * span] for p in range(3) for g in range(GRAD_GROUPS)], axis=1
    )
    pairs = ((g_qkv, w_qkv), (grad_out, w_out), (grad_up, w_up), (own_down, w_down))
    gain_grads = [jnp.sum(g * w.astype(F32), axis=1) / v.astype(F32) for (g, w), v in zip(pairs, shards)]
    return (result, grad_tokens, g_qkv, grad_out, grad_up, own_down, *gain_grads)


def solution(mesh):
    matrix, vector = P(AXES, None), P(AXES)
    fast = mesh.shape["dp"] == 4 and mesh.shape["fsdp"] == 2 * Z
    return jax.shard_map(
        functools.partial(local, fast),
        mesh=mesh,
        in_specs=(matrix,) * 7 + (vector,) * 4,
        out_specs=(matrix,) * 6 + (vector,) * 4,
        check_vma=False,
    )
```

```python
import functools
import math

import jax
import jax.numpy as jnp
import numpy as np
from jax import lax
from jax.experimental import pallas as pl
from jax.experimental.pallas import tpu as pltpu
from jax.sharding import PartitionSpec as P

HEADS = 12
HEAD_DIM = 64
PAIR = 2 * HEAD_DIM
PAIRS = HEADS // 2
EPSILON = 1e-05
MASKED_SCORE = -1e30
ROOT_HALF = 0.7071067811865476
INV_ROOT_TAU = 0.3989422804014327
BF = jnp.bfloat16
F32 = jnp.float32
MIB = 1 << 20
AXES = ("dp", "fsdp")
BLOCK = 256
ROWS = 256
LANES = 768
VMEM_MIB = 60
GRAD_GROUPS = 3


def dot(a, b, dims=((1,), (0,))):
    return lax.dot_general(a, b, (dims, ((), ())), preferred_element_type=F32)


def params(mib):
    return pltpu.CompilerParams(vmem_limit_bytes=max(mib, VMEM_MIB) * MIB)


def swap_halves(x):
    lane = lax.broadcasted_iota(jnp.int32, x.shape, 1)
    low = lax.rem(lane, HEAD_DIM) < HEAD_DIM // 2
    half = HEAD_DIM // 2
    return jnp.where(low, pltpu.roll(x, PAIR - half, 1), pltpu.roll(x, half, 1))


def unit_norm(x):
    mean = jnp.mean(x, axis=-1, keepdims=True)
    centred = x - mean
    inv = lax.rsqrt(jnp.mean(centred * centred, axis=-1, keepdims=True) + EPSILON)
    return centred * inv, inv


def norm_back(grad, gain, unit, inv):
    d_unit = grad * gain
    return inv * (
        d_unit
        - jnp.mean(d_unit, axis=-1, keepdims=True)
        - unit * jnp.mean(d_unit * unit, axis=-1, keepdims=True)
    )


def whole(shape):
    return pl.BlockSpec(shape, lambda *_: (0,) * len(shape), pipeline_mode=pl.Buffered(1))


def rows(width, block=ROWS):
    return pl.BlockSpec((block, width), lambda i: (i, 0))


def shaped(shape, dtype):
    return jax.ShapeDtypeStruct(shape, dtype)


def hbm():
    return pl.BlockSpec(memory_space=pl.ANY)


def fetch(order, parts, places, sem):
    if len(parts) < 8 and parts[0].ndim == 2:
        for part, (_, _, buffer, _) in zip(parts, places):
            pltpu.make_async_copy(part, buffer, sem).start()
        return
    count = parts[0].shape[0]
    for p, part in enumerate(parts):
        for b in range(count):
            owner = b if order is None else order[p * count + b]
            for first, size, buffer, column in places:
                row = owner * size if order is None else pl.multiple_of(owner * size, 8)
                pltpu.make_async_copy(
                    part.at[b, pl.ds(first, size), :],
                    buffer.at[pl.ds(row, size), pl.ds(column, LANES)],
                    sem,
                ).start()


def arrive(buffers, sem):
    for buffer in buffers:
        pltpu.make_async_copy(buffer, buffer, sem).wait()


def deal(back, tile, outs, row, size):
    quarter = outs[0].shape[0]
    for q, out in enumerate(outs):

        @pl.loop(0, quarter)
        def _(j):
            block = tile[pl.ds(pl.multiple_of(back[q * quarter + j] * size, 8), size), :]
            out[j, pl.ds(row, size), :] = block.astype(out.dtype)


def slabs(first, size, buffer, width):
    return [(first + s * size, size, buffer, s * LANES) for s in range(width // LANES)]


def pack_kernel(wq_ref, wo_ref, wu_ref, gains_ref, one_ref, two_ref):
    row = 0
    for c in range(wq_ref.shape[1] // LANES):
        one_ref[row : row + wq_ref.shape[0], :] = wq_ref[:, c * LANES : (c + 1) * LANES]
        row += wq_ref.shape[0]
    one_ref[row:, :] = gains_ref[...]
    row = 0
    for ref in (wo_ref, wu_ref):
        for c in range(ref.shape[1] // LANES):
            two_ref[row : row + ref.shape[0], :] = ref[:, c * LANES : (c + 1) * LANES]
            row += ref.shape[0]


def pack(w_qkv, w_out, w_up, gains):
    first = w_qkv.size // LANES + gains.shape[0]
    second = (w_out.size + w_up.size) // LANES
    return pl.pallas_call(
        pack_kernel, out_shape=[shaped((first, LANES), BF), shaped((second, LANES), BF)], name="pack"
    )(w_qkv, w_out, w_up, gains)


def spread(rows_in, offset, count, owners):
    lanes = rows_in.shape[1]
    wide = owners * count
    lane = lax.broadcasted_iota(jnp.int32, (lanes, wide), 0)
    column = lax.broadcasted_iota(jnp.int32, (lanes, wide), 1)
    pick = (lane - offset == lax.rem(column, count)).astype(F32).astype(BF)
    full = dot(rows_in, pick)
    owner = lax.broadcasted_iota(jnp.int32, (owners, wide), 0)
    column = lax.broadcasted_iota(jnp.int32, (owners, wide), 1)
    own = (column >= owner * count) & (column < owner * count + count)
    return jnp.sum(jnp.where(own, full, 0.0), axis=0, keepdims=True)


def qkv_kernel(split, sizes, *refs):
    if split:
        order, x_ref, cos_ref, sin_ref, *refs = refs
        parts, refs = refs[:8], refs[8:]
        h_ref, other_ref, qkv_ref, w_ref, ga_ref, gi_ref, gf_ref, gm_ref, gains, sem, gain_sem = refs
        h_refs = (h_ref, other_ref)
    else:
        order, x_ref, cos_ref, sin_ref, ga_ref, *refs = refs
        parts, refs = refs[:1], refs[1:]
        h_ref, qkv_ref, w_ref, sem = refs
        h_refs = (h_ref,)
    width = x_ref.shape[1]
    step = pl.program_id(0)
    if split:
        size = width // 32
        weight = slabs(0, size, w_ref, 3 * width)

        @pl.when(step == 0)
        def _():
            fetch(order, parts, [(3 * size, 8, gains, 0)], gain_sem)
            fetch(order, parts, weight, sem)
            arrive([gains], gain_sem)
            owner = lax.broadcasted_iota(jnp.int32, (32, 256), 0)
            lane = lax.broadcasted_iota(jnp.int32, (32, 256), 1)
            pick = (lane == owner * 8).astype(F32).astype(BF)
            per_owner = dot(pick, gains[:, :256]).astype(BF)
            at = 0
            for ref, count in zip((ga_ref, gi_ref, gf_ref, gm_ref), sizes):
                ref[...] = spread(per_owner, at, count, 32)
                at += count
            arrive([w_ref], sem)
    else:

        @pl.when(step == 0)
        def _():
            fetch(None, parts, [(0, 0, w_ref, 0)], sem)
            arrive([w_ref], sem)

    unit, _ = unit_norm(x_ref[...].astype(F32))
    h = (unit * ga_ref[...]).astype(BF)
    store_low(split, order[32] if split else 0, h, h_refs)
    cos, sin = cos_ref[...], sin_ref[...]
    for part in range(3):
        y = dot(h, w_ref[:, part * width : (part + 1) * width])
        for c in range(width // PAIR):
            z = y[:, c * PAIR : (c + 1) * PAIR]
            if part < 2:
                z = z * cos + swap_halves(z) * sin
            if part == 0:
                z = z * (1.0 / math.sqrt(HEAD_DIM))
            at = part * width + c * PAIR
            qkv_ref[:, at : at + PAIR] = z.astype(BF)


def prefetched(kernel, order, inputs, in_specs, out_specs, out_shape, scratch, grid, mib, name, flops, data):
    return pl.pallas_call(
        kernel,
        grid_spec=pltpu.PrefetchScalarGridSpec(
            num_scalar_prefetch=1,
            grid=grid,
            in_specs=in_specs,
            out_specs=out_specs,
            scratch_shapes=scratch,
        ),
        out_shape=out_shape,
        compiler_params=params(mib),
        cost_estimate=pl.CostEstimate(flops=flops, transcendentals=0, bytes_accessed=data),
        name=name,
    )(order, *inputs)


def rows(width, block=ROWS):
    return pl.BlockSpec((block, width), lambda i, *_: (i, 0))


def whole(shape):
    return pl.BlockSpec(shape, lambda *_: (0,) * len(shape), pipeline_mode=pl.Buffered(1))


def qkv_forward(split, order, tokens, cos, sin, parts, gain, sizes):
    t, d = tokens.shape
    n = 3 * d
    inputs = [tokens, cos, sin]
    in_specs = [rows(d), rows(PAIR), rows(PAIR)]
    out_specs, out_shape = low_specs(split, t, d)
    lows = len(out_specs)
    out_specs = out_specs + [rows(n), whole((d, n))]
    out_shape = out_shape + [shaped((t, n), BF), shaped((d, n), BF)]
    scratch = [pltpu.SemaphoreType.DMA]
    if split:
        widths = [32 * s for s in sizes]
        out_specs += [whole((1, w)) for w in widths]
        out_shape += [shaped((1, w), F32) for w in widths]
        scratch = [pltpu.VMEM((32 * 8, LANES), BF), pltpu.SemaphoreType.DMA, pltpu.SemaphoreType.DMA]
    else:
        inputs.append(gain)
        in_specs.append(whole((1, d)))
    outs = prefetched(
        functools.partial(qkv_kernel, split, sizes), order, inputs + list(parts), in_specs + [hbm()] * len(parts),
        out_specs, out_shape, scratch, (t // ROWS,), 40, "qkv_forward",
        2 * t * d * n, 4 * d * n + 12 * t * d,
    )
    return (outs[:lows], *outs[lows:])


def window(i, n):
    return slice((i - n + 1) * BLOCK, (i + 1) * BLOCK)


def head_masks(shape):
    lane = lax.broadcasted_iota(jnp.int32, shape, 1)
    return lane < HEAD_DIM


def attention_forward_kernel(wide, reach, q_ref, k_ref, v_ref, start_ref, o_ref, lse_ref, bias):
    row, pair = pl.program_id(0), pl.program_id(1)
    seq = q_ref.shape[0]
    blocks = seq // BLOCK

    @pl.when(pair == 0)
    def _():
        for i in range(blocks):
            at = slice(i * BLOCK, (i + 1) * BLOCK)
            shape = (BLOCK, wide * BLOCK)
            key = (i - wide + 1) * BLOCK + lax.broadcasted_iota(jnp.int32, shape, 1)
            query = i * BLOCK + lax.broadcasted_iota(jnp.int32, shape, 0)
            keep = (key >= start_ref[at, :]) & (key <= query)
            bias[at, :] = jnp.where(keep, 0.0, MASKED_SCORE)

    first = head_masks((BLOCK, PAIR))
    for i in range(blocks):
        at = slice(i * BLOCK, (i + 1) * BLOCK)
        most = min(wide, i + 1)
        for n in range(1, most + 1):

            @pl.when(reach[row * blocks + i] == n)
            def _():
                q = q_ref[at, :]
                w = window(i, n)
                k, v = k_ref[w, :], v_ref[w, :]
                b = bias[at, (wide - n) * BLOCK :]
                mask = head_masks(k.shape)
                zero = jnp.zeros_like(k)
                total, lses = None, []
                scale = None
                for h in range(2):
                    pick = mask if h == 0 else jnp.logical_not(mask)
                    s = dot(q, jnp.where(pick, k, zero), ((1,), (1,))) + b
                    top = jnp.max(s, axis=-1, keepdims=True)
                    p = jnp.exp(s - top)
                    den = jnp.sum(p, axis=-1, keepdims=True)
                    probs = (p * (1.0 / den)).astype(BF)
                    part = dot(probs, jnp.where(pick, v, zero))
                    total = part if total is None else total + part
                    lses.append(top + jnp.log(den))
                o_ref[at, :] = total
                both = jnp.where(first, lses[0], lses[1]).T
                lse_ref[0, 0:1, at] = both[0:1, :]
                lse_ref[0, 1:2, at] = both[HEAD_DIM : HEAD_DIM + 1, :]


def attention_forward(reach, qkv, start, row_count, wide):
    t = qkv.shape[0]
    seq = t // row_count
    d = qkv.shape[1] // 3

    def columns(part):
        return pl.BlockSpec((seq, PAIR), lambda r, p, *_: (r, part * PAIRS + p))

    return pl.pallas_call(
        functools.partial(attention_forward_kernel, wide),
        grid_spec=pltpu.PrefetchScalarGridSpec(
            num_scalar_prefetch=1,
            grid=(row_count, PAIRS),
            in_specs=[
                columns(0),
                columns(1),
                columns(2),
                pl.BlockSpec((seq, 1), lambda r, p, *_: (r, 0)),
            ],
            out_specs=[
                pl.BlockSpec((seq, PAIR), lambda r, p, *_: (r, p)),
                pl.BlockSpec((1, 8, seq), lambda r, p, *_: (r * PAIRS + p, 0, 0)),
            ],
            scratch_shapes=[pltpu.VMEM((seq, wide * BLOCK), F32)],
        ),
        out_shape=[shaped((t, d), F32), shaped((row_count * PAIRS, 8, seq), F32)],
        compiler_params=params(32),
        cost_estimate=pl.CostEstimate(
            flops=8 * t * d * BLOCK, transcendentals=t * HEADS * 512, bytes_accessed=12 * t * d
        ),
        name="attention_forward",
    )(reach, qkv, qkv, qkv, start)


def attention_backward_kernel(wide, reach, q_ref, k_ref, v_ref, do_ref, o_ref, lse_ref, start_ref, cos_ref, sin_ref, *refs):
    grad_ref, bias, ks, vs, qs, dos, dk_acc, dv_acc, dq_acc = refs[-9:]
    row, pair = pl.program_id(0), pl.program_id(1)
    seq = q_ref.shape[0]
    blocks = seq // BLOCK

    @pl.when(pair == 0)
    def _():
        for i in range(blocks):
            at = slice(i * BLOCK, (i + 1) * BLOCK)
            shape = (wide * BLOCK, BLOCK)
            key = (i - wide + 1) * BLOCK + lax.broadcasted_iota(jnp.int32, shape, 0)
            query = i * BLOCK + lax.broadcasted_iota(jnp.int32, shape, 1)
            keep = (key >= start_ref[0:1, at]) & (key <= query)
            bias[:, at] = jnp.where(keep, 0.0, MASKED_SCORE)

    mask = head_masks((seq, PAIR))
    for src, dst in ((k_ref, ks), (v_ref, vs), (q_ref, qs), (do_ref, dos)):
        x = src[...]
        zero = jnp.zeros_like(x)
        dst[0] = jnp.where(mask, x, zero)
        dst[1] = jnp.where(mask, zero, x)
    dk_acc[...] = jnp.zeros_like(dk_acc)
    dv_acc[...] = jnp.zeros_like(dv_acc)
    lane8 = lax.broadcasted_iota(jnp.int32, (8, PAIR), 1) // HEAD_DIM
    row8 = lax.broadcasted_iota(jnp.int32, (8, PAIR), 0)
    picks = (lane8 == row8).astype(F32)
    delta = lax.dot_general(
        picks, do_ref[...].astype(F32) * o_ref[...], (((1,), (1,)), ((), ())),
        precision=lax.Precision.HIGHEST, preferred_element_type=F32,
    )
    for i in range(blocks):
        at = slice(i * BLOCK, (i + 1) * BLOCK)
        most = min(wide, i + 1)
        for n in range(1, most + 1):

            @pl.when(reach[row * blocks + i] == n)
            def _():
                w = window(i, n)
                b = bias[(wide - n) * BLOCK :, at]
                q, do = q_ref[at, :], do_ref[at, :]
                ps, dss = [], []
                for h in range(2):
                    s = dot(ks[h, w, :], q, ((1,), (1,))) + b
                    p = jnp.exp(s - lse_ref[0, h : h + 1, at])
                    dp = dot(vs[h, w, :], do, ((1,), (1,)))
                    ds = (p * (dp - delta[h : h + 1, at])).astype(BF)
                    ps.append(p.astype(BF))
                    dss.append(ds)
                dv_acc[w, :] += dot(ps[0], dos[0, at, :]) + dot(ps[1], dos[1, at, :])
                dk_acc[w, :] += dot(dss[0], qs[0, at, :]) + dot(dss[1], qs[1, at, :])
                dq_acc[at, :] = dot(dss[0], ks[0, w, :], ((0,), (0,))) + dot(
                    dss[1], ks[1, w, :], ((0,), (0,))
                )

    cos, sin = cos_ref[...], sin_ref[...]
    dq = dq_acc[...] * (1.0 / math.sqrt(HEAD_DIM))
    dk = dk_acc[...]
    span = grad_ref.shape[2] // 3
    slot = lax.rem(pair, span // PAIR)
    grads = (dq * cos - swap_halves(dq) * sin, dk * cos - swap_halves(dk) * sin, dv_acc[...])
    for part, value in enumerate(grads):
        grad_ref[0, :, pl.ds(pl.multiple_of(part * span + slot * PAIR, PAIR), PAIR)] = value.astype(BF)


def attention_backward(reach, qkv, d_mixed, mixed, lse, start_row, cos, sin, row_count, wide, group, groups, so_far):
    pairs = PAIRS // GRAD_GROUPS
    t = qkv.shape[0]
    seq = t // row_count
    base = group * pairs
    span = 3 * pairs * PAIR

    def columns(part):
        return pl.BlockSpec((seq, PAIR), lambda r, p, *_: (r, part * PAIRS + base + p))

    table = pl.BlockSpec((seq, PAIR), lambda r, p, *_: (r, 0))
    inputs = [reach, qkv, qkv, qkv, d_mixed, mixed, lse, start_row, cos, sin]
    in_specs = [
        columns(0), columns(1), columns(2), columns(0), columns(0),
        pl.BlockSpec((1, 8, seq), lambda r, p, *_: (r * PAIRS + base + p, 0, 0)),
        pl.BlockSpec((8, seq), lambda r, p, *_: (r, 0)),
        table, table,
    ]
    aliases = {}
    if so_far is not None:
        aliases = {len(inputs): 0}
        inputs.append(so_far)
        in_specs.append(hbm())
    return pl.pallas_call(
        functools.partial(attention_backward_kernel, wide),
        grid_spec=pltpu.PrefetchScalarGridSpec(
            num_scalar_prefetch=1,
            grid=(row_count, pairs * groups),
            in_specs=in_specs,
            out_specs=pl.BlockSpec((1, seq, span), lambda r, p, *_: (group + p // pairs, r, 0)),
            scratch_shapes=[
                pltpu.VMEM((wide * BLOCK, seq), F32),
                pltpu.VMEM((2, seq, PAIR), BF),
                pltpu.VMEM((2, seq, PAIR), BF),
                pltpu.VMEM((2, seq, PAIR), BF),
                pltpu.VMEM((2, seq, PAIR), BF),
                pltpu.VMEM((seq, PAIR), F32),
                pltpu.VMEM((seq, PAIR), F32),
                pltpu.VMEM((seq, PAIR), F32),
            ],
        ),
        out_shape=shaped((GRAD_GROUPS, t, span), BF),
        input_output_aliases=aliases,
        compiler_params=params(40),
        cost_estimate=pl.CostEstimate(
            flops=20 * t * span * BLOCK // 3 * groups, transcendentals=t * HEADS * 128 * groups,
            bytes_accessed=20 * t * span // 3 * groups
        ),
        name="attention_backward",
    )(*inputs)


def halves(x):
    quarter = x.shape[1] // 4
    piece = [x[:, i * quarter : (i + 1) * quarter] for i in range(4)]
    return jnp.concatenate(piece[0::2], axis=1), jnp.concatenate(piece[1::2], axis=1)


def store_low(split, core, x, refs):
    if not split:
        refs[0][...] = x
        return
    pair = halves(x)
    for c in range(2):

        @pl.when(core == c)
        def _():
            refs[0][...] = pair[c]
            refs[1][...] = pair[1 - c]


def low_specs(split, t, d):
    if split:
        return [rows(d // 2)] * 2, [shaped((t, d // 2), BF)] * 2
    return [rows(d)], [shaped((t, d), BF)]


def ffn_kernel(split, *refs):
    order, o_ref, x_ref, gy_ref, gi_ref, gf_ref, gm_ref, *refs = refs
    count = 9 if split else 3
    parts, refs = refs[:count], refs[count:]
    a_ref, h2_ref, x1_ref, m_ref, dpre_ref, dx1_ref, low_ref, do_ref, wd_ref, wo_ref, wu_ref, *refs = refs
    theirs_ref, other_ref, *refs = refs if split else (None, None, *refs)
    act, slope, dm, sem, down_sem = refs
    d, f = wu_ref.shape
    size = d // 32
    step = pl.program_id(0)
    core = order[32] if split else 0
    chunks = [slice(c, c + LANES) for c in range(0, f, LANES)]

    @pl.when(step == 0)
    def _():
        if split:
            fetch(order, parts[:8], [(0, size, wo_ref, 0)] + slabs(size, size, wu_ref, f), sem)
            fetch(None, parts[8:], [(0, 0, wd_ref, 0)], down_sem)
        else:
            fetch(order, parts[:2], [(0, 0, wo_ref, 0), (0, 0, wu_ref, 0)], sem)
            fetch(order, parts[2:], [(0, 0, wd_ref, 0)], down_sem)

    mixed = o_ref[...]
    unit_in, inv_in = unit_norm(mixed)
    a = (unit_in * gi_ref[...]).astype(BF)
    store_low(split, core, a, (a_ref, theirs_ref.at[0] if split else None))

    @pl.when(step == 0)
    def _():
        arrive([wo_ref, wu_ref], sem)
        arrive([wd_ref], down_sem)

    x1 = x_ref[...].astype(F32) + dot(a, wo_ref[...])
    x1_ref[...] = x1
    unit_two, inv_two = unit_norm(x1)
    h2 = (unit_two * gf_ref[...]).astype(BF)
    store_low(split, core, h2, (h2_ref, theirs_ref.at[1] if split else None))
    gy = gy_ref[...]
    total = None
    for at in chunks:
        hidden = dot(h2, wu_ref[:, at])
        dm[:, at] = dot(gy, wd_ref[at, :], ((1,), (1,)))
        cdf = 0.5 + 0.5 * lax.erf(hidden * ROOT_HALF)
        slope[:, at] = cdf + hidden * (jnp.exp(-0.5 * hidden * hidden) * INV_ROOT_TAU)
        value = hidden * cdf
        act[:, at] = value
        part = jnp.sum(value, axis=-1, keepdims=True)
        total = part if total is None else total + part
    mean = total * (1.0 / f)
    total = None
    for at in chunks:
        centred = act[:, at] - mean
        part = jnp.sum(centred * centred, axis=-1, keepdims=True)
        total = part if total is None else total + part
    inv = lax.rsqrt(total * (1.0 / f) + EPSILON)
    first = second = None
    for at in chunks:
        gain = gm_ref[:, at]
        unit = (act[:, at] - mean) * inv
        act[:, at] = unit
        m_ref[:, at] = (unit * gain).astype(BF)
        d_unit = dm[:, at] * gain
        dm[:, at] = d_unit
        part = jnp.sum(d_unit, axis=-1, keepdims=True)
        first = part if first is None else first + part
        part = jnp.sum(d_unit * unit, axis=-1, keepdims=True)
        second = part if second is None else second + part
    first, second = first * (1.0 / f), second * (1.0 / f)
    dh2 = None
    for at in chunks:
        d_act = inv * (dm[:, at] - first - act[:, at] * second)
        dpre = (d_act * slope[:, at]).astype(BF)
        dpre_ref[:, at] = dpre
        part = dot(dpre, wu_ref[:, at], ((1,), (1,)))
        dh2 = part if dh2 is None else dh2 + part
    dx1 = gy.astype(F32) + norm_back(dh2, gf_ref[...], unit_two, inv_two)
    dx1_ref[...] = dx1
    low = dx1.astype(BF)
    low_ref[...] = low
    da = dot(low, wo_ref[...], ((1,), (1,)))
    do_ref[...] = norm_back(da, gi_ref[...], unit_in, inv_in).astype(BF)

    if split:
        quarter = f // 4
        for j in range(2):
            at = pl.multiple_of((2 * j + 1 - core) * quarter, PAIR)
            other_ref[:, j * quarter : (j + 1) * quarter] = m_ref[:, pl.ds(at, quarter)]


def ffn_both(split, order, mixed, tokens, gy, gain_inner, gain_ffn, gain_mid, parts):
    t, d = tokens.shape
    f = gain_mid.shape[1]
    width = d // 2 if split else d
    more = [(rows(f // 2), shaped((t, f // 2), BF))] * split
    if split:
        theirs = pl.BlockSpec((2, ROWS, width), lambda i, *_: (0, i, 0))
        more.insert(0, (theirs, shaped((2, t, width), BF)))
    return prefetched(
        functools.partial(ffn_kernel, split), order, [mixed, tokens, gy, gain_inner, gain_ffn, gain_mid, *parts],
        [rows(d), rows(d), rows(d), whole((1, d)), whole((1, d)), whole((1, f))] + [hbm()] * len(parts),
        [rows(width), rows(width), rows(d), rows(f), rows(f), rows(d), rows(d), rows(d), whole((f, d)), whole((d, d)),
         whole((d, f))] + [m[0] for m in more],
        [
            shaped((t, width), BF), shaped((t, width), BF), shaped((t, d), F32), shaped((t, f), BF), shaped((t, f), BF),
            shaped((t, d), F32), shaped((t, d), BF), shaped((t, d), BF), shaped((f, d), BF), shaped((d, d), BF),
            shaped((d, f), BF),
        ] + [m[1] for m in more],
        [
            pltpu.VMEM((ROWS, f), F32), pltpu.VMEM((ROWS, f), F32), pltpu.VMEM((ROWS, f), F32), pltpu.SemaphoreType.DMA,
            pltpu.SemaphoreType.DMA,
        ],
        (t // ROWS,), 60, "ffn_both", 2 * t * d * (2 * d + 3 * f), 6 * d * f + 4 * t * f + 30 * t * d,
    )


def result_kernel(m_ref, x1_ref, wd_ref, y_ref):
    y_ref[...] = (x1_ref[...] + dot(m_ref[...], wd_ref[...])).astype(BF)


def down_forward(m, x1, w_down):
    t, d = x1.shape
    f = m.shape[1]
    return pl.pallas_call(
        result_kernel,
        grid=(t // ROWS,),
        in_specs=[rows(f), rows(d), whole((f, d))],
        out_specs=rows(d),
        out_shape=shaped((t, d), BF),
        compiler_params=params(48),
        cost_estimate=pl.CostEstimate(flops=2 * t * d * f, transcendentals=0, bytes_accessed=2 * d * f + 2 * t * f + 6 * t * d),
        name="down_forward",
    )(m, x1, w_down)


def grads_kernel(split, products, *refs):
    back, *refs = refs
    count = 2 if split else 1
    left, refs = refs[: len(products) * count], refs[len(products) * count :]
    right, refs = refs[: len(products) * count], refs[len(products) * count :]
    outs, refs = refs[: 4 if split else len(products)], refs[4 if split else len(products) :]
    tile, turned = refs[0], refs[1:]
    step = pl.program_id(0)
    first, row = 0, 0
    for n, (by_left, tiles, size) in enumerate(products):
        mine = [left[n * count + c] for c in range(count)]
        value = [right[n * count + c] for c in range(count)]

        if not by_left:

            @pl.when(step == first)
            def _():
                t = mine[0].shape[0]
                for c in range(count):
                    flat = mine[c][...] if len(mine[c].shape) == 2 else mine[c][0]
                    turned[0][:, c * t : (c + 1) * t] = flat.T

        @pl.when((step >= first) & (step < first + tiles))
        def _():
            total = None
            for c in range(count):
                v = value[c][...] if len(value[c].shape) == 2 else value[c][0]
                t = v.shape[0]
                if by_left:
                    part = dot(mine[c][...], v, ((0,), (0,)))
                else:
                    part = dot(turned[0][:, c * t : (c + 1) * t], v)
                total = part if total is None else total + part
            if not split:
                outs[n][...] = total
            else:
                tile[...] = total
                if by_left:
                    owners = tile.shape[0] // size
                    for e in range(owners):
                        at = back[16 + (step - first) * owners + e]
                        for q in range(4):

                            @pl.when(at // 4 == q)
                            def _():
                                block = tile[e * size : (e + 1) * size, :]
                                outs[q][at - 4 * q, row : row + size, :] = block.astype(outs[q].dtype)
                else:
                    deal(back, tile, outs, row + pl.multiple_of((step - first) * size, 8), size)

        first += tiles
        row += size if by_left else tiles * size


def weight_grads(split, back, products):
    count = 2 if split else 1
    t = products[0][0][0].shape[0]
    left_specs, right_specs, lefts, rights, plan = [], [], [], [], []
    out_specs, out_shape = [], []
    at = row = 0
    for left, right, tiles, by_left in products:
        width = 0
        for c in range(count):
            a, b = left[c], right[c]
            a, part = a if isinstance(a, tuple) else (a, None)

            if by_left and c == 0:
                tiles = tiles // count
                width = a.shape[1] // (tiles * count)

            def step(i, at=at, tiles=tiles):
                return jnp.clip(i - at, 0, tiles - 1)

            if by_left:
                per = tiles // 2
                if split and c == 0:
                    left_specs.append(pl.BlockSpec(
                        (t, width), lambda i, back, step=step, per=per: (0, (2 * (step(i) // per) + back[32]) * per + step(i) % per)
                    ))
                else:
                    left_specs.append(pl.BlockSpec((t, width), lambda i, *_, step=step: (0, step(i))))
                right_specs.append(whole(b.shape))
            else:
                width = a.shape[-1]
                if part is None:
                    left_specs.append(whole(a.shape))
                else:
                    left_specs.append(pl.BlockSpec(
                        (1, t, width), lambda *_, part=part: (part, 0, 0), pipeline_mode=pl.Buffered(1)
                    ))
                if b.ndim == 3:
                    right_specs.append(pl.BlockSpec((1, t, LANES), lambda i, *_, step=step: (step(i), 0, 0)))
                else:
                    right_specs.append(pl.BlockSpec((t, LANES), lambda i, *_, step=step: (0, step(i))))
            lefts.append(a)
            rights.append(b)
        size = (width * tiles if by_left else width) // 16
        if not split:
            shape = (width * tiles, LANES) if by_left else (width, tiles * LANES)
            block = (width, LANES)
            out_specs.append(pl.BlockSpec(
                block, (lambda i, *_, step=step: (step(i), 0)) if by_left else (lambda i, *_, step=step: (0, step(i)))
            ))
            out_shape.append(shaped(shape, F32))
        plan.append((by_left, tiles, size))
        at += tiles
        row += size if by_left else tiles * size
    narrow = next(p[0][0].shape[1] for p in products if not p[3])
    if split:
        out_specs = [whole((4, row, LANES))] * 4
        out_shape = [shaped((4, row, LANES), BF)] * 4
    flops = 2 * count * t * narrow * at * LANES
    return prefetched(
        functools.partial(grads_kernel, split, tuple(plan)), back, lefts + rights, left_specs + right_specs,
        out_specs, out_shape, [pltpu.VMEM((narrow, LANES), F32), pltpu.VMEM((narrow, count * t), BF)],
        (at,), 60, "weight_grads", flops, flops // 256,
    )


def qkv_back_kernel(d_ref, x_ref, dx1_ref, w_ref, gain_ref, dx_ref):
    d = x_ref.shape[1]
    groups, _, span = d_ref.shape
    span //= 3
    dh = None
    for part in range(3):
        for g in range(groups):
            at = part * d + g * span
            piece = dot(d_ref[g, :, part * span : (part + 1) * span], w_ref[:, at : at + span], ((1,), (1,)))
            dh = piece if dh is None else dh + piece
    unit, inv = unit_norm(x_ref[...].astype(F32))
    dx_ref[...] = dx1_ref[...] + norm_back(dh, gain_ref[...], unit, inv)


def qkv_backward(d_qkv, tokens, dx1, w_qkv, gain):
    t, d = tokens.shape
    groups, _, span = d_qkv.shape
    return pl.pallas_call(
        qkv_back_kernel,
        grid=(t // ROWS,),
        in_specs=[pl.BlockSpec((groups, ROWS, span), lambda i: (0, i, 0))] + [rows(d)] * 2
        + [whole((d, 3 * d)), whole((1, d))],
        out_specs=rows(d),
        out_shape=shaped((t, d), F32),
        compiler_params=params(48),
        cost_estimate=pl.CostEstimate(flops=6 * t * d * d, transcendentals=0, bytes_accessed=6 * d * d + 16 * t * d),
        name="qkv_backward",
    )(d_qkv, tokens, dx1, w_qkv, gain)


def layout(doc_lengths, seq):
    docs = doc_lengths.shape[-1]
    upto = jnp.arange(docs)[:, None] <= jnp.arange(docs)[None, :]
    ends = jnp.sum(jnp.where(upto[None], doc_lengths[:, :, None], 0), axis=1)
    places = jnp.arange(seq, dtype=jnp.int32)
    passed = places[None, :, None] >= ends[:, None, :]
    start = jnp.sum(jnp.where(passed, doc_lengths[:, None, :], 0), axis=-1)
    valid = places[None, :] < ends[:, docs - 2 : docs - 1]
    return start.astype(jnp.int32), places[None, :] - start, valid


def tables(position):
    half = HEAD_DIM // 2
    lane = jnp.arange(PAIR)
    frequency = jnp.exp((lane % half).astype(F32) * (-2.0 * math.log(10000.0) / HEAD_DIM))
    angles = position.reshape(-1, 1).astype(F32) * frequency[None, :]
    sign = jnp.where(lane % HEAD_DIM < half, -1.0, 1.0)
    return jnp.cos(angles), jnp.sin(angles) * sign[None, :]


Z = 4
GROUPS = ((0, 2), (1, 3))


def index(x, core, z, y):
    return ((x * 2 + core) * Z + z) * 2 + y


def permute(value, move):
    places = [(x, c, z, y) for x in range(2) for c in range(2) for z in range(Z) for y in range(2)]
    return lax.ppermute(value, AXES, [(index(*p), index(*move(*p))) for p in places])


def over_x(v):
    return permute(v, lambda x, c, z, y: (1 - x, c, z, y))


def over_y(v):
    return permute(v, lambda x, c, z, y: (x, c, z, 1 - y))


def over_core(v):
    return permute(v, lambda x, c, z, y: (x, 1 - c, z, y))


def over_z(v, bits):
    return permute(v, lambda x, c, z, y: (x, c, z ^ bits, y))


def place():
    dp, fs = lax.axis_index("dp"), lax.axis_index("fsdp")
    return dp >> 1, dp & 1, fs >> 1, fs & 1


def gather_order():
    rows_of = []
    for core in range(2):
        for group, first in zip(GROUPS, ("x", "y")):
            for second in range(2):
                for one in range(2):
                    dx, dy = (one, second) if first == "x" else (second, one)
                    rows_of += [(dx, core, dz, dy) for dz in group]
    dx, dc, dz, dy = np.array(rows_of, np.int32).T
    x, c, z, y = place()
    order = index(x ^ dx, c ^ dc, z ^ dz, y ^ dy)
    return jnp.concatenate([order, c[None]]).astype(jnp.int32)


def scatter_order():
    rows_of = []
    for group, first in zip(GROUPS, ("y", "x")):
        for one in (1, 0):
            for second in (1, 0):
                dx, dy = (second, one) if first == "y" else (one, second)
                rows_of += [(dx, dz, dy) for dz in group]
    dx, dz, dy = np.array(rows_of, np.int32).T
    x, c, z, y = place()
    order = ((x ^ dx) * Z + (z ^ dz)) * 2 + (y ^ dy)
    spots = jnp.arange(len(rows_of), dtype=jnp.int32)
    where = jnp.sum(jnp.where(order[None, :] == spots[:, None], spots[None, :], 0), axis=1)
    return jnp.concatenate([order, where, c[None]]).astype(jnp.int32)


def tie(value, other):
    return lax.optimization_barrier((value, other))[0]


class Gather:
    def __init__(self, block):
        self.block = block

    def far_z(self, after=None):
        block = self.block if after is None else tie(self.block, after)
        self.even = jnp.stack([block, over_z(block, 2)])
        return self.even

    def near_z(self, after=None):
        if after is not None:
            self.even = tie(self.even, after)
        self.odd = over_z(self.even, 1)
        return self.odd

    def first(self, after=None):
        even, odd = (self.even, self.odd) if after is None else tie((self.even, self.odd), after)
        self.even, self.odd = even, odd
        self.got = (over_x(even), over_y(odd))
        return self.got

    def second(self, after=None):
        got = self.got if after is None else tie(self.got, after)
        even, odd = jnp.concatenate([self.even, got[0]]), jnp.concatenate([self.odd, got[1]])
        self.near = [even, odd, over_core(even), over_core(odd)]
        self.far = [over_y(even), over_x(odd)]
        return self.far

    def core(self, after=None):
        far = self.far if after is None else tie(self.far, after)
        even, odd, even_core, odd_core = self.near
        return [even, far[0], odd, far[1], even_core, over_core(far[0]), odd_core, over_core(far[1])]


class Reduce:
    def __init__(self, send_a, keep_a, send_b, keep_b):
        self.sends, self.a, self.b = (send_a, send_b), keep_a.astype(F32), keep_b.astype(F32)

    def first(self, after=None):
        sends = self.sends if after is None else tie(self.sends, after)
        self.got = (over_y(sends[0]), over_x(sends[1]))
        return self.got

    def wait_for(self, after):
        if after is not None:
            self.got = tie(self.got, after)

    def second(self, after=None):
        self.wait_for(after)
        self.a = self.a + self.got[0].astype(F32)
        self.b = self.b + self.got[1].astype(F32)
        self.got = (over_x(self.a[:2].astype(BF)), over_y(self.b[:2].astype(BF)))
        return self.got

    def near_z(self, after=None):
        self.wait_for(after)
        self.a = self.a[2:] + self.got[0].astype(F32)
        self.got = over_z((self.b[2:] + self.got[1].astype(F32)).astype(BF), 1)
        return self.got

    def far_z(self, after=None):
        self.wait_for(after)
        self.a = self.a + self.got.astype(F32)
        self.got = over_z(self.a[1].astype(BF), 2)
        return self.got

    def own(self):
        return self.a[0] + self.got.astype(F32)


def unslab(block, width):
    size = block.shape[0] * LANES // width
    return jnp.concatenate([block[s * size : (s + 1) * size] for s in range(width // LANES)], axis=1)


def slab(block):
    return [block[:, s * LANES : (s + 1) * LANES] for s in range(block.shape[1] // LANES)]


def local(fast, tokens, doc_lengths, cotangent, w_qkv, w_out, w_up, w_down,
          gain_attn, gain_inner, gain_ffn, gain_mid):
    row_count = doc_lengths.shape[0]
    seq = tokens.shape[0] // row_count
    d, f = tokens.shape[1], w_up.shape[1]
    wide = min(seq, 512) // BLOCK + 1
    blocks = seq // BLOCK
    shards = (gain_attn, gain_inner, gain_ffn, gain_mid)
    sizes = [g.shape[0] for g in shards]

    start, position, valid = layout(doc_lengths, seq)
    cos, sin = tables(position)
    firsts = start[:, ::BLOCK] // BLOCK
    reach = (jnp.arange(blocks, dtype=jnp.int32)[None, :] - firsts + 1).reshape(-1)
    start_col = start.reshape(-1, 1)
    start_row = jnp.repeat(start, 8, axis=0)
    gy = jnp.where(valid.reshape(-1, 1), cotangent, jnp.zeros_like(cotangent))

    def scatter(g):
        return lax.psum_scatter(g, AXES, scatter_dimension=0, tiled=True)

    def gather(v):
        return lax.all_gather(v, AXES, axis=0, tiled=True)

    if fast:
        order, back = gather_order(), scatter_order()
        parts_down = gather(w_down)
        gains_row = jnp.pad(jnp.concatenate(shards)[None], ((0, 7), (0, LANES - sum(sizes))))
        one, two = (Gather(b) for b in pack(w_qkv, w_out, w_up, gains_row))
        seen = one.far_z()
        two.far_z(seen)
        one.near_z()
        one.first()
        far = one.second(two.even)
        two.near_z()
        two.first(far)
        parts_qkv = one.core()
        gy_both = (gy, over_core(gy))
        cos, sin = tie((cos, sin), (gy, start_col, start_row, reach, order, back))
        gains = [None]
    else:
        order = back = jnp.zeros((8,), jnp.int32)
        parts_qkv, parts_up, parts_down = [gather(w_qkv)], [gather(w_out), gather(w_up)], gather(w_down)
        gains = [gather(g).astype(F32).reshape(1, -1) for g in shards]

    h1, qkv, full_qkv, *rest = qkv_forward(fast, order, tokens, cos, sin, parts_qkv, gains[0], sizes)
    g_attn, g_inner, g_ffn, g_mid = rest if fast else gains
    if fast:
        two.second(g_attn)
        start_col = tie(start_col, gy_both[1])
    mixed, lse = attention_forward(reach, qkv, start_col, row_count, wide)
    parts = two.core(lse) + [parts_down] if fast else parts_up + [parts_down]
    a, h2, x1, m, dpre, dx1, low, d_mixed, full_down, _, _, *other = ffn_both(
        fast, order, mixed, tokens, gy, g_inner, g_ffn, g_mid, parts
    )

    def shared(value):
        return (value, over_core(value)) if fast else (value,)

    if fast:
        m_both = (m, over_core(other[1]))
        theirs = over_core(other[0])
        a_both, h2_both = (a, (theirs, 0)), (h2, (theirs, 1))
    else:
        gy_both, m_both, a_both, h2_both = (gy,), (m,), (a,), (h2,)
    low, dpre = shared(low), shared(dpre)

    def attend(group, groups, lse, so_far):
        return attention_backward(
            reach, qkv, d_mixed, mixed, lse, start_row, cos, sin, row_count, wide, group, groups, so_far
        )

    f = w_up.shape[1]
    d_qkv = attend(0, 1, lse, None)
    if fast:
        low = tie(low, d_qkv)
    grads = weight_grads(
        fast, back,
        [(m_both, gy_both, f // 384, True), (a_both, low, d // LANES, False), (h2_both, dpre, f // LANES, False)],
    )
    if fast:
        red = Reduce(*grads)
        first = red.first()
        h1 = tie(h1, grads[-1])
    d_qkv = attend(1, 2, tie(lse, grads[-1]), d_qkv)
    if fast:
        h1 = (h1[0], over_core(h1[1]))
        d_both = (d_qkv, over_core(tie(d_qkv, (first, h1[1]))))
        second = red.second(d_qkv)
        dx1 = tie(dx1, (d_qkv, first))
    else:
        d_both = (d_qkv,)
    grad_tokens = qkv_backward(d_qkv, tokens, dx1, full_qkv, g_attn)
    if fast:
        near = red.near_z(grad_tokens)
        h1 = tie(h1, (grad_tokens, second))
    grad_qkv = weight_grads(fast, back, [(h1, d_both, 3 * d // LANES, False)])
    if fast:
        red_qkv = Reduce(*grad_qkv)
        first = red_qkv.first()
        far = red.far_z(grad_qkv[-1])
        m = tie(m, (grad_qkv[-1], near))
    result = down_forward(m, x1, full_down)
    if fast:
        red_qkv.second((result, far))
        own = red.own()
        red_qkv.near_z()
        red_qkv.far_z()
        g_qkv = red_qkv.own()
        cuts = (w_down.shape[0], w_down.shape[0] + w_out.shape[0])
        own_down, grad_out, grad_up = own[: cuts[0]], own[cuts[0] : cuts[1]], unslab(own[cuts[1] :], f)
    else:
        own_down, grad_out, grad_up, g_qkv = (scatter(g.astype(BF)).astype(F32) for g in (*grads, *grad_qkv))
        g_qkv = jnp.concatenate(slab(g_qkv))
    size = w_qkv.shape[0]
    span = LANES // 3
    g_qkv = jnp.concatenate(
        [g_qkv[g * size : (g + 1) * size, p * span : (p + 1) * span] for p in range(3) for g in range(GRAD_GROUPS)], axis=1
    )
    pairs = ((g_qkv, w_qkv), (grad_out, w_out), (grad_up, w_up), (own_down, w_down))
    gain_grads = [jnp.sum(g * w.astype(F32), axis=1) / v.astype(F32) for (g, w), v in zip(pairs, shards)]
    return (result, grad_tokens, g_qkv, grad_out, grad_up, own_down, *gain_grads)


def solution(mesh):
    matrix, vector = P(AXES, None), P(AXES)
    fast = mesh.shape["dp"] == 4 and mesh.shape["fsdp"] == 2 * Z
    return jax.shard_map(
        functools.partial(local, fast),
        mesh=mesh,
        in_specs=(matrix,) * 7 + (vector,) * 4,
        out_specs=(matrix,) * 6 + (vector,) * 4,
        check_vma=False,
    )
```

```python
import functools
import math

import jax
import jax.numpy as jnp
import numpy as np
from jax import lax
from jax.experimental import pallas as pl
from jax.experimental.pallas import tpu as pltpu
from jax.sharding import PartitionSpec as P

HEADS = 12
HEAD_DIM = 64
PAIR = 2 * HEAD_DIM
PAIRS = HEADS // 2
EPSILON = 1e-05
MASKED_SCORE = -1e30
ROOT_HALF = 0.7071067811865476
INV_ROOT_TAU = 0.3989422804014327
BF = jnp.bfloat16
F32 = jnp.float32
MIB = 1 << 20
AXES = ("dp", "fsdp")
BLOCK = 256
ROWS = 256
LANES = 768
VMEM_MIB = 60
GRAD_GROUPS = 3


def dot(a, b, dims=((1,), (0,))):
    return lax.dot_general(a, b, (dims, ((), ())), preferred_element_type=F32)


def params(mib):
    return pltpu.CompilerParams(vmem_limit_bytes=max(mib, VMEM_MIB) * MIB)


def swap_halves(x):
    lane = lax.broadcasted_iota(jnp.int32, x.shape, 1)
    low = lax.rem(lane, HEAD_DIM) < HEAD_DIM // 2
    half = HEAD_DIM // 2
    return jnp.where(low, pltpu.roll(x, PAIR - half, 1), pltpu.roll(x, half, 1))


def unit_norm(x):
    mean = jnp.mean(x, axis=-1, keepdims=True)
    centred = x - mean
    inv = lax.rsqrt(jnp.mean(centred * centred, axis=-1, keepdims=True) + EPSILON)
    return centred * inv, inv


def norm_back(grad, gain, unit, inv):
    d_unit = grad * gain
    return inv * (
        d_unit
        - jnp.mean(d_unit, axis=-1, keepdims=True)
        - unit * jnp.mean(d_unit * unit, axis=-1, keepdims=True)
    )


def whole(shape):
    return pl.BlockSpec(shape, lambda *_: (0,) * len(shape), pipeline_mode=pl.Buffered(1))


def rows(width, block=ROWS):
    return pl.BlockSpec((block, width), lambda i: (i, 0))


def shaped(shape, dtype):
    return jax.ShapeDtypeStruct(shape, dtype)


def hbm():
    return pl.BlockSpec(memory_space=pl.ANY)


def fetch(order, parts, places, sem):
    if len(parts) < 8 and parts[0].ndim == 2:
        for part, (_, _, buffer, _) in zip(parts, places):
            pltpu.make_async_copy(part, buffer, sem).start()
        return
    count = parts[0].shape[0]
    for p, part in enumerate(parts):
        for b in range(count):
            owner = b if order is None else order[p * count + b]
            for first, size, buffer, column in places:
                row = owner * size if order is None else pl.multiple_of(owner * size, 8)
                pltpu.make_async_copy(
                    part.at[b, pl.ds(first, size), :],
                    buffer.at[pl.ds(row, size), pl.ds(column, LANES)],
                    sem,
                ).start()


def arrive(buffers, sem):
    for buffer in buffers:
        pltpu.make_async_copy(buffer, buffer, sem).wait()


def deal(back, tile, outs, row, size):
    quarter = outs[0].shape[0]
    for q, out in enumerate(outs):

        @pl.loop(0, quarter)
        def _(j):
            block = tile[pl.ds(pl.multiple_of(back[q * quarter + j] * size, 8), size), :]
            out[j, pl.ds(row, size), :] = block.astype(out.dtype)


def slabs(first, size, buffer, width):
    return [(first + s * size, size, buffer, s * LANES) for s in range(width // LANES)]


def pack_kernel(wq_ref, wo_ref, wu_ref, wd_ref, gains_ref, one_ref, two_ref):
    row = 0
    for c in range(wq_ref.shape[1] // LANES):
        one_ref[row : row + wq_ref.shape[0], :] = wq_ref[:, c * LANES : (c + 1) * LANES]
        row += wq_ref.shape[0]
    one_ref[row:, :] = gains_ref[...]
    row = 0
    for ref in (wd_ref, wo_ref, wu_ref):
        for c in range(ref.shape[1] // LANES):
            two_ref[row : row + ref.shape[0], :] = ref[:, c * LANES : (c + 1) * LANES]
            row += ref.shape[0]


def pack(w_qkv, w_out, w_up, w_down, gains):
    first = w_qkv.size // LANES + gains.shape[0]
    second = (w_out.size + w_up.size + w_down.size) // LANES
    return pl.pallas_call(
        pack_kernel, out_shape=[shaped((first, LANES), BF), shaped((second, LANES), BF)], name="pack"
    )(w_qkv, w_out, w_up, w_down, gains)


def spread(rows_in, offset, count, owners):
    lanes = rows_in.shape[1]
    wide = owners * count
    lane = lax.broadcasted_iota(jnp.int32, (lanes, wide), 0)
    column = lax.broadcasted_iota(jnp.int32, (lanes, wide), 1)
    pick = (lane - offset == lax.rem(column, count)).astype(F32).astype(BF)
    full = dot(rows_in, pick)
    owner = lax.broadcasted_iota(jnp.int32, (owners, wide), 0)
    column = lax.broadcasted_iota(jnp.int32, (owners, wide), 1)
    own = (column >= owner * count) & (column < owner * count + count)
    return jnp.sum(jnp.where(own, full, 0.0), axis=0, keepdims=True)


def qkv_kernel(split, sizes, *refs):
    if split:
        order, x_ref, cos_ref, sin_ref, *refs = refs
        parts, refs = refs[:8], refs[8:]
        h_ref, other_ref, qkv_ref, w_ref, ga_ref, gi_ref, gf_ref, gm_ref, gains, sem, gain_sem = refs
        h_refs = (h_ref, other_ref)
    else:
        order, x_ref, cos_ref, sin_ref, ga_ref, *refs = refs
        parts, refs = refs[:1], refs[1:]
        h_ref, qkv_ref, w_ref, sem = refs
        h_refs = (h_ref,)
    width = x_ref.shape[1]
    step = pl.program_id(0)
    if split:
        size = width // 32
        weight = slabs(0, size, w_ref, 3 * width)

        @pl.when(step == 0)
        def _():
            fetch(order, parts, [(3 * size, 8, gains, 0)], gain_sem)
            fetch(order, parts, weight, sem)
            arrive([gains], gain_sem)
            owner = lax.broadcasted_iota(jnp.int32, (32, 256), 0)
            lane = lax.broadcasted_iota(jnp.int32, (32, 256), 1)
            pick = (lane == owner * 8).astype(F32).astype(BF)
            per_owner = dot(pick, gains[:, :256]).astype(BF)
            at = 0
            for ref, count in zip((ga_ref, gi_ref, gf_ref, gm_ref), sizes):
                ref[...] = spread(per_owner, at, count, 32)
                at += count
            arrive([w_ref], sem)
    else:

        @pl.when(step == 0)
        def _():
            fetch(None, parts, [(0, 0, w_ref, 0)], sem)
            arrive([w_ref], sem)

    unit, _ = unit_norm(x_ref[...].astype(F32))
    h = (unit * ga_ref[...]).astype(BF)
    store_low(split, order[32] if split else 0, h, h_refs)
    cos, sin = cos_ref[...], sin_ref[...]
    for part in range(3):
        y = dot(h, w_ref[:, part * width : (part + 1) * width])
        for c in range(width // PAIR):
            z = y[:, c * PAIR : (c + 1) * PAIR]
            if part < 2:
                z = z * cos + swap_halves(z) * sin
            if part == 0:
                z = z * (1.0 / math.sqrt(HEAD_DIM))
            at = part * width + c * PAIR
            qkv_ref[:, at : at + PAIR] = z.astype(BF)


def prefetched(kernel, order, inputs, in_specs, out_specs, out_shape, scratch, grid, mib, name, flops, data):
    return pl.pallas_call(
        kernel,
        grid_spec=pltpu.PrefetchScalarGridSpec(
            num_scalar_prefetch=1,
            grid=grid,
            in_specs=in_specs,
            out_specs=out_specs,
            scratch_shapes=scratch,
        ),
        out_shape=out_shape,
        compiler_params=params(mib),
        cost_estimate=pl.CostEstimate(flops=flops, transcendentals=0, bytes_accessed=data),
        name=name,
    )(order, *inputs)


def rows(width, block=ROWS):
    return pl.BlockSpec((block, width), lambda i, *_: (i, 0))


def whole(shape):
    return pl.BlockSpec(shape, lambda *_: (0,) * len(shape), pipeline_mode=pl.Buffered(1))


def qkv_forward(split, order, tokens, cos, sin, parts, gain, sizes):
    t, d = tokens.shape
    n = 3 * d
    inputs = [tokens, cos, sin]
    in_specs = [rows(d), rows(PAIR), rows(PAIR)]
    out_specs, out_shape = low_specs(split, t, d)
    lows = len(out_specs)
    out_specs = out_specs + [rows(n), whole((d, n))]
    out_shape = out_shape + [shaped((t, n), BF), shaped((d, n), BF)]
    scratch = [pltpu.SemaphoreType.DMA]
    if split:
        widths = [32 * s for s in sizes]
        out_specs += [whole((1, w)) for w in widths]
        out_shape += [shaped((1, w), F32) for w in widths]
        scratch = [pltpu.VMEM((32 * 8, LANES), BF), pltpu.SemaphoreType.DMA, pltpu.SemaphoreType.DMA]
    else:
        inputs.append(gain)
        in_specs.append(whole((1, d)))
    outs = prefetched(
        functools.partial(qkv_kernel, split, sizes), order, inputs + list(parts), in_specs + [hbm()] * len(parts),
        out_specs, out_shape, scratch, (t // ROWS,), 40, "qkv_forward",
        2 * t * d * n, 4 * d * n + 12 * t * d,
    )
    return (outs[:lows], *outs[lows:])


def window(i, n):
    return slice((i - n + 1) * BLOCK, (i + 1) * BLOCK)


def head_masks(shape):
    lane = lax.broadcasted_iota(jnp.int32, shape, 1)
    return lane < HEAD_DIM


def attention_forward_kernel(wide, reach, q_ref, k_ref, v_ref, start_ref, o_ref, lse_ref, bias):
    row, pair = pl.program_id(0), pl.program_id(1)
    seq = q_ref.shape[0]
    blocks = seq // BLOCK

    @pl.when(pair == 0)
    def _():
        for i in range(blocks):
            at = slice(i * BLOCK, (i + 1) * BLOCK)
            shape = (BLOCK, wide * BLOCK)
            key = (i - wide + 1) * BLOCK + lax.broadcasted_iota(jnp.int32, shape, 1)
            query = i * BLOCK + lax.broadcasted_iota(jnp.int32, shape, 0)
            keep = (key >= start_ref[at, :]) & (key <= query)
            bias[at, :] = jnp.where(keep, 0.0, MASKED_SCORE)

    first = head_masks((BLOCK, PAIR))
    for i in range(blocks):
        at = slice(i * BLOCK, (i + 1) * BLOCK)
        most = min(wide, i + 1)
        for n in range(1, most + 1):

            @pl.when(reach[row * blocks + i] == n)
            def _():
                q = q_ref[at, :]
                w = window(i, n)
                k, v = k_ref[w, :], v_ref[w, :]
                b = bias[at, (wide - n) * BLOCK :]
                mask = head_masks(k.shape)
                zero = jnp.zeros_like(k)
                total, lses = None, []
                scale = None
                for h in range(2):
                    pick = mask if h == 0 else jnp.logical_not(mask)
                    s = dot(q, jnp.where(pick, k, zero), ((1,), (1,))) + b
                    top = jnp.max(s, axis=-1, keepdims=True)
                    p = jnp.exp(s - top)
                    den = jnp.sum(p, axis=-1, keepdims=True)
                    probs = (p * (1.0 / den)).astype(BF)
                    part = dot(probs, jnp.where(pick, v, zero))
                    total = part if total is None else total + part
                    lses.append(top + jnp.log(den))
                o_ref[at, :] = total
                both = jnp.where(first, lses[0], lses[1]).T
                lse_ref[0, 0:1, at] = both[0:1, :]
                lse_ref[0, 1:2, at] = both[HEAD_DIM : HEAD_DIM + 1, :]


def attention_forward(reach, qkv, start, row_count, wide):
    t = qkv.shape[0]
    seq = t // row_count
    d = qkv.shape[1] // 3

    def columns(part):
        return pl.BlockSpec((seq, PAIR), lambda r, p, *_: (r, part * PAIRS + p))

    return pl.pallas_call(
        functools.partial(attention_forward_kernel, wide),
        grid_spec=pltpu.PrefetchScalarGridSpec(
            num_scalar_prefetch=1,
            grid=(row_count, PAIRS),
            in_specs=[
                columns(0),
                columns(1),
                columns(2),
                pl.BlockSpec((seq, 1), lambda r, p, *_: (r, 0)),
            ],
            out_specs=[
                pl.BlockSpec((seq, PAIR), lambda r, p, *_: (r, p)),
                pl.BlockSpec((1, 8, seq), lambda r, p, *_: (r * PAIRS + p, 0, 0)),
            ],
            scratch_shapes=[pltpu.VMEM((seq, wide * BLOCK), F32)],
        ),
        out_shape=[shaped((t, d), F32), shaped((row_count * PAIRS, 8, seq), F32)],
        compiler_params=params(32),
        cost_estimate=pl.CostEstimate(
            flops=8 * t * d * BLOCK, transcendentals=t * HEADS * 512, bytes_accessed=12 * t * d
        ),
        name="attention_forward",
    )(reach, qkv, qkv, qkv, start)


def attention_backward_kernel(wide, reach, q_ref, k_ref, v_ref, do_ref, o_ref, lse_ref, start_ref, cos_ref, sin_ref, *refs):
    grad_ref, bias, ks, vs, qs, dos, dk_acc, dv_acc, dq_acc = refs[-9:]
    row, pair = pl.program_id(0), pl.program_id(1)
    seq = q_ref.shape[0]
    blocks = seq // BLOCK

    @pl.when(pair == 0)
    def _():
        for i in range(blocks):
            at = slice(i * BLOCK, (i + 1) * BLOCK)
            shape = (wide * BLOCK, BLOCK)
            key = (i - wide + 1) * BLOCK + lax.broadcasted_iota(jnp.int32, shape, 0)
            query = i * BLOCK + lax.broadcasted_iota(jnp.int32, shape, 1)
            keep = (key >= start_ref[0:1, at]) & (key <= query)
            bias[:, at] = jnp.where(keep, 0.0, MASKED_SCORE)

    mask = head_masks((seq, PAIR))
    for src, dst in ((k_ref, ks), (v_ref, vs), (q_ref, qs), (do_ref, dos)):
        x = src[...]
        zero = jnp.zeros_like(x)
        dst[0] = jnp.where(mask, x, zero)
        dst[1] = jnp.where(mask, zero, x)
    dk_acc[...] = jnp.zeros_like(dk_acc)
    dv_acc[...] = jnp.zeros_like(dv_acc)
    lane8 = lax.broadcasted_iota(jnp.int32, (8, PAIR), 1) // HEAD_DIM
    row8 = lax.broadcasted_iota(jnp.int32, (8, PAIR), 0)
    picks = (lane8 == row8).astype(F32)
    delta = lax.dot_general(
        picks, do_ref[...].astype(F32) * o_ref[...], (((1,), (1,)), ((), ())),
        precision=lax.Precision.HIGHEST, preferred_element_type=F32,
    )
    for i in range(blocks):
        at = slice(i * BLOCK, (i + 1) * BLOCK)
        most = min(wide, i + 1)
        for n in range(1, most + 1):

            @pl.when(reach[row * blocks + i] == n)
            def _():
                w = window(i, n)
                b = bias[(wide - n) * BLOCK :, at]
                q, do = q_ref[at, :], do_ref[at, :]
                ps, dss = [], []
                for h in range(2):
                    s = dot(ks[h, w, :], q, ((1,), (1,))) + b
                    p = jnp.exp(s - lse_ref[0, h : h + 1, at])
                    dp = dot(vs[h, w, :], do, ((1,), (1,)))
                    ds = (p * (dp - delta[h : h + 1, at])).astype(BF)
                    ps.append(p.astype(BF))
                    dss.append(ds)
                dv_acc[w, :] += dot(ps[0], dos[0, at, :]) + dot(ps[1], dos[1, at, :])
                dk_acc[w, :] += dot(dss[0], qs[0, at, :]) + dot(dss[1], qs[1, at, :])
                dq_acc[at, :] = dot(dss[0], ks[0, w, :], ((0,), (0,))) + dot(
                    dss[1], ks[1, w, :], ((0,), (0,))
                )

    cos, sin = cos_ref[...], sin_ref[...]
    dq = dq_acc[...] * (1.0 / math.sqrt(HEAD_DIM))
    dk = dk_acc[...]
    span = grad_ref.shape[2] // 3
    slot = lax.rem(pair, span // PAIR)
    grads = (dq * cos - swap_halves(dq) * sin, dk * cos - swap_halves(dk) * sin, dv_acc[...])
    for part, value in enumerate(grads):
        grad_ref[0, :, pl.ds(pl.multiple_of(part * span + slot * PAIR, PAIR), PAIR)] = value.astype(BF)


def attention_backward(reach, qkv, d_mixed, mixed, lse, start_row, cos, sin, row_count, wide, group, groups, so_far):
    pairs = PAIRS // GRAD_GROUPS
    t = qkv.shape[0]
    seq = t // row_count
    base = group * pairs
    span = 3 * pairs * PAIR

    def columns(part):
        return pl.BlockSpec((seq, PAIR), lambda r, p, *_: (r, part * PAIRS + base + p))

    table = pl.BlockSpec((seq, PAIR), lambda r, p, *_: (r, 0))
    inputs = [reach, qkv, qkv, qkv, d_mixed, mixed, lse, start_row, cos, sin]
    in_specs = [
        columns(0), columns(1), columns(2), columns(0), columns(0),
        pl.BlockSpec((1, 8, seq), lambda r, p, *_: (r * PAIRS + base + p, 0, 0)),
        pl.BlockSpec((8, seq), lambda r, p, *_: (r, 0)),
        table, table,
    ]
    aliases = {}
    if so_far is not None:
        aliases = {len(inputs): 0}
        inputs.append(so_far)
        in_specs.append(hbm())
    return pl.pallas_call(
        functools.partial(attention_backward_kernel, wide),
        grid_spec=pltpu.PrefetchScalarGridSpec(
            num_scalar_prefetch=1,
            grid=(row_count, pairs * groups),
            in_specs=in_specs,
            out_specs=pl.BlockSpec((1, seq, span), lambda r, p, *_: (group + p // pairs, r, 0)),
            scratch_shapes=[
                pltpu.VMEM((wide * BLOCK, seq), F32),
                pltpu.VMEM((2, seq, PAIR), BF),
                pltpu.VMEM((2, seq, PAIR), BF),
                pltpu.VMEM((2, seq, PAIR), BF),
                pltpu.VMEM((2, seq, PAIR), BF),
                pltpu.VMEM((seq, PAIR), F32),
                pltpu.VMEM((seq, PAIR), F32),
                pltpu.VMEM((seq, PAIR), F32),
            ],
        ),
        out_shape=shaped((GRAD_GROUPS, t, span), BF),
        input_output_aliases=aliases,
        compiler_params=params(40),
        cost_estimate=pl.CostEstimate(
            flops=20 * t * span * BLOCK // 3 * groups, transcendentals=t * HEADS * 128 * groups,
            bytes_accessed=20 * t * span // 3 * groups
        ),
        name="attention_backward",
    )(*inputs)


def halves(x):
    quarter = x.shape[1] // 4
    piece = [x[:, i * quarter : (i + 1) * quarter] for i in range(4)]
    return jnp.concatenate(piece[0::2], axis=1), jnp.concatenate(piece[1::2], axis=1)


def store_low(split, core, x, refs):
    if not split:
        refs[0][...] = x
        return
    pair = halves(x)
    for c in range(2):

        @pl.when(core == c)
        def _():
            refs[0][...] = pair[c]
            refs[1][...] = pair[1 - c]


def low_specs(split, t, d):
    if split:
        return [rows(d // 2)] * 2, [shaped((t, d // 2), BF)] * 2
    return [rows(d)], [shaped((t, d), BF)]


def ffn_kernel(split, *refs):
    order, o_ref, x_ref, gy_ref, gi_ref, gf_ref, gm_ref, *refs = refs
    count = 8 if split else 3
    parts, refs = refs[:count], refs[count:]
    a_ref, h2_ref, x1_ref, m_ref, dpre_ref, dx1_ref, low_ref, do_ref, wd_ref, wo_ref, wu_ref, *refs = refs
    theirs_ref, other_ref, *refs = refs if split else (None, None, *refs)
    act, slope, dm, sem, down_sem = refs
    d, f = wu_ref.shape
    size, skip = d // 32, f // 32
    step = pl.program_id(0)
    core = order[32] if split else 0
    chunks = [slice(c, c + LANES) for c in range(0, f, LANES)]

    @pl.when(step == 0)
    def _():
        if split:
            fetch(order, parts, [(skip, size, wo_ref, 0)] + slabs(skip + size, size, wu_ref, f), sem)
            fetch(order, parts, [(0, skip, wd_ref, 0)], down_sem)
        else:
            fetch(order, parts[:2], [(0, 0, wo_ref, 0), (0, 0, wu_ref, 0)], sem)
            fetch(order, parts[2:], [(0, 0, wd_ref, 0)], down_sem)

    mixed = o_ref[...]
    unit_in, inv_in = unit_norm(mixed)
    a = (unit_in * gi_ref[...]).astype(BF)
    store_low(split, core, a, (a_ref, theirs_ref.at[0] if split else None))

    @pl.when(step == 0)
    def _():
        arrive([wo_ref, wu_ref], sem)
        arrive([wd_ref], down_sem)

    x1 = x_ref[...].astype(F32) + dot(a, wo_ref[...])
    x1_ref[...] = x1
    unit_two, inv_two = unit_norm(x1)
    h2 = (unit_two * gf_ref[...]).astype(BF)
    store_low(split, core, h2, (h2_ref, theirs_ref.at[1] if split else None))
    gy = gy_ref[...]
    total = None
    for at in chunks:
        hidden = dot(h2, wu_ref[:, at])
        dm[:, at] = dot(gy, wd_ref[at, :], ((1,), (1,)))
        cdf = 0.5 + 0.5 * lax.erf(hidden * ROOT_HALF)
        slope[:, at] = cdf + hidden * (jnp.exp(-0.5 * hidden * hidden) * INV_ROOT_TAU)
        value = hidden * cdf
        act[:, at] = value
        part = jnp.sum(value, axis=-1, keepdims=True)
        total = part if total is None else total + part
    mean = total * (1.0 / f)
    total = None
    for at in chunks:
        centred = act[:, at] - mean
        part = jnp.sum(centred * centred, axis=-1, keepdims=True)
        total = part if total is None else total + part
    inv = lax.rsqrt(total * (1.0 / f) + EPSILON)
    first = second = None
    for at in chunks:
        gain = gm_ref[:, at]
        unit = (act[:, at] - mean) * inv
        act[:, at] = unit
        m_ref[:, at] = (unit * gain).astype(BF)
        d_unit = dm[:, at] * gain
        dm[:, at] = d_unit
        part = jnp.sum(d_unit, axis=-1, keepdims=True)
        first = part if first is None else first + part
        part = jnp.sum(d_unit * unit, axis=-1, keepdims=True)
        second = part if second is None else second + part
    first, second = first * (1.0 / f), second * (1.0 / f)
    dh2 = None
    for at in chunks:
        d_act = inv * (dm[:, at] - first - act[:, at] * second)
        dpre = (d_act * slope[:, at]).astype(BF)
        dpre_ref[:, at] = dpre
        part = dot(dpre, wu_ref[:, at], ((1,), (1,)))
        dh2 = part if dh2 is None else dh2 + part
    dx1 = gy.astype(F32) + norm_back(dh2, gf_ref[...], unit_two, inv_two)
    dx1_ref[...] = dx1
    low = dx1.astype(BF)
    low_ref[...] = low
    da = dot(low, wo_ref[...], ((1,), (1,)))
    do_ref[...] = norm_back(da, gi_ref[...], unit_in, inv_in).astype(BF)

    if split:
        quarter = f // 4
        for j in range(2):
            at = pl.multiple_of((2 * j + 1 - core) * quarter, PAIR)
            other_ref[:, j * quarter : (j + 1) * quarter] = m_ref[:, pl.ds(at, quarter)]


def ffn_both(split, order, mixed, tokens, gy, gain_inner, gain_ffn, gain_mid, parts):
    t, d = tokens.shape
    f = gain_mid.shape[1]
    width = d // 2 if split else d
    more = [(rows(f // 2), shaped((t, f // 2), BF))] * split
    if split:
        theirs = pl.BlockSpec((2, ROWS, width), lambda i, *_: (0, i, 0))
        more.insert(0, (theirs, shaped((2, t, width), BF)))
    return prefetched(
        functools.partial(ffn_kernel, split), order, [mixed, tokens, gy, gain_inner, gain_ffn, gain_mid, *parts],
        [rows(d), rows(d), rows(d), whole((1, d)), whole((1, d)), whole((1, f))] + [hbm()] * len(parts),
        [rows(width), rows(width), rows(d), rows(f), rows(f), rows(d), rows(d), rows(d), whole((f, d)), whole((d, d)),
         whole((d, f))] + [m[0] for m in more],
        [
            shaped((t, width), BF), shaped((t, width), BF), shaped((t, d), F32), shaped((t, f), BF), shaped((t, f), BF),
            shaped((t, d), F32), shaped((t, d), BF), shaped((t, d), BF), shaped((f, d), BF), shaped((d, d), BF),
            shaped((d, f), BF),
        ] + [m[1] for m in more],
        [
            pltpu.VMEM((ROWS, f), F32), pltpu.VMEM((ROWS, f), F32), pltpu.VMEM((ROWS, f), F32), pltpu.SemaphoreType.DMA,
            pltpu.SemaphoreType.DMA,
        ],
        (t // ROWS,), 60, "ffn_both", 2 * t * d * (2 * d + 3 * f), 6 * d * f + 4 * t * f + 30 * t * d,
    )


def result_kernel(m_ref, x1_ref, wd_ref, y_ref):
    y_ref[...] = (x1_ref[...] + dot(m_ref[...], wd_ref[...])).astype(BF)


def down_forward(m, x1, w_down):
    t, d = x1.shape
    f = m.shape[1]
    return pl.pallas_call(
        result_kernel,
        grid=(t // ROWS,),
        in_specs=[rows(f), rows(d), whole((f, d))],
        out_specs=rows(d),
        out_shape=shaped((t, d), BF),
        compiler_params=params(48),
        cost_estimate=pl.CostEstimate(flops=2 * t * d * f, transcendentals=0, bytes_accessed=2 * d * f + 2 * t * f + 6 * t * d),
        name="down_forward",
    )(m, x1, w_down)


def grads_kernel(split, products, *refs):
    back, *refs = refs
    count = 2 if split else 1
    left, refs = refs[: len(products) * count], refs[len(products) * count :]
    right, refs = refs[: len(products) * count], refs[len(products) * count :]
    outs, refs = refs[: 4 if split else len(products)], refs[4 if split else len(products) :]
    tile, turned = refs[0], refs[1:]
    step = pl.program_id(0)
    first, row = 0, 0
    for n, (by_left, tiles, size) in enumerate(products):
        mine = [left[n * count + c] for c in range(count)]
        value = [right[n * count + c] for c in range(count)]

        if not by_left:

            @pl.when(step == first)
            def _():
                t = mine[0].shape[0]
                for c in range(count):
                    flat = mine[c][...] if len(mine[c].shape) == 2 else mine[c][0]
                    turned[0][:, c * t : (c + 1) * t] = flat.T

        @pl.when((step >= first) & (step < first + tiles))
        def _():
            total = None
            for c in range(count):
                v = value[c][...] if len(value[c].shape) == 2 else value[c][0]
                t = v.shape[0]
                if by_left:
                    part = dot(mine[c][...], v, ((0,), (0,)))
                else:
                    part = dot(turned[0][:, c * t : (c + 1) * t], v)
                total = part if total is None else total + part
            if not split:
                outs[n][...] = total
            else:
                tile[...] = total
                if by_left:
                    owners = tile.shape[0] // size
                    for e in range(owners):
                        at = back[16 + (step - first) * owners + e]
                        for q in range(4):

                            @pl.when(at // 4 == q)
                            def _():
                                block = tile[e * size : (e + 1) * size, :]
                                outs[q][at - 4 * q, row : row + size, :] = block.astype(outs[q].dtype)
                else:
                    deal(back, tile, outs, row + pl.multiple_of((step - first) * size, 8), size)

        first += tiles
        row += size if by_left else tiles * size


def weight_grads(split, back, products):
    count = 2 if split else 1
    t = products[0][0][0].shape[0]
    left_specs, right_specs, lefts, rights, plan = [], [], [], [], []
    out_specs, out_shape = [], []
    at = row = 0
    for left, right, tiles, by_left in products:
        width = 0
        for c in range(count):
            a, b = left[c], right[c]
            a, part = a if isinstance(a, tuple) else (a, None)

            if by_left and c == 0:
                tiles = tiles // count
                width = a.shape[1] // (tiles * count)

            def step(i, at=at, tiles=tiles):
                return jnp.clip(i - at, 0, tiles - 1)

            if by_left:
                per = tiles // 2
                if split and c == 0:
                    left_specs.append(pl.BlockSpec(
                        (t, width), lambda i, back, step=step, per=per: (0, (2 * (step(i) // per) + back[32]) * per + step(i) % per)
                    ))
                else:
                    left_specs.append(pl.BlockSpec((t, width), lambda i, *_, step=step: (0, step(i))))
                right_specs.append(whole(b.shape))
            else:
                width = a.shape[-1]
                if part is None:
                    left_specs.append(whole(a.shape))
                else:
                    left_specs.append(pl.BlockSpec(
                        (1, t, width), lambda *_, part=part: (part, 0, 0), pipeline_mode=pl.Buffered(1)
                    ))
                if b.ndim == 3:
                    right_specs.append(pl.BlockSpec((1, t, LANES), lambda i, *_, step=step: (step(i), 0, 0)))
                else:
                    right_specs.append(pl.BlockSpec((t, LANES), lambda i, *_, step=step: (0, step(i))))
            lefts.append(a)
            rights.append(b)
        size = (width * tiles if by_left else width) // 16
        if not split:
            shape = (width * tiles, LANES) if by_left else (width, tiles * LANES)
            block = (width, LANES)
            out_specs.append(pl.BlockSpec(
                block, (lambda i, *_, step=step: (step(i), 0)) if by_left else (lambda i, *_, step=step: (0, step(i)))
            ))
            out_shape.append(shaped(shape, F32))
        plan.append((by_left, tiles, size))
        at += tiles
        row += size if by_left else tiles * size
    narrow = next(p[0][0].shape[1] for p in products if not p[3])
    if split:
        out_specs = [whole((4, row, LANES))] * 4
        out_shape = [shaped((4, row, LANES), BF)] * 4
    flops = 2 * count * t * narrow * at * LANES
    return prefetched(
        functools.partial(grads_kernel, split, tuple(plan)), back, lefts + rights, left_specs + right_specs,
        out_specs, out_shape, [pltpu.VMEM((narrow, LANES), F32), pltpu.VMEM((narrow, count * t), BF)],
        (at,), 60, "weight_grads", flops, flops // 256,
    )


def qkv_back_kernel(d_ref, x_ref, dx1_ref, w_ref, gain_ref, dx_ref):
    d = x_ref.shape[1]
    groups, _, span = d_ref.shape
    span //= 3
    dh = None
    for part in range(3):
        for g in range(groups):
            at = part * d + g * span
            piece = dot(d_ref[g, :, part * span : (part + 1) * span], w_ref[:, at : at + span], ((1,), (1,)))
            dh = piece if dh is None else dh + piece
    unit, inv = unit_norm(x_ref[...].astype(F32))
    dx_ref[...] = dx1_ref[...] + norm_back(dh, gain_ref[...], unit, inv)


def qkv_backward(d_qkv, tokens, dx1, w_qkv, gain):
    t, d = tokens.shape
    groups, _, span = d_qkv.shape
    return pl.pallas_call(
        qkv_back_kernel,
        grid=(t // ROWS,),
        in_specs=[pl.BlockSpec((groups, ROWS, span), lambda i: (0, i, 0))] + [rows(d)] * 2
        + [whole((d, 3 * d)), whole((1, d))],
        out_specs=rows(d),
        out_shape=shaped((t, d), F32),
        compiler_params=params(48),
        cost_estimate=pl.CostEstimate(flops=6 * t * d * d, transcendentals=0, bytes_accessed=6 * d * d + 16 * t * d),
        name="qkv_backward",
    )(d_qkv, tokens, dx1, w_qkv, gain)


def layout(doc_lengths, seq):
    docs = doc_lengths.shape[-1]
    upto = jnp.arange(docs)[:, None] <= jnp.arange(docs)[None, :]
    ends = jnp.sum(jnp.where(upto[None], doc_lengths[:, :, None], 0), axis=1)
    places = jnp.arange(seq, dtype=jnp.int32)
    passed = places[None, :, None] >= ends[:, None, :]
    start = jnp.sum(jnp.where(passed, doc_lengths[:, None, :], 0), axis=-1)
    valid = places[None, :] < ends[:, docs - 2 : docs - 1]
    return start.astype(jnp.int32), places[None, :] - start, valid


def tables(position):
    half = HEAD_DIM // 2
    lane = jnp.arange(PAIR)
    frequency = jnp.exp((lane % half).astype(F32) * (-2.0 * math.log(10000.0) / HEAD_DIM))
    angles = position.reshape(-1, 1).astype(F32) * frequency[None, :]
    sign = jnp.where(lane % HEAD_DIM < half, -1.0, 1.0)
    return jnp.cos(angles), jnp.sin(angles) * sign[None, :]


Z = 4
GROUPS = ((0, 2), (1, 3))


def index(x, core, z, y):
    return ((x * 2 + core) * Z + z) * 2 + y


def permute(value, move):
    places = [(x, c, z, y) for x in range(2) for c in range(2) for z in range(Z) for y in range(2)]
    return lax.ppermute(value, AXES, [(index(*p), index(*move(*p))) for p in places])


def over_x(v):
    return permute(v, lambda x, c, z, y: (1 - x, c, z, y))


def over_y(v):
    return permute(v, lambda x, c, z, y: (x, c, z, 1 - y))


def over_core(v):
    return permute(v, lambda x, c, z, y: (x, 1 - c, z, y))


def over_z(v, bits):
    return permute(v, lambda x, c, z, y: (x, c, z ^ bits, y))


def place():
    dp, fs = lax.axis_index("dp"), lax.axis_index("fsdp")
    return dp >> 1, dp & 1, fs >> 1, fs & 1


def gather_order():
    rows_of = []
    for core in range(2):
        for group, first in zip(GROUPS, ("x", "y")):
            for second in range(2):
                for one in range(2):
                    dx, dy = (one, second) if first == "x" else (second, one)
                    rows_of += [(dx, core, dz, dy) for dz in group]
    dx, dc, dz, dy = np.array(rows_of, np.int32).T
    x, c, z, y = place()
    order = index(x ^ dx, c ^ dc, z ^ dz, y ^ dy)
    return jnp.concatenate([order, c[None]]).astype(jnp.int32)


def scatter_order():
    rows_of = []
    for group, first in zip(GROUPS, ("y", "x")):
        for one in (1, 0):
            for second in (1, 0):
                dx, dy = (second, one) if first == "y" else (one, second)
                rows_of += [(dx, dz, dy) for dz in group]
    dx, dz, dy = np.array(rows_of, np.int32).T
    x, c, z, y = place()
    order = ((x ^ dx) * Z + (z ^ dz)) * 2 + (y ^ dy)
    spots = jnp.arange(len(rows_of), dtype=jnp.int32)
    where = jnp.sum(jnp.where(order[None, :] == spots[:, None], spots[None, :], 0), axis=1)
    return jnp.concatenate([order, where, c[None]]).astype(jnp.int32)


def tie(value, other):
    return lax.optimization_barrier((value, other))[0]


class Gather:
    def __init__(self, block):
        self.block = block

    def far_z(self, after=None):
        block = self.block if after is None else tie(self.block, after)
        self.even = jnp.stack([block, over_z(block, 2)])
        return self.even

    def near_z(self, after=None):
        if after is not None:
            self.even = tie(self.even, after)
        self.odd = over_z(self.even, 1)
        return self.odd

    def first(self):
        self.got = (over_x(self.even), over_y(self.odd))
        return self.got

    def second(self, after=None):
        got = self.got if after is None else tie(self.got, after)
        even, odd = jnp.concatenate([self.even, got[0]]), jnp.concatenate([self.odd, got[1]])
        self.near = [even, odd, over_core(even), over_core(odd)]
        self.far = [over_y(even), over_x(odd)]
        return self.far

    def core(self, after=None):
        far = self.far if after is None else tie(self.far, after)
        even, odd, even_core, odd_core = self.near
        return [even, far[0], odd, far[1], even_core, over_core(far[0]), odd_core, over_core(far[1])]


class Reduce:
    def __init__(self, send_a, keep_a, send_b, keep_b):
        self.sends, self.a, self.b = (send_a, send_b), keep_a.astype(F32), keep_b.astype(F32)

    def first(self, after=None):
        sends = self.sends if after is None else tie(self.sends, after)
        self.got = (over_y(sends[0]), over_x(sends[1]))
        return self.got

    def wait_for(self, after):
        if after is not None:
            self.got = tie(self.got, after)

    def second(self, after=None):
        self.wait_for(after)
        self.a = self.a + self.got[0].astype(F32)
        self.b = self.b + self.got[1].astype(F32)
        self.got = (over_x(self.a[:2].astype(BF)), over_y(self.b[:2].astype(BF)))
        return self.got

    def near_z(self, after=None):
        self.wait_for(after)
        self.a = self.a[2:] + self.got[0].astype(F32)
        self.got = over_z((self.b[2:] + self.got[1].astype(F32)).astype(BF), 1)
        return self.got

    def far_z(self, after=None):
        self.wait_for(after)
        self.a = self.a + self.got.astype(F32)
        self.got = over_z(self.a[1].astype(BF), 2)
        return self.got

    def own(self):
        return self.a[0] + self.got.astype(F32)


def unslab(block, width):
    size = block.shape[0] * LANES // width
    return jnp.concatenate([block[s * size : (s + 1) * size] for s in range(width // LANES)], axis=1)


def slab(block):
    return [block[:, s * LANES : (s + 1) * LANES] for s in range(block.shape[1] // LANES)]


def local(fast, tokens, doc_lengths, cotangent, w_qkv, w_out, w_up, w_down,
          gain_attn, gain_inner, gain_ffn, gain_mid):
    row_count = doc_lengths.shape[0]
    seq = tokens.shape[0] // row_count
    d, f = tokens.shape[1], w_up.shape[1]
    wide = min(seq, 512) // BLOCK + 1
    blocks = seq // BLOCK
    shards = (gain_attn, gain_inner, gain_ffn, gain_mid)
    sizes = [g.shape[0] for g in shards]

    start, position, valid = layout(doc_lengths, seq)
    cos, sin = tables(position)
    firsts = start[:, ::BLOCK] // BLOCK
    reach = (jnp.arange(blocks, dtype=jnp.int32)[None, :] - firsts + 1).reshape(-1)
    start_col = start.reshape(-1, 1)
    start_row = jnp.repeat(start, 8, axis=0)
    gy = jnp.where(valid.reshape(-1, 1), cotangent, jnp.zeros_like(cotangent))

    def scatter(g):
        return lax.psum_scatter(g, AXES, scatter_dimension=0, tiled=True)

    def gather(v):
        return lax.all_gather(v, AXES, axis=0, tiled=True)

    if fast:
        order, back = gather_order(), scatter_order()
        gains_row = jnp.pad(jnp.concatenate(shards)[None], ((0, 7), (0, LANES - sum(sizes))))
        one, two = (Gather(b) for b in pack(w_qkv, w_out, w_up, w_down, gains_row))
        seen = one.far_z()
        two.far_z(seen)
        one.even = tie(one.even, (cos, sin))
        one.near_z()
        one.first()
        one.second(two.even)
        two.near_z()
        two.first()
        parts_qkv = one.core()
        gy_both = (gy, over_core(gy))
        cos, sin = tie((cos, sin), (gy, start_col, start_row, reach, order, back))
        gains = [None]
    else:
        order = back = jnp.zeros((8,), jnp.int32)
        parts_qkv, parts_up, parts_down = [gather(w_qkv)], [gather(w_out), gather(w_up)], [gather(w_down)]
        gains = [gather(g).astype(F32).reshape(1, -1) for g in shards]

    h1, qkv, full_qkv, *rest = qkv_forward(fast, order, tokens, cos, sin, parts_qkv, gains[0], sizes)
    g_attn, g_inner, g_ffn, g_mid = rest if fast else gains
    if fast:
        two.second(g_attn)
        start_col = tie(start_col, (gy_both[1], two.near[2:]))
    mixed, lse = attention_forward(reach, qkv, start_col, row_count, wide)
    parts = two.core(lse) if fast else parts_up + parts_down
    a, h2, x1, m, dpre, dx1, low, d_mixed, full_down, _, _, *other = ffn_both(
        fast, order, mixed, tokens, gy, g_inner, g_ffn, g_mid, parts
    )

    def shared(value):
        return (value, over_core(value)) if fast else (value,)

    if fast:
        m_both = (m, over_core(other[1]))
        theirs = over_core(other[0])
        a_both, h2_both = (a, (theirs, 0)), (h2, (theirs, 1))
    else:
        gy_both, m_both, a_both, h2_both = (gy,), (m,), (a,), (h2,)
    low, dpre = shared(low), shared(dpre)

    def attend(group, groups, lse, so_far):
        return attention_backward(
            reach, qkv, d_mixed, mixed, lse, start_row, cos, sin, row_count, wide, group, groups, so_far
        )

    f = w_up.shape[1]
    d_qkv = attend(0, 1, lse, None)
    if fast:
        low = tie(low, d_qkv)
    grads = weight_grads(
        fast, back,
        [(m_both, gy_both, f // 384, True), (a_both, low, d // LANES, False), (h2_both, dpre, f // LANES, False)],
    )
    if fast:
        red = Reduce(*grads)
        first = red.first()
        h1 = tie(h1, grads[-1])
    d_qkv = attend(1, 2, tie(lse, grads[-1]), d_qkv)
    if fast:
        h1 = (h1[0], over_core(h1[1]))
        d_both = (d_qkv, over_core(tie(d_qkv, (first, h1[1]))))
        second = red.second(d_qkv)
        dx1 = tie(dx1, (d_qkv, first))
    else:
        d_both = (d_qkv,)
    grad_tokens = qkv_backward(d_qkv, tokens, dx1, full_qkv, g_attn)
    if fast:
        near = red.near_z(grad_tokens)
        h1 = tie(h1, (grad_tokens, second))
    grad_qkv = weight_grads(fast, back, [(h1, d_both, 3 * d // LANES, False)])
    if fast:
        red_qkv = Reduce(*grad_qkv)
        first = red_qkv.first()
        far = red.far_z(grad_qkv[-1])
        m = tie(m, (grad_qkv[-1], near))
    result = down_forward(m, x1, full_down)
    if fast:
        red_qkv.second((result, far))
        own = red.own()
        red_qkv.near_z()
        red_qkv.far_z()
        g_qkv = red_qkv.own()
        cuts = (w_down.shape[0], w_down.shape[0] + w_out.shape[0])
        own_down, grad_out, grad_up = own[: cuts[0]], own[cuts[0] : cuts[1]], unslab(own[cuts[1] :], f)
    else:
        own_down, grad_out, grad_up, g_qkv = (scatter(g.astype(BF)).astype(F32) for g in (*grads, *grad_qkv))
        g_qkv = jnp.concatenate(slab(g_qkv))
    size = w_qkv.shape[0]
    span = LANES // 3
    g_qkv = jnp.concatenate(
        [g_qkv[g * size : (g + 1) * size, p * span : (p + 1) * span] for p in range(3) for g in range(GRAD_GROUPS)], axis=1
    )
    pairs = ((g_qkv, w_qkv), (grad_out, w_out), (grad_up, w_up), (own_down, w_down))
    gain_grads = [jnp.sum(g * w.astype(F32), axis=1) / v.astype(F32) for (g, w), v in zip(pairs, shards)]
    return (result, grad_tokens, g_qkv, grad_out, grad_up, own_down, *gain_grads)


def solution(mesh):
    matrix, vector = P(AXES, None), P(AXES)
    fast = mesh.shape["dp"] == 4 and mesh.shape["fsdp"] == 2 * Z
    return jax.shard_map(
        functools.partial(local, fast),
        mesh=mesh,
        in_specs=(matrix,) * 7 + (vector,) * 4,
        out_specs=(matrix,) * 6 + (vector,) * 4,
        check_vma=False,
    )
```

```python
import functools
import math

import jax
import jax.numpy as jnp
import numpy as np
from jax import lax
from jax.experimental import pallas as pl
from jax.experimental.pallas import tpu as pltpu
from jax.sharding import PartitionSpec as P

HEADS = 12
HEAD_DIM = 64
PAIR = 2 * HEAD_DIM
PAIRS = HEADS // 2
EPSILON = 1e-05
MASKED_SCORE = -1e30
ROOT_HALF = 0.7071067811865476
INV_ROOT_TAU = 0.3989422804014327
BF = jnp.bfloat16
F32 = jnp.float32
MIB = 1 << 20
AXES = ("dp", "fsdp")
BLOCK = 256
ROWS = 256
LANES = 768
VMEM_MIB = 60
GRAD_GROUPS = 3


def dot(a, b, dims=((1,), (0,))):
    return lax.dot_general(a, b, (dims, ((), ())), preferred_element_type=F32)


def params(mib):
    return pltpu.CompilerParams(vmem_limit_bytes=max(mib, VMEM_MIB) * MIB)


def swap_halves(x):
    lane = lax.broadcasted_iota(jnp.int32, x.shape, 1)
    low = lax.rem(lane, HEAD_DIM) < HEAD_DIM // 2
    half = HEAD_DIM // 2
    return jnp.where(low, pltpu.roll(x, PAIR - half, 1), pltpu.roll(x, half, 1))


def unit_norm(x):
    mean = jnp.mean(x, axis=-1, keepdims=True)
    centred = x - mean
    inv = lax.rsqrt(jnp.mean(centred * centred, axis=-1, keepdims=True) + EPSILON)
    return centred * inv, inv


def norm_back(d_unit, unit, inv):
    return inv * (
        d_unit
        - jnp.mean(d_unit, axis=-1, keepdims=True)
        - unit * jnp.mean(d_unit * unit, axis=-1, keepdims=True)
    )


def whole(shape):
    return pl.BlockSpec(shape, lambda *_: (0,) * len(shape), pipeline_mode=pl.Buffered(1))


def rows(width, block=ROWS):
    return pl.BlockSpec((block, width), lambda i: (i, 0))


def shaped(shape, dtype):
    return jax.ShapeDtypeStruct(shape, dtype)


def hbm():
    return pl.BlockSpec(memory_space=pl.ANY)


def fetch(order, parts, places, sem):
    if len(parts) < 8 and parts[0].ndim == 2:
        for part, (_, _, buffer, _) in zip(parts, places):
            pltpu.make_async_copy(part, buffer, sem).start()
        return
    count = parts[0].shape[0]
    for p, part in enumerate(parts):
        for b in range(count):
            owner = b if order is None else order[p * count + b]
            for first, size, buffer, column in places:
                row = owner * size if order is None else pl.multiple_of(owner * size, 8)
                pltpu.make_async_copy(
                    part.at[b, pl.ds(first, size), :],
                    buffer.at[pl.ds(row, size), pl.ds(column, LANES)],
                    sem,
                ).start()


def arrive(buffers, sem):
    for buffer in buffers:
        pltpu.make_async_copy(buffer, buffer, sem).wait()


def deal(back, tile, outs, row, size):
    quarter = outs[0].shape[0]
    for q, out in enumerate(outs):

        @pl.loop(0, quarter)
        def _(j):
            block = tile[pl.ds(pl.multiple_of(back[q * quarter + j] * size, 8), size), :]
            out[j, pl.ds(row, size), :] = block.astype(out.dtype)


def slabs(first, size, buffer, width):
    return [(first + s * size, size, buffer, s * LANES) for s in range(width // LANES)]


def scale_rows(w, gain):
    n = w.shape[0]
    square = lax.broadcasted_iota(jnp.int32, (n, n), 0) == lax.broadcasted_iota(jnp.int32, (n, n), 1)
    return dot(jnp.where(square, gain.astype(F32), 0.0).astype(BF), w).astype(BF)


def pack_kernel(wq_ref, wo_ref, wu_ref, wd_ref, ga_ref, gi_ref, gf_ref, gm_ref, one_ref, two_ref):
    def place(out, row, ref, gain):
        for c in range(ref.shape[1] // LANES):
            out[row : row + ref.shape[0], :] = scale_rows(ref[:, c * LANES : (c + 1) * LANES], gain)
            row += ref.shape[0]
        return row

    place(one_ref, 0, wq_ref, ga_ref[...])
    row = 0
    for ref, gain in ((wd_ref, gm_ref), (wo_ref, gi_ref), (wu_ref, gf_ref)):
        row = place(two_ref, row, ref, gain[...])


def pack(w_qkv, w_out, w_up, w_down, gains):
    first = w_qkv.size // LANES
    second = (w_out.size + w_up.size + w_down.size) // LANES
    return pl.pallas_call(
        pack_kernel, out_shape=[shaped((first, LANES), BF), shaped((second, LANES), BF)], name="pack"
    )(w_qkv, w_out, w_up, w_down, *(g.reshape(1, -1) for g in gains))


def qkv_kernel(split, *refs):
    order, x_ref, cos_ref, sin_ref, *refs = refs
    parts, refs = refs[: 8 if split else 1], refs[8 if split else 1 :]
    h_refs, refs = (refs[:2], refs[2:]) if split else (refs[:1], refs[1:])
    qkv_ref, w_ref, sem = refs
    width = x_ref.shape[1]

    @pl.when(pl.program_id(0) == 0)
    def _():
        fetch(order, parts, slabs(0, width // 32, w_ref, 3 * width) if split else [(0, 0, w_ref, 0)], sem)

    unit, _ = unit_norm(x_ref[...].astype(F32))
    h = unit.astype(BF)
    store_low(split, order[32] if split else 0, h, h_refs)

    @pl.when(pl.program_id(0) == 0)
    def _():
        arrive([w_ref], sem)

    cos, sin = cos_ref[...], sin_ref[...]
    for part in range(3):
        y = dot(h, w_ref[:, part * width : (part + 1) * width])
        for c in range(width // PAIR):
            z = y[:, c * PAIR : (c + 1) * PAIR]
            if part < 2:
                z = z * cos + swap_halves(z) * sin
            if part == 0:
                z = z * (1.0 / math.sqrt(HEAD_DIM))
            at = part * width + c * PAIR
            qkv_ref[:, at : at + PAIR] = z.astype(BF)


def prefetched(kernel, order, inputs, in_specs, out_specs, out_shape, scratch, grid, mib, name, flops, data):
    return pl.pallas_call(
        kernel,
        grid_spec=pltpu.PrefetchScalarGridSpec(
            num_scalar_prefetch=1,
            grid=grid,
            in_specs=in_specs,
            out_specs=out_specs,
            scratch_shapes=scratch,
        ),
        out_shape=out_shape,
        compiler_params=params(mib),
        cost_estimate=pl.CostEstimate(flops=flops, transcendentals=0, bytes_accessed=data),
        name=name,
    )(order, *inputs)


def rows(width, block=ROWS):
    return pl.BlockSpec((block, width), lambda i, *_: (i, 0))


def whole(shape):
    return pl.BlockSpec(shape, lambda *_: (0,) * len(shape), pipeline_mode=pl.Buffered(1))


def qkv_forward(split, order, tokens, cos, sin, parts):
    t, d = tokens.shape
    n = 3 * d
    out_specs, out_shape = low_specs(split, t, d)
    lows = len(out_specs)
    outs = prefetched(
        functools.partial(qkv_kernel, split), order, [tokens, cos, sin, *parts],
        [rows(d), rows(PAIR), rows(PAIR)] + [hbm()] * len(parts),
        out_specs + [rows(n), whole((d, n))], out_shape + [shaped((t, n), BF), shaped((d, n), BF)],
        [pltpu.SemaphoreType.DMA], (t // ROWS,), 40, "qkv_forward", 2 * t * d * n, 4 * d * n + 12 * t * d,
    )
    return (outs[:lows], *outs[lows:])


def window(i, n):
    return slice((i - n + 1) * BLOCK, (i + 1) * BLOCK)


def head_masks(shape):
    lane = lax.broadcasted_iota(jnp.int32, shape, 1)
    return lane < HEAD_DIM


def attention_forward_kernel(wide, reach, q_ref, k_ref, v_ref, start_ref, o_ref, lse_ref, bias):
    row, pair = pl.program_id(0), pl.program_id(1)
    seq = q_ref.shape[0]
    blocks = seq // BLOCK

    @pl.when(pair == 0)
    def _():
        for i in range(blocks):
            at = slice(i * BLOCK, (i + 1) * BLOCK)
            shape = (BLOCK, wide * BLOCK)
            key = (i - wide + 1) * BLOCK + lax.broadcasted_iota(jnp.int32, shape, 1)
            query = i * BLOCK + lax.broadcasted_iota(jnp.int32, shape, 0)
            keep = (key >= start_ref[at, :]) & (key <= query)
            bias[at, :] = jnp.where(keep, 0.0, MASKED_SCORE)

    first = head_masks((BLOCK, PAIR))
    for i in range(blocks):
        at = slice(i * BLOCK, (i + 1) * BLOCK)
        most = min(wide, i + 1)
        for n in range(1, most + 1):

            @pl.when(reach[row * blocks + i] == n)
            def _():
                q = q_ref[at, :]
                w = window(i, n)
                k, v = k_ref[w, :], v_ref[w, :]
                b = bias[at, (wide - n) * BLOCK :]
                mask = head_masks(k.shape)
                zero = jnp.zeros_like(k)
                masks = (mask, jnp.logical_not(mask))
                scores = [dot(q, jnp.where(pick, k, zero), ((1,), (1,))) for pick in masks]
                total, lses = None, []
                for s, pick in zip(scores, masks):
                    s = s + b
                    top = jnp.max(s, axis=-1, keepdims=True)
                    p = jnp.exp(s - top)
                    den = jnp.sum(p, axis=-1, keepdims=True)
                    part = dot((p * (1.0 / den)).astype(BF), jnp.where(pick, v, zero))
                    total = part if total is None else total + part
                    lses.append(top + jnp.log(den))
                o_ref[at, :] = total
                both = jnp.where(first, lses[0], lses[1]).T
                lse_ref[0, 0:1, at] = both[0:1, :]
                lse_ref[0, 1:2, at] = both[HEAD_DIM : HEAD_DIM + 1, :]


def attention_forward(reach, qkv, start, row_count, wide):
    t = qkv.shape[0]
    seq = t // row_count
    d = qkv.shape[1] // 3

    def columns(part):
        return pl.BlockSpec((seq, PAIR), lambda r, p, *_: (r, part * PAIRS + p))

    return pl.pallas_call(
        functools.partial(attention_forward_kernel, wide),
        grid_spec=pltpu.PrefetchScalarGridSpec(
            num_scalar_prefetch=1,
            grid=(row_count, PAIRS),
            in_specs=[
                columns(0),
                columns(1),
                columns(2),
                pl.BlockSpec((seq, 1), lambda r, p, *_: (r, 0)),
            ],
            out_specs=[
                pl.BlockSpec((seq, PAIR), lambda r, p, *_: (r, p)),
                pl.BlockSpec((1, 8, seq), lambda r, p, *_: (r * PAIRS + p, 0, 0)),
            ],
            scratch_shapes=[pltpu.VMEM((seq, wide * BLOCK), F32)],
        ),
        out_shape=[shaped((t, d), F32), shaped((row_count * PAIRS, 8, seq), F32)],
        compiler_params=params(32),
        cost_estimate=pl.CostEstimate(
            flops=8 * t * d * BLOCK, transcendentals=t * HEADS * 512, bytes_accessed=12 * t * d
        ),
        name="attention_forward",
    )(reach, qkv, qkv, qkv, start)


def attention_backward_kernel(wide, reach, q_ref, k_ref, v_ref, do_ref, o_ref, lse_ref, start_ref, cos_ref, sin_ref, *refs):
    grad_ref, bias, ks, vs, qs, dos, dk_acc, dv_acc, dq_acc = refs[-9:]
    row, pair = pl.program_id(0), pl.program_id(1)
    seq = q_ref.shape[0]
    blocks = seq // BLOCK

    @pl.when(pair == 0)
    def _():
        for i in range(blocks):
            at = slice(i * BLOCK, (i + 1) * BLOCK)
            shape = (wide * BLOCK, BLOCK)
            key = (i - wide + 1) * BLOCK + lax.broadcasted_iota(jnp.int32, shape, 0)
            query = i * BLOCK + lax.broadcasted_iota(jnp.int32, shape, 1)
            keep = (key >= start_ref[0:1, at]) & (key <= query)
            bias[:, at] = jnp.where(keep, 0.0, MASKED_SCORE)

    mask = head_masks((seq, PAIR))
    for src, dst in ((k_ref, ks), (v_ref, vs), (q_ref, qs), (do_ref, dos)):
        x = src[...]
        zero = jnp.zeros_like(x)
        dst[0] = jnp.where(mask, x, zero)
        dst[1] = jnp.where(mask, zero, x)
    dk_acc[...] = jnp.zeros_like(dk_acc)
    dv_acc[...] = jnp.zeros_like(dv_acc)
    lane8 = lax.broadcasted_iota(jnp.int32, (8, PAIR), 1) // HEAD_DIM
    row8 = lax.broadcasted_iota(jnp.int32, (8, PAIR), 0)
    picks = (lane8 == row8).astype(F32)
    delta = lax.dot_general(
        picks, do_ref[...].astype(F32) * o_ref[...], (((1,), (1,)), ((), ())),
        precision=lax.Precision.HIGHEST, preferred_element_type=F32,
    )
    for i in range(blocks):
        at = slice(i * BLOCK, (i + 1) * BLOCK)
        most = min(wide, i + 1)
        for n in range(1, most + 1):

            @pl.when(reach[row * blocks + i] == n)
            def _():
                w = window(i, n)
                b = bias[(wide - n) * BLOCK :, at]
                q, do = q_ref[at, :], do_ref[at, :]
                ps, dss = [], []
                for h in range(2):
                    s = dot(ks[h, w, :], q, ((1,), (1,))) + b
                    p = jnp.exp(s - lse_ref[0, h : h + 1, at])
                    dp = dot(vs[h, w, :], do, ((1,), (1,)))
                    ds = (p * (dp - delta[h : h + 1, at])).astype(BF)
                    ps.append(p.astype(BF))
                    dss.append(ds)
                dv_acc[w, :] += dot(ps[0], dos[0, at, :]) + dot(ps[1], dos[1, at, :])
                dk_acc[w, :] += dot(dss[0], qs[0, at, :]) + dot(dss[1], qs[1, at, :])
                dq_acc[at, :] = dot(dss[0], ks[0, w, :], ((0,), (0,))) + dot(
                    dss[1], ks[1, w, :], ((0,), (0,))
                )

    cos, sin = cos_ref[...], sin_ref[...]
    dq = dq_acc[...] * (1.0 / math.sqrt(HEAD_DIM))
    dk = dk_acc[...]
    span = grad_ref.shape[2] // 3
    slot = lax.rem(pair, span // PAIR)
    grads = (dq * cos - swap_halves(dq) * sin, dk * cos - swap_halves(dk) * sin, dv_acc[...])
    for part, value in enumerate(grads):
        grad_ref[0, :, pl.ds(pl.multiple_of(part * span + slot * PAIR, PAIR), PAIR)] = value.astype(BF)


def attention_backward(reach, qkv, d_mixed, mixed, lse, start_row, cos, sin, row_count, wide, group, groups, so_far):
    pairs = PAIRS // GRAD_GROUPS
    t = qkv.shape[0]
    seq = t // row_count
    base = group * pairs
    span = 3 * pairs * PAIR

    def columns(part):
        return pl.BlockSpec((seq, PAIR), lambda r, p, *_: (r, part * PAIRS + base + p))

    table = pl.BlockSpec((seq, PAIR), lambda r, p, *_: (r, 0))
    inputs = [reach, qkv, qkv, qkv, d_mixed, mixed, lse, start_row, cos, sin]
    in_specs = [
        columns(0), columns(1), columns(2), columns(0), columns(0),
        pl.BlockSpec((1, 8, seq), lambda r, p, *_: (r * PAIRS + base + p, 0, 0)),
        pl.BlockSpec((8, seq), lambda r, p, *_: (r, 0)),
        table, table,
    ]
    aliases = {}
    if so_far is not None:
        aliases = {len(inputs): 0}
        inputs.append(so_far)
        in_specs.append(hbm())
    return pl.pallas_call(
        functools.partial(attention_backward_kernel, wide),
        grid_spec=pltpu.PrefetchScalarGridSpec(
            num_scalar_prefetch=1,
            grid=(row_count, pairs * groups),
            in_specs=in_specs,
            out_specs=pl.BlockSpec((1, seq, span), lambda r, p, *_: (group + p // pairs, r, 0)),
            scratch_shapes=[
                pltpu.VMEM((wide * BLOCK, seq), F32),
                pltpu.VMEM((2, seq, PAIR), BF),
                pltpu.VMEM((2, seq, PAIR), BF),
                pltpu.VMEM((2, seq, PAIR), BF),
                pltpu.VMEM((2, seq, PAIR), BF),
                pltpu.VMEM((seq, PAIR), F32),
                pltpu.VMEM((seq, PAIR), F32),
                pltpu.VMEM((seq, PAIR), F32),
            ],
        ),
        out_shape=shaped((GRAD_GROUPS, t, span), BF),
        input_output_aliases=aliases,
        compiler_params=params(40),
        cost_estimate=pl.CostEstimate(
            flops=20 * t * span * BLOCK // 3 * groups, transcendentals=t * HEADS * 128 * groups,
            bytes_accessed=20 * t * span // 3 * groups
        ),
        name="attention_backward",
    )(*inputs)


def halves(x):
    quarter = x.shape[1] // 4
    piece = [x[:, i * quarter : (i + 1) * quarter] for i in range(4)]
    return jnp.concatenate(piece[0::2], axis=1), jnp.concatenate(piece[1::2], axis=1)


def store_low(split, core, x, refs):
    if not split:
        refs[0][...] = x
        return
    pair = halves(x)
    for c in range(2):

        @pl.when(core == c)
        def _():
            refs[0][...] = pair[c]
            refs[1][...] = pair[1 - c]


def low_specs(split, t, d):
    if split:
        return [rows(d // 2)] * 2, [shaped((t, d // 2), BF)] * 2
    return [rows(d)], [shaped((t, d), BF)]


def ffn_kernel(split, *refs):
    order, o_ref, x_ref, gy_ref, *refs = refs
    count = 8 if split else 3
    parts, refs = refs[:count], refs[count:]
    a_ref, h2_ref, x1_ref, m_ref, dpre_ref, dx1_ref, low_ref, do_ref, wd_ref, wo_ref, wu_ref, *refs = refs
    theirs_ref, other_ref, *refs = refs if split else (None, None, *refs)
    act, slope, dm, out_sem, up_sem, down_sem = refs
    d, f = wu_ref.shape
    size, skip = d // 32, f // 32
    step = pl.program_id(0)
    core = order[32] if split else 0
    chunks = [slice(c, c + LANES) for c in range(0, f, LANES)]

    @pl.when(step == 0)
    def _():
        if split:
            fetch(order, parts, [(skip, size, wo_ref, 0)], out_sem)
            fetch(order, parts, slabs(skip + size, size, wu_ref, f), up_sem)
            fetch(order, parts, [(0, skip, wd_ref, 0)], down_sem)
        else:
            fetch(order, parts[:1], [(0, 0, wo_ref, 0)], out_sem)
            fetch(order, parts[1:2], [(0, 0, wu_ref, 0)], up_sem)
            fetch(order, parts[2:], [(0, 0, wd_ref, 0)], down_sem)

    mixed = o_ref[...]
    unit_in, inv_in = unit_norm(mixed)
    a = unit_in.astype(BF)
    store_low(split, core, a, (a_ref, theirs_ref.at[0] if split else None))

    @pl.when(step == 0)
    def _():
        arrive([wo_ref], out_sem)

    x1 = x_ref[...].astype(F32) + dot(a, wo_ref[...])
    x1_ref[...] = x1
    unit_two, inv_two = unit_norm(x1)
    h2 = unit_two.astype(BF)
    store_low(split, core, h2, (h2_ref, theirs_ref.at[1] if split else None))
    gy = gy_ref[...]

    @pl.when(step == 0)
    def _():
        arrive([wu_ref], up_sem)
        arrive([wd_ref], down_sem)

    total = None
    for at in chunks:
        hidden = dot(h2, wu_ref[:, at])
        dm[:, at] = dot(gy, wd_ref[at, :], ((1,), (1,)))
        cdf = 0.5 + 0.5 * lax.erf(hidden * ROOT_HALF)
        slope[:, at] = cdf + hidden * (jnp.exp(-0.5 * hidden * hidden) * INV_ROOT_TAU)
        value = hidden * cdf
        act[:, at] = value
        part = jnp.sum(value, axis=-1, keepdims=True)
        total = part if total is None else total + part
    mean = total * (1.0 / f)
    total = None
    for at in chunks:
        centred = act[:, at] - mean
        part = jnp.sum(centred * centred, axis=-1, keepdims=True)
        total = part if total is None else total + part
    inv = lax.rsqrt(total * (1.0 / f) + EPSILON)
    first = second = None
    for at in chunks:
        unit = (act[:, at] - mean) * inv
        act[:, at] = unit
        m_ref[:, at] = unit.astype(BF)
        d_unit = dm[:, at]
        part = jnp.sum(d_unit, axis=-1, keepdims=True)
        first = part if first is None else first + part
        part = jnp.sum(d_unit * unit, axis=-1, keepdims=True)
        second = part if second is None else second + part
    first, second = first * (1.0 / f), second * (1.0 / f)
    dh2 = None
    for at in chunks:
        d_act = inv * (dm[:, at] - first - act[:, at] * second)
        dpre = (d_act * slope[:, at]).astype(BF)
        dpre_ref[:, at] = dpre
        part = dot(dpre, wu_ref[:, at], ((1,), (1,)))
        dh2 = part if dh2 is None else dh2 + part
    dx1 = gy.astype(F32) + norm_back(dh2, unit_two, inv_two)
    dx1_ref[...] = dx1
    low = dx1.astype(BF)
    low_ref[...] = low
    da = dot(low, wo_ref[...], ((1,), (1,)))
    do_ref[...] = norm_back(da, unit_in, inv_in).astype(BF)

    if split:
        quarter = f // 4
        for j in range(2):
            at = pl.multiple_of((2 * j + 1 - core) * quarter, PAIR)
            other_ref[:, j * quarter : (j + 1) * quarter] = m_ref[:, pl.ds(at, quarter)]


def ffn_both(split, order, mixed, tokens, gy, parts, f):
    t, d = tokens.shape
    width = d // 2 if split else d
    more = [(rows(f // 2), shaped((t, f // 2), BF))] * split
    if split:
        theirs = pl.BlockSpec((2, ROWS, width), lambda i, *_: (0, i, 0))
        more.insert(0, (theirs, shaped((2, t, width), BF)))
    return prefetched(
        functools.partial(ffn_kernel, split), order, [mixed, tokens, gy, *parts],
        [rows(d), rows(d), rows(d)] + [hbm()] * len(parts),
        [rows(width), rows(width), rows(d), rows(f), rows(f), rows(d), rows(d), rows(d), whole((f, d)), whole((d, d)),
         whole((d, f))] + [m[0] for m in more],
        [
            shaped((t, width), BF), shaped((t, width), BF), shaped((t, d), F32), shaped((t, f), BF), shaped((t, f), BF),
            shaped((t, d), F32), shaped((t, d), BF), shaped((t, d), BF), shaped((f, d), BF), shaped((d, d), BF),
            shaped((d, f), BF),
        ] + [m[1] for m in more],
        [
            pltpu.VMEM((ROWS, f), F32), pltpu.VMEM((ROWS, f), F32), pltpu.VMEM((ROWS, f), F32), pltpu.SemaphoreType.DMA,
            pltpu.SemaphoreType.DMA, pltpu.SemaphoreType.DMA,
        ],
        (t // ROWS,), 60, "ffn_both", 2 * t * d * (2 * d + 3 * f), 6 * d * f + 4 * t * f + 30 * t * d,
    )


def result_kernel(m_ref, x1_ref, wd_ref, y_ref):
    y_ref[...] = (x1_ref[...] + dot(m_ref[...], wd_ref[...])).astype(BF)


def down_forward(m, x1, w_down):
    t, d = x1.shape
    f = m.shape[1]
    return pl.pallas_call(
        result_kernel,
        grid=(t // ROWS,),
        in_specs=[rows(f), rows(d), whole((f, d))],
        out_specs=rows(d),
        out_shape=shaped((t, d), BF),
        compiler_params=params(48),
        cost_estimate=pl.CostEstimate(flops=2 * t * d * f, transcendentals=0, bytes_accessed=2 * d * f + 2 * t * f + 6 * t * d),
        name="down_forward",
    )(m, x1, w_down)


def grads_kernel(split, products, *refs):
    back, *refs = refs
    count = 2 if split else 1
    left, refs = refs[: len(products) * count], refs[len(products) * count :]
    right, refs = refs[: len(products) * count], refs[len(products) * count :]
    outs, refs = refs[: 4 if split else len(products)], refs[4 if split else len(products) :]
    tile, turned = refs[0], refs[1:]
    step = pl.program_id(0)
    first, row = 0, 0
    for n, (by_left, tiles, size) in enumerate(products):
        mine = [left[n * count + c] for c in range(count)]
        value = [right[n * count + c] for c in range(count)]

        if not by_left:

            @pl.when(step == first)
            def _():
                t = mine[0].shape[0]
                for c in range(count):
                    flat = mine[c][...] if len(mine[c].shape) == 2 else mine[c][0]
                    turned[0][:, c * t : (c + 1) * t] = flat.T

        @pl.when((step >= first) & (step < first + tiles))
        def _():
            total = None
            for c in range(count):
                v = value[c][...] if len(value[c].shape) == 2 else value[c][0]
                t = v.shape[0]
                if by_left:
                    part = dot(mine[c][...], v, ((0,), (0,)))
                else:
                    part = dot(turned[0][:, c * t : (c + 1) * t], v)
                total = part if total is None else total + part
            if not split:
                outs[n][...] = total
            else:
                tile[...] = total
                if by_left:
                    owners = tile.shape[0] // size
                    for e in range(owners):
                        at = back[16 + (step - first) * owners + e]
                        for q in range(4):

                            @pl.when(at // 4 == q)
                            def _():
                                block = tile[e * size : (e + 1) * size, :]
                                outs[q][at - 4 * q, row : row + size, :] = block.astype(outs[q].dtype)
                else:
                    deal(back, tile, outs, row + pl.multiple_of((step - first) * size, 8), size)

        first += tiles
        row += size if by_left else tiles * size


def weight_grads(split, back, products):
    count = 2 if split else 1
    t = products[0][0][0].shape[0]
    left_specs, right_specs, lefts, rights, plan = [], [], [], [], []
    out_specs, out_shape = [], []
    at = row = 0
    for left, right, tiles, by_left in products:
        width = 0
        for c in range(count):
            a, b = left[c], right[c]
            a, part = a if isinstance(a, tuple) else (a, None)

            if by_left and c == 0:
                tiles = tiles // count
                width = a.shape[1] // (tiles * count)

            def step(i, at=at, tiles=tiles):
                return jnp.clip(i - at, 0, tiles - 1)

            if by_left:
                per = tiles // 2
                if split and c == 0:
                    left_specs.append(pl.BlockSpec(
                        (t, width), lambda i, back, step=step, per=per: (0, (2 * (step(i) // per) + back[32]) * per + step(i) % per)
                    ))
                else:
                    left_specs.append(pl.BlockSpec((t, width), lambda i, *_, step=step: (0, step(i))))
                right_specs.append(whole(b.shape))
            else:
                width = a.shape[-1]
                if part is None:
                    left_specs.append(whole(a.shape))
                else:
                    left_specs.append(pl.BlockSpec(
                        (1, t, width), lambda *_, part=part: (part, 0, 0), pipeline_mode=pl.Buffered(1)
                    ))
                if b.ndim == 3:
                    right_specs.append(pl.BlockSpec((1, t, LANES), lambda i, *_, step=step: (step(i), 0, 0)))
                else:
                    right_specs.append(pl.BlockSpec((t, LANES), lambda i, *_, step=step: (0, step(i))))
            lefts.append(a)
            rights.append(b)
        size = (width * tiles if by_left else width) // 16
        if not split:
            shape = (width * tiles, LANES) if by_left else (width, tiles * LANES)
            block = (width, LANES)
            out_specs.append(pl.BlockSpec(
                block, (lambda i, *_, step=step: (step(i), 0)) if by_left else (lambda i, *_, step=step: (0, step(i)))
            ))
            out_shape.append(shaped(shape, F32))
        plan.append((by_left, tiles, size))
        at += tiles
        row += size if by_left else tiles * size
    narrow = next(p[0][0].shape[1] for p in products if not p[3])
    if split:
        out_specs = [whole((4, row, LANES))] * 4
        out_shape = [shaped((4, row, LANES), BF)] * 4
    flops = 2 * count * t * narrow * at * LANES
    return prefetched(
        functools.partial(grads_kernel, split, tuple(plan)), back, lefts + rights, left_specs + right_specs,
        out_specs, out_shape, [pltpu.VMEM((narrow, LANES), F32), pltpu.VMEM((narrow, count * t), BF)],
        (at,), 60, "weight_grads", flops, flops // 256,
    )


def qkv_back_kernel(d_ref, x_ref, dx1_ref, w_ref, dx_ref):
    d = x_ref.shape[1]
    groups, _, span = d_ref.shape
    span //= 3
    dh = None
    for part in range(3):
        for g in range(groups):
            at = part * d + g * span
            piece = dot(d_ref[g, :, part * span : (part + 1) * span], w_ref[:, at : at + span], ((1,), (1,)))
            dh = piece if dh is None else dh + piece
    unit, inv = unit_norm(x_ref[...].astype(F32))
    dx_ref[...] = dx1_ref[...] + norm_back(dh, unit, inv)


def qkv_backward(d_qkv, tokens, dx1, w_qkv):
    t, d = tokens.shape
    groups, _, span = d_qkv.shape
    return pl.pallas_call(
        qkv_back_kernel,
        grid=(t // ROWS,),
        in_specs=[pl.BlockSpec((groups, ROWS, span), lambda i: (0, i, 0))] + [rows(d)] * 2
        + [whole((d, 3 * d))],
        out_specs=rows(d),
        out_shape=shaped((t, d), F32),
        compiler_params=params(48),
        cost_estimate=pl.CostEstimate(flops=6 * t * d * d, transcendentals=0, bytes_accessed=6 * d * d + 16 * t * d),
        name="qkv_backward",
    )(d_qkv, tokens, dx1, w_qkv)


def layout(doc_lengths, seq):
    docs = doc_lengths.shape[-1]
    upto = jnp.arange(docs)[:, None] <= jnp.arange(docs)[None, :]
    ends = jnp.sum(jnp.where(upto[None], doc_lengths[:, :, None], 0), axis=1)
    places = jnp.arange(seq, dtype=jnp.int32)
    passed = places[None, :, None] >= ends[:, None, :]
    start = jnp.sum(jnp.where(passed, doc_lengths[:, None, :], 0), axis=-1)
    valid = places[None, :] < ends[:, docs - 2 : docs - 1]
    return start.astype(jnp.int32), places[None, :] - start, valid


def tables(position):
    half = HEAD_DIM // 2
    lane = jnp.arange(PAIR)
    frequency = jnp.exp((lane % half).astype(F32) * (-2.0 * math.log(10000.0) / HEAD_DIM))
    angles = position.reshape(-1, 1).astype(F32) * frequency[None, :]
    sign = jnp.where(lane % HEAD_DIM < half, -1.0, 1.0)
    return jnp.cos(angles), jnp.sin(angles) * sign[None, :]


Z = 4
GROUPS = ((0, 2), (1, 3))


def index(x, core, z, y):
    return ((x * 2 + core) * Z + z) * 2 + y


def permute(value, move):
    places = [(x, c, z, y) for x in range(2) for c in range(2) for z in range(Z) for y in range(2)]
    return lax.ppermute(value, AXES, [(index(*p), index(*move(*p))) for p in places])


def over_x(v):
    return permute(v, lambda x, c, z, y: (1 - x, c, z, y))


def over_y(v):
    return permute(v, lambda x, c, z, y: (x, c, z, 1 - y))


def over_core(v):
    return permute(v, lambda x, c, z, y: (x, 1 - c, z, y))


def over_z(v, bits):
    return permute(v, lambda x, c, z, y: (x, c, z ^ bits, y))


def place():
    dp, fs = lax.axis_index("dp"), lax.axis_index("fsdp")
    return dp >> 1, dp & 1, fs >> 1, fs & 1


def gather_order():
    rows_of = []
    for core in range(2):
        for group, first in zip(GROUPS, ("x", "y")):
            for second in range(2):
                for one in range(2):
                    dx, dy = (one, second) if first == "x" else (second, one)
                    rows_of += [(dx, core, dz, dy) for dz in group]
    dx, dc, dz, dy = np.array(rows_of, np.int32).T
    x, c, z, y = place()
    order = index(x ^ dx, c ^ dc, z ^ dz, y ^ dy)
    return jnp.concatenate([order, c[None]]).astype(jnp.int32)


def scatter_order():
    rows_of = []
    for group, first in zip(GROUPS, ("y", "x")):
        for one in (1, 0):
            for second in (1, 0):
                dx, dy = (second, one) if first == "y" else (one, second)
                rows_of += [(dx, dz, dy) for dz in group]
    dx, dz, dy = np.array(rows_of, np.int32).T
    x, c, z, y = place()
    order = ((x ^ dx) * Z + (z ^ dz)) * 2 + (y ^ dy)
    spots = jnp.arange(len(rows_of), dtype=jnp.int32)
    where = jnp.sum(jnp.where(order[None, :] == spots[:, None], spots[None, :], 0), axis=1)
    return jnp.concatenate([order, where, c[None]]).astype(jnp.int32)


def tie(value, other):
    return lax.optimization_barrier((value, other))[0]


class Gather:
    def __init__(self, block):
        self.block = block

    def far_z(self, after=None):
        block = self.block if after is None else tie(self.block, after)
        self.even = jnp.stack([block, over_z(block, 2)])
        return self.even

    def near_z(self, after=None):
        if after is not None:
            self.even = tie(self.even, after)
        self.odd = over_z(self.even, 1)
        return self.odd

    def first(self):
        self.got = (over_x(self.even), over_y(self.odd))
        return self.got

    def second(self, after=None):
        got = self.got if after is None else tie(self.got, after)
        even, odd = jnp.concatenate([self.even, got[0]]), jnp.concatenate([self.odd, got[1]])
        self.near = [even, odd, over_core(even), over_core(odd)]
        self.far = [over_y(even), over_x(odd)]
        return self.far

    def core(self, after=None):
        far = self.far if after is None else tie(self.far, after)
        even, odd, even_core, odd_core = self.near
        return [even, far[0], odd, far[1], even_core, over_core(far[0]), odd_core, over_core(far[1])]


class Reduce:
    def __init__(self, send_a, keep_a, send_b, keep_b):
        self.sends, self.a, self.b = (send_a, send_b), keep_a.astype(F32), keep_b.astype(F32)

    def first(self, after=None):
        sends = self.sends if after is None else tie(self.sends, after)
        self.got = (over_y(sends[0]), over_x(sends[1]))
        return self.got

    def wait_for(self, after):
        if after is not None:
            self.got = tie(self.got, after)

    def second(self, after=None):
        self.wait_for(after)
        self.a = self.a + self.got[0].astype(F32)
        self.b = self.b + self.got[1].astype(F32)
        self.got = (over_x(self.a[:2].astype(BF)), over_y(self.b[:2].astype(BF)))
        return self.got

    def near_z(self, after=None):
        self.wait_for(after)
        self.a = self.a[2:] + self.got[0].astype(F32)
        self.got = over_z((self.b[2:] + self.got[1].astype(F32)).astype(BF), 1)
        return self.got

    def far_z(self, after=None):
        self.wait_for(after)
        self.a = self.a + self.got.astype(F32)
        self.got = over_z(self.a[1].astype(BF), 2)
        return self.got

    def own(self):
        return self.a[0] + self.got.astype(F32)


def unslab(block, width):
    size = block.shape[0] * LANES // width
    return jnp.concatenate([block[s * size : (s + 1) * size] for s in range(width // LANES)], axis=1)


def slab(block):
    return [block[:, s * LANES : (s + 1) * LANES] for s in range(block.shape[1] // LANES)]


def local(fast, tokens, doc_lengths, cotangent, w_qkv, w_out, w_up, w_down,
          gain_attn, gain_inner, gain_ffn, gain_mid):
    row_count = doc_lengths.shape[0]
    seq = tokens.shape[0] // row_count
    d, f = tokens.shape[1], w_up.shape[1]
    wide = min(seq, 512) // BLOCK + 1
    blocks = seq // BLOCK
    shards = (gain_attn, gain_inner, gain_ffn, gain_mid)

    start, position, valid = layout(doc_lengths, seq)
    cos, sin = tables(position)
    firsts = start[:, ::BLOCK] // BLOCK
    reach = (jnp.arange(blocks, dtype=jnp.int32)[None, :] - firsts + 1).reshape(-1)
    start_col = start.reshape(-1, 1)
    start_row = jnp.repeat(start, 8, axis=0)
    gy = jnp.where(valid.reshape(-1, 1), cotangent, jnp.zeros_like(cotangent))

    def scatter(g):
        return lax.psum_scatter(g, AXES, scatter_dimension=0, tiled=True)

    def gather(v):
        return lax.all_gather(v, AXES, axis=0, tiled=True)

    if fast:
        order, back = gather_order(), scatter_order()
        one, two = (Gather(b) for b in pack(w_qkv, w_out, w_up, w_down, shards))
        seen = one.far_z()
        two.far_z(seen)
        one.even = tie(one.even, (cos, sin))
        one.near_z()
        one.first()
        one.second(two.even)
        two.near_z()
        two.first()
        parts_qkv = one.core()
        gy_both = (gy, over_core(gy))
        cos, sin = tie((cos, sin), (gy, start_col, start_row, reach, order, back))
    else:
        order = back = jnp.zeros((8,), jnp.int32)

        def scaled(w, gain):
            return gather((w.astype(F32) * gain.astype(F32)[:, None]).astype(BF))

        parts_qkv, parts_up, parts_down = [scaled(w_qkv, gain_attn)], [scaled(w_out, gain_inner), scaled(w_up, gain_ffn)], [scaled(w_down, gain_mid)]

    h1, qkv, full_qkv = qkv_forward(fast, order, tokens, cos, sin, parts_qkv)
    if fast:
        two.second(h1)
        start_col = tie(start_col, (gy_both[1], two.near[2:]))
    mixed, lse = attention_forward(reach, qkv, start_col, row_count, wide)
    parts = two.core(lse) if fast else parts_up + parts_down
    a, h2, x1, m, dpre, dx1, low, d_mixed, full_down, _, _, *other = ffn_both(
        fast, order, mixed, tokens, gy, parts, f
    )

    def shared(value):
        return (value, over_core(value)) if fast else (value,)

    if fast:
        m_both = (m, over_core(other[1]))
        theirs = over_core(other[0])
        a_both, h2_both = (a, (theirs, 0)), (h2, (theirs, 1))
    else:
        gy_both, m_both, a_both, h2_both = (gy,), (m,), (a,), (h2,)
    low, dpre = shared(low), shared(dpre)

    def attend(group, groups, lse, so_far):
        return attention_backward(
            reach, qkv, d_mixed, mixed, lse, start_row, cos, sin, row_count, wide, group, groups, so_far
        )

    f = w_up.shape[1]
    d_qkv = attend(0, 1, lse, None)
    if fast:
        low = tie(low, d_qkv)
    grads = weight_grads(
        fast, back,
        [(m_both, gy_both, f // 384, True), (a_both, low, d // LANES, False), (h2_both, dpre, f // LANES, False)],
    )
    if fast:
        red = Reduce(*grads)
        first = red.first()
        h1 = tie(h1, grads[-1])
    d_qkv = attend(1, 2, tie(lse, grads[-1]), d_qkv)
    if fast:
        h1 = (h1[0], over_core(h1[1]))
        d_both = (d_qkv, over_core(tie(d_qkv, (first, h1[1]))))
        second = red.second(d_qkv)
        dx1 = tie(dx1, (d_qkv, first))
    else:
        d_both = (d_qkv,)
    grad_tokens = qkv_backward(d_qkv, tokens, dx1, full_qkv)
    if fast:
        near = red.near_z(grad_tokens)
        h1 = tie(h1, (grad_tokens, second))
    grad_qkv = weight_grads(fast, back, [(h1, d_both, 3 * d // LANES, False)])
    if fast:
        red_qkv = Reduce(*grad_qkv)
        first = red_qkv.first()
        far = red.far_z(grad_qkv[-1])
        m = tie(m, (grad_qkv[-1], near))
    result = down_forward(m, x1, full_down)
    if fast:
        red_qkv.second((result, far))
        own = red.own()
        red_qkv.near_z()
        red_qkv.far_z()
        g_qkv = red_qkv.own()
        cuts = (w_down.shape[0], w_down.shape[0] + w_out.shape[0])
        own_down, grad_out, grad_up = own[: cuts[0]], own[cuts[0] : cuts[1]], unslab(own[cuts[1] :], f)
    else:
        own_down, grad_out, grad_up, g_qkv = (scatter(g.astype(BF)).astype(F32) for g in (*grads, *grad_qkv))
        g_qkv = jnp.concatenate(slab(g_qkv))
    size = w_qkv.shape[0]
    span = LANES // 3
    g_qkv = jnp.concatenate(
        [g_qkv[g * size : (g + 1) * size, p * span : (p + 1) * span] for p in range(3) for g in range(GRAD_GROUPS)], axis=1
    )
    raw = (g_qkv, grad_out, grad_up, own_down)
    gain_grads = [jnp.sum(g * w.astype(F32), axis=1) for g, w in zip(raw, (w_qkv, w_out, w_up, w_down))]
    weight_grads_of = [g * v.astype(F32)[:, None] for g, v in zip(raw, shards)]
    return (result, grad_tokens, *weight_grads_of, *gain_grads)


def solution(mesh):
    matrix, vector = P(AXES, None), P(AXES)
    fast = mesh.shape["dp"] == 4 and mesh.shape["fsdp"] == 2 * Z
    return jax.shard_map(
        functools.partial(local, fast),
        mesh=mesh,
        in_specs=(matrix,) * 7 + (vector,) * 4,
        out_specs=(matrix,) * 6 + (vector,) * 4,
        check_vma=False,
    )
```

```python
import functools
import math

import jax
import jax.numpy as jnp
import numpy as np
from jax import lax
from jax.experimental import pallas as pl
from jax.experimental.pallas import tpu as pltpu
from jax.sharding import PartitionSpec as P

HEADS = 12
HEAD_DIM = 64
PAIR = 2 * HEAD_DIM
PAIRS = HEADS // 2
EPSILON = 1e-05
MASKED_SCORE = -1e30
ROOT_HALF = 0.7071067811865476
INV_ROOT_TAU = 0.3989422804014327
BF = jnp.bfloat16
F32 = jnp.float32
MIB = 1 << 20
AXES = ("dp", "fsdp")
BLOCK = 256
ROWS = 256
LANES = 768
VMEM_MIB = 60
GRAD_GROUPS = 3


def dot(a, b, dims=((1,), (0,))):
    return lax.dot_general(a, b, (dims, ((), ())), preferred_element_type=F32)


def params(mib):
    return pltpu.CompilerParams(vmem_limit_bytes=max(mib, VMEM_MIB) * MIB)


def swap_halves(x):
    lane = lax.broadcasted_iota(jnp.int32, x.shape, 1)
    low = lax.rem(lane, HEAD_DIM) < HEAD_DIM // 2
    half = HEAD_DIM // 2
    return jnp.where(low, pltpu.roll(x, PAIR - half, 1), pltpu.roll(x, half, 1))


def unit_norm(x):
    mean = jnp.mean(x, axis=-1, keepdims=True)
    centred = x - mean
    inv = lax.rsqrt(jnp.mean(centred * centred, axis=-1, keepdims=True) + EPSILON)
    return centred * inv, inv


def norm_back(grad, gain, unit, inv):
    d_unit = grad * gain
    return inv * (
        d_unit
        - jnp.mean(d_unit, axis=-1, keepdims=True)
        - unit * jnp.mean(d_unit * unit, axis=-1, keepdims=True)
    )


def whole(shape):
    return pl.BlockSpec(shape, lambda *_: (0,) * len(shape), pipeline_mode=pl.Buffered(1))


def rows(width, block=ROWS):
    return pl.BlockSpec((block, width), lambda i: (i, 0))


def shaped(shape, dtype):
    return jax.ShapeDtypeStruct(shape, dtype)


def hbm():
    return pl.BlockSpec(memory_space=pl.ANY)


def fetch(order, parts, places, sem):
    if len(parts) < 8 and parts[0].ndim == 2:
        for part, (_, _, buffer, _) in zip(parts, places):
            pltpu.make_async_copy(part, buffer, sem).start()
        return
    count = parts[0].shape[0]
    for p, part in enumerate(parts):
        for b in range(count):
            owner = b if order is None else order[p * count + b]
            for first, size, buffer, column in places:
                row = owner * size if order is None else pl.multiple_of(owner * size, 8)
                pltpu.make_async_copy(
                    part.at[b, pl.ds(first, size), :],
                    buffer.at[pl.ds(row, size), pl.ds(column, LANES)],
                    sem,
                ).start()


def arrive(buffers, sem):
    for buffer in buffers:
        pltpu.make_async_copy(buffer, buffer, sem).wait()


def deal(back, tile, outs, row, size):
    quarter = outs[0].shape[0]
    for q, out in enumerate(outs):

        @pl.loop(0, quarter)
        def _(j):
            block = tile[pl.ds(pl.multiple_of(back[q * quarter + j] * size, 8), size), :]
            out[j, pl.ds(row, size), :] = block.astype(out.dtype)


def slabs(first, size, buffer, width):
    return [(first + s * size, size, buffer, s * LANES) for s in range(width // LANES)]


def pack_kernel(wq_ref, wo_ref, wu_ref, wd_ref, gains_ref, one_ref, two_ref):
    row = 0
    for c in range(wq_ref.shape[1] // LANES):
        one_ref[row : row + wq_ref.shape[0], :] = wq_ref[:, c * LANES : (c + 1) * LANES]
        row += wq_ref.shape[0]
    one_ref[row:, :] = gains_ref[...]
    row = 0
    for ref in (wd_ref, wo_ref, wu_ref):
        for c in range(ref.shape[1] // LANES):
            two_ref[row : row + ref.shape[0], :] = ref[:, c * LANES : (c + 1) * LANES]
            row += ref.shape[0]


def pack(w_qkv, w_out, w_up, w_down, gains):
    first = w_qkv.size // LANES + gains.shape[0]
    second = (w_out.size + w_up.size + w_down.size) // LANES
    return pl.pallas_call(
        pack_kernel, out_shape=[shaped((first, LANES), BF), shaped((second, LANES), BF)], name="pack"
    )(w_qkv, w_out, w_up, w_down, gains)


def spread(rows_in, offset, count, owners):
    lanes = rows_in.shape[1]
    wide = owners * count
    lane = lax.broadcasted_iota(jnp.int32, (lanes, wide), 0)
    column = lax.broadcasted_iota(jnp.int32, (lanes, wide), 1)
    pick = (lane - offset == lax.rem(column, count)).astype(F32).astype(BF)
    full = dot(rows_in, pick)
    owner = lax.broadcasted_iota(jnp.int32, (owners, wide), 0)
    column = lax.broadcasted_iota(jnp.int32, (owners, wide), 1)
    own = (column >= owner * count) & (column < owner * count + count)
    return jnp.sum(jnp.where(own, full, 0.0), axis=0, keepdims=True)


def qkv_kernel(split, sizes, *refs):
    if split:
        order, x_ref, cos_ref, sin_ref, *refs = refs
        parts, refs = refs[:8], refs[8:]
        h_ref, other_ref, qkv_ref, w_ref, ga_ref, gi_ref, gf_ref, gm_ref, gains, sem, gain_sem = refs
        h_refs = (h_ref, other_ref)
    else:
        order, x_ref, cos_ref, sin_ref, ga_ref, *refs = refs
        parts, refs = refs[:1], refs[1:]
        h_ref, qkv_ref, w_ref, sem = refs
        h_refs = (h_ref,)
    width = x_ref.shape[1]
    step = pl.program_id(0)
    if split:
        size = width // 32
        weight = slabs(0, size, w_ref, 3 * width)

        @pl.when(step == 0)
        def _():
            fetch(order, parts, [(3 * size, 8, gains, 0)], gain_sem)
            fetch(order, parts, weight, sem)
            arrive([gains], gain_sem)
            owner = lax.broadcasted_iota(jnp.int32, (32, 256), 0)
            lane = lax.broadcasted_iota(jnp.int32, (32, 256), 1)
            pick = (lane == owner * 8).astype(F32).astype(BF)
            per_owner = dot(pick, gains[:, :256]).astype(BF)
            at = 0
            for ref, count in zip((ga_ref, gi_ref, gf_ref, gm_ref), sizes):
                ref[...] = spread(per_owner, at, count, 32)
                at += count
            arrive([w_ref], sem)
    else:

        @pl.when(step == 0)
        def _():
            fetch(None, parts, [(0, 0, w_ref, 0)], sem)
            arrive([w_ref], sem)

    unit, _ = unit_norm(x_ref[...].astype(F32))
    h = (unit * ga_ref[...]).astype(BF)
    store_low(split, order[32] if split else 0, h, h_refs)
    cos, sin = cos_ref[...], sin_ref[...]
    for part in range(3):
        y = dot(h, w_ref[:, part * width : (part + 1) * width])
        for c in range(width // PAIR):
            z = y[:, c * PAIR : (c + 1) * PAIR]
            if part < 2:
                z = z * cos + swap_halves(z) * sin
            if part == 0:
                z = z * (1.0 / math.sqrt(HEAD_DIM))
            at = part * width + c * PAIR
            qkv_ref[:, at : at + PAIR] = z.astype(BF)


def prefetched(kernel, order, inputs, in_specs, out_specs, out_shape, scratch, grid, mib, name, flops, data):
    return pl.pallas_call(
        kernel,
        grid_spec=pltpu.PrefetchScalarGridSpec(
            num_scalar_prefetch=1,
            grid=grid,
            in_specs=in_specs,
            out_specs=out_specs,
            scratch_shapes=scratch,
        ),
        out_shape=out_shape,
        compiler_params=params(mib),
        cost_estimate=pl.CostEstimate(flops=flops, transcendentals=0, bytes_accessed=data),
        name=name,
    )(order, *inputs)


def rows(width, block=ROWS):
    return pl.BlockSpec((block, width), lambda i, *_: (i, 0))


def whole(shape):
    return pl.BlockSpec(shape, lambda *_: (0,) * len(shape), pipeline_mode=pl.Buffered(1))


def qkv_forward(split, order, tokens, cos, sin, parts, gain, sizes):
    t, d = tokens.shape
    n = 3 * d
    inputs = [tokens, cos, sin]
    in_specs = [rows(d), rows(PAIR), rows(PAIR)]
    out_specs, out_shape = low_specs(split, t, d)
    lows = len(out_specs)
    out_specs = out_specs + [rows(n), whole((d, n))]
    out_shape = out_shape + [shaped((t, n), BF), shaped((d, n), BF)]
    scratch = [pltpu.SemaphoreType.DMA]
    if split:
        widths = [32 * s for s in sizes]
        out_specs += [whole((1, w)) for w in widths]
        out_shape += [shaped((1, w), F32) for w in widths]
        scratch = [pltpu.VMEM((32 * 8, LANES), BF), pltpu.SemaphoreType.DMA, pltpu.SemaphoreType.DMA]
    else:
        inputs.append(gain)
        in_specs.append(whole((1, d)))
    outs = prefetched(
        functools.partial(qkv_kernel, split, sizes), order, inputs + list(parts), in_specs + [hbm()] * len(parts),
        out_specs, out_shape, scratch, (t // ROWS,), 40, "qkv_forward",
        2 * t * d * n, 4 * d * n + 12 * t * d,
    )
    return (outs[:lows], *outs[lows:])


def window(i, n):
    return slice((i - n + 1) * BLOCK, (i + 1) * BLOCK)


def head_masks(shape):
    lane = lax.broadcasted_iota(jnp.int32, shape, 1)
    return lane < HEAD_DIM


def attention_forward_kernel(wide, reach, q_ref, k_ref, v_ref, start_ref, o_ref, lse_ref, bias):
    row, pair = pl.program_id(0), pl.program_id(1)
    seq = q_ref.shape[0]
    blocks = seq // BLOCK

    @pl.when(pair == 0)
    def _():
        for i in range(blocks):
            at = slice(i * BLOCK, (i + 1) * BLOCK)
            shape = (BLOCK, wide * BLOCK)
            key = (i - wide + 1) * BLOCK + lax.broadcasted_iota(jnp.int32, shape, 1)
            query = i * BLOCK + lax.broadcasted_iota(jnp.int32, shape, 0)
            row_of = start_ref[0:1, at].astype(F32)
            start = jnp.broadcast_to(row_of, (PAIR, BLOCK)).T[:, 0:1].astype(jnp.int32)
            keep = (key >= start) & (key <= query)
            bias[at, :] = jnp.where(keep, 0.0, MASKED_SCORE)

    first = head_masks((BLOCK, PAIR))
    for i in range(blocks):
        at = slice(i * BLOCK, (i + 1) * BLOCK)
        most = min(wide, i + 1)
        for n in range(1, most + 1):

            @pl.when(reach[row * blocks + i] == n)
            def _():
                q = q_ref[at, :]
                w = window(i, n)
                k, v = k_ref[w, :], v_ref[w, :]
                b = bias[at, (wide - n) * BLOCK :]
                mask = head_masks(k.shape)
                zero = jnp.zeros_like(k)
                masks = (mask, jnp.logical_not(mask))
                scores = [dot(q, jnp.where(pick, k, zero), ((1,), (1,))) for pick in masks]
                total, lses = None, []
                for s, pick in zip(scores, masks):
                    s = s + b
                    top = jnp.max(s, axis=-1, keepdims=True)
                    p = jnp.exp(s - top)
                    den = jnp.sum(p, axis=-1, keepdims=True)
                    part = dot((p * (1.0 / den)).astype(BF), jnp.where(pick, v, zero))
                    total = part if total is None else total + part
                    lses.append(top + jnp.log(den))
                o_ref[at, :] = total
                both = jnp.where(first, lses[0], lses[1]).T
                lse_ref[0, 0:1, at] = both[0:1, :]
                lse_ref[0, 1:2, at] = both[HEAD_DIM : HEAD_DIM + 1, :]


def attention_forward(reach, qkv, start, row_count, wide):
    t = qkv.shape[0]
    seq = t // row_count
    d = qkv.shape[1] // 3

    def columns(part):
        return pl.BlockSpec((seq, PAIR), lambda r, p, *_: (r, part * PAIRS + p))

    return pl.pallas_call(
        functools.partial(attention_forward_kernel, wide),
        grid_spec=pltpu.PrefetchScalarGridSpec(
            num_scalar_prefetch=1,
            grid=(row_count, PAIRS),
            in_specs=[
                columns(0),
                columns(1),
                columns(2),
                pl.BlockSpec((8, seq), lambda r, p, *_: (r, 0)),
            ],
            out_specs=[
                pl.BlockSpec((seq, PAIR), lambda r, p, *_: (r, p)),
                pl.BlockSpec((1, 8, seq), lambda r, p, *_: (r * PAIRS + p, 0, 0)),
            ],
            scratch_shapes=[pltpu.VMEM((seq, wide * BLOCK), F32)],
        ),
        out_shape=[shaped((t, d), F32), shaped((row_count * PAIRS, 8, seq), F32)],
        compiler_params=params(32),
        cost_estimate=pl.CostEstimate(
            flops=8 * t * d * BLOCK, transcendentals=t * HEADS * 512, bytes_accessed=12 * t * d
        ),
        name="attention_forward",
    )(reach, qkv, qkv, qkv, start)


def attention_backward_kernel(wide, reach, q_ref, k_ref, v_ref, do_ref, o_ref, lse_ref, start_ref, cos_ref, sin_ref, *refs):
    grad_ref, bias, ks, vs, qs, dos, dk_acc, dv_acc, dq_acc = refs[-9:]
    row, pair = pl.program_id(0), pl.program_id(1)
    seq = q_ref.shape[0]
    blocks = seq // BLOCK

    @pl.when(pair == 0)
    def _():
        for i in range(blocks):
            at = slice(i * BLOCK, (i + 1) * BLOCK)
            shape = (wide * BLOCK, BLOCK)
            key = (i - wide + 1) * BLOCK + lax.broadcasted_iota(jnp.int32, shape, 0)
            query = i * BLOCK + lax.broadcasted_iota(jnp.int32, shape, 1)
            keep = (key >= start_ref[0:1, at]) & (key <= query)
            bias[:, at] = jnp.where(keep, 0.0, MASKED_SCORE)

    mask = head_masks((seq, PAIR))
    for src, dst in ((k_ref, ks), (v_ref, vs), (q_ref, qs), (do_ref, dos)):
        x = src[...]
        zero = jnp.zeros_like(x)
        dst[0] = jnp.where(mask, x, zero)
        dst[1] = jnp.where(mask, zero, x)
    dk_acc[...] = jnp.zeros_like(dk_acc)
    dv_acc[...] = jnp.zeros_like(dv_acc)
    lane8 = lax.broadcasted_iota(jnp.int32, (8, PAIR), 1) // HEAD_DIM
    row8 = lax.broadcasted_iota(jnp.int32, (8, PAIR), 0)
    picks = (lane8 == row8).astype(F32)
    delta = lax.dot_general(
        picks, do_ref[...].astype(F32) * o_ref[...], (((1,), (1,)), ((), ())),
        precision=lax.Precision.HIGHEST, preferred_element_type=F32,
    )
    for i in range(blocks):
        at = slice(i * BLOCK, (i + 1) * BLOCK)
        most = min(wide, i + 1)
        for n in range(1, most + 1):

            @pl.when(reach[row * blocks + i] == n)
            def _():
                w = window(i, n)
                b = bias[(wide - n) * BLOCK :, at]
                q, do = q_ref[at, :], do_ref[at, :]
                ps, dss = [], []
                for h in range(2):
                    s = dot(ks[h, w, :], q, ((1,), (1,))) + b
                    p = jnp.exp(s - lse_ref[0, h : h + 1, at])
                    dp = dot(vs[h, w, :], do, ((1,), (1,)))
                    ds = (p * (dp - delta[h : h + 1, at])).astype(BF)
                    ps.append(p.astype(BF))
                    dss.append(ds)
                dv_acc[w, :] += dot(ps[0], dos[0, at, :]) + dot(ps[1], dos[1, at, :])
                dk_acc[w, :] += dot(dss[0], qs[0, at, :]) + dot(dss[1], qs[1, at, :])
                dq_acc[at, :] = dot(dss[0], ks[0, w, :], ((0,), (0,))) + dot(
                    dss[1], ks[1, w, :], ((0,), (0,))
                )

    cos, sin = cos_ref[...], sin_ref[...]
    dq = dq_acc[...] * (1.0 / math.sqrt(HEAD_DIM))
    dk = dk_acc[...]
    span = grad_ref.shape[2] // 3
    slot = lax.rem(pair, span // PAIR)
    grads = (dq * cos - swap_halves(dq) * sin, dk * cos - swap_halves(dk) * sin, dv_acc[...])
    for part, value in enumerate(grads):
        grad_ref[0, :, pl.ds(pl.multiple_of(part * span + slot * PAIR, PAIR), PAIR)] = value.astype(BF)


def attention_backward(reach, qkv, d_mixed, mixed, lse, start_row, cos, sin, row_count, wide, group, groups, so_far):
    pairs = PAIRS // GRAD_GROUPS
    t = qkv.shape[0]
    seq = t // row_count
    base = group * pairs
    span = 3 * pairs * PAIR

    def columns(part):
        return pl.BlockSpec((seq, PAIR), lambda r, p, *_: (r, part * PAIRS + base + p))

    table = pl.BlockSpec((seq, PAIR), lambda r, p, *_: (r, 0))
    inputs = [reach, qkv, qkv, qkv, d_mixed, mixed, lse, start_row, cos, sin]
    in_specs = [
        columns(0), columns(1), columns(2), columns(0), columns(0),
        pl.BlockSpec((1, 8, seq), lambda r, p, *_: (r * PAIRS + base + p, 0, 0)),
        pl.BlockSpec((8, seq), lambda r, p, *_: (r, 0)),
        table, table,
    ]
    aliases = {}
    if so_far is not None:
        aliases = {len(inputs): 0}
        inputs.append(so_far)
        in_specs.append(hbm())
    return pl.pallas_call(
        functools.partial(attention_backward_kernel, wide),
        grid_spec=pltpu.PrefetchScalarGridSpec(
            num_scalar_prefetch=1,
            grid=(row_count, pairs * groups),
            in_specs=in_specs,
            out_specs=pl.BlockSpec((1, seq, span), lambda r, p, *_: (group + p // pairs, r, 0)),
            scratch_shapes=[
                pltpu.VMEM((wide * BLOCK, seq), F32),
                pltpu.VMEM((2, seq, PAIR), BF),
                pltpu.VMEM((2, seq, PAIR), BF),
                pltpu.VMEM((2, seq, PAIR), BF),
                pltpu.VMEM((2, seq, PAIR), BF),
                pltpu.VMEM((seq, PAIR), F32),
                pltpu.VMEM((seq, PAIR), F32),
                pltpu.VMEM((seq, PAIR), F32),
            ],
        ),
        out_shape=shaped((GRAD_GROUPS, t, span), BF),
        input_output_aliases=aliases,
        compiler_params=params(40),
        cost_estimate=pl.CostEstimate(
            flops=20 * t * span * BLOCK // 3 * groups, transcendentals=t * HEADS * 128 * groups,
            bytes_accessed=20 * t * span // 3 * groups
        ),
        name="attention_backward",
    )(*inputs)


def halves(x):
    quarter = x.shape[1] // 4
    piece = [x[:, i * quarter : (i + 1) * quarter] for i in range(4)]
    return jnp.concatenate(piece[0::2], axis=1), jnp.concatenate(piece[1::2], axis=1)


def store_low(split, core, x, refs):
    if not split:
        refs[0][...] = x
        return
    pair = halves(x)
    for c in range(2):

        @pl.when(core == c)
        def _():
            refs[0][...] = pair[c]
            refs[1][...] = pair[1 - c]


def low_specs(split, t, d):
    if split:
        return [rows(d // 2)] * 2, [shaped((t, d // 2), BF)] * 2
    return [rows(d)], [shaped((t, d), BF)]


def ffn_kernel(split, *refs):
    order, o_ref, x_ref, gy_ref, gi_ref, gf_ref, gm_ref, *refs = refs
    count = 8 if split else 3
    parts, refs = refs[:count], refs[count:]
    a_ref, h2_ref, x1_ref, m_ref, dpre_ref, dx1_ref, low_ref, do_ref, wd_ref, wo_ref, wu_ref, *refs = refs
    theirs_ref, other_ref, *refs = refs if split else (None, None, *refs)
    act, slope, dm, out_sem, up_sem, down_sem = refs
    d, f = wu_ref.shape
    size, skip = d // 32, f // 32
    step = pl.program_id(0)
    core = order[32] if split else 0
    chunks = [slice(c, c + LANES) for c in range(0, f, LANES)]

    @pl.when(step == 0)
    def _():
        if split:
            fetch(order, parts, [(skip, size, wo_ref, 0)], out_sem)
            fetch(order, parts, slabs(skip + size, size, wu_ref, f), up_sem)
            fetch(order, parts, [(0, skip, wd_ref, 0)], down_sem)
        else:
            fetch(order, parts[:1], [(0, 0, wo_ref, 0)], out_sem)
            fetch(order, parts[1:2], [(0, 0, wu_ref, 0)], up_sem)
            fetch(order, parts[2:], [(0, 0, wd_ref, 0)], down_sem)

    mixed = o_ref[...]
    unit_in, inv_in = unit_norm(mixed)
    a = (unit_in * gi_ref[...]).astype(BF)
    store_low(split, core, a, (a_ref, theirs_ref.at[0] if split else None))

    @pl.when(step == 0)
    def _():
        arrive([wo_ref], out_sem)

    x1 = x_ref[...].astype(F32) + dot(a, wo_ref[...])
    x1_ref[...] = x1
    unit_two, inv_two = unit_norm(x1)
    h2 = (unit_two * gf_ref[...]).astype(BF)
    store_low(split, core, h2, (h2_ref, theirs_ref.at[1] if split else None))
    gy = gy_ref[...]

    @pl.when(step == 0)
    def _():
        arrive([wu_ref], up_sem)
        arrive([wd_ref], down_sem)

    total = None
    for at in chunks:
        hidden = dot(h2, wu_ref[:, at])
        dm[:, at] = dot(gy, wd_ref[at, :], ((1,), (1,)))
        cdf = 0.5 + 0.5 * lax.erf(hidden * ROOT_HALF)
        slope[:, at] = cdf + hidden * (jnp.exp(-0.5 * hidden * hidden) * INV_ROOT_TAU)
        value = hidden * cdf
        act[:, at] = value
        part = jnp.sum(value, axis=-1, keepdims=True)
        total = part if total is None else total + part
    mean = total * (1.0 / f)
    total = None
    for at in chunks:
        centred = act[:, at] - mean
        part = jnp.sum(centred * centred, axis=-1, keepdims=True)
        total = part if total is None else total + part
    inv = lax.rsqrt(total * (1.0 / f) + EPSILON)
    first = second = None
    for at in chunks:
        gain = gm_ref[:, at]
        unit = (act[:, at] - mean) * inv
        act[:, at] = unit
        m_ref[:, at] = (unit * gain).astype(BF)
        d_unit = dm[:, at] * gain
        dm[:, at] = d_unit
        part = jnp.sum(d_unit, axis=-1, keepdims=True)
        first = part if first is None else first + part
        part = jnp.sum(d_unit * unit, axis=-1, keepdims=True)
        second = part if second is None else second + part
    first, second = first * (1.0 / f), second * (1.0 / f)
    dh2 = None
    for at in chunks:
        d_act = inv * (dm[:, at] - first - act[:, at] * second)
        dpre = (d_act * slope[:, at]).astype(BF)
        dpre_ref[:, at] = dpre
        part = dot(dpre, wu_ref[:, at], ((1,), (1,)))
        dh2 = part if dh2 is None else dh2 + part
    dx1 = gy.astype(F32) + norm_back(dh2, gf_ref[...], unit_two, inv_two)
    dx1_ref[...] = dx1
    low = dx1.astype(BF)
    low_ref[...] = low
    da = dot(low, wo_ref[...], ((1,), (1,)))
    do_ref[...] = norm_back(da, gi_ref[...], unit_in, inv_in).astype(BF)

    if split:
        quarter = f // 4
        for j in range(2):
            at = pl.multiple_of((2 * j + 1 - core) * quarter, PAIR)
            other_ref[:, j * quarter : (j + 1) * quarter] = m_ref[:, pl.ds(at, quarter)]


def ffn_both(split, order, mixed, tokens, gy, gain_inner, gain_ffn, gain_mid, parts):
    t, d = tokens.shape
    f = gain_mid.shape[1]
    width = d // 2 if split else d
    more = [(rows(f // 2), shaped((t, f // 2), BF))] * split
    if split:
        theirs = pl.BlockSpec((2, ROWS, width), lambda i, *_: (0, i, 0))
        more.insert(0, (theirs, shaped((2, t, width), BF)))
    return prefetched(
        functools.partial(ffn_kernel, split), order, [mixed, tokens, gy, gain_inner, gain_ffn, gain_mid, *parts],
        [rows(d), rows(d), rows(d), whole((1, d)), whole((1, d)), whole((1, f))] + [hbm()] * len(parts),
        [rows(width), rows(width), rows(d), rows(f), rows(f), rows(d), rows(d), rows(d), whole((f, d)), whole((d, d)),
         whole((d, f))] + [m[0] for m in more],
        [
            shaped((t, width), BF), shaped((t, width), BF), shaped((t, d), F32), shaped((t, f), BF), shaped((t, f), BF),
            shaped((t, d), F32), shaped((t, d), BF), shaped((t, d), BF), shaped((f, d), BF), shaped((d, d), BF),
            shaped((d, f), BF),
        ] + [m[1] for m in more],
        [
            pltpu.VMEM((ROWS, f), F32), pltpu.VMEM((ROWS, f), F32), pltpu.VMEM((ROWS, f), F32), pltpu.SemaphoreType.DMA,
            pltpu.SemaphoreType.DMA, pltpu.SemaphoreType.DMA,
        ],
        (t // ROWS,), 60, "ffn_both", 2 * t * d * (2 * d + 3 * f), 6 * d * f + 4 * t * f + 30 * t * d,
    )


def result_kernel(m_ref, x1_ref, wd_ref, y_ref):
    y_ref[...] = (x1_ref[...] + dot(m_ref[...], wd_ref[...])).astype(BF)


def down_forward(m, x1, w_down):
    t, d = x1.shape
    f = m.shape[1]
    return pl.pallas_call(
        result_kernel,
        grid=(t // ROWS,),
        in_specs=[rows(f), rows(d), whole((f, d))],
        out_specs=rows(d),
        out_shape=shaped((t, d), BF),
        compiler_params=params(48),
        cost_estimate=pl.CostEstimate(flops=2 * t * d * f, transcendentals=0, bytes_accessed=2 * d * f + 2 * t * f + 6 * t * d),
        name="down_forward",
    )(m, x1, w_down)


def grads_kernel(split, products, *refs):
    back, *refs = refs
    count = 2 if split else 1
    left, refs = refs[: len(products) * count], refs[len(products) * count :]
    right, refs = refs[: len(products) * count], refs[len(products) * count :]
    outs, refs = refs[: 4 if split else len(products)], refs[4 if split else len(products) :]
    tile, turned = refs[0], refs[1:]
    step = pl.program_id(0)
    first, row = 0, 0
    for n, (by_left, tiles, size) in enumerate(products):
        mine = [left[n * count + c] for c in range(count)]
        value = [right[n * count + c] for c in range(count)]

        if not by_left:

            @pl.when(step == first)
            def _():
                t = mine[0].shape[0]
                for c in range(count):
                    flat = mine[c][...] if len(mine[c].shape) == 2 else mine[c][0]
                    turned[0][:, c * t : (c + 1) * t] = flat.T

        @pl.when((step >= first) & (step < first + tiles))
        def _():
            total = None
            for c in range(count):
                v = value[c][...] if len(value[c].shape) == 2 else value[c][0]
                t = v.shape[0]
                if by_left:
                    part = dot(mine[c][...], v, ((0,), (0,)))
                else:
                    part = dot(turned[0][:, c * t : (c + 1) * t], v)
                total = part if total is None else total + part
            if not split:
                outs[n][...] = total
            else:
                tile[...] = total
                if by_left:
                    owners = tile.shape[0] // size
                    for e in range(owners):
                        at = back[16 + (step - first) * owners + e]
                        for q in range(4):

                            @pl.when(at // 4 == q)
                            def _():
                                block = tile[e * size : (e + 1) * size, :]
                                outs[q][at - 4 * q, row : row + size, :] = block.astype(outs[q].dtype)
                else:
                    deal(back, tile, outs, row + pl.multiple_of((step - first) * size, 8), size)

        first += tiles
        row += size if by_left else tiles * size


def weight_grads(split, back, products):
    count = 2 if split else 1
    t = products[0][0][0].shape[0]
    left_specs, right_specs, lefts, rights, plan = [], [], [], [], []
    out_specs, out_shape = [], []
    at = row = 0
    for left, right, tiles, by_left in products:
        width = 0
        for c in range(count):
            a, b = left[c], right[c]
            a, part = a if isinstance(a, tuple) else (a, None)

            if by_left and c == 0:
                tiles = tiles // count
                width = a.shape[1] // (tiles * count)

            def step(i, at=at, tiles=tiles):
                return jnp.clip(i - at, 0, tiles - 1)

            if by_left:
                per = tiles // 2
                if split and c == 0:
                    left_specs.append(pl.BlockSpec(
                        (t, width), lambda i, back, step=step, per=per: (0, (2 * (step(i) // per) + back[32]) * per + step(i) % per)
                    ))
                else:
                    left_specs.append(pl.BlockSpec((t, width), lambda i, *_, step=step: (0, step(i))))
                right_specs.append(whole(b.shape))
            else:
                width = a.shape[-1]
                if part is None:
                    left_specs.append(whole(a.shape))
                else:
                    left_specs.append(pl.BlockSpec(
                        (1, t, width), lambda *_, part=part: (part, 0, 0), pipeline_mode=pl.Buffered(1)
                    ))
                if b.ndim == 3:
                    right_specs.append(pl.BlockSpec((1, t, LANES), lambda i, *_, step=step: (step(i), 0, 0)))
                else:
                    right_specs.append(pl.BlockSpec((t, LANES), lambda i, *_, step=step: (0, step(i))))
            lefts.append(a)
            rights.append(b)
        size = (width * tiles if by_left else width) // 16
        if not split:
            shape = (width * tiles, LANES) if by_left else (width, tiles * LANES)
            block = (width, LANES)
            out_specs.append(pl.BlockSpec(
                block, (lambda i, *_, step=step: (step(i), 0)) if by_left else (lambda i, *_, step=step: (0, step(i)))
            ))
            out_shape.append(shaped(shape, F32))
        plan.append((by_left, tiles, size))
        at += tiles
        row += size if by_left else tiles * size
    narrow = next(p[0][0].shape[1] for p in products if not p[3])
    if split:
        out_specs = [whole((4, row, LANES))] * 4
        out_shape = [shaped((4, row, LANES), BF)] * 4
    flops = 2 * count * t * narrow * at * LANES
    return prefetched(
        functools.partial(grads_kernel, split, tuple(plan)), back, lefts + rights, left_specs + right_specs,
        out_specs, out_shape, [pltpu.VMEM((narrow, LANES), F32), pltpu.VMEM((narrow, count * t), BF)],
        (at,), 60, "weight_grads", flops, flops // 256,
    )


def qkv_back_kernel(d_ref, x_ref, dx1_ref, w_ref, gain_ref, dx_ref):
    d = x_ref.shape[1]
    groups, _, span = d_ref.shape
    span //= 3
    dh = None
    for part in range(3):
        for g in range(groups):
            at = part * d + g * span
            piece = dot(d_ref[g, :, part * span : (part + 1) * span], w_ref[:, at : at + span], ((1,), (1,)))
            dh = piece if dh is None else dh + piece
    unit, inv = unit_norm(x_ref[...].astype(F32))
    dx_ref[...] = dx1_ref[...] + norm_back(dh, gain_ref[...], unit, inv)


def qkv_backward(d_qkv, tokens, dx1, w_qkv, gain):
    t, d = tokens.shape
    groups, _, span = d_qkv.shape
    return pl.pallas_call(
        qkv_back_kernel,
        grid=(t // ROWS,),
        in_specs=[pl.BlockSpec((groups, ROWS, span), lambda i: (0, i, 0))] + [rows(d)] * 2
        + [whole((d, 3 * d)), whole((1, d))],
        out_specs=rows(d),
        out_shape=shaped((t, d), F32),
        compiler_params=params(48),
        cost_estimate=pl.CostEstimate(flops=6 * t * d * d, transcendentals=0, bytes_accessed=6 * d * d + 16 * t * d),
        name="qkv_backward",
    )(d_qkv, tokens, dx1, w_qkv, gain)


def layout(doc_lengths, seq):
    docs = doc_lengths.shape[-1]
    upto = jnp.arange(docs)[:, None] <= jnp.arange(docs)[None, :]
    ends = jnp.sum(jnp.where(upto[None], doc_lengths[:, :, None], 0), axis=1)
    places = jnp.arange(seq, dtype=jnp.int32)
    passed = places[None, :, None] >= ends[:, None, :]
    start = jnp.sum(jnp.where(passed, doc_lengths[:, None, :], 0), axis=-1)
    valid = places[None, :] < ends[:, docs - 2 : docs - 1]
    return start.astype(jnp.int32), places[None, :] - start, valid


def tables(position):
    half = HEAD_DIM // 2
    lane = jnp.arange(PAIR)
    frequency = jnp.exp((lane % half).astype(F32) * (-2.0 * math.log(10000.0) / HEAD_DIM))
    angles = position.reshape(-1, 1).astype(F32) * frequency[None, :]
    sign = jnp.where(lane % HEAD_DIM < half, -1.0, 1.0)
    return jnp.cos(angles), jnp.sin(angles) * sign[None, :]


Z = 4
GROUPS = ((0, 2), (1, 3))


def index(x, core, z, y):
    return ((x * 2 + core) * Z + z) * 2 + y


def permute(value, move):
    places = [(x, c, z, y) for x in range(2) for c in range(2) for z in range(Z) for y in range(2)]
    return lax.ppermute(value, AXES, [(index(*p), index(*move(*p))) for p in places])


def over_x(v):
    return permute(v, lambda x, c, z, y: (1 - x, c, z, y))


def over_y(v):
    return permute(v, lambda x, c, z, y: (x, c, z, 1 - y))


def over_core(v):
    return permute(v, lambda x, c, z, y: (x, 1 - c, z, y))


def over_z(v, bits):
    return permute(v, lambda x, c, z, y: (x, c, z ^ bits, y))


def place():
    dp, fs = lax.axis_index("dp"), lax.axis_index("fsdp")
    return dp >> 1, dp & 1, fs >> 1, fs & 1


def gather_order():
    rows_of = []
    for core in range(2):
        for group, first in zip(GROUPS, ("x", "y")):
            for second in range(2):
                for one in range(2):
                    dx, dy = (one, second) if first == "x" else (second, one)
                    rows_of += [(dx, core, dz, dy) for dz in group]
    dx, dc, dz, dy = np.array(rows_of, np.int32).T
    x, c, z, y = place()
    order = index(x ^ dx, c ^ dc, z ^ dz, y ^ dy)
    return jnp.concatenate([order, c[None]]).astype(jnp.int32)


def scatter_order():
    rows_of = []
    for group, first in zip(GROUPS, ("y", "x")):
        for one in (1, 0):
            for second in (1, 0):
                dx, dy = (second, one) if first == "y" else (one, second)
                rows_of += [(dx, dz, dy) for dz in group]
    dx, dz, dy = np.array(rows_of, np.int32).T
    x, c, z, y = place()
    order = ((x ^ dx) * Z + (z ^ dz)) * 2 + (y ^ dy)
    spots = jnp.arange(len(rows_of), dtype=jnp.int32)
    where = jnp.sum(jnp.where(order[None, :] == spots[:, None], spots[None, :], 0), axis=1)
    return jnp.concatenate([order, where, c[None]]).astype(jnp.int32)


def tie(value, other):
    return lax.optimization_barrier((value, other))[0]


class Gather:
    def __init__(self, block):
        self.block = block

    def far_z(self, after=None):
        block = self.block if after is None else tie(self.block, after)
        self.even = jnp.stack([block, over_z(block, 2)])
        return self.even

    def near_z(self, after=None):
        if after is not None:
            self.even = tie(self.even, after)
        self.odd = over_z(self.even, 1)
        return self.odd

    def first(self):
        self.got = (over_x(self.even), over_y(self.odd))
        return self.got

    def second(self, after=None):
        got = self.got if after is None else tie(self.got, after)
        even, odd = jnp.concatenate([self.even, got[0]]), jnp.concatenate([self.odd, got[1]])
        self.near = [even, odd, over_core(even), over_core(odd)]
        self.far = [over_y(even), over_x(odd)]
        return self.far

    def core(self, after=None):
        far = self.far if after is None else tie(self.far, after)
        even, odd, even_core, odd_core = self.near
        return [even, far[0], odd, far[1], even_core, over_core(far[0]), odd_core, over_core(far[1])]


def merge_kernel(keep_a, got_a, keep_b, got_b, send_a, next_a, send_b, next_b):
    half = send_a.shape[0]
    for keep, got, send, after in ((keep_a, got_a, send_a, next_a), (keep_b, got_b, send_b, next_b)):
        send[...] = (keep[:half].astype(F32) + got[:half].astype(F32)).astype(BF)
        after[...] = keep[half:].astype(F32) + got[half:].astype(F32)


def merge(keep_a, got_a, keep_b, got_b):
    count, size, width = keep_a.shape
    step = 24
    both = pl.BlockSpec((count, step, width), lambda i: (0, i, 0))
    half = pl.BlockSpec((count // 2, step, width), lambda i: (0, i, 0))
    shape = (count // 2, size, width)
    return pl.pallas_call(
        merge_kernel,
        grid=(size // step,),
        in_specs=[both] * 4,
        out_specs=[half] * 4,
        out_shape=[shaped(shape, BF), shaped(shape, F32)] * 2,
        cost_estimate=pl.CostEstimate(
            flops=2 * keep_a.size, transcendentals=0, bytes_accessed=12 * keep_a.size
        ),
        name="merge",
    )(keep_a, got_a, keep_b, got_b)


class Reduce:
    def __init__(self, send_a, keep_a, send_b, keep_b):
        self.sends, self.a, self.b = (send_a, send_b), keep_a, keep_b

    def first(self):
        self.got = (over_y(self.sends[0]), over_x(self.sends[1]))
        return self.got

    def wait_for(self, after):
        if after is not None:
            self.got = tie(self.got, after)

    def second(self, after=None):
        self.wait_for(after)
        send_a, self.a, send_b, self.b = merge(self.a, self.got[0], self.b, self.got[1])
        self.got = (over_x(send_a), over_y(send_b))
        return self.got

    def near_z(self, after=None):
        self.wait_for(after)
        self.a = self.a + self.got[0].astype(F32)
        self.got = over_z((self.b + self.got[1].astype(F32)).astype(BF), 1)
        return self.got

    def far_z(self, after=None):
        self.wait_for(after)
        self.a = self.a + self.got.astype(F32)
        self.got = over_z(self.a[1].astype(BF), 2)
        return self.got

    def own(self):
        return self.a[0] + self.got.astype(F32)


def unslab(block, width):
    size = block.shape[0] * LANES // width
    return jnp.concatenate([block[s * size : (s + 1) * size] for s in range(width // LANES)], axis=1)


def slab(block):
    return [block[:, s * LANES : (s + 1) * LANES] for s in range(block.shape[1] // LANES)]


def local(fast, tokens, doc_lengths, cotangent, w_qkv, w_out, w_up, w_down,
          gain_attn, gain_inner, gain_ffn, gain_mid):
    row_count = doc_lengths.shape[0]
    seq = tokens.shape[0] // row_count
    d, f = tokens.shape[1], w_up.shape[1]
    wide = min(seq, 512) // BLOCK + 1
    blocks = seq // BLOCK
    shards = (gain_attn, gain_inner, gain_ffn, gain_mid)
    sizes = [g.shape[0] for g in shards]

    start, position, valid = layout(doc_lengths, seq)
    cos, sin = tables(position)
    firsts = start[:, ::BLOCK] // BLOCK
    reach = (jnp.arange(blocks, dtype=jnp.int32)[None, :] - firsts + 1).reshape(-1)
    start_row = jnp.repeat(start, 8, axis=0)
    gy = jnp.where(valid.reshape(-1, 1), cotangent, jnp.zeros_like(cotangent))

    def scatter(g):
        return lax.psum_scatter(g, AXES, scatter_dimension=0, tiled=True)

    def gather(v):
        return lax.all_gather(v, AXES, axis=0, tiled=True)

    if fast:
        order, back = gather_order(), scatter_order()
        gains_row = jnp.pad(jnp.concatenate(shards)[None], ((0, 7), (0, LANES - sum(sizes))))
        one, two = (Gather(b) for b in pack(w_qkv, w_out, w_up, w_down, gains_row))
        seen = one.far_z()
        two.far_z(seen)
        one.even = tie(one.even, (cos, sin))
        one.near_z()
        one.first()
        one.second(two.even)
        two.near_z()
        two.first()
        parts_qkv = one.core()
        gy_both = (gy, over_core(gy))
        cos, sin = tie((cos, sin), (gy, start_row, reach, order, back))
        gains = [None]
    else:
        order = back = jnp.zeros((8,), jnp.int32)
        parts_qkv, parts_up, parts_down = [gather(w_qkv)], [gather(w_out), gather(w_up)], [gather(w_down)]
        gains = [gather(g).astype(F32).reshape(1, -1) for g in shards]

    h1, qkv, full_qkv, *rest = qkv_forward(fast, order, tokens, cos, sin, parts_qkv, gains[0], sizes)
    g_attn, g_inner, g_ffn, g_mid = rest if fast else gains
    if fast:
        two.second(g_attn)
        start_row = tie(start_row, (gy_both[1], two.near[2:]))
    mixed, lse = attention_forward(reach, qkv, start_row, row_count, wide)
    parts = two.core(lse) if fast else parts_up + parts_down
    a, h2, x1, m, dpre, dx1, low, d_mixed, full_down, _, _, *other = ffn_both(
        fast, order, mixed, tokens, gy, g_inner, g_ffn, g_mid, parts
    )

    def shared(value):
        return (value, over_core(value)) if fast else (value,)

    if fast:
        m_both = (m, over_core(other[1]))
        theirs = over_core(other[0])
        a_both, h2_both = (a, (theirs, 0)), (h2, (theirs, 1))
    else:
        gy_both, m_both, a_both, h2_both = (gy,), (m,), (a,), (h2,)
    low, dpre = shared(low), shared(dpre)

    def attend(group, groups, lse, so_far):
        return attention_backward(
            reach, qkv, d_mixed, mixed, lse, start_row, cos, sin, row_count, wide, group, groups, so_far
        )

    f = w_up.shape[1]
    d_qkv = attend(0, 1, lse, None)
    if fast:
        low = tie(low, d_qkv)
    grads = weight_grads(
        fast, back,
        [(m_both, gy_both, f // 384, True), (a_both, low, d // LANES, False), (h2_both, dpre, f // LANES, False)],
    )
    if fast:
        red = Reduce(*grads)
        first = red.first()
        h1 = tie(h1, grads[-1])
    d_qkv = attend(1, 2, tie(lse, grads[-1]), d_qkv)
    if fast:
        h1 = (h1[0], over_core(h1[1]))
        d_both = (d_qkv, over_core(tie(d_qkv, (first, h1[1]))))
        second = red.second(d_qkv)
        dx1 = tie(dx1, (d_qkv, first))
    else:
        d_both = (d_qkv,)
    grad_tokens = qkv_backward(d_qkv, tokens, dx1, full_qkv, g_attn)
    if fast:
        near = red.near_z(grad_tokens)
        h1 = tie(h1, (grad_tokens, second))
    grad_qkv = weight_grads(fast, back, [(h1, d_both, 3 * d // LANES, False)])
    if fast:
        red_qkv = Reduce(*grad_qkv)
        first = red_qkv.first()
        far = red.far_z(grad_qkv[-1])
        m = tie(m, (grad_qkv[-1], near))
    result = down_forward(m, x1, full_down)
    if fast:
        red_qkv.second((result, far))
        own = red.own()
        red_qkv.near_z()
        red_qkv.far_z()
        g_qkv = red_qkv.own()
        cuts = (w_down.shape[0], w_down.shape[0] + w_out.shape[0])
        own_down, grad_out, grad_up = own[: cuts[0]], own[cuts[0] : cuts[1]], unslab(own[cuts[1] :], f)
    else:
        own_down, grad_out, grad_up, g_qkv = (scatter(g.astype(BF)).astype(F32) for g in (*grads, *grad_qkv))
        g_qkv = jnp.concatenate(slab(g_qkv))
    size = w_qkv.shape[0]
    span = LANES // 3
    g_qkv = jnp.concatenate(
        [g_qkv[g * size : (g + 1) * size, p * span : (p + 1) * span] for p in range(3) for g in range(GRAD_GROUPS)], axis=1
    )
    pairs = ((g_qkv, w_qkv), (grad_out, w_out), (grad_up, w_up), (own_down, w_down))
    gain_grads = [jnp.sum(g * w.astype(F32), axis=1) / v.astype(F32) for (g, w), v in zip(pairs, shards)]
    return (result, grad_tokens, g_qkv, grad_out, grad_up, own_down, *gain_grads)


def solution(mesh):
    matrix, vector = P(AXES, None), P(AXES)
    fast = mesh.shape["dp"] == 4 and mesh.shape["fsdp"] == 2 * Z
    return jax.shard_map(
        functools.partial(local, fast),
        mesh=mesh,
        in_specs=(matrix,) * 7 + (vector,) * 4,
        out_specs=(matrix,) * 6 + (vector,) * 4,
        check_vma=False,
    )
```

```python
import functools
import math

import jax
import jax.numpy as jnp
import numpy as np
from jax import lax
from jax.experimental import pallas as pl
from jax.experimental.pallas import tpu as pltpu
from jax.sharding import PartitionSpec as P

HEADS = 12
HEAD_DIM = 64
PAIR = 2 * HEAD_DIM
PAIRS = HEADS // 2
EPSILON = 1e-05
MASKED_SCORE = -1e30
ROOT_HALF = 0.7071067811865476
INV_ROOT_TAU = 0.3989422804014327
BF = jnp.bfloat16
F32 = jnp.float32
MIB = 1 << 20
AXES = ("dp", "fsdp")
BLOCK = 256
ROWS = 256
LANES = 768
VMEM_MIB = 60
GRAD_GROUPS = 3


def dot(a, b, dims=((1,), (0,))):
    return lax.dot_general(a, b, (dims, ((), ())), preferred_element_type=F32)


def params(mib):
    return pltpu.CompilerParams(vmem_limit_bytes=max(mib, VMEM_MIB) * MIB)


def swap_halves(x):
    lane = lax.broadcasted_iota(jnp.int32, x.shape, 1)
    low = lax.rem(lane, HEAD_DIM) < HEAD_DIM // 2
    half = HEAD_DIM // 2
    return jnp.where(low, pltpu.roll(x, PAIR - half, 1), pltpu.roll(x, half, 1))


def unit_norm(x):
    mean = jnp.mean(x, axis=-1, keepdims=True)
    centred = x - mean
    inv = lax.rsqrt(jnp.mean(centred * centred, axis=-1, keepdims=True) + EPSILON)
    return centred * inv, inv


def norm_back(grad, gain, unit, inv):
    d_unit = grad * gain
    return inv * (
        d_unit
        - jnp.mean(d_unit, axis=-1, keepdims=True)
        - unit * jnp.mean(d_unit * unit, axis=-1, keepdims=True)
    )


def whole(shape):
    return pl.BlockSpec(shape, lambda *_: (0,) * len(shape), pipeline_mode=pl.Buffered(1))


def rows(width, block=ROWS):
    return pl.BlockSpec((block, width), lambda i: (i, 0))


def shaped(shape, dtype):
    return jax.ShapeDtypeStruct(shape, dtype)


def hbm():
    return pl.BlockSpec(memory_space=pl.ANY)


def fetch(order, parts, places, sem):
    if len(parts) < 8 and parts[0].ndim == 2:
        for part, (_, _, buffer, _) in zip(parts, places):
            pltpu.make_async_copy(part, buffer, sem).start()
        return
    count = parts[0].shape[0]
    for p, part in enumerate(parts):
        for b in range(count):
            owner = b if order is None else order[p * count + b]
            for first, size, buffer, column in places:
                row = owner * size if order is None else pl.multiple_of(owner * size, 8)
                pltpu.make_async_copy(
                    part.at[b, pl.ds(first, size), :],
                    buffer.at[pl.ds(row, size), pl.ds(column, LANES)],
                    sem,
                ).start()


def arrive(buffers, sem):
    for buffer in buffers:
        pltpu.make_async_copy(buffer, buffer, sem).wait()


def deal(back, tile, outs, row, size):
    quarter = outs[0].shape[0]
    for q, out in enumerate(outs):

        @pl.loop(0, quarter)
        def _(j):
            block = tile[pl.ds(pl.multiple_of(back[q * quarter + j] * size, 8), size), :]
            out[j, pl.ds(row, size), :] = block.astype(out.dtype)


def slabs(first, size, buffer, width):
    return [(first + s * size, size, buffer, s * LANES) for s in range(width // LANES)]


def pack_kernel(wq_ref, wo_ref, wu_ref, wd_ref, gains_ref, one_ref, two_ref):
    row = 0
    for c in range(wq_ref.shape[1] // LANES):
        one_ref[row : row + wq_ref.shape[0], :] = wq_ref[:, c * LANES : (c + 1) * LANES]
        row += wq_ref.shape[0]
    one_ref[row:, :] = gains_ref[...]
    row = 0
    for ref in (wd_ref, wo_ref, wu_ref):
        for c in range(ref.shape[1] // LANES):
            two_ref[row : row + ref.shape[0], :] = ref[:, c * LANES : (c + 1) * LANES]
            row += ref.shape[0]


def pack(w_qkv, w_out, w_up, w_down, gains):
    first = w_qkv.size // LANES + gains.shape[0]
    second = (w_out.size + w_up.size + w_down.size) // LANES
    return pl.pallas_call(
        pack_kernel, out_shape=[shaped((first, LANES), BF), shaped((second, LANES), BF)], name="pack"
    )(w_qkv, w_out, w_up, w_down, gains)


def spread(rows_in, offset, count, owners):
    lanes = rows_in.shape[1]
    wide = owners * count
    lane = lax.broadcasted_iota(jnp.int32, (lanes, wide), 0)
    column = lax.broadcasted_iota(jnp.int32, (lanes, wide), 1)
    pick = (lane - offset == lax.rem(column, count)).astype(F32).astype(BF)
    full = dot(rows_in, pick)
    owner = lax.broadcasted_iota(jnp.int32, (owners, wide), 0)
    column = lax.broadcasted_iota(jnp.int32, (owners, wide), 1)
    own = (column >= owner * count) & (column < owner * count + count)
    return jnp.sum(jnp.where(own, full, 0.0), axis=0, keepdims=True)


def qkv_kernel(split, sizes, *refs):
    if split:
        order, x_ref, cos_ref, sin_ref, *refs = refs
        parts, refs = refs[:8], refs[8:]
        h_ref, other_ref, qkv_ref, w_ref, ga_ref, gi_ref, gf_ref, gm_ref, gains, sem, gain_sem = refs
        h_refs = (h_ref, other_ref)
    else:
        order, x_ref, cos_ref, sin_ref, ga_ref, *refs = refs
        parts, refs = refs[:1], refs[1:]
        h_ref, qkv_ref, w_ref, sem = refs
        h_refs = (h_ref,)
    width = x_ref.shape[1]
    step = pl.program_id(0)
    if split:
        size = width // 32
        weight = slabs(0, size, w_ref, 3 * width)

        @pl.when(step == 0)
        def _():
            fetch(order, parts, [(3 * size, 8, gains, 0)], gain_sem)
            fetch(order, parts, weight, sem)
            arrive([gains], gain_sem)
            owner = lax.broadcasted_iota(jnp.int32, (32, 256), 0)
            lane = lax.broadcasted_iota(jnp.int32, (32, 256), 1)
            pick = (lane == owner * 8).astype(F32).astype(BF)
            per_owner = dot(pick, gains[:, :256]).astype(BF)
            at = 0
            for ref, count in zip((ga_ref, gi_ref, gf_ref, gm_ref), sizes):
                ref[...] = spread(per_owner, at, count, 32)
                at += count
            arrive([w_ref], sem)
    else:

        @pl.when(step == 0)
        def _():
            fetch(None, parts, [(0, 0, w_ref, 0)], sem)
            arrive([w_ref], sem)

    unit, _ = unit_norm(x_ref[...].astype(F32))
    h = (unit * ga_ref[...]).astype(BF)
    store_low(split, order[32] if split else 0, h, h_refs)
    cos, sin = cos_ref[...], sin_ref[...]
    for part in range(3):
        y = dot(h, w_ref[:, part * width : (part + 1) * width])
        for c in range(width // PAIR):
            z = y[:, c * PAIR : (c + 1) * PAIR]
            if part < 2:
                z = z * cos + swap_halves(z) * sin
            if part == 0:
                z = z * (1.0 / math.sqrt(HEAD_DIM))
            at = part * width + c * PAIR
            qkv_ref[:, at : at + PAIR] = z.astype(BF)


def prefetched(kernel, order, inputs, in_specs, out_specs, out_shape, scratch, grid, mib, name, flops, data):
    return pl.pallas_call(
        kernel,
        grid_spec=pltpu.PrefetchScalarGridSpec(
            num_scalar_prefetch=1,
            grid=grid,
            in_specs=in_specs,
            out_specs=out_specs,
            scratch_shapes=scratch,
        ),
        out_shape=out_shape,
        compiler_params=params(mib),
        cost_estimate=pl.CostEstimate(flops=flops, transcendentals=0, bytes_accessed=data),
        name=name,
    )(order, *inputs)


def rows(width, block=ROWS):
    return pl.BlockSpec((block, width), lambda i, *_: (i, 0))


def whole(shape):
    return pl.BlockSpec(shape, lambda *_: (0,) * len(shape), pipeline_mode=pl.Buffered(1))


def qkv_forward(split, order, tokens, cos, sin, parts, gain, sizes):
    t, d = tokens.shape
    n = 3 * d
    inputs = [tokens, cos, sin]
    in_specs = [rows(d), rows(PAIR), rows(PAIR)]
    out_specs, out_shape = low_specs(split, t, d)
    lows = len(out_specs)
    out_specs = out_specs + [rows(n), whole((d, n))]
    out_shape = out_shape + [shaped((t, n), BF), shaped((d, n), BF)]
    scratch = [pltpu.SemaphoreType.DMA]
    if split:
        widths = [32 * s for s in sizes]
        out_specs += [whole((1, w)) for w in widths]
        out_shape += [shaped((1, w), F32) for w in widths]
        scratch = [pltpu.VMEM((32 * 8, LANES), BF), pltpu.SemaphoreType.DMA, pltpu.SemaphoreType.DMA]
    else:
        inputs.append(gain)
        in_specs.append(whole((1, d)))
    outs = prefetched(
        functools.partial(qkv_kernel, split, sizes), order, inputs + list(parts), in_specs + [hbm()] * len(parts),
        out_specs, out_shape, scratch, (t // ROWS,), 40, "qkv_forward",
        2 * t * d * n, 4 * d * n + 12 * t * d,
    )
    return (outs[:lows], *outs[lows:])


def window(i, n):
    return slice((i - n + 1) * BLOCK, (i + 1) * BLOCK)


def head_masks(shape):
    lane = lax.broadcasted_iota(jnp.int32, shape, 1)
    return lane < HEAD_DIM


def attention_forward_kernel(wide, reach, q_ref, k_ref, v_ref, start_ref, o_ref, lse_ref, bias):
    row, pair = pl.program_id(0), pl.program_id(1)
    seq = q_ref.shape[0]
    blocks = seq // BLOCK

    @pl.when(pair == 0)
    def _():
        for i in range(blocks):
            at = slice(i * BLOCK, (i + 1) * BLOCK)
            shape = (BLOCK, wide * BLOCK)
            key = (i - wide + 1) * BLOCK + lax.broadcasted_iota(jnp.int32, shape, 1)
            query = i * BLOCK + lax.broadcasted_iota(jnp.int32, shape, 0)
            row_of = start_ref[0:1, at].astype(F32)
            start = jnp.broadcast_to(row_of, (PAIR, BLOCK)).T[:, 0:1].astype(jnp.int32)
            keep = (key >= start) & (key <= query)
            bias[at, :] = jnp.where(keep, 0.0, MASKED_SCORE)

    first = head_masks((BLOCK, PAIR))
    for i in range(blocks):
        at = slice(i * BLOCK, (i + 1) * BLOCK)
        most = min(wide, i + 1)
        for n in range(1, most + 1):

            @pl.when(reach[row * blocks + i] == n)
            def _():
                q = q_ref[at, :]
                w = window(i, n)
                k, v = k_ref[w, :], v_ref[w, :]
                b = bias[at, (wide - n) * BLOCK :]
                mask = head_masks(k.shape)
                zero = jnp.zeros_like(k)
                masks = (mask, jnp.logical_not(mask))
                scores = [dot(q, jnp.where(pick, k, zero), ((1,), (1,))) for pick in masks]
                total, lses = None, []
                for s, pick in zip(scores, masks):
                    s = s + b
                    top = jnp.max(s, axis=-1, keepdims=True)
                    p = jnp.exp(s - top)
                    den = jnp.sum(p, axis=-1, keepdims=True)
                    part = dot((p * (1.0 / den)).astype(BF), jnp.where(pick, v, zero))
                    total = part if total is None else total + part
                    lses.append(top + jnp.log(den))
                o_ref[at, :] = total
                both = jnp.where(first, lses[0], lses[1]).T
                lse_ref[0, 0:1, at] = both[0:1, :]
                lse_ref[0, 1:2, at] = both[HEAD_DIM : HEAD_DIM + 1, :]


def attention_forward(reach, qkv, start, row_count, wide):
    t = qkv.shape[0]
    seq = t // row_count
    d = qkv.shape[1] // 3

    def columns(part):
        return pl.BlockSpec((seq, PAIR), lambda r, p, *_: (r, part * PAIRS + p))

    return pl.pallas_call(
        functools.partial(attention_forward_kernel, wide),
        grid_spec=pltpu.PrefetchScalarGridSpec(
            num_scalar_prefetch=1,
            grid=(row_count, PAIRS),
            in_specs=[
                columns(0),
                columns(1),
                columns(2),
                pl.BlockSpec((8, seq), lambda r, p, *_: (r, 0)),
            ],
            out_specs=[
                pl.BlockSpec((seq, PAIR), lambda r, p, *_: (r, p)),
                pl.BlockSpec((1, 8, seq), lambda r, p, *_: (r * PAIRS + p, 0, 0)),
            ],
            scratch_shapes=[pltpu.VMEM((seq, wide * BLOCK), F32)],
        ),
        out_shape=[shaped((t, d), F32), shaped((row_count * PAIRS, 8, seq), F32)],
        compiler_params=params(32),
        cost_estimate=pl.CostEstimate(
            flops=8 * t * d * BLOCK, transcendentals=t * HEADS * 512, bytes_accessed=12 * t * d
        ),
        name="attention_forward",
    )(reach, qkv, qkv, qkv, start)


def attention_backward_kernel(wide, reach, q_ref, k_ref, v_ref, do_ref, o_ref, lse_ref, start_ref, cos_ref, sin_ref, *refs):
    grad_ref, bias, ks, vs, qs, dos, dk_acc, dv_acc, dq_acc = refs[-9:]
    row, pair = pl.program_id(0), pl.program_id(1)
    seq = q_ref.shape[0]
    blocks = seq // BLOCK

    @pl.when(pair == 0)
    def _():
        for i in range(blocks):
            at = slice(i * BLOCK, (i + 1) * BLOCK)
            shape = (wide * BLOCK, BLOCK)
            key = (i - wide + 1) * BLOCK + lax.broadcasted_iota(jnp.int32, shape, 0)
            query = i * BLOCK + lax.broadcasted_iota(jnp.int32, shape, 1)
            keep = (key >= start_ref[0:1, at]) & (key <= query)
            bias[:, at] = jnp.where(keep, 0.0, MASKED_SCORE)

    mask = head_masks((seq, PAIR))
    for src, dst in ((k_ref, ks), (v_ref, vs), (q_ref, qs), (do_ref, dos)):
        x = src[...]
        zero = jnp.zeros_like(x)
        dst[0] = jnp.where(mask, x, zero)
        dst[1] = jnp.where(mask, zero, x)
    dk_acc[...] = jnp.zeros_like(dk_acc)
    dv_acc[...] = jnp.zeros_like(dv_acc)
    lane8 = lax.broadcasted_iota(jnp.int32, (8, PAIR), 1) // HEAD_DIM
    row8 = lax.broadcasted_iota(jnp.int32, (8, PAIR), 0)
    picks = (lane8 == row8).astype(F32)
    delta = lax.dot_general(
        picks, do_ref[...].astype(F32) * o_ref[...], (((1,), (1,)), ((), ())),
        precision=lax.Precision.HIGHEST, preferred_element_type=F32,
    )
    for i in range(blocks):
        at = slice(i * BLOCK, (i + 1) * BLOCK)
        most = min(wide, i + 1)
        for n in range(1, most + 1):

            @pl.when(reach[row * blocks + i] == n)
            def _():
                w = window(i, n)
                b = bias[(wide - n) * BLOCK :, at]
                q, do = q_ref[at, :], do_ref[at, :]
                ps, dss = [], []
                for h in range(2):
                    s = dot(ks[h, w, :], q, ((1,), (1,))) + b
                    p = jnp.exp(s - lse_ref[0, h : h + 1, at])
                    dp = dot(vs[h, w, :], do, ((1,), (1,)))
                    ds = (p * (dp - delta[h : h + 1, at])).astype(BF)
                    ps.append(p.astype(BF))
                    dss.append(ds)
                dv_acc[w, :] += dot(ps[0], dos[0, at, :]) + dot(ps[1], dos[1, at, :])
                dk_acc[w, :] += dot(dss[0], qs[0, at, :]) + dot(dss[1], qs[1, at, :])
                dq_acc[at, :] = dot(dss[0], ks[0, w, :], ((0,), (0,))) + dot(
                    dss[1], ks[1, w, :], ((0,), (0,))
                )

    cos, sin = cos_ref[...], sin_ref[...]
    dq = dq_acc[...] * (1.0 / math.sqrt(HEAD_DIM))
    dk = dk_acc[...]
    span = grad_ref.shape[2] // 3
    slot = lax.rem(pair, span // PAIR)
    grads = (dq * cos - swap_halves(dq) * sin, dk * cos - swap_halves(dk) * sin, dv_acc[...])
    for part, value in enumerate(grads):
        grad_ref[0, :, pl.ds(pl.multiple_of(part * span + slot * PAIR, PAIR), PAIR)] = value.astype(BF)


def attention_backward(reach, qkv, d_mixed, mixed, lse, start_row, cos, sin, row_count, wide, group, groups, so_far):
    pairs = PAIRS // GRAD_GROUPS
    t = qkv.shape[0]
    seq = t // row_count
    base = group * pairs
    span = 3 * pairs * PAIR

    def columns(part):
        return pl.BlockSpec((seq, PAIR), lambda r, p, *_: (r, part * PAIRS + base + p))

    table = pl.BlockSpec((seq, PAIR), lambda r, p, *_: (r, 0))
    inputs = [reach, qkv, qkv, qkv, d_mixed, mixed, lse, start_row, cos, sin]
    in_specs = [
        columns(0), columns(1), columns(2), columns(0), columns(0),
        pl.BlockSpec((1, 8, seq), lambda r, p, *_: (r * PAIRS + base + p, 0, 0)),
        pl.BlockSpec((8, seq), lambda r, p, *_: (r, 0)),
        table, table,
    ]
    aliases = {}
    if so_far is not None:
        aliases = {len(inputs): 0}
        inputs.append(so_far)
        in_specs.append(hbm())
    return pl.pallas_call(
        functools.partial(attention_backward_kernel, wide),
        grid_spec=pltpu.PrefetchScalarGridSpec(
            num_scalar_prefetch=1,
            grid=(row_count, pairs * groups),
            in_specs=in_specs,
            out_specs=pl.BlockSpec((1, seq, span), lambda r, p, *_: (group + p // pairs, r, 0)),
            scratch_shapes=[
                pltpu.VMEM((wide * BLOCK, seq), F32),
                pltpu.VMEM((2, seq, PAIR), BF),
                pltpu.VMEM((2, seq, PAIR), BF),
                pltpu.VMEM((2, seq, PAIR), BF),
                pltpu.VMEM((2, seq, PAIR), BF),
                pltpu.VMEM((seq, PAIR), F32),
                pltpu.VMEM((seq, PAIR), F32),
                pltpu.VMEM((seq, PAIR), F32),
            ],
        ),
        out_shape=shaped((GRAD_GROUPS, t, span), BF),
        input_output_aliases=aliases,
        compiler_params=params(40),
        cost_estimate=pl.CostEstimate(
            flops=20 * t * span * BLOCK // 3 * groups, transcendentals=t * HEADS * 128 * groups,
            bytes_accessed=20 * t * span // 3 * groups
        ),
        name="attention_backward",
    )(*inputs)


def halves(x):
    quarter = x.shape[1] // 4
    piece = [x[:, i * quarter : (i + 1) * quarter] for i in range(4)]
    return jnp.concatenate(piece[0::2], axis=1), jnp.concatenate(piece[1::2], axis=1)


def store_low(split, core, x, refs):
    if not split:
        refs[0][...] = x
        return
    pair = halves(x)
    for c in range(2):

        @pl.when(core == c)
        def _():
            refs[0][...] = pair[c]
            refs[1][...] = pair[1 - c]


def low_specs(split, t, d):
    if split:
        return [rows(d // 2)] * 2, [shaped((t, d // 2), BF)] * 2
    return [rows(d)], [shaped((t, d), BF)]


def ffn_kernel(split, *refs):
    order, o_ref, x_ref, gy_ref, gi_ref, gf_ref, gm_ref, *refs = refs
    count = 8 if split else 3
    parts, refs = refs[:count], refs[count:]
    a_ref, h2_ref, x1_ref, m_ref, dpre_ref, dx1_ref, low_ref, do_ref, wd_ref, wo_ref, wu_ref, *refs = refs
    theirs_ref, other_ref, *refs = refs if split else (None, None, *refs)
    act, slope, dm, out_sem, up_sem, down_sem = refs
    d, f = wu_ref.shape
    size, skip = d // 32, f // 32
    step = pl.program_id(0)
    core = order[32] if split else 0
    chunks = [slice(c, c + LANES) for c in range(0, f, LANES)]

    @pl.when(step == 0)
    def _():
        if split:
            fetch(order, parts, [(skip, size, wo_ref, 0)], out_sem)
            fetch(order, parts, slabs(skip + size, size, wu_ref, f), up_sem)
            fetch(order, parts, [(0, skip, wd_ref, 0)], down_sem)
        else:
            fetch(order, parts[:1], [(0, 0, wo_ref, 0)], out_sem)
            fetch(order, parts[1:2], [(0, 0, wu_ref, 0)], up_sem)
            fetch(order, parts[2:], [(0, 0, wd_ref, 0)], down_sem)

    mixed = o_ref[...]
    unit_in, inv_in = unit_norm(mixed)
    a = (unit_in * gi_ref[...]).astype(BF)
    store_low(split, core, a, (a_ref, theirs_ref.at[0] if split else None))

    @pl.when(step == 0)
    def _():
        arrive([wo_ref], out_sem)

    x1 = x_ref[...].astype(F32) + dot(a, wo_ref[...])
    x1_ref[...] = x1
    unit_two, inv_two = unit_norm(x1)
    h2 = (unit_two * gf_ref[...]).astype(BF)
    store_low(split, core, h2, (h2_ref, theirs_ref.at[1] if split else None))
    gy = gy_ref[...]

    @pl.when(step == 0)
    def _():
        arrive([wu_ref], up_sem)
        arrive([wd_ref], down_sem)

    total = None
    for at in chunks:
        hidden = dot(h2, wu_ref[:, at])
        dm[:, at] = dot(gy, wd_ref[at, :], ((1,), (1,)))
        cdf = 0.5 + 0.5 * lax.erf(hidden * ROOT_HALF)
        slope[:, at] = cdf + hidden * (jnp.exp(-0.5 * hidden * hidden) * INV_ROOT_TAU)
        value = hidden * cdf
        act[:, at] = value
        part = jnp.sum(value, axis=-1, keepdims=True)
        total = part if total is None else total + part
    mean = total * (1.0 / f)
    total = None
    for at in chunks:
        centred = act[:, at] - mean
        part = jnp.sum(centred * centred, axis=-1, keepdims=True)
        total = part if total is None else total + part
    inv = lax.rsqrt(total * (1.0 / f) + EPSILON)
    first = second = None
    for at in chunks:
        gain = gm_ref[:, at]
        unit = (act[:, at] - mean) * inv
        act[:, at] = unit
        m_ref[:, at] = (unit * gain).astype(BF)
        d_unit = dm[:, at] * gain
        dm[:, at] = d_unit
        part = jnp.sum(d_unit, axis=-1, keepdims=True)
        first = part if first is None else first + part
        part = jnp.sum(d_unit * unit, axis=-1, keepdims=True)
        second = part if second is None else second + part
    first, second = first * (1.0 / f), second * (1.0 / f)
    dh2 = None
    for at in chunks:
        d_act = inv * (dm[:, at] - first - act[:, at] * second)
        dpre = (d_act * slope[:, at]).astype(BF)
        dpre_ref[:, at] = dpre
        part = dot(dpre, wu_ref[:, at], ((1,), (1,)))
        dh2 = part if dh2 is None else dh2 + part
    dx1 = gy.astype(F32) + norm_back(dh2, gf_ref[...], unit_two, inv_two)
    dx1_ref[...] = dx1
    low = dx1.astype(BF)
    low_ref[...] = low
    da = dot(low, wo_ref[...], ((1,), (1,)))
    do_ref[...] = norm_back(da, gi_ref[...], unit_in, inv_in).astype(BF)

    if split:
        quarter = f // 4
        for j in range(2):
            at = pl.multiple_of((2 * j + 1 - core) * quarter, PAIR)
            other_ref[:, j * quarter : (j + 1) * quarter] = m_ref[:, pl.ds(at, quarter)]


def ffn_both(split, order, mixed, tokens, gy, gain_inner, gain_ffn, gain_mid, parts):
    t, d = tokens.shape
    f = gain_mid.shape[1]
    width = d // 2 if split else d
    more = [(rows(f // 2), shaped((t, f // 2), BF))] * split
    if split:
        theirs = pl.BlockSpec((2, ROWS, width), lambda i, *_: (0, i, 0))
        more.insert(0, (theirs, shaped((2, t, width), BF)))
    return prefetched(
        functools.partial(ffn_kernel, split), order, [mixed, tokens, gy, gain_inner, gain_ffn, gain_mid, *parts],
        [rows(d), rows(d), rows(d), whole((1, d)), whole((1, d)), whole((1, f))] + [hbm()] * len(parts),
        [rows(width), rows(width), rows(d), rows(f), rows(f), rows(d), rows(d), rows(d), whole((f, d)), whole((d, d)),
         whole((d, f))] + [m[0] for m in more],
        [
            shaped((t, width), BF), shaped((t, width), BF), shaped((t, d), F32), shaped((t, f), BF), shaped((t, f), BF),
            shaped((t, d), F32), shaped((t, d), BF), shaped((t, d), BF), shaped((f, d), BF), shaped((d, d), BF),
            shaped((d, f), BF),
        ] + [m[1] for m in more],
        [
            pltpu.VMEM((ROWS, f), F32), pltpu.VMEM((ROWS, f), F32), pltpu.VMEM((ROWS, f), F32), pltpu.SemaphoreType.DMA,
            pltpu.SemaphoreType.DMA, pltpu.SemaphoreType.DMA,
        ],
        (t // ROWS,), 60, "ffn_both", 2 * t * d * (2 * d + 3 * f), 6 * d * f + 4 * t * f + 30 * t * d,
    )


def result_kernel(m_ref, x1_ref, wd_ref, y_ref):
    y_ref[...] = (x1_ref[...] + dot(m_ref[...], wd_ref[...])).astype(BF)


def down_forward(m, x1, w_down):
    t, d = x1.shape
    f = m.shape[1]
    return pl.pallas_call(
        result_kernel,
        grid=(t // ROWS,),
        in_specs=[rows(f), rows(d), whole((f, d))],
        out_specs=rows(d),
        out_shape=shaped((t, d), BF),
        compiler_params=params(48),
        cost_estimate=pl.CostEstimate(flops=2 * t * d * f, transcendentals=0, bytes_accessed=2 * d * f + 2 * t * f + 6 * t * d),
        name="down_forward",
    )(m, x1, w_down)


def grads_kernel(split, products, *refs):
    back, *refs = refs
    count = 2 if split else 1
    left, refs = refs[: len(products) * count], refs[len(products) * count :]
    right, refs = refs[: len(products) * count], refs[len(products) * count :]
    outs, refs = refs[: 4 if split else len(products)], refs[4 if split else len(products) :]
    tile, turned = refs[0], refs[1:]
    step = pl.program_id(0)
    first, row = 0, 0
    for n, (by_left, tiles, size) in enumerate(products):
        mine = [left[n * count + c] for c in range(count)]
        value = [right[n * count + c] for c in range(count)]

        if not by_left:

            @pl.when(step == first)
            def _():
                t = mine[0].shape[0]
                for c in range(count):
                    flat = mine[c][...] if len(mine[c].shape) == 2 else mine[c][0]
                    turned[0][:, c * t : (c + 1) * t] = flat.T

        @pl.when((step >= first) & (step < first + tiles))
        def _():
            total = None
            for c in range(count):
                v = value[c][...] if len(value[c].shape) == 2 else value[c][0]
                t = v.shape[0]
                if by_left:
                    part = dot(mine[c][...], v, ((0,), (0,)))
                else:
                    part = dot(turned[0][:, c * t : (c + 1) * t], v)
                total = part if total is None else total + part
            if not split:
                outs[n][...] = total
            else:
                tile[...] = total
                if by_left:
                    owners = tile.shape[0] // size
                    for e in range(owners):
                        at = back[16 + (step - first) * owners + e]
                        for q in range(4):

                            @pl.when(at // 4 == q)
                            def _():
                                block = tile[e * size : (e + 1) * size, :]
                                outs[q][at - 4 * q, row : row + size, :] = block.astype(outs[q].dtype)
                else:
                    deal(back, tile, outs, row + pl.multiple_of((step - first) * size, 8), size)

        first += tiles
        row += size if by_left else tiles * size


def weight_grads(split, back, products):
    count = 2 if split else 1
    t = products[0][0][0].shape[0]
    left_specs, right_specs, lefts, rights, plan = [], [], [], [], []
    out_specs, out_shape = [], []
    at = row = 0
    for left, right, tiles, by_left in products:
        width = 0
        for c in range(count):
            a, b = left[c], right[c]
            a, part = a if isinstance(a, tuple) else (a, None)

            if by_left and c == 0:
                tiles = tiles // count
                width = a.shape[1] // (tiles * count)

            def step(i, at=at, tiles=tiles):
                return jnp.clip(i - at, 0, tiles - 1)

            if by_left:
                per = tiles // 2
                if split and c == 0:
                    left_specs.append(pl.BlockSpec(
                        (t, width), lambda i, back, step=step, per=per: (0, (2 * (step(i) // per) + back[32]) * per + step(i) % per)
                    ))
                else:
                    left_specs.append(pl.BlockSpec((t, width), lambda i, *_, step=step: (0, step(i))))
                right_specs.append(whole(b.shape))
            else:
                width = a.shape[-1]
                if part is None:
                    left_specs.append(whole(a.shape))
                else:
                    left_specs.append(pl.BlockSpec(
                        (1, t, width), lambda *_, part=part: (part, 0, 0), pipeline_mode=pl.Buffered(1)
                    ))
                if b.ndim == 3:
                    right_specs.append(pl.BlockSpec((1, t, LANES), lambda i, *_, step=step: (step(i), 0, 0)))
                else:
                    right_specs.append(pl.BlockSpec((t, LANES), lambda i, *_, step=step: (0, step(i))))
            lefts.append(a)
            rights.append(b)
        size = (width * tiles if by_left else width) // 16
        if not split:
            shape = (width * tiles, LANES) if by_left else (width, tiles * LANES)
            block = (width, LANES)
            out_specs.append(pl.BlockSpec(
                block, (lambda i, *_, step=step: (step(i), 0)) if by_left else (lambda i, *_, step=step: (0, step(i)))
            ))
            out_shape.append(shaped(shape, F32))
        plan.append((by_left, tiles, size))
        at += tiles
        row += size if by_left else tiles * size
    narrow = next(p[0][0].shape[1] for p in products if not p[3])
    if split:
        out_specs = [whole((4, row, LANES))] * 4
        out_shape = [shaped((4, row, LANES), BF)] * 4
    flops = 2 * count * t * narrow * at * LANES
    return prefetched(
        functools.partial(grads_kernel, split, tuple(plan)), back, lefts + rights, left_specs + right_specs,
        out_specs, out_shape, [pltpu.VMEM((narrow, LANES), F32), pltpu.VMEM((narrow, count * t), BF)],
        (at,), 60, "weight_grads", flops, flops // 256,
    )


def qkv_back_kernel(d_ref, x_ref, dx1_ref, w_ref, gain_ref, dx_ref):
    d = x_ref.shape[1]
    groups, _, span = d_ref.shape
    span //= 3
    dh = None
    for part in range(3):
        for g in range(groups):
            at = part * d + g * span
            piece = dot(d_ref[g, :, part * span : (part + 1) * span], w_ref[:, at : at + span], ((1,), (1,)))
            dh = piece if dh is None else dh + piece
    unit, inv = unit_norm(x_ref[...].astype(F32))
    dx_ref[...] = dx1_ref[...] + norm_back(dh, gain_ref[...], unit, inv)


def qkv_backward(d_qkv, tokens, dx1, w_qkv, gain):
    t, d = tokens.shape
    groups, _, span = d_qkv.shape
    return pl.pallas_call(
        qkv_back_kernel,
        grid=(t // ROWS,),
        in_specs=[pl.BlockSpec((groups, ROWS, span), lambda i: (0, i, 0))] + [rows(d)] * 2
        + [whole((d, 3 * d)), whole((1, d))],
        out_specs=rows(d),
        out_shape=shaped((t, d), F32),
        compiler_params=params(48),
        cost_estimate=pl.CostEstimate(flops=6 * t * d * d, transcendentals=0, bytes_accessed=6 * d * d + 16 * t * d),
        name="qkv_backward",
    )(d_qkv, tokens, dx1, w_qkv, gain)


def layout(doc_lengths, seq):
    docs = doc_lengths.shape[-1]
    upto = jnp.arange(docs)[:, None] <= jnp.arange(docs)[None, :]
    ends = jnp.sum(jnp.where(upto[None], doc_lengths[:, :, None], 0), axis=1)
    places = jnp.arange(seq, dtype=jnp.int32)
    passed = places[None, :, None] >= ends[:, None, :]
    start = jnp.sum(jnp.where(passed, doc_lengths[:, None, :], 0), axis=-1)
    valid = places[None, :] < ends[:, docs - 2 : docs - 1]
    return start.astype(jnp.int32), places[None, :] - start, valid


def tables(position):
    half = HEAD_DIM // 2
    lane = jnp.arange(PAIR)
    frequency = jnp.exp((lane % half).astype(F32) * (-2.0 * math.log(10000.0) / HEAD_DIM))
    angles = position.reshape(-1, 1).astype(F32) * frequency[None, :]
    sign = jnp.where(lane % HEAD_DIM < half, -1.0, 1.0)
    return jnp.cos(angles), jnp.sin(angles) * sign[None, :]


Z = 4
GROUPS = ((0, 2), (1, 3))


def index(x, core, z, y):
    return ((x * 2 + core) * Z + z) * 2 + y


def permute(value, move):
    places = [(x, c, z, y) for x in range(2) for c in range(2) for z in range(Z) for y in range(2)]
    return lax.ppermute(value, AXES, [(index(*p), index(*move(*p))) for p in places])


def over_x(v):
    return permute(v, lambda x, c, z, y: (1 - x, c, z, y))


def over_y(v):
    return permute(v, lambda x, c, z, y: (x, c, z, 1 - y))


def over_core(v):
    return permute(v, lambda x, c, z, y: (x, 1 - c, z, y))


def over_z(v, bits):
    return permute(v, lambda x, c, z, y: (x, c, z ^ bits, y))


def place():
    dp, fs = lax.axis_index("dp"), lax.axis_index("fsdp")
    return dp >> 1, dp & 1, fs >> 1, fs & 1


def gather_order():
    rows_of = []
    for core in range(2):
        for group, first in zip(GROUPS, ("x", "y")):
            for second in range(2):
                for one in range(2):
                    dx, dy = (one, second) if first == "x" else (second, one)
                    rows_of += [(dx, core, dz, dy) for dz in group]
    dx, dc, dz, dy = np.array(rows_of, np.int32).T
    x, c, z, y = place()
    order = index(x ^ dx, c ^ dc, z ^ dz, y ^ dy)
    return jnp.concatenate([order, c[None]]).astype(jnp.int32)


def scatter_order():
    rows_of = []
    for group, first in zip(GROUPS, ("y", "x")):
        for one in (1, 0):
            for second in (1, 0):
                dx, dy = (second, one) if first == "y" else (one, second)
                rows_of += [(dx, dz, dy) for dz in group]
    dx, dz, dy = np.array(rows_of, np.int32).T
    x, c, z, y = place()
    order = ((x ^ dx) * Z + (z ^ dz)) * 2 + (y ^ dy)
    spots = jnp.arange(len(rows_of), dtype=jnp.int32)
    where = jnp.sum(jnp.where(order[None, :] == spots[:, None], spots[None, :], 0), axis=1)
    return jnp.concatenate([order, where, c[None]]).astype(jnp.int32)


def tie(value, other):
    return lax.optimization_barrier((value, other))[0]


class Gather:
    def __init__(self, block):
        self.block = block

    def far_z(self, after=None):
        block = self.block if after is None else tie(self.block, after)
        self.even = jnp.stack([block, over_z(block, 2)])
        return self.even

    def near_z(self, after=None):
        if after is not None:
            self.even = tie(self.even, after)
        self.odd = over_z(self.even, 1)
        return self.odd

    def first(self):
        self.got = (over_x(self.even), over_y(self.odd))
        return self.got

    def second(self, after=None):
        got = self.got if after is None else tie(self.got, after)
        even, odd = jnp.concatenate([self.even, got[0]]), jnp.concatenate([self.odd, got[1]])
        self.near = [even, odd, over_core(even), over_core(odd)]
        self.far = [over_y(even), over_x(odd)]
        return self.far

    def core(self, after=None):
        far = self.far if after is None else tie(self.far, after)
        even, odd, even_core, odd_core = self.near
        return [even, far[0], odd, far[1], even_core, over_core(far[0]), odd_core, over_core(far[1])]


class Reduce:
    def __init__(self, send_a, keep_a, send_b, keep_b):
        self.sends, self.a, self.b = (send_a, send_b), keep_a.astype(F32), keep_b.astype(F32)

    def first(self, after=None):
        sends = self.sends if after is None else tie(self.sends, after)
        self.got = (over_y(sends[0]), over_x(sends[1]))
        return self.got

    def wait_for(self, after):
        if after is not None:
            self.got = tie(self.got, after)

    def second(self, after=None):
        self.wait_for(after)
        self.a = self.a + self.got[0].astype(F32)
        self.b = self.b + self.got[1].astype(F32)
        self.got = (over_x(self.a[:2].astype(BF)), over_y(self.b[:2].astype(BF)))
        return self.got

    def near_z(self, after=None):
        self.wait_for(after)
        self.a = self.a[2:] + self.got[0].astype(F32)
        self.got = over_z((self.b[2:] + self.got[1].astype(F32)).astype(BF), 1)
        return self.got

    def far_z(self, after=None):
        self.wait_for(after)
        self.a = self.a + self.got.astype(F32)
        self.got = over_z(self.a[1].astype(BF), 2)
        return self.got

    def own(self):
        return self.a[0] + self.got.astype(F32)


def unslab(block, width):
    size = block.shape[0] * LANES // width
    return jnp.concatenate([block[s * size : (s + 1) * size] for s in range(width // LANES)], axis=1)


def slab(block):
    return [block[:, s * LANES : (s + 1) * LANES] for s in range(block.shape[1] // LANES)]


def local(fast, tokens, doc_lengths, cotangent, w_qkv, w_out, w_up, w_down,
          gain_attn, gain_inner, gain_ffn, gain_mid):
    row_count = doc_lengths.shape[0]
    seq = tokens.shape[0] // row_count
    d, f = tokens.shape[1], w_up.shape[1]
    wide = min(seq, 512) // BLOCK + 1
    blocks = seq // BLOCK
    shards = (gain_attn, gain_inner, gain_ffn, gain_mid)
    sizes = [g.shape[0] for g in shards]

    start, position, valid = layout(doc_lengths, seq)
    cos, sin = tables(position)
    firsts = start[:, ::BLOCK] // BLOCK
    reach = (jnp.arange(blocks, dtype=jnp.int32)[None, :] - firsts + 1).reshape(-1)
    start_row = jnp.repeat(start, 8, axis=0)
    gy = jnp.where(valid.reshape(-1, 1), cotangent, jnp.zeros_like(cotangent))

    def scatter(g):
        return lax.psum_scatter(g, AXES, scatter_dimension=0, tiled=True)

    def gather(v):
        return lax.all_gather(v, AXES, axis=0, tiled=True)

    if fast:
        order, back = gather_order(), scatter_order()
        gains_row = jnp.pad(jnp.concatenate(shards)[None], ((0, 7), (0, LANES - sum(sizes))))
        one, two = (Gather(b) for b in pack(w_qkv, w_out, w_up, w_down, gains_row))
        seen = one.far_z()
        two.far_z(seen)
        one.even = tie(one.even, (cos, sin))
        one.near_z()
        one.first()
        one.second(two.even)
        two.near_z()
        two.first()
        parts_qkv = one.core()
        gy_both = (gy, over_core(gy))
        cos, sin = tie((cos, sin), (gy, start_row, reach, order, back))
        gains = [None]
    else:
        order = back = jnp.zeros((8,), jnp.int32)
        parts_qkv, parts_up, parts_down = [gather(w_qkv)], [gather(w_out), gather(w_up)], [gather(w_down)]
        gains = [gather(g).astype(F32).reshape(1, -1) for g in shards]

    h1, qkv, full_qkv, *rest = qkv_forward(fast, order, tokens, cos, sin, parts_qkv, gains[0], sizes)
    g_attn, g_inner, g_ffn, g_mid = rest if fast else gains
    if fast:
        two.second(g_attn)
        start_row = tie(start_row, (gy_both[1], two.near[2:]))
    mixed, lse = attention_forward(reach, qkv, start_row, row_count, wide)
    parts = two.core(lse) if fast else parts_up + parts_down
    a, h2, x1, m, dpre, dx1, low, d_mixed, full_down, _, _, *other = ffn_both(
        fast, order, mixed, tokens, gy, g_inner, g_ffn, g_mid, parts
    )

    def shared(value):
        return (value, over_core(value)) if fast else (value,)

    if fast:
        m_both = (m, over_core(other[1]))
        theirs = over_core(other[0])
        a_both, h2_both = (a, (theirs, 0)), (h2, (theirs, 1))
    else:
        gy_both, m_both, a_both, h2_both = (gy,), (m,), (a,), (h2,)
    low, dpre = shared(low), shared(dpre)

    def attend(group, groups, lse, so_far):
        return attention_backward(
            reach, qkv, d_mixed, mixed, lse, start_row, cos, sin, row_count, wide, group, groups, so_far
        )

    f = w_up.shape[1]
    d_qkv = attend(0, 1, lse, None)
    if fast:
        low = tie(low, d_qkv)
    grads = weight_grads(
        fast, back,
        [(m_both, gy_both, f // 384, True), (a_both, low, d // LANES, False), (h2_both, dpre, f // LANES, False)],
    )
    if fast:
        red = Reduce(*grads)
        first = red.first()
        h1 = tie(h1, grads[-1])
    d_qkv = attend(1, 2, tie(lse, grads[-1]), d_qkv)
    if fast:
        h1 = (h1[0], over_core(h1[1]))
        d_both = (d_qkv, over_core(tie(d_qkv, (first, h1[1]))))
        second = red.second(d_qkv)
        dx1 = tie(dx1, (d_qkv, first))
    else:
        d_both = (d_qkv,)
    grad_tokens = qkv_backward(d_qkv, tokens, dx1, full_qkv, g_attn)
    if fast:
        near = red.near_z(grad_tokens)
        h1 = tie(h1, (grad_tokens, second))
    grad_qkv = weight_grads(fast, back, [(h1, d_both, 3 * d // LANES, False)])
    if fast:
        red_qkv = Reduce(*grad_qkv)
        first = red_qkv.first()
        far = red.far_z(grad_qkv[-1])
        m = tie(m, (grad_qkv[-1], near))
    result = down_forward(m, x1, full_down)
    if fast:
        red_qkv.second((result, far))
        own = red.own()
        red_qkv.near_z()
        red_qkv.far_z()
        g_qkv = red_qkv.own()
        cuts = (w_down.shape[0], w_down.shape[0] + w_out.shape[0])
        own_down, grad_out, grad_up = own[: cuts[0]], own[cuts[0] : cuts[1]], unslab(own[cuts[1] :], f)
    else:
        own_down, grad_out, grad_up, g_qkv = (scatter(g.astype(BF)).astype(F32) for g in (*grads, *grad_qkv))
        g_qkv = jnp.concatenate(slab(g_qkv))
    size = w_qkv.shape[0]
    span = LANES // 3
    g_qkv = jnp.concatenate(
        [g_qkv[g * size : (g + 1) * size, p * span : (p + 1) * span] for p in range(3) for g in range(GRAD_GROUPS)], axis=1
    )
    pairs = ((g_qkv, w_qkv), (grad_out, w_out), (grad_up, w_up), (own_down, w_down))
    gain_grads = [jnp.sum(g * w.astype(F32), axis=1) / v.astype(F32) for (g, w), v in zip(pairs, shards)]
    return (result, grad_tokens, g_qkv, grad_out, grad_up, own_down, *gain_grads)


def solution(mesh):
    matrix, vector = P(AXES, None), P(AXES)
    fast = mesh.shape["dp"] == 4 and mesh.shape["fsdp"] == 2 * Z
    return jax.shard_map(
        functools.partial(local, fast),
        mesh=mesh,
        in_specs=(matrix,) * 7 + (vector,) * 4,
        out_specs=(matrix,) * 6 + (vector,) * 4,
        check_vma=False,
    )
```

```python
import functools
import math

import jax
import jax.numpy as jnp
import numpy as np
from jax import lax
from jax.experimental import pallas as pl
from jax.experimental.pallas import tpu as pltpu
from jax.sharding import PartitionSpec as P

HEADS = 12
HEAD_DIM = 64
PAIR = 2 * HEAD_DIM
PAIRS = HEADS // 2
EPSILON = 1e-05
MASKED_SCORE = -1e30
ROOT_HALF = 0.7071067811865476
INV_ROOT_TAU = 0.3989422804014327
BF = jnp.bfloat16
F32 = jnp.float32
MIB = 1 << 20
AXES = ("dp", "fsdp")
BLOCK = 256
ROWS = 256
LANES = 768
VMEM_MIB = 60
GRAD_GROUPS = 3


def dot(a, b, dims=((1,), (0,))):
    return lax.dot_general(a, b, (dims, ((), ())), preferred_element_type=F32)


def params(mib):
    return pltpu.CompilerParams(vmem_limit_bytes=max(mib, VMEM_MIB) * MIB)


def swap_halves(x):
    lane = lax.broadcasted_iota(jnp.int32, x.shape, 1)
    low = lax.rem(lane, HEAD_DIM) < HEAD_DIM // 2
    half = HEAD_DIM // 2
    return jnp.where(low, pltpu.roll(x, PAIR - half, 1), pltpu.roll(x, half, 1))


def unit_norm(x):
    mean = jnp.mean(x, axis=-1, keepdims=True)
    centred = x - mean
    inv = lax.rsqrt(jnp.mean(centred * centred, axis=-1, keepdims=True) + EPSILON)
    return centred * inv, inv


def norm_back(d_unit, unit, inv):
    return inv * (
        d_unit
        - jnp.mean(d_unit, axis=-1, keepdims=True)
        - unit * jnp.mean(d_unit * unit, axis=-1, keepdims=True)
    )


def whole(shape):
    return pl.BlockSpec(shape, lambda *_: (0,) * len(shape), pipeline_mode=pl.Buffered(1))


def rows(width, block=ROWS):
    return pl.BlockSpec((block, width), lambda i: (i, 0))


def shaped(shape, dtype):
    return jax.ShapeDtypeStruct(shape, dtype)


def hbm():
    return pl.BlockSpec(memory_space=pl.ANY)


def fetch(order, parts, places, sem):
    if len(parts) < 8 and parts[0].ndim == 2:
        for part, (_, _, buffer, _) in zip(parts, places):
            pltpu.make_async_copy(part, buffer, sem).start()
        return
    count = parts[0].shape[0]
    for p, part in enumerate(parts):
        for b in range(count):
            owner = b if order is None else order[p * count + b]
            for first, size, buffer, column in places:
                row = owner * size if order is None else pl.multiple_of(owner * size, 8)
                pltpu.make_async_copy(
                    part.at[b, pl.ds(first, size), :],
                    buffer.at[pl.ds(row, size), pl.ds(column, LANES)],
                    sem,
                ).start()


def arrive(buffers, sem):
    for buffer in buffers:
        pltpu.make_async_copy(buffer, buffer, sem).wait()


def deal(back, tile, outs, row, size):
    quarter = outs[0].shape[0]
    for q, out in enumerate(outs):

        @pl.loop(0, quarter)
        def _(j):
            block = tile[pl.ds(pl.multiple_of(back[q * quarter + j] * size, 8), size), :]
            out[j, pl.ds(row, size), :] = block.astype(out.dtype)


def slabs(first, size, buffer, width):
    return [(first + s * size, size, buffer, s * LANES) for s in range(width // LANES)]


def scale_rows(w, gain):
    n = w.shape[0]
    square = lax.broadcasted_iota(jnp.int32, (n, n), 0) == lax.broadcasted_iota(jnp.int32, (n, n), 1)
    return dot(jnp.where(square, gain.astype(F32), 0.0).astype(BF), w).astype(BF)


def pack_kernel(wq_ref, wo_ref, wu_ref, wd_ref, ga_ref, gi_ref, gf_ref, gm_ref, one_ref, two_ref):
    row = 0
    for c in range(wq_ref.shape[1] // LANES):
        one_ref[row : row + wq_ref.shape[0], :] = wq_ref[:, c * LANES : (c + 1) * LANES]
        row += wq_ref.shape[0]
    one_ref[row:, :] = ga_ref[...]
    row = 0
    for ref, gain in ((wd_ref, gm_ref), (wo_ref, gi_ref), (wu_ref, gf_ref)):
        for c in range(ref.shape[1] // LANES):
            two_ref[row : row + ref.shape[0], :] = scale_rows(ref[:, c * LANES : (c + 1) * LANES], gain[...])
            row += ref.shape[0]


def pack(w_qkv, w_out, w_up, w_down, gains):
    first = w_qkv.size // LANES + 8
    second = (w_out.size + w_up.size + w_down.size) // LANES
    row = jnp.pad(gains[0].reshape(1, -1), ((0, 7), (0, LANES - gains[0].shape[0])))
    return pl.pallas_call(
        pack_kernel, out_shape=[shaped((first, LANES), BF), shaped((second, LANES), BF)], name="pack"
    )(w_qkv, w_out, w_up, w_down, row, *(g.reshape(1, -1) for g in gains[1:]))


def spread(rows_in, offset, count, owners):
    lanes = rows_in.shape[1]
    wide = owners * count
    lane = lax.broadcasted_iota(jnp.int32, (lanes, wide), 0)
    column = lax.broadcasted_iota(jnp.int32, (lanes, wide), 1)
    pick = (lane - offset == lax.rem(column, count)).astype(F32).astype(BF)
    full = dot(rows_in, pick)
    owner = lax.broadcasted_iota(jnp.int32, (owners, wide), 0)
    column = lax.broadcasted_iota(jnp.int32, (owners, wide), 1)
    own = (column >= owner * count) & (column < owner * count + count)
    return jnp.sum(jnp.where(own, full, 0.0), axis=0, keepdims=True)


def qkv_kernel(split, *refs):
    if split:
        order, x_ref, cos_ref, sin_ref, *refs = refs
        parts, refs = refs[:8], refs[8:]
        h_ref, other_ref, qkv_ref, w_ref, ga_ref, gains, sem, gain_sem = refs
        h_refs = (h_ref, other_ref)
    else:
        order, x_ref, cos_ref, sin_ref, ga_ref, *refs = refs
        parts, refs = refs[:1], refs[1:]
        h_ref, qkv_ref, w_ref, sem = refs
        h_refs = (h_ref,)
    width = x_ref.shape[1]
    step = pl.program_id(0)
    if split:
        size = width // 32
        weight = slabs(0, size, w_ref, 3 * width)

        @pl.when(step == 0)
        def _():
            fetch(order, parts, [(3 * size, 8, gains, 0)], gain_sem)
            fetch(order, parts, weight, sem)
            arrive([gains], gain_sem)
            owner = lax.broadcasted_iota(jnp.int32, (32, 256), 0)
            lane = lax.broadcasted_iota(jnp.int32, (32, 256), 1)
            pick = (lane == owner * 8).astype(F32).astype(BF)
            per_owner = dot(pick, gains[:, :PAIR]).astype(BF)
            ga_ref[...] = spread(per_owner, 0, size, 32)
            arrive([w_ref], sem)
    else:

        @pl.when(step == 0)
        def _():
            fetch(None, parts, [(0, 0, w_ref, 0)], sem)
            arrive([w_ref], sem)

    unit, _ = unit_norm(x_ref[...].astype(F32))
    h = (unit * ga_ref[...]).astype(BF)
    store_low(split, order[32] if split else 0, h, h_refs)
    cos, sin = cos_ref[...], sin_ref[...]
    for part in range(3):
        y = dot(h, w_ref[:, part * width : (part + 1) * width])
        for c in range(width // PAIR):
            z = y[:, c * PAIR : (c + 1) * PAIR]
            if part < 2:
                z = z * cos + swap_halves(z) * sin
            if part == 0:
                z = z * (1.0 / math.sqrt(HEAD_DIM))
            at = part * width + c * PAIR
            qkv_ref[:, at : at + PAIR] = z.astype(BF)


def prefetched(kernel, order, inputs, in_specs, out_specs, out_shape, scratch, grid, mib, name, flops, data):
    return pl.pallas_call(
        kernel,
        grid_spec=pltpu.PrefetchScalarGridSpec(
            num_scalar_prefetch=1,
            grid=grid,
            in_specs=in_specs,
            out_specs=out_specs,
            scratch_shapes=scratch,
        ),
        out_shape=out_shape,
        compiler_params=params(mib),
        cost_estimate=pl.CostEstimate(flops=flops, transcendentals=0, bytes_accessed=data),
        name=name,
    )(order, *inputs)


def rows(width, block=ROWS):
    return pl.BlockSpec((block, width), lambda i, *_: (i, 0))


def whole(shape):
    return pl.BlockSpec(shape, lambda *_: (0,) * len(shape), pipeline_mode=pl.Buffered(1))


def qkv_forward(split, order, tokens, cos, sin, parts, gain):
    t, d = tokens.shape
    n = 3 * d
    inputs = [tokens, cos, sin]
    in_specs = [rows(d), rows(PAIR), rows(PAIR)]
    out_specs, out_shape = low_specs(split, t, d)
    lows = len(out_specs)
    out_specs = out_specs + [rows(n), whole((d, n))]
    out_shape = out_shape + [shaped((t, n), BF), shaped((d, n), BF)]
    scratch = [pltpu.SemaphoreType.DMA]
    if split:
        out_specs += [whole((1, d))]
        out_shape += [shaped((1, d), F32)]
        scratch = [pltpu.VMEM((32 * 8, LANES), BF), pltpu.SemaphoreType.DMA, pltpu.SemaphoreType.DMA]
    else:
        inputs.append(gain)
        in_specs.append(whole((1, d)))
    outs = prefetched(
        functools.partial(qkv_kernel, split), order, inputs + list(parts), in_specs + [hbm()] * len(parts),
        out_specs, out_shape, scratch, (t // ROWS,), 40, "qkv_forward",
        2 * t * d * n, 4 * d * n + 12 * t * d,
    )
    return (outs[:lows], *outs[lows:])


def window(i, n):
    return slice((i - n + 1) * BLOCK, (i + 1) * BLOCK)


def head_masks(shape):
    lane = lax.broadcasted_iota(jnp.int32, shape, 1)
    return lane < HEAD_DIM


def attention_forward_kernel(wide, reach, q_ref, k_ref, v_ref, start_ref, o_ref, lse_ref, bias):
    row, pair = pl.program_id(0), pl.program_id(1)
    seq = q_ref.shape[0]
    blocks = seq // BLOCK

    @pl.when(pair == 0)
    def _():
        for i in range(blocks):
            at = slice(i * BLOCK, (i + 1) * BLOCK)
            shape = (BLOCK, wide * BLOCK)
            key = (i - wide + 1) * BLOCK + lax.broadcasted_iota(jnp.int32, shape, 1)
            query = i * BLOCK + lax.broadcasted_iota(jnp.int32, shape, 0)
            row_of = start_ref[0:1, at].astype(F32)
            start = jnp.broadcast_to(row_of, (PAIR, BLOCK)).T[:, 0:1].astype(jnp.int32)
            keep = (key >= start) & (key <= query)
            bias[at, :] = jnp.where(keep, 0.0, MASKED_SCORE)

    first = head_masks((BLOCK, PAIR))
    for i in range(blocks):
        at = slice(i * BLOCK, (i + 1) * BLOCK)
        most = min(wide, i + 1)
        for n in range(1, most + 1):

            @pl.when(reach[row * blocks + i] == n)
            def _():
                q = q_ref[at, :]
                w = window(i, n)
                k, v = k_ref[w, :], v_ref[w, :]
                b = bias[at, (wide - n) * BLOCK :]
                mask = head_masks(k.shape)
                zero = jnp.zeros_like(k)
                masks = (mask, jnp.logical_not(mask))
                scores = [dot(q, jnp.where(pick, k, zero), ((1,), (1,))) for pick in masks]
                total, lses = None, []
                for s, pick in zip(scores, masks):
                    s = s + b
                    top = jnp.max(s, axis=-1, keepdims=True)
                    p = jnp.exp(s - top)
                    den = jnp.sum(p, axis=-1, keepdims=True)
                    part = dot((p * (1.0 / den)).astype(BF), jnp.where(pick, v, zero))
                    total = part if total is None else total + part
                    lses.append(top + jnp.log(den))
                o_ref[at, :] = total
                both = jnp.where(first, lses[0], lses[1]).T
                lse_ref[0, 0:1, at] = both[0:1, :]
                lse_ref[0, 1:2, at] = both[HEAD_DIM : HEAD_DIM + 1, :]


def attention_forward(reach, qkv, start, row_count, wide):
    t = qkv.shape[0]
    seq = t // row_count
    d = qkv.shape[1] // 3

    def columns(part):
        return pl.BlockSpec((seq, PAIR), lambda r, p, *_: (r, part * PAIRS + p))

    return pl.pallas_call(
        functools.partial(attention_forward_kernel, wide),
        grid_spec=pltpu.PrefetchScalarGridSpec(
            num_scalar_prefetch=1,
            grid=(row_count, PAIRS),
            in_specs=[
                columns(0),
                columns(1),
                columns(2),
                pl.BlockSpec((8, seq), lambda r, p, *_: (r, 0)),
            ],
            out_specs=[
                pl.BlockSpec((seq, PAIR), lambda r, p, *_: (r, p)),
                pl.BlockSpec((1, 8, seq), lambda r, p, *_: (r * PAIRS + p, 0, 0)),
            ],
            scratch_shapes=[pltpu.VMEM((seq, wide * BLOCK), F32)],
        ),
        out_shape=[shaped((t, d), F32), shaped((row_count * PAIRS, 8, seq), F32)],
        compiler_params=params(32),
        cost_estimate=pl.CostEstimate(
            flops=8 * t * d * BLOCK, transcendentals=t * HEADS * 512, bytes_accessed=12 * t * d
        ),
        name="attention_forward",
    )(reach, qkv, qkv, qkv, start)


def attention_backward_kernel(wide, reach, q_ref, k_ref, v_ref, do_ref, o_ref, lse_ref, start_ref, cos_ref, sin_ref, *refs):
    grad_ref, bias, ks, vs, qs, dos, dk_acc, dv_acc, dq_acc = refs[-9:]
    row, pair = pl.program_id(0), pl.program_id(1)
    seq = q_ref.shape[0]
    blocks = seq // BLOCK

    @pl.when(pair == 0)
    def _():
        for i in range(blocks):
            at = slice(i * BLOCK, (i + 1) * BLOCK)
            shape = (wide * BLOCK, BLOCK)
            key = (i - wide + 1) * BLOCK + lax.broadcasted_iota(jnp.int32, shape, 0)
            query = i * BLOCK + lax.broadcasted_iota(jnp.int32, shape, 1)
            keep = (key >= start_ref[0:1, at]) & (key <= query)
            bias[:, at] = jnp.where(keep, 0.0, MASKED_SCORE)

    mask = head_masks((seq, PAIR))
    for src, dst in ((k_ref, ks), (v_ref, vs), (q_ref, qs), (do_ref, dos)):
        x = src[...]
        zero = jnp.zeros_like(x)
        dst[0] = jnp.where(mask, x, zero)
        dst[1] = jnp.where(mask, zero, x)
    dk_acc[...] = jnp.zeros_like(dk_acc)
    dv_acc[...] = jnp.zeros_like(dv_acc)
    lane8 = lax.broadcasted_iota(jnp.int32, (8, PAIR), 1) // HEAD_DIM
    row8 = lax.broadcasted_iota(jnp.int32, (8, PAIR), 0)
    picks = (lane8 == row8).astype(F32)
    delta = lax.dot_general(
        picks, do_ref[...].astype(F32) * o_ref[...], (((1,), (1,)), ((), ())),
        precision=lax.Precision.HIGHEST, preferred_element_type=F32,
    )
    for i in range(blocks):
        at = slice(i * BLOCK, (i + 1) * BLOCK)
        most = min(wide, i + 1)
        for n in range(1, most + 1):

            @pl.when(reach[row * blocks + i] == n)
            def _():
                w = window(i, n)
                b = bias[(wide - n) * BLOCK :, at]
                q, do = q_ref[at, :], do_ref[at, :]
                ps, dss = [], []
                for h in range(2):
                    s = dot(ks[h, w, :], q, ((1,), (1,))) + b
                    p = jnp.exp(s - lse_ref[0, h : h + 1, at])
                    dp = dot(vs[h, w, :], do, ((1,), (1,)))
                    ds = (p * (dp - delta[h : h + 1, at])).astype(BF)
                    ps.append(p.astype(BF))
                    dss.append(ds)
                dv_acc[w, :] += dot(ps[0], dos[0, at, :]) + dot(ps[1], dos[1, at, :])
                dk_acc[w, :] += dot(dss[0], qs[0, at, :]) + dot(dss[1], qs[1, at, :])
                dq_acc[at, :] = dot(dss[0], ks[0, w, :], ((0,), (0,))) + dot(
                    dss[1], ks[1, w, :], ((0,), (0,))
                )

    cos, sin = cos_ref[...], sin_ref[...]
    dq = dq_acc[...] * (1.0 / math.sqrt(HEAD_DIM))
    dk = dk_acc[...]
    span = grad_ref.shape[2] // 3
    slot = lax.rem(pair, span // PAIR)
    grads = (dq * cos - swap_halves(dq) * sin, dk * cos - swap_halves(dk) * sin, dv_acc[...])
    for part, value in enumerate(grads):
        grad_ref[0, :, pl.ds(pl.multiple_of(part * span + slot * PAIR, PAIR), PAIR)] = value.astype(BF)


def attention_backward(reach, qkv, d_mixed, mixed, lse, start_row, cos, sin, row_count, wide, group, groups, so_far):
    pairs = PAIRS // GRAD_GROUPS
    t = qkv.shape[0]
    seq = t // row_count
    base = group * pairs
    span = 3 * pairs * PAIR

    def columns(part):
        return pl.BlockSpec((seq, PAIR), lambda r, p, *_: (r, part * PAIRS + base + p))

    table = pl.BlockSpec((seq, PAIR), lambda r, p, *_: (r, 0))
    inputs = [reach, qkv, qkv, qkv, d_mixed, mixed, lse, start_row, cos, sin]
    in_specs = [
        columns(0), columns(1), columns(2), columns(0), columns(0),
        pl.BlockSpec((1, 8, seq), lambda r, p, *_: (r * PAIRS + base + p, 0, 0)),
        pl.BlockSpec((8, seq), lambda r, p, *_: (r, 0)),
        table, table,
    ]
    aliases = {}
    if so_far is not None:
        aliases = {len(inputs): 0}
        inputs.append(so_far)
        in_specs.append(hbm())
    return pl.pallas_call(
        functools.partial(attention_backward_kernel, wide),
        grid_spec=pltpu.PrefetchScalarGridSpec(
            num_scalar_prefetch=1,
            grid=(row_count, pairs * groups),
            in_specs=in_specs,
            out_specs=pl.BlockSpec((1, seq, span), lambda r, p, *_: (group + p // pairs, r, 0)),
            scratch_shapes=[
                pltpu.VMEM((wide * BLOCK, seq), F32),
                pltpu.VMEM((2, seq, PAIR), BF),
                pltpu.VMEM((2, seq, PAIR), BF),
                pltpu.VMEM((2, seq, PAIR), BF),
                pltpu.VMEM((2, seq, PAIR), BF),
                pltpu.VMEM((seq, PAIR), F32),
                pltpu.VMEM((seq, PAIR), F32),
                pltpu.VMEM((seq, PAIR), F32),
            ],
        ),
        out_shape=shaped((GRAD_GROUPS, t, span), BF),
        input_output_aliases=aliases,
        compiler_params=params(40),
        cost_estimate=pl.CostEstimate(
            flops=20 * t * span * BLOCK // 3 * groups, transcendentals=t * HEADS * 128 * groups,
            bytes_accessed=20 * t * span // 3 * groups
        ),
        name="attention_backward",
    )(*inputs)


def halves(x):
    quarter = x.shape[1] // 4
    piece = [x[:, i * quarter : (i + 1) * quarter] for i in range(4)]
    return jnp.concatenate(piece[0::2], axis=1), jnp.concatenate(piece[1::2], axis=1)


def store_low(split, core, x, refs):
    if not split:
        refs[0][...] = x
        return
    pair = halves(x)
    for c in range(2):

        @pl.when(core == c)
        def _():
            refs[0][...] = pair[c]
            refs[1][...] = pair[1 - c]


def low_specs(split, t, d):
    if split:
        return [rows(d // 2)] * 2, [shaped((t, d // 2), BF)] * 2
    return [rows(d)], [shaped((t, d), BF)]


def ffn_kernel(split, *refs):
    order, o_ref, x_ref, gy_ref, *refs = refs
    count = 8 if split else 3
    parts, refs = refs[:count], refs[count:]
    a_ref, h2_ref, x1_ref, m_ref, dpre_ref, dx1_ref, low_ref, do_ref, wd_ref, wo_ref, wu_ref, *refs = refs
    theirs_ref, other_ref, *refs = refs if split else (None, None, *refs)
    act, slope, dm, out_sem, up_sem, down_sem = refs
    d, f = wu_ref.shape
    size, skip = d // 32, f // 32
    step = pl.program_id(0)
    core = order[32] if split else 0
    chunks = [slice(c, c + LANES) for c in range(0, f, LANES)]

    @pl.when(step == 0)
    def _():
        if split:
            fetch(order, parts, [(skip, size, wo_ref, 0)], out_sem)
            fetch(order, parts, slabs(skip + size, size, wu_ref, f), up_sem)
            fetch(order, parts, [(0, skip, wd_ref, 0)], down_sem)
        else:
            fetch(order, parts[:1], [(0, 0, wo_ref, 0)], out_sem)
            fetch(order, parts[1:2], [(0, 0, wu_ref, 0)], up_sem)
            fetch(order, parts[2:], [(0, 0, wd_ref, 0)], down_sem)

    mixed = o_ref[...]
    unit_in, inv_in = unit_norm(mixed)
    a = unit_in.astype(BF)
    store_low(split, core, a, (a_ref, theirs_ref.at[0] if split else None))

    @pl.when(step == 0)
    def _():
        arrive([wo_ref], out_sem)

    x1 = x_ref[...].astype(F32) + dot(a, wo_ref[...])
    x1_ref[...] = x1
    unit_two, inv_two = unit_norm(x1)
    h2 = unit_two.astype(BF)
    store_low(split, core, h2, (h2_ref, theirs_ref.at[1] if split else None))
    gy = gy_ref[...]

    @pl.when(step == 0)
    def _():
        arrive([wu_ref], up_sem)
        arrive([wd_ref], down_sem)

    total = None
    for at in chunks:
        hidden = dot(h2, wu_ref[:, at])
        dm[:, at] = dot(gy, wd_ref[at, :], ((1,), (1,)))
        cdf = 0.5 + 0.5 * lax.erf(hidden * ROOT_HALF)
        slope[:, at] = cdf + hidden * (jnp.exp(-0.5 * hidden * hidden) * INV_ROOT_TAU)
        value = hidden * cdf
        act[:, at] = value
        part = jnp.sum(value, axis=-1, keepdims=True)
        total = part if total is None else total + part
    mean = total * (1.0 / f)
    total = None
    for at in chunks:
        centred = act[:, at] - mean
        part = jnp.sum(centred * centred, axis=-1, keepdims=True)
        total = part if total is None else total + part
    inv = lax.rsqrt(total * (1.0 / f) + EPSILON)
    first = second = None
    for at in chunks:
        unit = (act[:, at] - mean) * inv
        act[:, at] = unit
        m_ref[:, at] = unit.astype(BF)
        d_unit = dm[:, at]
        part = jnp.sum(d_unit, axis=-1, keepdims=True)
        first = part if first is None else first + part
        part = jnp.sum(d_unit * unit, axis=-1, keepdims=True)
        second = part if second is None else second + part
    first, second = first * (1.0 / f), second * (1.0 / f)
    dh2 = None
    for at in chunks:
        d_act = inv * (dm[:, at] - first - act[:, at] * second)
        dpre = (d_act * slope[:, at]).astype(BF)
        dpre_ref[:, at] = dpre
        part = dot(dpre, wu_ref[:, at], ((1,), (1,)))
        dh2 = part if dh2 is None else dh2 + part
    dx1 = gy.astype(F32) + norm_back(dh2, unit_two, inv_two)
    dx1_ref[...] = dx1
    low = dx1.astype(BF)
    low_ref[...] = low
    da = dot(low, wo_ref[...], ((1,), (1,)))
    do_ref[...] = norm_back(da, unit_in, inv_in).astype(BF)

    if split:
        quarter = f // 4
        for j in range(2):
            at = pl.multiple_of((2 * j + 1 - core) * quarter, PAIR)
            other_ref[:, j * quarter : (j + 1) * quarter] = m_ref[:, pl.ds(at, quarter)]


def ffn_both(split, order, mixed, tokens, gy, parts, f):
    t, d = tokens.shape
    width = d // 2 if split else d
    more = [(rows(f // 2), shaped((t, f // 2), BF))] * split
    if split:
        theirs = pl.BlockSpec((2, ROWS, width), lambda i, *_: (0, i, 0))
        more.insert(0, (theirs, shaped((2, t, width), BF)))
    return prefetched(
        functools.partial(ffn_kernel, split), order, [mixed, tokens, gy, *parts],
        [rows(d), rows(d), rows(d)] + [hbm()] * len(parts),
        [rows(width), rows(width), rows(d), rows(f), rows(f), rows(d), rows(d), rows(d), whole((f, d)), whole((d, d)),
         whole((d, f))] + [m[0] for m in more],
        [
            shaped((t, width), BF), shaped((t, width), BF), shaped((t, d), F32), shaped((t, f), BF), shaped((t, f), BF),
            shaped((t, d), F32), shaped((t, d), BF), shaped((t, d), BF), shaped((f, d), BF), shaped((d, d), BF),
            shaped((d, f), BF),
        ] + [m[1] for m in more],
        [
            pltpu.VMEM((ROWS, f), F32), pltpu.VMEM((ROWS, f), F32), pltpu.VMEM((ROWS, f), F32), pltpu.SemaphoreType.DMA,
            pltpu.SemaphoreType.DMA, pltpu.SemaphoreType.DMA,
        ],
        (t // ROWS,), 60, "ffn_both", 2 * t * d * (2 * d + 3 * f), 6 * d * f + 4 * t * f + 30 * t * d,
    )


def result_kernel(m_ref, x1_ref, wd_ref, y_ref):
    y_ref[...] = (x1_ref[...] + dot(m_ref[...], wd_ref[...])).astype(BF)


def down_forward(m, x1, w_down):
    t, d = x1.shape
    f = m.shape[1]
    return pl.pallas_call(
        result_kernel,
        grid=(t // ROWS,),
        in_specs=[rows(f), rows(d), whole((f, d))],
        out_specs=rows(d),
        out_shape=shaped((t, d), BF),
        compiler_params=params(48),
        cost_estimate=pl.CostEstimate(flops=2 * t * d * f, transcendentals=0, bytes_accessed=2 * d * f + 2 * t * f + 6 * t * d),
        name="down_forward",
    )(m, x1, w_down)


def grads_kernel(split, products, *refs):
    back, *refs = refs
    count = 2 if split else 1
    left, refs = refs[: len(products) * count], refs[len(products) * count :]
    right, refs = refs[: len(products) * count], refs[len(products) * count :]
    outs, refs = refs[: 4 if split else len(products)], refs[4 if split else len(products) :]
    tile, turned = refs[0], refs[1:]
    step = pl.program_id(0)
    first, row = 0, 0
    for n, (by_left, tiles, size) in enumerate(products):
        mine = [left[n * count + c] for c in range(count)]
        value = [right[n * count + c] for c in range(count)]

        if not by_left:

            @pl.when(step == first)
            def _():
                t = mine[0].shape[0]
                for c in range(count):
                    flat = mine[c][...] if len(mine[c].shape) == 2 else mine[c][0]
                    turned[0][:, c * t : (c + 1) * t] = flat.T

        @pl.when((step >= first) & (step < first + tiles))
        def _():
            total = None
            for c in range(count):
                v = value[c][...] if len(value[c].shape) == 2 else value[c][0]
                t = v.shape[0]
                if by_left:
                    part = dot(mine[c][...], v, ((0,), (0,)))
                else:
                    part = dot(turned[0][:, c * t : (c + 1) * t], v)
                total = part if total is None else total + part
            if not split:
                outs[n][...] = total
            else:
                tile[...] = total
                if by_left:
                    owners = tile.shape[0] // size
                    for e in range(owners):
                        at = back[16 + (step - first) * owners + e]
                        for q in range(4):

                            @pl.when(at // 4 == q)
                            def _():
                                block = tile[e * size : (e + 1) * size, :]
                                outs[q][at - 4 * q, row : row + size, :] = block.astype(outs[q].dtype)
                else:
                    deal(back, tile, outs, row + pl.multiple_of((step - first) * size, 8), size)

        first += tiles
        row += size if by_left else tiles * size


def weight_grads(split, back, products):
    count = 2 if split else 1
    t = products[0][0][0].shape[0]
    left_specs, right_specs, lefts, rights, plan = [], [], [], [], []
    out_specs, out_shape = [], []
    at = row = 0
    for left, right, tiles, by_left in products:
        width = 0
        for c in range(count):
            a, b = left[c], right[c]
            a, part = a if isinstance(a, tuple) else (a, None)

            if by_left and c == 0:
                tiles = tiles // count
                width = a.shape[1] // (tiles * count)

            def step(i, at=at, tiles=tiles):
                return jnp.clip(i - at, 0, tiles - 1)

            if by_left:
                per = tiles // 2
                if split and c == 0:
                    left_specs.append(pl.BlockSpec(
                        (t, width), lambda i, back, step=step, per=per: (0, (2 * (step(i) // per) + back[32]) * per + step(i) % per)
                    ))
                else:
                    left_specs.append(pl.BlockSpec((t, width), lambda i, *_, step=step: (0, step(i))))
                right_specs.append(whole(b.shape))
            else:
                width = a.shape[-1]
                if part is None:
                    left_specs.append(whole(a.shape))
                else:
                    left_specs.append(pl.BlockSpec(
                        (1, t, width), lambda *_, part=part: (part, 0, 0), pipeline_mode=pl.Buffered(1)
                    ))
                if b.ndim == 3:
                    right_specs.append(pl.BlockSpec((1, t, LANES), lambda i, *_, step=step: (step(i), 0, 0)))
                else:
                    right_specs.append(pl.BlockSpec((t, LANES), lambda i, *_, step=step: (0, step(i))))
            lefts.append(a)
            rights.append(b)
        size = (width * tiles if by_left else width) // 16
        if not split:
            shape = (width * tiles, LANES) if by_left else (width, tiles * LANES)
            block = (width, LANES)
            out_specs.append(pl.BlockSpec(
                block, (lambda i, *_, step=step: (step(i), 0)) if by_left else (lambda i, *_, step=step: (0, step(i)))
            ))
            out_shape.append(shaped(shape, F32))
        plan.append((by_left, tiles, size))
        at += tiles
        row += size if by_left else tiles * size
    narrow = next(p[0][0].shape[1] for p in products if not p[3])
    if split:
        out_specs = [whole((4, row, LANES))] * 4
        out_shape = [shaped((4, row, LANES), BF)] * 4
    flops = 2 * count * t * narrow * at * LANES
    return prefetched(
        functools.partial(grads_kernel, split, tuple(plan)), back, lefts + rights, left_specs + right_specs,
        out_specs, out_shape, [pltpu.VMEM((narrow, LANES), F32), pltpu.VMEM((narrow, count * t), BF)],
        (at,), 60, "weight_grads", flops, flops // 256,
    )


def qkv_back_kernel(d_ref, x_ref, dx1_ref, w_ref, gain_ref, dx_ref):
    d = x_ref.shape[1]
    groups, _, span = d_ref.shape
    span //= 3
    dh = None
    for part in range(3):
        for g in range(groups):
            at = part * d + g * span
            piece = dot(d_ref[g, :, part * span : (part + 1) * span], w_ref[:, at : at + span], ((1,), (1,)))
            dh = piece if dh is None else dh + piece
    unit, inv = unit_norm(x_ref[...].astype(F32))
    dx_ref[...] = dx1_ref[...] + norm_back(dh * gain_ref[...], unit, inv)


def qkv_backward(d_qkv, tokens, dx1, w_qkv, gain):
    t, d = tokens.shape
    groups, _, span = d_qkv.shape
    return pl.pallas_call(
        qkv_back_kernel,
        grid=(t // ROWS,),
        in_specs=[pl.BlockSpec((groups, ROWS, span), lambda i: (0, i, 0))] + [rows(d)] * 2
        + [whole((d, 3 * d)), whole((1, d))],
        out_specs=rows(d),
        out_shape=shaped((t, d), F32),
        compiler_params=params(48),
        cost_estimate=pl.CostEstimate(flops=6 * t * d * d, transcendentals=0, bytes_accessed=6 * d * d + 16 * t * d),
        name="qkv_backward",
    )(d_qkv, tokens, dx1, w_qkv, gain)


def layout(doc_lengths, seq):
    docs = doc_lengths.shape[-1]
    upto = jnp.arange(docs)[:, None] <= jnp.arange(docs)[None, :]
    ends = jnp.sum(jnp.where(upto[None], doc_lengths[:, :, None], 0), axis=1)
    places = jnp.arange(seq, dtype=jnp.int32)
    passed = places[None, :, None] >= ends[:, None, :]
    start = jnp.sum(jnp.where(passed, doc_lengths[:, None, :], 0), axis=-1)
    valid = places[None, :] < ends[:, docs - 2 : docs - 1]
    return start.astype(jnp.int32), places[None, :] - start, valid


def tables(position):
    half = HEAD_DIM // 2
    lane = jnp.arange(PAIR)
    frequency = jnp.exp((lane % half).astype(F32) * (-2.0 * math.log(10000.0) / HEAD_DIM))
    angles = position.reshape(-1, 1).astype(F32) * frequency[None, :]
    sign = jnp.where(lane % HEAD_DIM < half, -1.0, 1.0)
    return jnp.cos(angles), jnp.sin(angles) * sign[None, :]


Z = 4
GROUPS = ((0, 2), (1, 3))


def index(x, core, z, y):
    return ((x * 2 + core) * Z + z) * 2 + y


def permute(value, move):
    places = [(x, c, z, y) for x in range(2) for c in range(2) for z in range(Z) for y in range(2)]
    return lax.ppermute(value, AXES, [(index(*p), index(*move(*p))) for p in places])


def over_x(v):
    return permute(v, lambda x, c, z, y: (1 - x, c, z, y))


def over_y(v):
    return permute(v, lambda x, c, z, y: (x, c, z, 1 - y))


def over_core(v):
    return permute(v, lambda x, c, z, y: (x, 1 - c, z, y))


def over_z(v, bits):
    return permute(v, lambda x, c, z, y: (x, c, z ^ bits, y))


def place():
    dp, fs = lax.axis_index("dp"), lax.axis_index("fsdp")
    return dp >> 1, dp & 1, fs >> 1, fs & 1


def gather_order():
    rows_of = []
    for core in range(2):
        for group, first in zip(GROUPS, ("x", "y")):
            for second in range(2):
                for one in range(2):
                    dx, dy = (one, second) if first == "x" else (second, one)
                    rows_of += [(dx, core, dz, dy) for dz in group]
    dx, dc, dz, dy = np.array(rows_of, np.int32).T
    x, c, z, y = place()
    order = index(x ^ dx, c ^ dc, z ^ dz, y ^ dy)
    return jnp.concatenate([order, c[None]]).astype(jnp.int32)


def scatter_order():
    rows_of = []
    for group, first in zip(GROUPS, ("y", "x")):
        for one in (1, 0):
            for second in (1, 0):
                dx, dy = (second, one) if first == "y" else (one, second)
                rows_of += [(dx, dz, dy) for dz in group]
    dx, dz, dy = np.array(rows_of, np.int32).T
    x, c, z, y = place()
    order = ((x ^ dx) * Z + (z ^ dz)) * 2 + (y ^ dy)
    spots = jnp.arange(len(rows_of), dtype=jnp.int32)
    where = jnp.sum(jnp.where(order[None, :] == spots[:, None], spots[None, :], 0), axis=1)
    return jnp.concatenate([order, where, c[None]]).astype(jnp.int32)


def tie(value, other):
    return lax.optimization_barrier((value, other))[0]


class Gather:
    def __init__(self, block):
        self.block = block

    def far_z(self, after=None):
        block = self.block if after is None else tie(self.block, after)
        self.even = jnp.stack([block, over_z(block, 2)])
        return self.even

    def near_z(self, after=None):
        if after is not None:
            self.even = tie(self.even, after)
        self.odd = over_z(self.even, 1)
        return self.odd

    def first(self):
        self.got = (over_x(self.even), over_y(self.odd))
        return self.got

    def second(self, after=None):
        got = self.got if after is None else tie(self.got, after)
        even, odd = jnp.concatenate([self.even, got[0]]), jnp.concatenate([self.odd, got[1]])
        self.near = [even, odd, over_core(even), over_core(odd)]
        self.far = [over_y(even), over_x(odd)]
        return self.far

    def core(self, after=None):
        far = self.far if after is None else tie(self.far, after)
        even, odd, even_core, odd_core = self.near
        return [even, far[0], odd, far[1], even_core, over_core(far[0]), odd_core, over_core(far[1])]


class Reduce:
    def __init__(self, send_a, keep_a, send_b, keep_b):
        self.sends, self.a, self.b = (send_a, send_b), keep_a.astype(F32), keep_b.astype(F32)

    def first(self, after=None):
        sends = self.sends if after is None else tie(self.sends, after)
        self.got = (over_y(sends[0]), over_x(sends[1]))
        return self.got

    def wait_for(self, after):
        if after is not None:
            self.got = tie(self.got, after)

    def second(self, after=None):
        self.wait_for(after)
        self.a = self.a + self.got[0].astype(F32)
        self.b = self.b + self.got[1].astype(F32)
        self.got = (over_x(self.a[:2].astype(BF)), over_y(self.b[:2].astype(BF)))
        return self.got

    def near_z(self, after=None):
        self.wait_for(after)
        self.a = self.a[2:] + self.got[0].astype(F32)
        self.got = over_z((self.b[2:] + self.got[1].astype(F32)).astype(BF), 1)
        return self.got

    def far_z(self, after=None):
        self.wait_for(after)
        self.a = self.a + self.got.astype(F32)
        self.got = over_z(self.a[1].astype(BF), 2)
        return self.got

    def own(self):
        return self.a[0] + self.got.astype(F32)


def unslab(block, width):
    size = block.shape[0] * LANES // width
    return jnp.concatenate([block[s * size : (s + 1) * size] for s in range(width // LANES)], axis=1)


def slab(block):
    return [block[:, s * LANES : (s + 1) * LANES] for s in range(block.shape[1] // LANES)]


def local(fast, tokens, doc_lengths, cotangent, w_qkv, w_out, w_up, w_down,
          gain_attn, gain_inner, gain_ffn, gain_mid):
    row_count = doc_lengths.shape[0]
    seq = tokens.shape[0] // row_count
    d, f = tokens.shape[1], w_up.shape[1]
    wide = min(seq, 512) // BLOCK + 1
    blocks = seq // BLOCK
    shards = (gain_attn, gain_inner, gain_ffn, gain_mid)

    start, position, valid = layout(doc_lengths, seq)
    cos, sin = tables(position)
    firsts = start[:, ::BLOCK] // BLOCK
    reach = (jnp.arange(blocks, dtype=jnp.int32)[None, :] - firsts + 1).reshape(-1)
    start_row = jnp.repeat(start, 8, axis=0)
    gy = jnp.where(valid.reshape(-1, 1), cotangent, jnp.zeros_like(cotangent))

    def scatter(g):
        return lax.psum_scatter(g, AXES, scatter_dimension=0, tiled=True)

    def gather(v):
        return lax.all_gather(v, AXES, axis=0, tiled=True)

    if fast:
        order, back = gather_order(), scatter_order()
        one, two = (Gather(b) for b in pack(w_qkv, w_out, w_up, w_down, shards))
        seen = one.far_z()
        two.far_z(seen)
        one.even = tie(one.even, (cos, sin))
        one.near_z()
        one.first()
        one.second(two.even)
        two.near_z()
        two.first()
        parts_qkv = one.core()
        gy_both = (gy, over_core(gy))
        cos, sin = tie((cos, sin), (gy, start_row, reach, order, back))
    else:
        order = back = jnp.zeros((8,), jnp.int32)

        def scaled(w, gain):
            return gather((w.astype(F32) * gain.astype(F32)[:, None]).astype(BF))

        parts_qkv, parts_down = [gather(w_qkv)], [scaled(w_down, gain_mid)]
        parts_up = [scaled(w_out, gain_inner), scaled(w_up, gain_ffn)]

    whole_gain = None if fast else gather(gain_attn).astype(F32).reshape(1, -1)
    h1, qkv, full_qkv, *rest = qkv_forward(fast, order, tokens, cos, sin, parts_qkv, whole_gain)
    g_attn = rest[0] if fast else whole_gain
    if fast:
        two.second(g_attn)
        start_row = tie(start_row, (gy_both[1], two.near[2:]))
    mixed, lse = attention_forward(reach, qkv, start_row, row_count, wide)
    parts = two.core(lse) if fast else parts_up + parts_down
    a, h2, x1, m, dpre, dx1, low, d_mixed, full_down, _, _, *other = ffn_both(
        fast, order, mixed, tokens, gy, parts, f
    )

    def shared(value):
        return (value, over_core(value)) if fast else (value,)

    if fast:
        m_both = (m, over_core(other[1]))
        theirs = over_core(other[0])
        a_both, h2_both = (a, (theirs, 0)), (h2, (theirs, 1))
    else:
        gy_both, m_both, a_both, h2_both = (gy,), (m,), (a,), (h2,)
    low, dpre = shared(low), shared(dpre)

    def attend(group, groups, lse, so_far):
        return attention_backward(
            reach, qkv, d_mixed, mixed, lse, start_row, cos, sin, row_count, wide, group, groups, so_far
        )

    f = w_up.shape[1]
    d_qkv = attend(0, 1, lse, None)
    if fast:
        low = tie(low, d_qkv)
    grads = weight_grads(
        fast, back,
        [(m_both, gy_both, f // 384, True), (a_both, low, d // LANES, False), (h2_both, dpre, f // LANES, False)],
    )
    if fast:
        red = Reduce(*grads)
        first = red.first()
        h1 = tie(h1, grads[-1])
    d_qkv = attend(1, 2, tie(lse, grads[-1]), d_qkv)
    if fast:
        h1 = (h1[0], over_core(h1[1]))
        d_both = (d_qkv, over_core(tie(d_qkv, (first, h1[1]))))
        second = red.second(d_qkv)
        dx1 = tie(dx1, (d_qkv, first))
    else:
        d_both = (d_qkv,)
    grad_tokens = qkv_backward(d_qkv, tokens, dx1, full_qkv, g_attn)
    if fast:
        near = red.near_z(grad_tokens)
        h1 = tie(h1, (grad_tokens, second))
    grad_qkv = weight_grads(fast, back, [(h1, d_both, 3 * d // LANES, False)])
    if fast:
        red_qkv = Reduce(*grad_qkv)
        first = red_qkv.first()
        far = red.far_z(grad_qkv[-1])
        m = tie(m, (grad_qkv[-1], near))
    result = down_forward(m, x1, full_down)
    if fast:
        red_qkv.second((result, far))
        own = red.own()
        red_qkv.near_z()
        red_qkv.far_z()
        g_qkv = red_qkv.own()
        cuts = (w_down.shape[0], w_down.shape[0] + w_out.shape[0])
        own_down, grad_out, grad_up = own[: cuts[0]], own[cuts[0] : cuts[1]], unslab(own[cuts[1] :], f)
    else:
        own_down, grad_out, grad_up, g_qkv = (scatter(g.astype(BF)).astype(F32) for g in (*grads, *grad_qkv))
        g_qkv = jnp.concatenate(slab(g_qkv))
    size = w_qkv.shape[0]
    span = LANES // 3
    g_qkv = jnp.concatenate(
        [g_qkv[g * size : (g + 1) * size, p * span : (p + 1) * span] for p in range(3) for g in range(GRAD_GROUPS)], axis=1
    )
    raw = (g_qkv, grad_out, grad_up, own_down)
    row_sums = [jnp.sum(g * w.astype(F32), axis=1) for g, w in zip(raw, (w_qkv, w_out, w_up, w_down))]
    row_sums[0] = row_sums[0] / gain_attn.astype(F32)
    scaled_grads = [g * v.astype(F32)[:, None] for g, v in zip(raw[1:], shards[1:])]
    return (result, grad_tokens, g_qkv, *scaled_grads, *row_sums)


def solution(mesh):
    matrix, vector = P(AXES, None), P(AXES)
    fast = mesh.shape["dp"] == 4 and mesh.shape["fsdp"] == 2 * Z
    return jax.shard_map(
        functools.partial(local, fast),
        mesh=mesh,
        in_specs=(matrix,) * 7 + (vector,) * 4,
        out_specs=(matrix,) * 6 + (vector,) * 4,
        check_vma=False,
    )
```

```python
import functools
import math

import jax
import jax.numpy as jnp
import numpy as np
from jax import lax
from jax.experimental import pallas as pl
from jax.experimental.pallas import tpu as pltpu
from jax.sharding import PartitionSpec as P

HEADS = 12
HEAD_DIM = 64
PAIR = 2 * HEAD_DIM
PAIRS = HEADS // 2
EPSILON = 1e-05
MASKED_SCORE = -1e30
ROOT_HALF = 0.7071067811865476
INV_ROOT_TAU = 0.3989422804014327
BF = jnp.bfloat16
F32 = jnp.float32
MIB = 1 << 20
AXES = ("dp", "fsdp")
BLOCK = 256
ROWS = 256
LANES = 768
VMEM_MIB = 63
GRAD_GROUPS = 3


def dot(a, b, dims=((1,), (0,))):
    return lax.dot_general(a, b, (dims, ((), ())), preferred_element_type=F32)


def params(mib):
    return pltpu.CompilerParams(vmem_limit_bytes=max(mib, VMEM_MIB) * MIB)


def swap_halves(x):
    lane = lax.broadcasted_iota(jnp.int32, x.shape, 1)
    low = lax.rem(lane, HEAD_DIM) < HEAD_DIM // 2
    half = HEAD_DIM // 2
    return jnp.where(low, pltpu.roll(x, PAIR - half, 1), pltpu.roll(x, half, 1))


def unit_norm(x):
    mean = jnp.mean(x, axis=-1, keepdims=True)
    centred = x - mean
    inv = lax.rsqrt(jnp.mean(centred * centred, axis=-1, keepdims=True) + EPSILON)
    return centred * inv, inv


def norm_back(d_unit, unit, inv):
    return inv * (
        d_unit
        - jnp.mean(d_unit, axis=-1, keepdims=True)
        - unit * jnp.mean(d_unit * unit, axis=-1, keepdims=True)
    )


def whole(shape):
    return pl.BlockSpec(shape, lambda *_: (0,) * len(shape), pipeline_mode=pl.Buffered(1))


def rows(width, block=ROWS):
    return pl.BlockSpec((block, width), lambda i: (i, 0))


def shaped(shape, dtype):
    return jax.ShapeDtypeStruct(shape, dtype)


def hbm():
    return pl.BlockSpec(memory_space=pl.ANY)


def fetch(order, parts, places, sem):
    if len(parts) < 8 and parts[0].ndim == 2:
        for part, (_, _, buffer, _) in zip(parts, places):
            pltpu.make_async_copy(part, buffer, sem).start()
        return
    count = parts[0].shape[0]
    for p, part in enumerate(parts):
        for b in range(count):
            owner = b if order is None else order[p * count + b]
            for first, size, buffer, column in places:
                row = owner * size if order is None else pl.multiple_of(owner * size, 8)
                pltpu.make_async_copy(
                    part.at[b, pl.ds(first, size), :],
                    buffer.at[pl.ds(row, size), pl.ds(column, LANES)],
                    sem,
                ).start()


def arrive(buffers, sem):
    for buffer in buffers:
        pltpu.make_async_copy(buffer, buffer, sem).wait()


def deal(back, tile, outs, row, size):
    quarter = outs[0].shape[0]
    for q, out in enumerate(outs):

        @pl.loop(0, quarter)
        def _(j):
            block = tile[pl.ds(pl.multiple_of(back[q * quarter + j] * size, 8), size), :]
            out[j, pl.ds(row, size), :] = block.astype(out.dtype)


def slabs(first, size, buffer, width):
    return [(first + s * size, size, buffer, s * LANES) for s in range(width // LANES)]


def scale_rows(w, gain):
    n = w.shape[0]
    square = lax.broadcasted_iota(jnp.int32, (n, n), 0) == lax.broadcasted_iota(jnp.int32, (n, n), 1)
    return dot(jnp.where(square, gain.astype(F32), 0.0).astype(BF), w).astype(BF)


def pack_kernel(wq_ref, wo_ref, wu_ref, wd_ref, ga_ref, gi_ref, gf_ref, gm_ref, one_ref, two_ref):
    row = 0
    for c in range(wq_ref.shape[1] // LANES):
        one_ref[row : row + wq_ref.shape[0], :] = wq_ref[:, c * LANES : (c + 1) * LANES]
        row += wq_ref.shape[0]
    one_ref[row:, :] = ga_ref[...]
    row = 0
    for ref, gain in ((wd_ref, gm_ref), (wo_ref, gi_ref), (wu_ref, gf_ref)):
        for c in range(ref.shape[1] // LANES):
            two_ref[row : row + ref.shape[0], :] = scale_rows(ref[:, c * LANES : (c + 1) * LANES], gain[...])
            row += ref.shape[0]


def pack(w_qkv, w_out, w_up, w_down, gains):
    first = w_qkv.size // LANES + 8
    second = (w_out.size + w_up.size + w_down.size) // LANES
    row = jnp.pad(gains[0].reshape(1, -1), ((0, 7), (0, LANES - gains[0].shape[0])))
    return pl.pallas_call(
        pack_kernel, out_shape=[shaped((first, LANES), BF), shaped((second, LANES), BF)], name="pack"
    )(w_qkv, w_out, w_up, w_down, row, *(g.reshape(1, -1) for g in gains[1:]))


def spread(rows_in, offset, count, owners):
    lanes = rows_in.shape[1]
    wide = owners * count
    lane = lax.broadcasted_iota(jnp.int32, (lanes, wide), 0)
    column = lax.broadcasted_iota(jnp.int32, (lanes, wide), 1)
    pick = (lane - offset == lax.rem(column, count)).astype(F32).astype(BF)
    full = dot(rows_in, pick)
    owner = lax.broadcasted_iota(jnp.int32, (owners, wide), 0)
    column = lax.broadcasted_iota(jnp.int32, (owners, wide), 1)
    own = (column >= owner * count) & (column < owner * count + count)
    return jnp.sum(jnp.where(own, full, 0.0), axis=0, keepdims=True)


def qkv_kernel(split, *refs):
    if split:
        order, x_ref, cos_ref, sin_ref, *refs = refs
        parts, refs = refs[:8], refs[8:]
        h_ref, other_ref, qkv_ref, w_ref, ga_ref, gains, sem, gain_sem = refs
        h_refs = (h_ref, other_ref)
    else:
        order, x_ref, cos_ref, sin_ref, ga_ref, *refs = refs
        parts, refs = refs[:1], refs[1:]
        h_ref, qkv_ref, w_ref, sem = refs
        h_refs = (h_ref,)
    width = x_ref.shape[1]
    step = pl.program_id(0)
    if split:
        size = width // 32
        weight = slabs(0, size, w_ref, 3 * width)

        @pl.when(step == 0)
        def _():
            fetch(order, parts, [(3 * size, 8, gains, 0)], gain_sem)
            fetch(order, parts, weight, sem)
            arrive([gains], gain_sem)
            owner = lax.broadcasted_iota(jnp.int32, (32, 256), 0)
            lane = lax.broadcasted_iota(jnp.int32, (32, 256), 1)
            pick = (lane == owner * 8).astype(F32).astype(BF)
            per_owner = dot(pick, gains[:, :PAIR]).astype(BF)
            ga_ref[...] = spread(per_owner, 0, size, 32)
            arrive([w_ref], sem)
    else:

        @pl.when(step == 0)
        def _():
            fetch(None, parts, [(0, 0, w_ref, 0)], sem)
            arrive([w_ref], sem)

    unit, _ = unit_norm(x_ref[...].astype(F32))
    h = (unit * ga_ref[...]).astype(BF)
    store_low(split, order[32] if split else 0, h, h_refs)
    cos, sin = cos_ref[...], sin_ref[...]
    for part in range(3):
        y = dot(h, w_ref[:, part * width : (part + 1) * width])
        for c in range(width // PAIR):
            z = y[:, c * PAIR : (c + 1) * PAIR]
            if part < 2:
                z = z * cos + swap_halves(z) * sin
            if part == 0:
                z = z * (1.0 / math.sqrt(HEAD_DIM))
            at = part * width + c * PAIR
            qkv_ref[:, at : at + PAIR] = z.astype(BF)


def prefetched(kernel, order, inputs, in_specs, out_specs, out_shape, scratch, grid, mib, name, flops, data):
    return pl.pallas_call(
        kernel,
        grid_spec=pltpu.PrefetchScalarGridSpec(
            num_scalar_prefetch=1,
            grid=grid,
            in_specs=in_specs,
            out_specs=out_specs,
            scratch_shapes=scratch,
        ),
        out_shape=out_shape,
        compiler_params=params(mib),
        cost_estimate=pl.CostEstimate(flops=flops, transcendentals=0, bytes_accessed=data),
        name=name,
    )(order, *inputs)


def rows(width, block=ROWS):
    return pl.BlockSpec((block, width), lambda i, *_: (i, 0))


def whole(shape):
    return pl.BlockSpec(shape, lambda *_: (0,) * len(shape), pipeline_mode=pl.Buffered(1))


def qkv_forward(split, order, tokens, cos, sin, parts, gain):
    t, d = tokens.shape
    n = 3 * d
    inputs = [tokens, cos, sin]
    in_specs = [rows(d), rows(PAIR), rows(PAIR)]
    out_specs, out_shape = low_specs(split, t, d)
    lows = len(out_specs)
    out_specs = out_specs + [rows(n), whole((d, n))]
    out_shape = out_shape + [shaped((t, n), BF), shaped((d, n), BF)]
    scratch = [pltpu.SemaphoreType.DMA]
    if split:
        out_specs += [whole((1, d))]
        out_shape += [shaped((1, d), F32)]
        scratch = [pltpu.VMEM((32 * 8, LANES), BF), pltpu.SemaphoreType.DMA, pltpu.SemaphoreType.DMA]
    else:
        inputs.append(gain)
        in_specs.append(whole((1, d)))
    outs = prefetched(
        functools.partial(qkv_kernel, split), order, inputs + list(parts), in_specs + [hbm()] * len(parts),
        out_specs, out_shape, scratch, (t // ROWS,), 40, "qkv_forward",
        2 * t * d * n, 4 * d * n + 12 * t * d,
    )
    return (outs[:lows], *outs[lows:])


def window(i, n):
    return slice((i - n + 1) * BLOCK, (i + 1) * BLOCK)


def head_masks(shape):
    lane = lax.broadcasted_iota(jnp.int32, shape, 1)
    return lane < HEAD_DIM


def attention_forward_kernel(wide, reach, q_ref, k_ref, v_ref, start_ref, o_ref, lse_ref, bias):
    row, pair = pl.program_id(0), pl.program_id(1)
    seq = q_ref.shape[0]
    blocks = seq // BLOCK

    @pl.when(pair == 0)
    def _():
        for i in range(blocks):
            at = slice(i * BLOCK, (i + 1) * BLOCK)
            shape = (BLOCK, wide * BLOCK)
            key = (i - wide + 1) * BLOCK + lax.broadcasted_iota(jnp.int32, shape, 1)
            query = i * BLOCK + lax.broadcasted_iota(jnp.int32, shape, 0)
            row_of = start_ref[0:1, at].astype(F32)
            start = jnp.broadcast_to(row_of, (PAIR, BLOCK)).T[:, 0:1].astype(jnp.int32)
            keep = (key >= start) & (key <= query)
            bias[at, :] = jnp.where(keep, 0.0, MASKED_SCORE)

    first = head_masks((BLOCK, PAIR))
    for i in range(blocks):
        at = slice(i * BLOCK, (i + 1) * BLOCK)
        most = min(wide, i + 1)
        for n in range(1, most + 1):

            @pl.when(reach[row * blocks + i] == n)
            def _():
                q = q_ref[at, :]
                w = window(i, n)
                k, v = k_ref[w, :], v_ref[w, :]
                b = bias[at, (wide - n) * BLOCK :]
                mask = head_masks(k.shape)
                zero = jnp.zeros_like(k)
                masks = (mask, jnp.logical_not(mask))
                scores = [dot(q, jnp.where(pick, k, zero), ((1,), (1,))) for pick in masks]
                total, lses = None, []
                for s, pick in zip(scores, masks):
                    s = s + b
                    top = jnp.max(s, axis=-1, keepdims=True)
                    p = jnp.exp(s - top)
                    den = jnp.sum(p, axis=-1, keepdims=True)
                    part = dot((p * (1.0 / den)).astype(BF), jnp.where(pick, v, zero))
                    total = part if total is None else total + part
                    lses.append(top + jnp.log(den))
                o_ref[at, :] = total
                both = jnp.where(first, lses[0], lses[1]).T
                lse_ref[0, 0:1, at] = both[0:1, :]
                lse_ref[0, 1:2, at] = both[HEAD_DIM : HEAD_DIM + 1, :]


def attention_forward(reach, qkv, start, row_count, wide):
    t = qkv.shape[0]
    seq = t // row_count
    d = qkv.shape[1] // 3

    def columns(part):
        return pl.BlockSpec((seq, PAIR), lambda r, p, *_: (r, part * PAIRS + p))

    return pl.pallas_call(
        functools.partial(attention_forward_kernel, wide),
        grid_spec=pltpu.PrefetchScalarGridSpec(
            num_scalar_prefetch=1,
            grid=(row_count, PAIRS),
            in_specs=[
                columns(0),
                columns(1),
                columns(2),
                pl.BlockSpec((8, seq), lambda r, p, *_: (r, 0)),
            ],
            out_specs=[
                pl.BlockSpec((seq, PAIR), lambda r, p, *_: (r, p)),
                pl.BlockSpec((1, 8, seq), lambda r, p, *_: (r * PAIRS + p, 0, 0)),
            ],
            scratch_shapes=[pltpu.VMEM((seq, wide * BLOCK), F32)],
        ),
        out_shape=[shaped((t, d), F32), shaped((row_count * PAIRS, 8, seq), F32)],
        compiler_params=params(32),
        cost_estimate=pl.CostEstimate(
            flops=8 * t * d * BLOCK, transcendentals=t * HEADS * 512, bytes_accessed=12 * t * d
        ),
        name="attention_forward",
    )(reach, qkv, qkv, qkv, start)


def attention_backward_kernel(wide, reach, q_ref, k_ref, v_ref, do_ref, o_ref, lse_ref, start_ref, cos_ref, sin_ref, *refs):
    grad_ref, bias, ks, vs, qs, dos, dk_acc, dv_acc, dq_acc = refs[-9:]
    row, pair = pl.program_id(0), pl.program_id(1)
    seq = q_ref.shape[0]
    blocks = seq // BLOCK

    @pl.when(pair == 0)
    def _():
        for i in range(blocks):
            at = slice(i * BLOCK, (i + 1) * BLOCK)
            shape = (wide * BLOCK, BLOCK)
            key = (i - wide + 1) * BLOCK + lax.broadcasted_iota(jnp.int32, shape, 0)
            query = i * BLOCK + lax.broadcasted_iota(jnp.int32, shape, 1)
            keep = (key >= start_ref[0:1, at]) & (key <= query)
            bias[:, at] = jnp.where(keep, 0.0, MASKED_SCORE)

    mask = head_masks((seq, PAIR))
    for src, dst in ((k_ref, ks), (v_ref, vs), (q_ref, qs), (do_ref, dos)):
        x = src[...]
        zero = jnp.zeros_like(x)
        dst[0] = jnp.where(mask, x, zero)
        dst[1] = jnp.where(mask, zero, x)
    dk_acc[...] = jnp.zeros_like(dk_acc)
    dv_acc[...] = jnp.zeros_like(dv_acc)
    lane8 = lax.broadcasted_iota(jnp.int32, (8, PAIR), 1) // HEAD_DIM
    row8 = lax.broadcasted_iota(jnp.int32, (8, PAIR), 0)
    picks = (lane8 == row8).astype(F32)
    delta = lax.dot_general(
        picks, do_ref[...].astype(F32) * o_ref[...], (((1,), (1,)), ((), ())),
        precision=lax.Precision.HIGHEST, preferred_element_type=F32,
    )
    for i in range(blocks):
        at = slice(i * BLOCK, (i + 1) * BLOCK)
        most = min(wide, i + 1)
        for n in range(1, most + 1):

            @pl.when(reach[row * blocks + i] == n)
            def _():
                w = window(i, n)
                b = bias[(wide - n) * BLOCK :, at]
                q, do = q_ref[at, :], do_ref[at, :]
                ps, dss = [], []
                for h in range(2):
                    s = dot(ks[h, w, :], q, ((1,), (1,))) + b
                    p = jnp.exp(s - lse_ref[0, h : h + 1, at])
                    dp = dot(vs[h, w, :], do, ((1,), (1,)))
                    ds = (p * (dp - delta[h : h + 1, at])).astype(BF)
                    ps.append(p.astype(BF))
                    dss.append(ds)
                dv_acc[w, :] += dot(ps[0], dos[0, at, :]) + dot(ps[1], dos[1, at, :])
                dk_acc[w, :] += dot(dss[0], qs[0, at, :]) + dot(dss[1], qs[1, at, :])
                dq_acc[at, :] = dot(dss[0], ks[0, w, :], ((0,), (0,))) + dot(
                    dss[1], ks[1, w, :], ((0,), (0,))
                )

    cos, sin = cos_ref[...], sin_ref[...]
    dq = dq_acc[...] * (1.0 / math.sqrt(HEAD_DIM))
    dk = dk_acc[...]
    span = grad_ref.shape[2] // 3
    slot = lax.rem(pair, span // PAIR)
    grads = (dq * cos - swap_halves(dq) * sin, dk * cos - swap_halves(dk) * sin, dv_acc[...])
    for part, value in enumerate(grads):
        grad_ref[0, :, pl.ds(pl.multiple_of(part * span + slot * PAIR, PAIR), PAIR)] = value.astype(BF)


def attention_backward(reach, qkv, d_mixed, mixed, lse, start_row, cos, sin, row_count, wide, group, groups, so_far):
    pairs = PAIRS // GRAD_GROUPS
    t = qkv.shape[0]
    seq = t // row_count
    base = group * pairs
    span = 3 * pairs * PAIR

    def columns(part):
        return pl.BlockSpec((seq, PAIR), lambda r, p, *_: (r, part * PAIRS + base + p))

    table = pl.BlockSpec((seq, PAIR), lambda r, p, *_: (r, 0))
    inputs = [reach, qkv, qkv, qkv, d_mixed, mixed, lse, start_row, cos, sin]
    in_specs = [
        columns(0), columns(1), columns(2), columns(0), columns(0),
        pl.BlockSpec((1, 8, seq), lambda r, p, *_: (r * PAIRS + base + p, 0, 0)),
        pl.BlockSpec((8, seq), lambda r, p, *_: (r, 0)),
        table, table,
    ]
    aliases = {}
    if so_far is not None:
        aliases = {len(inputs): 0}
        inputs.append(so_far)
        in_specs.append(hbm())
    return pl.pallas_call(
        functools.partial(attention_backward_kernel, wide),
        grid_spec=pltpu.PrefetchScalarGridSpec(
            num_scalar_prefetch=1,
            grid=(row_count, pairs * groups),
            in_specs=in_specs,
            out_specs=pl.BlockSpec((1, seq, span), lambda r, p, *_: (group + p // pairs, r, 0)),
            scratch_shapes=[
                pltpu.VMEM((wide * BLOCK, seq), F32),
                pltpu.VMEM((2, seq, PAIR), BF),
                pltpu.VMEM((2, seq, PAIR), BF),
                pltpu.VMEM((2, seq, PAIR), BF),
                pltpu.VMEM((2, seq, PAIR), BF),
                pltpu.VMEM((seq, PAIR), F32),
                pltpu.VMEM((seq, PAIR), F32),
                pltpu.VMEM((seq, PAIR), F32),
            ],
        ),
        out_shape=shaped((GRAD_GROUPS, t, span), BF),
        input_output_aliases=aliases,
        compiler_params=params(40),
        cost_estimate=pl.CostEstimate(
            flops=20 * t * span * BLOCK // 3 * groups, transcendentals=t * HEADS * 128 * groups,
            bytes_accessed=20 * t * span // 3 * groups
        ),
        name="attention_backward",
    )(*inputs)


def halves(x):
    quarter = x.shape[1] // 4
    piece = [x[:, i * quarter : (i + 1) * quarter] for i in range(4)]
    return jnp.concatenate(piece[0::2], axis=1), jnp.concatenate(piece[1::2], axis=1)


def store_low(split, core, x, refs):
    if not split:
        refs[0][...] = x
        return
    pair = halves(x)
    for c in range(2):

        @pl.when(core == c)
        def _():
            refs[0][...] = pair[c]
            refs[1][...] = pair[1 - c]


def low_specs(split, t, d):
    if split:
        return [rows(d // 2)] * 2, [shaped((t, d // 2), BF)] * 2
    return [rows(d)], [shaped((t, d), BF)]


def ffn_kernel(split, *refs):
    order, o_ref, x_ref, gy_ref, *refs = refs
    count = 8 if split else 3
    parts, refs = refs[:count], refs[count:]
    a_ref, h2_ref, x1_ref, m_ref, dpre_ref, dx1_ref, low_ref, do_ref, wd_ref, wo_ref, wu_ref, *refs = refs
    theirs_ref, other_ref, *refs = refs if split else (None, None, *refs)
    act, slope, dm, out_sem, up_sem, down_sem = refs
    d, f = wu_ref.shape
    size, skip = d // 32, f // 32
    step = pl.program_id(0)
    core = order[32] if split else 0
    chunks = [slice(c, c + LANES) for c in range(0, f, LANES)]

    @pl.when(step == 0)
    def _():
        if split:
            fetch(order, parts, [(skip, size, wo_ref, 0)], out_sem)
            fetch(order, parts, slabs(skip + size, size, wu_ref, f), up_sem)
            fetch(order, parts, [(0, skip, wd_ref, 0)], down_sem)
        else:
            fetch(order, parts[:1], [(0, 0, wo_ref, 0)], out_sem)
            fetch(order, parts[1:2], [(0, 0, wu_ref, 0)], up_sem)
            fetch(order, parts[2:], [(0, 0, wd_ref, 0)], down_sem)

    mixed = o_ref[...]
    unit_in, inv_in = unit_norm(mixed)
    a = unit_in.astype(BF)
    store_low(split, core, a, (a_ref, theirs_ref.at[0] if split else None))

    @pl.when(step == 0)
    def _():
        arrive([wo_ref], out_sem)

    x1 = x_ref[...].astype(F32) + dot(a, wo_ref[...])
    x1_ref[...] = x1
    unit_two, inv_two = unit_norm(x1)
    h2 = unit_two.astype(BF)
    store_low(split, core, h2, (h2_ref, theirs_ref.at[1] if split else None))
    gy = gy_ref[...]

    @pl.when(step == 0)
    def _():
        arrive([wu_ref], up_sem)
        arrive([wd_ref], down_sem)

    total = None
    for at in chunks:
        hidden = dot(h2, wu_ref[:, at])
        dm[:, at] = dot(gy, wd_ref[at, :], ((1,), (1,)))
        cdf = 0.5 + 0.5 * lax.erf(hidden * ROOT_HALF)
        slope[:, at] = cdf + hidden * (jnp.exp(-0.5 * hidden * hidden) * INV_ROOT_TAU)
        value = hidden * cdf
        act[:, at] = value
        part = jnp.sum(value, axis=-1, keepdims=True)
        total = part if total is None else total + part
    mean = total * (1.0 / f)
    total = None
    for at in chunks:
        centred = act[:, at] - mean
        part = jnp.sum(centred * centred, axis=-1, keepdims=True)
        total = part if total is None else total + part
    inv = lax.rsqrt(total * (1.0 / f) + EPSILON)
    first = second = None
    for at in chunks:
        unit = (act[:, at] - mean) * inv
        act[:, at] = unit
        m_ref[:, at] = unit.astype(BF)
        d_unit = dm[:, at]
        part = jnp.sum(d_unit, axis=-1, keepdims=True)
        first = part if first is None else first + part
        part = jnp.sum(d_unit * unit, axis=-1, keepdims=True)
        second = part if second is None else second + part
    first, second = first * (1.0 / f), second * (1.0 / f)
    dh2 = None
    for at in chunks:
        d_act = inv * (dm[:, at] - first - act[:, at] * second)
        dpre = (d_act * slope[:, at]).astype(BF)
        dpre_ref[:, at] = dpre
        part = dot(dpre, wu_ref[:, at], ((1,), (1,)))
        dh2 = part if dh2 is None else dh2 + part
    dx1 = gy.astype(F32) + norm_back(dh2, unit_two, inv_two)
    dx1_ref[...] = dx1
    low = dx1.astype(BF)
    low_ref[...] = low
    da = dot(low, wo_ref[...], ((1,), (1,)))
    do_ref[...] = norm_back(da, unit_in, inv_in).astype(BF)

    if split:
        quarter = f // 4
        for j in range(2):
            at = pl.multiple_of((2 * j + 1 - core) * quarter, PAIR)
            other_ref[:, j * quarter : (j + 1) * quarter] = m_ref[:, pl.ds(at, quarter)]


def ffn_both(split, order, mixed, tokens, gy, parts, f):
    t, d = tokens.shape
    width = d // 2 if split else d
    more = [(rows(f // 2), shaped((t, f // 2), BF))] * split
    if split:
        theirs = pl.BlockSpec((2, ROWS, width), lambda i, *_: (0, i, 0))
        more.insert(0, (theirs, shaped((2, t, width), BF)))
    return prefetched(
        functools.partial(ffn_kernel, split), order, [mixed, tokens, gy, *parts],
        [rows(d), rows(d), rows(d)] + [hbm()] * len(parts),
        [rows(width), rows(width), rows(d), rows(f), rows(f), rows(d), rows(d), rows(d), whole((f, d)), whole((d, d)),
         whole((d, f))] + [m[0] for m in more],
        [
            shaped((t, width), BF), shaped((t, width), BF), shaped((t, d), F32), shaped((t, f), BF), shaped((t, f), BF),
            shaped((t, d), F32), shaped((t, d), BF), shaped((t, d), BF), shaped((f, d), BF), shaped((d, d), BF),
            shaped((d, f), BF),
        ] + [m[1] for m in more],
        [
            pltpu.VMEM((ROWS, f), F32), pltpu.VMEM((ROWS, f), F32), pltpu.VMEM((ROWS, f), F32), pltpu.SemaphoreType.DMA,
            pltpu.SemaphoreType.DMA, pltpu.SemaphoreType.DMA,
        ],
        (t // ROWS,), 60, "ffn_both", 2 * t * d * (2 * d + 3 * f), 6 * d * f + 4 * t * f + 30 * t * d,
    )


def result_kernel(m_ref, x1_ref, wd_ref, y_ref):
    y_ref[...] = (x1_ref[...] + dot(m_ref[...], wd_ref[...])).astype(BF)


def down_forward(m, x1, w_down):
    t, d = x1.shape
    f = m.shape[1]
    return pl.pallas_call(
        result_kernel,
        grid=(t // ROWS,),
        in_specs=[rows(f), rows(d), whole((f, d))],
        out_specs=rows(d),
        out_shape=shaped((t, d), BF),
        compiler_params=params(48),
        cost_estimate=pl.CostEstimate(flops=2 * t * d * f, transcendentals=0, bytes_accessed=2 * d * f + 2 * t * f + 6 * t * d),
        name="down_forward",
    )(m, x1, w_down)


def grads_kernel(split, products, *refs):
    back, *refs = refs
    count = 2 if split else 1
    left, refs = refs[: len(products) * count], refs[len(products) * count :]
    right, refs = refs[: len(products) * count], refs[len(products) * count :]
    outs, refs = refs[: 4 if split else len(products)], refs[4 if split else len(products) :]
    tile, turned = refs[0], refs[1:]
    step = pl.program_id(0)
    first, row = 0, 0
    for n, (by_left, tiles, size) in enumerate(products):
        mine = [left[n * count + c] for c in range(count)]
        value = [right[n * count + c] for c in range(count)]

        if not by_left:

            @pl.when(step == first)
            def _():
                t = mine[0].shape[0]
                for c in range(count):
                    flat = mine[c][...] if len(mine[c].shape) == 2 else mine[c][0]
                    turned[0][:, c * t : (c + 1) * t] = flat.T

        @pl.when((step >= first) & (step < first + tiles))
        def _():
            total = None
            for c in range(count):
                v = value[c][...] if len(value[c].shape) == 2 else value[c][0]
                t = v.shape[0]
                if by_left:
                    part = dot(mine[c][...], v, ((0,), (0,)))
                else:
                    part = dot(turned[0][:, c * t : (c + 1) * t], v)
                total = part if total is None else total + part
            if not split:
                outs[n][...] = total
            else:
                tile[...] = total
                if by_left:
                    owners = tile.shape[0] // size
                    for e in range(owners):
                        at = back[16 + (step - first) * owners + e]
                        for q in range(4):

                            @pl.when(at // 4 == q)
                            def _():
                                block = tile[e * size : (e + 1) * size, :]
                                outs[q][at - 4 * q, row : row + size, :] = block.astype(outs[q].dtype)
                else:
                    deal(back, tile, outs, row + pl.multiple_of((step - first) * size, 8), size)

        first += tiles
        row += size if by_left else tiles * size


def weight_grads(split, back, products):
    count = 2 if split else 1
    t = products[0][0][0].shape[0]
    left_specs, right_specs, lefts, rights, plan = [], [], [], [], []
    out_specs, out_shape = [], []
    at = row = 0
    for left, right, tiles, by_left in products:
        width = 0
        for c in range(count):
            a, b = left[c], right[c]
            a, part = a if isinstance(a, tuple) else (a, None)

            if by_left and c == 0:
                tiles = tiles // count
                width = a.shape[1] // (tiles * count)

            def step(i, at=at, tiles=tiles):
                return jnp.clip(i - at, 0, tiles - 1)

            if by_left:
                per = tiles // 2
                if split and c == 0:
                    left_specs.append(pl.BlockSpec(
                        (t, width), lambda i, back, step=step, per=per: (0, (2 * (step(i) // per) + back[32]) * per + step(i) % per)
                    ))
                else:
                    left_specs.append(pl.BlockSpec((t, width), lambda i, *_, step=step: (0, step(i))))
                right_specs.append(whole(b.shape))
            else:
                width = a.shape[-1]
                if part is None:
                    left_specs.append(whole(a.shape))
                else:
                    left_specs.append(pl.BlockSpec(
                        (1, t, width), lambda *_, part=part: (part, 0, 0), pipeline_mode=pl.Buffered(1)
                    ))
                if b.ndim == 3:
                    right_specs.append(pl.BlockSpec((1, t, LANES), lambda i, *_, step=step: (step(i), 0, 0)))
                else:
                    right_specs.append(pl.BlockSpec((t, LANES), lambda i, *_, step=step: (0, step(i))))
            lefts.append(a)
            rights.append(b)
        size = (width * tiles if by_left else width) // 16
        if not split:
            shape = (width * tiles, LANES) if by_left else (width, tiles * LANES)
            block = (width, LANES)
            out_specs.append(pl.BlockSpec(
                block, (lambda i, *_, step=step: (step(i), 0)) if by_left else (lambda i, *_, step=step: (0, step(i)))
            ))
            out_shape.append(shaped(shape, F32))
        plan.append((by_left, tiles, size))
        at += tiles
        row += size if by_left else tiles * size
    narrow = next(p[0][0].shape[1] for p in products if not p[3])
    if split:
        out_specs = [whole((4, row, LANES))] * 4
        out_shape = [shaped((4, row, LANES), BF)] * 4
    flops = 2 * count * t * narrow * at * LANES
    return prefetched(
        functools.partial(grads_kernel, split, tuple(plan)), back, lefts + rights, left_specs + right_specs,
        out_specs, out_shape, [pltpu.VMEM((narrow, LANES), F32), pltpu.VMEM((narrow, count * t), BF)],
        (at,), 60, "weight_grads", flops, flops // 256,
    )


def qkv_back_kernel(d_ref, x_ref, dx1_ref, w_ref, gain_ref, dx_ref):
    d = x_ref.shape[1]
    groups, _, span = d_ref.shape
    span //= 3
    dh = None
    for part in range(3):
        for g in range(groups):
            at = part * d + g * span
            piece = dot(d_ref[g, :, part * span : (part + 1) * span], w_ref[:, at : at + span], ((1,), (1,)))
            dh = piece if dh is None else dh + piece
    unit, inv = unit_norm(x_ref[...].astype(F32))
    dx_ref[...] = dx1_ref[...] + norm_back(dh * gain_ref[...], unit, inv)


def qkv_backward(d_qkv, tokens, dx1, w_qkv, gain):
    t, d = tokens.shape
    groups, _, span = d_qkv.shape
    return pl.pallas_call(
        qkv_back_kernel,
        grid=(t // ROWS,),
        in_specs=[pl.BlockSpec((groups, ROWS, span), lambda i: (0, i, 0))] + [rows(d)] * 2
        + [whole((d, 3 * d)), whole((1, d))],
        out_specs=rows(d),
        out_shape=shaped((t, d), F32),
        compiler_params=params(48),
        cost_estimate=pl.CostEstimate(flops=6 * t * d * d, transcendentals=0, bytes_accessed=6 * d * d + 16 * t * d),
        name="qkv_backward",
    )(d_qkv, tokens, dx1, w_qkv, gain)


def layout(doc_lengths, seq):
    docs = doc_lengths.shape[-1]
    upto = jnp.arange(docs)[:, None] <= jnp.arange(docs)[None, :]
    ends = jnp.sum(jnp.where(upto[None], doc_lengths[:, :, None], 0), axis=1)
    places = jnp.arange(seq, dtype=jnp.int32)
    passed = places[None, :, None] >= ends[:, None, :]
    start = jnp.sum(jnp.where(passed, doc_lengths[:, None, :], 0), axis=-1)
    valid = places[None, :] < ends[:, docs - 2 : docs - 1]
    return start.astype(jnp.int32), places[None, :] - start, valid


def tables(position):
    half = HEAD_DIM // 2
    lane = jnp.arange(PAIR)
    frequency = jnp.exp((lane % half).astype(F32) * (-2.0 * math.log(10000.0) / HEAD_DIM))
    angles = position.reshape(-1, 1).astype(F32) * frequency[None, :]
    sign = jnp.where(lane % HEAD_DIM < half, -1.0, 1.0)
    return jnp.cos(angles), jnp.sin(angles) * sign[None, :]


Z = 4
GROUPS = ((0, 2), (1, 3))


def index(x, core, z, y):
    return ((x * 2 + core) * Z + z) * 2 + y


def permute(value, move):
    places = [(x, c, z, y) for x in range(2) for c in range(2) for z in range(Z) for y in range(2)]
    return lax.ppermute(value, AXES, [(index(*p), index(*move(*p))) for p in places])


def over_x(v):
    return permute(v, lambda x, c, z, y: (1 - x, c, z, y))


def over_y(v):
    return permute(v, lambda x, c, z, y: (x, c, z, 1 - y))


def over_core(v):
    return permute(v, lambda x, c, z, y: (x, 1 - c, z, y))


def over_z(v, bits):
    return permute(v, lambda x, c, z, y: (x, c, z ^ bits, y))


def place():
    dp, fs = lax.axis_index("dp"), lax.axis_index("fsdp")
    return dp >> 1, dp & 1, fs >> 1, fs & 1


def gather_order():
    rows_of = []
    for core in range(2):
        for group, first in zip(GROUPS, ("x", "y")):
            for second in range(2):
                for one in range(2):
                    dx, dy = (one, second) if first == "x" else (second, one)
                    rows_of += [(dx, core, dz, dy) for dz in group]
    dx, dc, dz, dy = np.array(rows_of, np.int32).T
    x, c, z, y = place()
    order = index(x ^ dx, c ^ dc, z ^ dz, y ^ dy)
    return jnp.concatenate([order, c[None]]).astype(jnp.int32)


def scatter_order():
    rows_of = []
    for group, first in zip(GROUPS, ("y", "x")):
        for one in (1, 0):
            for second in (1, 0):
                dx, dy = (second, one) if first == "y" else (one, second)
                rows_of += [(dx, dz, dy) for dz in group]
    dx, dz, dy = np.array(rows_of, np.int32).T
    x, c, z, y = place()
    order = ((x ^ dx) * Z + (z ^ dz)) * 2 + (y ^ dy)
    spots = jnp.arange(len(rows_of), dtype=jnp.int32)
    where = jnp.sum(jnp.where(order[None, :] == spots[:, None], spots[None, :], 0), axis=1)
    return jnp.concatenate([order, where, c[None]]).astype(jnp.int32)


def tie(value, other):
    return lax.optimization_barrier((value, other))[0]


class Gather:
    def __init__(self, block):
        self.block = block

    def far_z(self, after=None):
        block = self.block if after is None else tie(self.block, after)
        self.even = jnp.stack([block, over_z(block, 2)])
        return self.even

    def near_z(self, after=None):
        if after is not None:
            self.even = tie(self.even, after)
        self.odd = over_z(self.even, 1)
        return self.odd

    def first(self):
        self.got = (over_x(self.even), over_y(self.odd))
        return self.got

    def second(self, after=None):
        got = self.got if after is None else tie(self.got, after)
        even, odd = jnp.concatenate([self.even, got[0]]), jnp.concatenate([self.odd, got[1]])
        self.near = [even, odd, over_core(even), over_core(odd)]
        self.far = [over_y(even), over_x(odd)]
        return self.far

    def core(self, after=None):
        far = self.far if after is None else tie(self.far, after)
        even, odd, even_core, odd_core = self.near
        return [even, far[0], odd, far[1], even_core, over_core(far[0]), odd_core, over_core(far[1])]


class Reduce:
    def __init__(self, send_a, keep_a, send_b, keep_b):
        self.sends, self.a, self.b = (send_a, send_b), keep_a.astype(F32), keep_b.astype(F32)

    def first(self, after=None):
        sends = self.sends if after is None else tie(self.sends, after)
        self.got = (over_y(sends[0]), over_x(sends[1]))
        return self.got

    def wait_for(self, after):
        if after is not None:
            self.got = tie(self.got, after)

    def second(self, after=None):
        self.wait_for(after)
        self.a = self.a + self.got[0].astype(F32)
        self.b = self.b + self.got[1].astype(F32)
        self.got = (over_x(self.a[:2].astype(BF)), over_y(self.b[:2].astype(BF)))
        return self.got

    def near_z(self, after=None):
        self.wait_for(after)
        self.a = self.a[2:] + self.got[0].astype(F32)
        self.got = over_z((self.b[2:] + self.got[1].astype(F32)).astype(BF), 1)
        return self.got

    def far_z(self, after=None):
        self.wait_for(after)
        self.a = self.a + self.got.astype(F32)
        self.got = over_z(self.a[1].astype(BF), 2)
        return self.got

    def own(self):
        return self.a[0] + self.got.astype(F32)


def unslab(block, width):
    size = block.shape[0] * LANES // width
    return jnp.concatenate([block[s * size : (s + 1) * size] for s in range(width // LANES)], axis=1)


def slab(block):
    return [block[:, s * LANES : (s + 1) * LANES] for s in range(block.shape[1] // LANES)]


def local(fast, tokens, doc_lengths, cotangent, w_qkv, w_out, w_up, w_down,
          gain_attn, gain_inner, gain_ffn, gain_mid):
    row_count = doc_lengths.shape[0]
    seq = tokens.shape[0] // row_count
    d, f = tokens.shape[1], w_up.shape[1]
    wide = min(seq, 512) // BLOCK + 1
    blocks = seq // BLOCK
    shards = (gain_attn, gain_inner, gain_ffn, gain_mid)

    start, position, valid = layout(doc_lengths, seq)
    cos, sin = tables(position)
    firsts = start[:, ::BLOCK] // BLOCK
    reach = (jnp.arange(blocks, dtype=jnp.int32)[None, :] - firsts + 1).reshape(-1)
    start_row = jnp.repeat(start, 8, axis=0)
    gy = jnp.where(valid.reshape(-1, 1), cotangent, jnp.zeros_like(cotangent))

    def scatter(g):
        return lax.psum_scatter(g, AXES, scatter_dimension=0, tiled=True)

    def gather(v):
        return lax.all_gather(v, AXES, axis=0, tiled=True)

    if fast:
        order, back = gather_order(), scatter_order()
        one, two = (Gather(b) for b in pack(w_qkv, w_out, w_up, w_down, shards))
        seen = one.far_z()
        two.far_z(seen)
        one.even = tie(one.even, (cos, sin))
        one.near_z()
        one.first()
        one.second(two.even)
        two.near_z()
        two.first()
        parts_qkv = one.core()
        gy_both = (gy, over_core(gy))
        cos, sin = tie((cos, sin), (gy, start_row, reach, order, back))
    else:
        order = back = jnp.zeros((8,), jnp.int32)

        def scaled(w, gain):
            return gather((w.astype(F32) * gain.astype(F32)[:, None]).astype(BF))

        parts_qkv, parts_down = [gather(w_qkv)], [scaled(w_down, gain_mid)]
        parts_up = [scaled(w_out, gain_inner), scaled(w_up, gain_ffn)]

    whole_gain = None if fast else gather(gain_attn).astype(F32).reshape(1, -1)
    h1, qkv, full_qkv, *rest = qkv_forward(fast, order, tokens, cos, sin, parts_qkv, whole_gain)
    g_attn = rest[0] if fast else whole_gain
    if fast:
        two.second(g_attn)
        start_row = tie(start_row, (gy_both[1], two.near[2:]))
    mixed, lse = attention_forward(reach, qkv, start_row, row_count, wide)
    parts = two.core(lse) if fast else parts_up + parts_down
    a, h2, x1, m, dpre, dx1, low, d_mixed, full_down, _, _, *other = ffn_both(
        fast, order, mixed, tokens, gy, parts, f
    )

    def shared(value):
        return (value, over_core(value)) if fast else (value,)

    if fast:
        m_both = (m, over_core(other[1]))
        theirs = over_core(other[0])
        a_both, h2_both = (a, (theirs, 0)), (h2, (theirs, 1))
    else:
        gy_both, m_both, a_both, h2_both = (gy,), (m,), (a,), (h2,)
    low, dpre = shared(low), shared(dpre)

    def attend(group, groups, lse, so_far):
        return attention_backward(
            reach, qkv, d_mixed, mixed, lse, start_row, cos, sin, row_count, wide, group, groups, so_far
        )

    f = w_up.shape[1]
    d_qkv = attend(0, 1, lse, None)
    if fast:
        low = tie(low, d_qkv)
    grads = weight_grads(
        fast, back,
        [(m_both, gy_both, f // 384, True), (a_both, low, d // LANES, False), (h2_both, dpre, f // LANES, False)],
    )
    if fast:
        red = Reduce(*grads)
        first = red.first()
        h1 = tie(h1, grads[-1])
    d_qkv = attend(1, 2, tie(lse, grads[-1]), d_qkv)
    if fast:
        h1 = (h1[0], over_core(h1[1]))
        d_both = (d_qkv, over_core(tie(d_qkv, (first, h1[1]))))
        second = red.second(d_qkv)
        dx1 = tie(dx1, (d_qkv, first))
    else:
        d_both = (d_qkv,)
    grad_tokens = qkv_backward(d_qkv, tokens, dx1, full_qkv, g_attn)
    if fast:
        near = red.near_z(grad_tokens)
        h1 = tie(h1, (grad_tokens, second))
    grad_qkv = weight_grads(fast, back, [(h1, d_both, 3 * d // LANES, False)])
    if fast:
        red_qkv = Reduce(*grad_qkv)
        first = red_qkv.first()
        far = red.far_z(grad_qkv[-1])
        m = tie(m, (grad_qkv[-1], near))
    result = down_forward(m, x1, full_down)
    if fast:
        red_qkv.second((result, far))
        own = red.own()
        red_qkv.near_z()
        red_qkv.far_z()
        g_qkv = red_qkv.own()
        cuts = (w_down.shape[0], w_down.shape[0] + w_out.shape[0])
        own_down, grad_out, grad_up = own[: cuts[0]], own[cuts[0] : cuts[1]], unslab(own[cuts[1] :], f)
    else:
        own_down, grad_out, grad_up, g_qkv = (scatter(g.astype(BF)).astype(F32) for g in (*grads, *grad_qkv))
        g_qkv = jnp.concatenate(slab(g_qkv))
    size = w_qkv.shape[0]
    span = LANES // 3
    g_qkv = jnp.concatenate(
        [g_qkv[g * size : (g + 1) * size, p * span : (p + 1) * span] for p in range(3) for g in range(GRAD_GROUPS)], axis=1
    )
    raw = (g_qkv, grad_out, grad_up, own_down)
    row_sums = [jnp.sum(g * w.astype(F32), axis=1) for g, w in zip(raw, (w_qkv, w_out, w_up, w_down))]
    row_sums[0] = row_sums[0] / gain_attn.astype(F32)
    scaled_grads = [g * v.astype(F32)[:, None] for g, v in zip(raw[1:], shards[1:])]
    return (result, grad_tokens, g_qkv, *scaled_grads, *row_sums)


def solution(mesh):
    matrix, vector = P(AXES, None), P(AXES)
    fast = mesh.shape["dp"] == 4 and mesh.shape["fsdp"] == 2 * Z
    return jax.shard_map(
        functools.partial(local, fast),
        mesh=mesh,
        in_specs=(matrix,) * 7 + (vector,) * 4,
        out_specs=(matrix,) * 6 + (vector,) * 4,
        check_vma=False,
    )
```

```python
import functools
import math

import jax
import jax.numpy as jnp
import numpy as np
from jax import lax
from jax.experimental import pallas as pl
from jax.experimental.pallas import tpu as pltpu
from jax.sharding import PartitionSpec as P

HEADS = 12
HEAD_DIM = 64
PAIR = 2 * HEAD_DIM
PAIRS = HEADS // 2
EPSILON = 1e-05
MASKED_SCORE = -1e30
ROOT_HALF = 0.7071067811865476
INV_ROOT_TAU = 0.3989422804014327
BF = jnp.bfloat16
F32 = jnp.float32
MIB = 1 << 20
AXES = ("dp", "fsdp")
BLOCK = 256
ROWS = 256
LANES = 768
VMEM_MIB = 57
GRAD_GROUPS = 3


def dot(a, b, dims=((1,), (0,))):
    return lax.dot_general(a, b, (dims, ((), ())), preferred_element_type=F32)


def params(mib):
    return pltpu.CompilerParams(vmem_limit_bytes=max(mib, VMEM_MIB) * MIB)


def swap_halves(x):
    lane = lax.broadcasted_iota(jnp.int32, x.shape, 1)
    low = lax.rem(lane, HEAD_DIM) < HEAD_DIM // 2
    half = HEAD_DIM // 2
    return jnp.where(low, pltpu.roll(x, PAIR - half, 1), pltpu.roll(x, half, 1))


def unit_norm(x):
    mean = jnp.mean(x, axis=-1, keepdims=True)
    centred = x - mean
    inv = lax.rsqrt(jnp.mean(centred * centred, axis=-1, keepdims=True) + EPSILON)
    return centred * inv, inv


def norm_back(d_unit, unit, inv):
    return inv * (
        d_unit
        - jnp.mean(d_unit, axis=-1, keepdims=True)
        - unit * jnp.mean(d_unit * unit, axis=-1, keepdims=True)
    )


def whole(shape):
    return pl.BlockSpec(shape, lambda *_: (0,) * len(shape), pipeline_mode=pl.Buffered(1))


def rows(width, block=ROWS):
    return pl.BlockSpec((block, width), lambda i: (i, 0))


def shaped(shape, dtype):
    return jax.ShapeDtypeStruct(shape, dtype)


def hbm():
    return pl.BlockSpec(memory_space=pl.ANY)


def fetch(order, parts, places, sem):
    if len(parts) < 8 and parts[0].ndim == 2:
        for part, (_, _, buffer, _) in zip(parts, places):
            pltpu.make_async_copy(part, buffer, sem).start()
        return
    count = parts[0].shape[0]
    for p, part in enumerate(parts):
        for b in range(count):
            owner = b if order is None else order[p * count + b]
            for first, size, buffer, column in places:
                row = owner * size if order is None else pl.multiple_of(owner * size, 8)
                pltpu.make_async_copy(
                    part.at[b, pl.ds(first, size), :],
                    buffer.at[pl.ds(row, size), pl.ds(column, LANES)],
                    sem,
                ).start()


def arrive(buffers, sem):
    for buffer in buffers:
        pltpu.make_async_copy(buffer, buffer, sem).wait()


def deal(back, tile, outs, row, size):
    quarter = outs[0].shape[0]
    for q, out in enumerate(outs):

        @pl.loop(0, quarter)
        def _(j):
            block = tile[pl.ds(pl.multiple_of(back[q * quarter + j] * size, 8), size), :]
            out[j, pl.ds(row, size), :] = block.astype(out.dtype)


def slabs(first, size, buffer, width):
    return [(first + s * size, size, buffer, s * LANES) for s in range(width // LANES)]


def scale_rows(w, gain):
    n = w.shape[0]
    square = lax.broadcasted_iota(jnp.int32, (n, n), 0) == lax.broadcasted_iota(jnp.int32, (n, n), 1)
    return dot(jnp.where(square, gain.astype(F32), 0.0).astype(BF), w).astype(BF)


def pack_kernel(wq_ref, wo_ref, wu_ref, wd_ref, ga_ref, gi_ref, gf_ref, gm_ref, one_ref, two_ref):
    row = 0
    for c in range(wq_ref.shape[1] // LANES):
        one_ref[row : row + wq_ref.shape[0], :] = wq_ref[:, c * LANES : (c + 1) * LANES]
        row += wq_ref.shape[0]
    one_ref[row:, :] = ga_ref[...]
    row = 0
    for ref, gain in ((wd_ref, gm_ref), (wo_ref, gi_ref), (wu_ref, gf_ref)):
        for c in range(ref.shape[1] // LANES):
            two_ref[row : row + ref.shape[0], :] = scale_rows(ref[:, c * LANES : (c + 1) * LANES], gain[...])
            row += ref.shape[0]


def pack(w_qkv, w_out, w_up, w_down, gains):
    first = w_qkv.size // LANES + 8
    second = (w_out.size + w_up.size + w_down.size) // LANES
    row = jnp.pad(gains[0].reshape(1, -1), ((0, 7), (0, LANES - gains[0].shape[0])))
    return pl.pallas_call(
        pack_kernel, out_shape=[shaped((first, LANES), BF), shaped((second, LANES), BF)], name="pack"
    )(w_qkv, w_out, w_up, w_down, row, *(g.reshape(1, -1) for g in gains[1:]))


def spread(rows_in, offset, count, owners):
    lanes = rows_in.shape[1]
    wide = owners * count
    lane = lax.broadcasted_iota(jnp.int32, (lanes, wide), 0)
    column = lax.broadcasted_iota(jnp.int32, (lanes, wide), 1)
    pick = (lane - offset == lax.rem(column, count)).astype(F32).astype(BF)
    full = dot(rows_in, pick)
    owner = lax.broadcasted_iota(jnp.int32, (owners, wide), 0)
    column = lax.broadcasted_iota(jnp.int32, (owners, wide), 1)
    own = (column >= owner * count) & (column < owner * count + count)
    return jnp.sum(jnp.where(own, full, 0.0), axis=0, keepdims=True)


def qkv_kernel(split, *refs):
    if split:
        order, x_ref, cos_ref, sin_ref, *refs = refs
        parts, refs = refs[:8], refs[8:]
        h_ref, other_ref, qkv_ref, w_ref, ga_ref, gains, sem, gain_sem = refs
        h_refs = (h_ref, other_ref)
    else:
        order, x_ref, cos_ref, sin_ref, ga_ref, *refs = refs
        parts, refs = refs[:1], refs[1:]
        h_ref, qkv_ref, w_ref, sem = refs
        h_refs = (h_ref,)
    width = x_ref.shape[1]
    step = pl.program_id(0)
    if split:
        size = width // 32
        weight = slabs(0, size, w_ref, 3 * width)

        @pl.when(step == 0)
        def _():
            fetch(order, parts, [(3 * size, 8, gains, 0)], gain_sem)
            fetch(order, parts, weight, sem)
            arrive([gains], gain_sem)
            owner = lax.broadcasted_iota(jnp.int32, (32, 256), 0)
            lane = lax.broadcasted_iota(jnp.int32, (32, 256), 1)
            pick = (lane == owner * 8).astype(F32).astype(BF)
            per_owner = dot(pick, gains[:, :PAIR]).astype(BF)
            ga_ref[...] = spread(per_owner, 0, size, 32)
            arrive([w_ref], sem)
    else:

        @pl.when(step == 0)
        def _():
            fetch(None, parts, [(0, 0, w_ref, 0)], sem)
            arrive([w_ref], sem)

    unit, _ = unit_norm(x_ref[...].astype(F32))
    h = (unit * ga_ref[...]).astype(BF)
    store_low(split, order[32] if split else 0, h, h_refs)
    cos, sin = cos_ref[...], sin_ref[...]
    for part in range(3):
        y = dot(h, w_ref[:, part * width : (part + 1) * width])
        for c in range(width // PAIR):
            z = y[:, c * PAIR : (c + 1) * PAIR]
            if part < 2:
                z = z * cos + swap_halves(z) * sin
            if part == 0:
                z = z * (1.0 / math.sqrt(HEAD_DIM))
            at = part * width + c * PAIR
            qkv_ref[:, at : at + PAIR] = z.astype(BF)


def prefetched(kernel, order, inputs, in_specs, out_specs, out_shape, scratch, grid, mib, name, flops, data):
    return pl.pallas_call(
        kernel,
        grid_spec=pltpu.PrefetchScalarGridSpec(
            num_scalar_prefetch=1,
            grid=grid,
            in_specs=in_specs,
            out_specs=out_specs,
            scratch_shapes=scratch,
        ),
        out_shape=out_shape,
        compiler_params=params(mib),
        cost_estimate=pl.CostEstimate(flops=flops, transcendentals=0, bytes_accessed=data),
        name=name,
    )(order, *inputs)


def rows(width, block=ROWS):
    return pl.BlockSpec((block, width), lambda i, *_: (i, 0))


def whole(shape):
    return pl.BlockSpec(shape, lambda *_: (0,) * len(shape), pipeline_mode=pl.Buffered(1))


def qkv_forward(split, order, tokens, cos, sin, parts, gain):
    t, d = tokens.shape
    n = 3 * d
    inputs = [tokens, cos, sin]
    in_specs = [rows(d), rows(PAIR), rows(PAIR)]
    out_specs, out_shape = low_specs(split, t, d)
    lows = len(out_specs)
    out_specs = out_specs + [rows(n), whole((d, n))]
    out_shape = out_shape + [shaped((t, n), BF), shaped((d, n), BF)]
    scratch = [pltpu.SemaphoreType.DMA]
    if split:
        out_specs += [whole((1, d))]
        out_shape += [shaped((1, d), F32)]
        scratch = [pltpu.VMEM((32 * 8, LANES), BF), pltpu.SemaphoreType.DMA, pltpu.SemaphoreType.DMA]
    else:
        inputs.append(gain)
        in_specs.append(whole((1, d)))
    outs = prefetched(
        functools.partial(qkv_kernel, split), order, inputs + list(parts), in_specs + [hbm()] * len(parts),
        out_specs, out_shape, scratch, (t // ROWS,), 40, "qkv_forward",
        2 * t * d * n, 4 * d * n + 12 * t * d,
    )
    return (outs[:lows], *outs[lows:])


def window(i, n):
    return slice((i - n + 1) * BLOCK, (i + 1) * BLOCK)


def head_masks(shape):
    lane = lax.broadcasted_iota(jnp.int32, shape, 1)
    return lane < HEAD_DIM


def attention_forward_kernel(wide, reach, q_ref, k_ref, v_ref, start_ref, o_ref, lse_ref, bias):
    row, pair = pl.program_id(0), pl.program_id(1)
    seq = q_ref.shape[0]
    blocks = seq // BLOCK

    @pl.when(pair == 0)
    def _():
        for i in range(blocks):
            at = slice(i * BLOCK, (i + 1) * BLOCK)
            shape = (BLOCK, wide * BLOCK)
            key = (i - wide + 1) * BLOCK + lax.broadcasted_iota(jnp.int32, shape, 1)
            query = i * BLOCK + lax.broadcasted_iota(jnp.int32, shape, 0)
            row_of = start_ref[0:1, at].astype(F32)
            start = jnp.broadcast_to(row_of, (PAIR, BLOCK)).T[:, 0:1].astype(jnp.int32)
            keep = (key >= start) & (key <= query)
            bias[at, :] = jnp.where(keep, 0.0, MASKED_SCORE)

    first = head_masks((BLOCK, PAIR))
    for i in range(blocks):
        at = slice(i * BLOCK, (i + 1) * BLOCK)
        most = min(wide, i + 1)
        for n in range(1, most + 1):

            @pl.when(reach[row * blocks + i] == n)
            def _():
                q = q_ref[at, :]
                w = window(i, n)
                k, v = k_ref[w, :], v_ref[w, :]
                b = bias[at, (wide - n) * BLOCK :]
                mask = head_masks(k.shape)
                zero = jnp.zeros_like(k)
                masks = (mask, jnp.logical_not(mask))
                scores = [dot(q, jnp.where(pick, k, zero), ((1,), (1,))) for pick in masks]
                total, lses = None, []
                for s, pick in zip(scores, masks):
                    s = s + b
                    top = jnp.max(s, axis=-1, keepdims=True)
                    p = jnp.exp(s - top)
                    den = jnp.sum(p, axis=-1, keepdims=True)
                    part = dot((p * (1.0 / den)).astype(BF), jnp.where(pick, v, zero))
                    total = part if total is None else total + part
                    lses.append(top + jnp.log(den))
                o_ref[at, :] = total
                both = jnp.where(first, lses[0], lses[1]).T
                lse_ref[0, 0:1, at] = both[0:1, :]
                lse_ref[0, 1:2, at] = both[HEAD_DIM : HEAD_DIM + 1, :]


def attention_forward(reach, qkv, start, row_count, wide):
    t = qkv.shape[0]
    seq = t // row_count
    d = qkv.shape[1] // 3

    def columns(part):
        return pl.BlockSpec((seq, PAIR), lambda r, p, *_: (r, part * PAIRS + p))

    return pl.pallas_call(
        functools.partial(attention_forward_kernel, wide),
        grid_spec=pltpu.PrefetchScalarGridSpec(
            num_scalar_prefetch=1,
            grid=(row_count, PAIRS),
            in_specs=[
                columns(0),
                columns(1),
                columns(2),
                pl.BlockSpec((8, seq), lambda r, p, *_: (r, 0)),
            ],
            out_specs=[
                pl.BlockSpec((seq, PAIR), lambda r, p, *_: (r, p)),
                pl.BlockSpec((1, 8, seq), lambda r, p, *_: (r * PAIRS + p, 0, 0)),
            ],
            scratch_shapes=[pltpu.VMEM((seq, wide * BLOCK), F32)],
        ),
        out_shape=[shaped((t, d), F32), shaped((row_count * PAIRS, 8, seq), F32)],
        compiler_params=params(32),
        cost_estimate=pl.CostEstimate(
            flops=8 * t * d * BLOCK, transcendentals=t * HEADS * 512, bytes_accessed=12 * t * d
        ),
        name="attention_forward",
    )(reach, qkv, qkv, qkv, start)


def attention_backward_kernel(wide, reach, q_ref, k_ref, v_ref, do_ref, o_ref, lse_ref, start_ref, cos_ref, sin_ref, *refs):
    grad_ref, bias, ks, vs, qs, dos, dk_acc, dv_acc, dq_acc = refs[-9:]
    row, pair = pl.program_id(0), pl.program_id(1)
    seq = q_ref.shape[0]
    blocks = seq // BLOCK

    @pl.when(pair == 0)
    def _():
        for i in range(blocks):
            at = slice(i * BLOCK, (i + 1) * BLOCK)
            shape = (wide * BLOCK, BLOCK)
            key = (i - wide + 1) * BLOCK + lax.broadcasted_iota(jnp.int32, shape, 0)
            query = i * BLOCK + lax.broadcasted_iota(jnp.int32, shape, 1)
            keep = (key >= start_ref[0:1, at]) & (key <= query)
            bias[:, at] = jnp.where(keep, 0.0, MASKED_SCORE)

    mask = head_masks((seq, PAIR))
    for src, dst in ((k_ref, ks), (v_ref, vs), (q_ref, qs), (do_ref, dos)):
        x = src[...]
        zero = jnp.zeros_like(x)
        dst[0] = jnp.where(mask, x, zero)
        dst[1] = jnp.where(mask, zero, x)
    dk_acc[...] = jnp.zeros_like(dk_acc)
    dv_acc[...] = jnp.zeros_like(dv_acc)
    lane8 = lax.broadcasted_iota(jnp.int32, (8, PAIR), 1) // HEAD_DIM
    row8 = lax.broadcasted_iota(jnp.int32, (8, PAIR), 0)
    picks = (lane8 == row8).astype(F32)
    delta = lax.dot_general(
        picks, do_ref[...].astype(F32) * o_ref[...], (((1,), (1,)), ((), ())),
        precision=lax.Precision.HIGHEST, preferred_element_type=F32,
    )
    for i in range(blocks):
        at = slice(i * BLOCK, (i + 1) * BLOCK)
        most = min(wide, i + 1)
        for n in range(1, most + 1):

            @pl.when(reach[row * blocks + i] == n)
            def _():
                w = window(i, n)
                b = bias[(wide - n) * BLOCK :, at]
                q, do = q_ref[at, :], do_ref[at, :]
                ps, dss = [], []
                for h in range(2):
                    s = dot(ks[h, w, :], q, ((1,), (1,))) + b
                    p = jnp.exp(s - lse_ref[0, h : h + 1, at])
                    dp = dot(vs[h, w, :], do, ((1,), (1,)))
                    ds = (p * (dp - delta[h : h + 1, at])).astype(BF)
                    ps.append(p.astype(BF))
                    dss.append(ds)
                dv_acc[w, :] += dot(ps[0], dos[0, at, :]) + dot(ps[1], dos[1, at, :])
                dk_acc[w, :] += dot(dss[0], qs[0, at, :]) + dot(dss[1], qs[1, at, :])
                dq_acc[at, :] = dot(dss[0], ks[0, w, :], ((0,), (0,))) + dot(
                    dss[1], ks[1, w, :], ((0,), (0,))
                )

    cos, sin = cos_ref[...], sin_ref[...]
    dq = dq_acc[...] * (1.0 / math.sqrt(HEAD_DIM))
    dk = dk_acc[...]
    span = grad_ref.shape[2] // 3
    slot = lax.rem(pair, span // PAIR)
    grads = (dq * cos - swap_halves(dq) * sin, dk * cos - swap_halves(dk) * sin, dv_acc[...])
    for part, value in enumerate(grads):
        grad_ref[0, :, pl.ds(pl.multiple_of(part * span + slot * PAIR, PAIR), PAIR)] = value.astype(BF)


def attention_backward(reach, qkv, d_mixed, mixed, lse, start_row, cos, sin, row_count, wide, group, groups, so_far):
    pairs = PAIRS // GRAD_GROUPS
    t = qkv.shape[0]
    seq = t // row_count
    base = group * pairs
    span = 3 * pairs * PAIR

    def columns(part):
        return pl.BlockSpec((seq, PAIR), lambda r, p, *_: (r, part * PAIRS + base + p))

    table = pl.BlockSpec((seq, PAIR), lambda r, p, *_: (r, 0))
    inputs = [reach, qkv, qkv, qkv, d_mixed, mixed, lse, start_row, cos, sin]
    in_specs = [
        columns(0), columns(1), columns(2), columns(0), columns(0),
        pl.BlockSpec((1, 8, seq), lambda r, p, *_: (r * PAIRS + base + p, 0, 0)),
        pl.BlockSpec((8, seq), lambda r, p, *_: (r, 0)),
        table, table,
    ]
    aliases = {}
    if so_far is not None:
        aliases = {len(inputs): 0}
        inputs.append(so_far)
        in_specs.append(hbm())
    return pl.pallas_call(
        functools.partial(attention_backward_kernel, wide),
        grid_spec=pltpu.PrefetchScalarGridSpec(
            num_scalar_prefetch=1,
            grid=(row_count, pairs * groups),
            in_specs=in_specs,
            out_specs=pl.BlockSpec((1, seq, span), lambda r, p, *_: (group + p // pairs, r, 0)),
            scratch_shapes=[
                pltpu.VMEM((wide * BLOCK, seq), F32),
                pltpu.VMEM((2, seq, PAIR), BF),
                pltpu.VMEM((2, seq, PAIR), BF),
                pltpu.VMEM((2, seq, PAIR), BF),
                pltpu.VMEM((2, seq, PAIR), BF),
                pltpu.VMEM((seq, PAIR), F32),
                pltpu.VMEM((seq, PAIR), F32),
                pltpu.VMEM((seq, PAIR), F32),
            ],
        ),
        out_shape=shaped((GRAD_GROUPS, t, span), BF),
        input_output_aliases=aliases,
        compiler_params=params(40),
        cost_estimate=pl.CostEstimate(
            flops=20 * t * span * BLOCK // 3 * groups, transcendentals=t * HEADS * 128 * groups,
            bytes_accessed=20 * t * span // 3 * groups
        ),
        name="attention_backward",
    )(*inputs)


def halves(x):
    quarter = x.shape[1] // 4
    piece = [x[:, i * quarter : (i + 1) * quarter] for i in range(4)]
    return jnp.concatenate(piece[0::2], axis=1), jnp.concatenate(piece[1::2], axis=1)


def store_low(split, core, x, refs):
    if not split:
        refs[0][...] = x
        return
    pair = halves(x)
    for c in range(2):

        @pl.when(core == c)
        def _():
            refs[0][...] = pair[c]
            refs[1][...] = pair[1 - c]


def low_specs(split, t, d):
    if split:
        return [rows(d // 2)] * 2, [shaped((t, d // 2), BF)] * 2
    return [rows(d)], [shaped((t, d), BF)]


def ffn_kernel(split, *refs):
    order, o_ref, x_ref, gy_ref, *refs = refs
    count = 8 if split else 3
    parts, refs = refs[:count], refs[count:]
    a_ref, h2_ref, x1_ref, m_ref, dpre_ref, dx1_ref, low_ref, do_ref, wd_ref, wo_ref, wu_ref, *refs = refs
    theirs_ref, other_ref, *refs = refs if split else (None, None, *refs)
    act, slope, dm, out_sem, up_sem, down_sem = refs
    d, f = wu_ref.shape
    size, skip = d // 32, f // 32
    step = pl.program_id(0)
    core = order[32] if split else 0
    chunks = [slice(c, c + LANES) for c in range(0, f, LANES)]

    @pl.when(step == 0)
    def _():
        if split:
            fetch(order, parts, [(skip, size, wo_ref, 0)], out_sem)
            fetch(order, parts, slabs(skip + size, size, wu_ref, f), up_sem)
            fetch(order, parts, [(0, skip, wd_ref, 0)], down_sem)
        else:
            fetch(order, parts[:1], [(0, 0, wo_ref, 0)], out_sem)
            fetch(order, parts[1:2], [(0, 0, wu_ref, 0)], up_sem)
            fetch(order, parts[2:], [(0, 0, wd_ref, 0)], down_sem)

    mixed = o_ref[...]
    unit_in, inv_in = unit_norm(mixed)
    a = unit_in.astype(BF)
    store_low(split, core, a, (a_ref, theirs_ref.at[0] if split else None))

    @pl.when(step == 0)
    def _():
        arrive([wo_ref], out_sem)

    x1 = x_ref[...].astype(F32) + dot(a, wo_ref[...])
    x1_ref[...] = x1
    unit_two, inv_two = unit_norm(x1)
    h2 = unit_two.astype(BF)
    store_low(split, core, h2, (h2_ref, theirs_ref.at[1] if split else None))
    gy = gy_ref[...]

    @pl.when(step == 0)
    def _():
        arrive([wu_ref], up_sem)
        arrive([wd_ref], down_sem)

    total = None
    for at in chunks:
        hidden = dot(h2, wu_ref[:, at])
        dm[:, at] = dot(gy, wd_ref[at, :], ((1,), (1,)))
        cdf = 0.5 + 0.5 * lax.erf(hidden * ROOT_HALF)
        slope[:, at] = cdf + hidden * (jnp.exp(-0.5 * hidden * hidden) * INV_ROOT_TAU)
        value = hidden * cdf
        act[:, at] = value
        part = jnp.sum(value, axis=-1, keepdims=True)
        total = part if total is None else total + part
    mean = total * (1.0 / f)
    total = None
    for at in chunks:
        centred = act[:, at] - mean
        part = jnp.sum(centred * centred, axis=-1, keepdims=True)
        total = part if total is None else total + part
    inv = lax.rsqrt(total * (1.0 / f) + EPSILON)
    first = second = None
    for at in chunks:
        unit = (act[:, at] - mean) * inv
        act[:, at] = unit
        m_ref[:, at] = unit.astype(BF)
        d_unit = dm[:, at]
        part = jnp.sum(d_unit, axis=-1, keepdims=True)
        first = part if first is None else first + part
        part = jnp.sum(d_unit * unit, axis=-1, keepdims=True)
        second = part if second is None else second + part
    first, second = first * (1.0 / f), second * (1.0 / f)
    dh2 = None
    for at in chunks:
        d_act = inv * (dm[:, at] - first - act[:, at] * second)
        dpre = (d_act * slope[:, at]).astype(BF)
        dpre_ref[:, at] = dpre
        part = dot(dpre, wu_ref[:, at], ((1,), (1,)))
        dh2 = part if dh2 is None else dh2 + part
    dx1 = gy.astype(F32) + norm_back(dh2, unit_two, inv_two)
    dx1_ref[...] = dx1
    low = dx1.astype(BF)
    low_ref[...] = low
    da = dot(low, wo_ref[...], ((1,), (1,)))
    do_ref[...] = norm_back(da, unit_in, inv_in).astype(BF)

    if split:
        quarter = f // 4
        for j in range(2):
            at = pl.multiple_of((2 * j + 1 - core) * quarter, PAIR)
            other_ref[:, j * quarter : (j + 1) * quarter] = m_ref[:, pl.ds(at, quarter)]


def ffn_both(split, order, mixed, tokens, gy, parts, f):
    t, d = tokens.shape
    width = d // 2 if split else d
    more = [(rows(f // 2), shaped((t, f // 2), BF))] * split
    if split:
        theirs = pl.BlockSpec((2, ROWS, width), lambda i, *_: (0, i, 0))
        more.insert(0, (theirs, shaped((2, t, width), BF)))
    return prefetched(
        functools.partial(ffn_kernel, split), order, [mixed, tokens, gy, *parts],
        [rows(d), rows(d), rows(d)] + [hbm()] * len(parts),
        [rows(width), rows(width), rows(d), rows(f), rows(f), rows(d), rows(d), rows(d), whole((f, d)), whole((d, d)),
         whole((d, f))] + [m[0] for m in more],
        [
            shaped((t, width), BF), shaped((t, width), BF), shaped((t, d), F32), shaped((t, f), BF), shaped((t, f), BF),
            shaped((t, d), F32), shaped((t, d), BF), shaped((t, d), BF), shaped((f, d), BF), shaped((d, d), BF),
            shaped((d, f), BF),
        ] + [m[1] for m in more],
        [
            pltpu.VMEM((ROWS, f), F32), pltpu.VMEM((ROWS, f), F32), pltpu.VMEM((ROWS, f), F32), pltpu.SemaphoreType.DMA,
            pltpu.SemaphoreType.DMA, pltpu.SemaphoreType.DMA,
        ],
        (t // ROWS,), 60, "ffn_both", 2 * t * d * (2 * d + 3 * f), 6 * d * f + 4 * t * f + 30 * t * d,
    )


def result_kernel(m_ref, x1_ref, wd_ref, y_ref):
    y_ref[...] = (x1_ref[...] + dot(m_ref[...], wd_ref[...])).astype(BF)


def down_forward(m, x1, w_down):
    t, d = x1.shape
    f = m.shape[1]
    return pl.pallas_call(
        result_kernel,
        grid=(t // ROWS,),
        in_specs=[rows(f), rows(d), whole((f, d))],
        out_specs=rows(d),
        out_shape=shaped((t, d), BF),
        compiler_params=params(48),
        cost_estimate=pl.CostEstimate(flops=2 * t * d * f, transcendentals=0, bytes_accessed=2 * d * f + 2 * t * f + 6 * t * d),
        name="down_forward",
    )(m, x1, w_down)


def grads_kernel(split, products, *refs):
    back, *refs = refs
    count = 2 if split else 1
    left, refs = refs[: len(products) * count], refs[len(products) * count :]
    right, refs = refs[: len(products) * count], refs[len(products) * count :]
    outs, refs = refs[: 4 if split else len(products)], refs[4 if split else len(products) :]
    tile, turned = refs[0], refs[1:]
    step = pl.program_id(0)
    first, row = 0, 0
    for n, (by_left, tiles, size) in enumerate(products):
        mine = [left[n * count + c] for c in range(count)]
        value = [right[n * count + c] for c in range(count)]

        if not by_left:

            @pl.when(step == first)
            def _():
                t = mine[0].shape[0]
                for c in range(count):
                    flat = mine[c][...] if len(mine[c].shape) == 2 else mine[c][0]
                    turned[0][:, c * t : (c + 1) * t] = flat.T

        @pl.when((step >= first) & (step < first + tiles))
        def _():
            total = None
            for c in range(count):
                v = value[c][...] if len(value[c].shape) == 2 else value[c][0]
                t = v.shape[0]
                if by_left:
                    part = dot(mine[c][...], v, ((0,), (0,)))
                else:
                    part = dot(turned[0][:, c * t : (c + 1) * t], v)
                total = part if total is None else total + part
            if not split:
                outs[n][...] = total
            else:
                tile[...] = total
                if by_left:
                    owners = tile.shape[0] // size
                    for e in range(owners):
                        at = back[16 + (step - first) * owners + e]
                        for q in range(4):

                            @pl.when(at // 4 == q)
                            def _():
                                block = tile[e * size : (e + 1) * size, :]
                                outs[q][at - 4 * q, row : row + size, :] = block.astype(outs[q].dtype)
                else:
                    deal(back, tile, outs, row + pl.multiple_of((step - first) * size, 8), size)

        first += tiles
        row += size if by_left else tiles * size


def weight_grads(split, back, products):
    count = 2 if split else 1
    t = products[0][0][0].shape[0]
    left_specs, right_specs, lefts, rights, plan = [], [], [], [], []
    out_specs, out_shape = [], []
    at = row = 0
    for left, right, tiles, by_left in products:
        width = 0
        for c in range(count):
            a, b = left[c], right[c]
            a, part = a if isinstance(a, tuple) else (a, None)

            if by_left and c == 0:
                tiles = tiles // count
                width = a.shape[1] // (tiles * count)

            def step(i, at=at, tiles=tiles):
                return jnp.clip(i - at, 0, tiles - 1)

            if by_left:
                per = tiles // 2
                if split and c == 0:
                    left_specs.append(pl.BlockSpec(
                        (t, width), lambda i, back, step=step, per=per: (0, (2 * (step(i) // per) + back[32]) * per + step(i) % per)
                    ))
                else:
                    left_specs.append(pl.BlockSpec((t, width), lambda i, *_, step=step: (0, step(i))))
                right_specs.append(whole(b.shape))
            else:
                width = a.shape[-1]
                if part is None:
                    left_specs.append(whole(a.shape))
                else:
                    left_specs.append(pl.BlockSpec(
                        (1, t, width), lambda *_, part=part: (part, 0, 0), pipeline_mode=pl.Buffered(1)
                    ))
                if b.ndim == 3:
                    right_specs.append(pl.BlockSpec((1, t, LANES), lambda i, *_, step=step: (step(i), 0, 0)))
                else:
                    right_specs.append(pl.BlockSpec((t, LANES), lambda i, *_, step=step: (0, step(i))))
            lefts.append(a)
            rights.append(b)
        size = (width * tiles if by_left else width) // 16
        if not split:
            shape = (width * tiles, LANES) if by_left else (width, tiles * LANES)
            block = (width, LANES)
            out_specs.append(pl.BlockSpec(
                block, (lambda i, *_, step=step: (step(i), 0)) if by_left else (lambda i, *_, step=step: (0, step(i)))
            ))
            out_shape.append(shaped(shape, F32))
        plan.append((by_left, tiles, size))
        at += tiles
        row += size if by_left else tiles * size
    narrow = next(p[0][0].shape[1] for p in products if not p[3])
    if split:
        out_specs = [whole((4, row, LANES))] * 4
        out_shape = [shaped((4, row, LANES), BF)] * 4
    flops = 2 * count * t * narrow * at * LANES
    return prefetched(
        functools.partial(grads_kernel, split, tuple(plan)), back, lefts + rights, left_specs + right_specs,
        out_specs, out_shape, [pltpu.VMEM((narrow, LANES), F32), pltpu.VMEM((narrow, count * t), BF)],
        (at,), 60, "weight_grads", flops, flops // 256,
    )


def qkv_back_kernel(d_ref, x_ref, dx1_ref, w_ref, gain_ref, dx_ref):
    d = x_ref.shape[1]
    groups, _, span = d_ref.shape
    span //= 3
    dh = None
    for part in range(3):
        for g in range(groups):
            at = part * d + g * span
            piece = dot(d_ref[g, :, part * span : (part + 1) * span], w_ref[:, at : at + span], ((1,), (1,)))
            dh = piece if dh is None else dh + piece
    unit, inv = unit_norm(x_ref[...].astype(F32))
    dx_ref[...] = dx1_ref[...] + norm_back(dh * gain_ref[...], unit, inv)


def qkv_backward(d_qkv, tokens, dx1, w_qkv, gain):
    t, d = tokens.shape
    groups, _, span = d_qkv.shape
    return pl.pallas_call(
        qkv_back_kernel,
        grid=(t // ROWS,),
        in_specs=[pl.BlockSpec((groups, ROWS, span), lambda i: (0, i, 0))] + [rows(d)] * 2
        + [whole((d, 3 * d)), whole((1, d))],
        out_specs=rows(d),
        out_shape=shaped((t, d), F32),
        compiler_params=params(48),
        cost_estimate=pl.CostEstimate(flops=6 * t * d * d, transcendentals=0, bytes_accessed=6 * d * d + 16 * t * d),
        name="qkv_backward",
    )(d_qkv, tokens, dx1, w_qkv, gain)


def layout(doc_lengths, seq):
    docs = doc_lengths.shape[-1]
    upto = jnp.arange(docs)[:, None] <= jnp.arange(docs)[None, :]
    ends = jnp.sum(jnp.where(upto[None], doc_lengths[:, :, None], 0), axis=1)
    places = jnp.arange(seq, dtype=jnp.int32)
    passed = places[None, :, None] >= ends[:, None, :]
    start = jnp.sum(jnp.where(passed, doc_lengths[:, None, :], 0), axis=-1)
    valid = places[None, :] < ends[:, docs - 2 : docs - 1]
    return start.astype(jnp.int32), places[None, :] - start, valid


def tables(position):
    half = HEAD_DIM // 2
    lane = jnp.arange(PAIR)
    frequency = jnp.exp((lane % half).astype(F32) * (-2.0 * math.log(10000.0) / HEAD_DIM))
    angles = position.reshape(-1, 1).astype(F32) * frequency[None, :]
    sign = jnp.where(lane % HEAD_DIM < half, -1.0, 1.0)
    return jnp.cos(angles), jnp.sin(angles) * sign[None, :]


Z = 4
GROUPS = ((0, 2), (1, 3))


def index(x, core, z, y):
    return ((x * 2 + core) * Z + z) * 2 + y


def permute(value, move):
    places = [(x, c, z, y) for x in range(2) for c in range(2) for z in range(Z) for y in range(2)]
    return lax.ppermute(value, AXES, [(index(*p), index(*move(*p))) for p in places])


def over_x(v):
    return permute(v, lambda x, c, z, y: (1 - x, c, z, y))


def over_y(v):
    return permute(v, lambda x, c, z, y: (x, c, z, 1 - y))


def over_core(v):
    return permute(v, lambda x, c, z, y: (x, 1 - c, z, y))


def over_z(v, bits):
    return permute(v, lambda x, c, z, y: (x, c, z ^ bits, y))


def place():
    dp, fs = lax.axis_index("dp"), lax.axis_index("fsdp")
    return dp >> 1, dp & 1, fs >> 1, fs & 1


def gather_order():
    rows_of = []
    for core in range(2):
        for group, first in zip(GROUPS, ("x", "y")):
            for second in range(2):
                for one in range(2):
                    dx, dy = (one, second) if first == "x" else (second, one)
                    rows_of += [(dx, core, dz, dy) for dz in group]
    dx, dc, dz, dy = np.array(rows_of, np.int32).T
    x, c, z, y = place()
    order = index(x ^ dx, c ^ dc, z ^ dz, y ^ dy)
    return jnp.concatenate([order, c[None]]).astype(jnp.int32)


def scatter_order():
    rows_of = []
    for group, first in zip(GROUPS, ("y", "x")):
        for one in (1, 0):
            for second in (1, 0):
                dx, dy = (second, one) if first == "y" else (one, second)
                rows_of += [(dx, dz, dy) for dz in group]
    dx, dz, dy = np.array(rows_of, np.int32).T
    x, c, z, y = place()
    order = ((x ^ dx) * Z + (z ^ dz)) * 2 + (y ^ dy)
    spots = jnp.arange(len(rows_of), dtype=jnp.int32)
    where = jnp.sum(jnp.where(order[None, :] == spots[:, None], spots[None, :], 0), axis=1)
    return jnp.concatenate([order, where, c[None]]).astype(jnp.int32)


def tie(value, other):
    return lax.optimization_barrier((value, other))[0]


class Gather:
    def __init__(self, block):
        self.block = block

    def far_z(self, after=None):
        block = self.block if after is None else tie(self.block, after)
        self.even = jnp.stack([block, over_z(block, 2)])
        return self.even

    def near_z(self, after=None):
        if after is not None:
            self.even = tie(self.even, after)
        self.odd = over_z(self.even, 1)
        return self.odd

    def first(self):
        self.got = (over_x(self.even), over_y(self.odd))
        return self.got

    def second(self, after=None):
        got = self.got if after is None else tie(self.got, after)
        even, odd = jnp.concatenate([self.even, got[0]]), jnp.concatenate([self.odd, got[1]])
        self.near = [even, odd, over_core(even), over_core(odd)]
        self.far = [over_y(even), over_x(odd)]
        return self.far

    def core(self, after=None):
        far = self.far if after is None else tie(self.far, after)
        even, odd, even_core, odd_core = self.near
        return [even, far[0], odd, far[1], even_core, over_core(far[0]), odd_core, over_core(far[1])]


class Reduce:
    def __init__(self, send_a, keep_a, send_b, keep_b):
        self.sends, self.a, self.b = (send_a, send_b), keep_a.astype(F32), keep_b.astype(F32)

    def first(self, after=None):
        sends = self.sends if after is None else tie(self.sends, after)
        self.got = (over_y(sends[0]), over_x(sends[1]))
        return self.got

    def wait_for(self, after):
        if after is not None:
            self.got = tie(self.got, after)

    def second(self, after=None):
        self.wait_for(after)
        self.a = self.a + self.got[0].astype(F32)
        self.b = self.b + self.got[1].astype(F32)
        self.got = (over_x(self.a[:2].astype(BF)), over_y(self.b[:2].astype(BF)))
        return self.got

    def near_z(self, after=None):
        self.wait_for(after)
        self.a = self.a[2:] + self.got[0].astype(F32)
        self.got = over_z((self.b[2:] + self.got[1].astype(F32)).astype(BF), 1)
        return self.got

    def far_z(self, after=None):
        self.wait_for(after)
        self.a = self.a + self.got.astype(F32)
        self.got = over_z(self.a[1].astype(BF), 2)
        return self.got

    def own(self):
        return self.a[0] + self.got.astype(F32)


def unslab(block, width):
    size = block.shape[0] * LANES // width
    return jnp.concatenate([block[s * size : (s + 1) * size] for s in range(width // LANES)], axis=1)


def slab(block):
    return [block[:, s * LANES : (s + 1) * LANES] for s in range(block.shape[1] // LANES)]


def local(fast, tokens, doc_lengths, cotangent, w_qkv, w_out, w_up, w_down,
          gain_attn, gain_inner, gain_ffn, gain_mid):
    row_count = doc_lengths.shape[0]
    seq = tokens.shape[0] // row_count
    d, f = tokens.shape[1], w_up.shape[1]
    wide = min(seq, 512) // BLOCK + 1
    blocks = seq // BLOCK
    shards = (gain_attn, gain_inner, gain_ffn, gain_mid)

    start, position, valid = layout(doc_lengths, seq)
    cos, sin = tables(position)
    firsts = start[:, ::BLOCK] // BLOCK
    reach = (jnp.arange(blocks, dtype=jnp.int32)[None, :] - firsts + 1).reshape(-1)
    start_row = jnp.repeat(start, 8, axis=0)
    gy = jnp.where(valid.reshape(-1, 1), cotangent, jnp.zeros_like(cotangent))

    def scatter(g):
        return lax.psum_scatter(g, AXES, scatter_dimension=0, tiled=True)

    def gather(v):
        return lax.all_gather(v, AXES, axis=0, tiled=True)

    if fast:
        order, back = gather_order(), scatter_order()
        one, two = (Gather(b) for b in pack(w_qkv, w_out, w_up, w_down, shards))
        seen = one.far_z()
        two.far_z(seen)
        one.even = tie(one.even, (cos, sin))
        one.near_z()
        one.first()
        one.second(two.even)
        two.near_z()
        two.first()
        parts_qkv = one.core()
        gy_both = (gy, over_core(gy))
        cos, sin = tie((cos, sin), (gy, start_row, reach, order, back))
    else:
        order = back = jnp.zeros((8,), jnp.int32)

        def scaled(w, gain):
            return gather((w.astype(F32) * gain.astype(F32)[:, None]).astype(BF))

        parts_qkv, parts_down = [gather(w_qkv)], [scaled(w_down, gain_mid)]
        parts_up = [scaled(w_out, gain_inner), scaled(w_up, gain_ffn)]

    whole_gain = None if fast else gather(gain_attn).astype(F32).reshape(1, -1)
    h1, qkv, full_qkv, *rest = qkv_forward(fast, order, tokens, cos, sin, parts_qkv, whole_gain)
    g_attn = rest[0] if fast else whole_gain
    if fast:
        two.second(g_attn)
        start_row = tie(start_row, (gy_both[1], two.near[2:]))
    mixed, lse = attention_forward(reach, qkv, start_row, row_count, wide)
    parts = two.core(lse) if fast else parts_up + parts_down
    a, h2, x1, m, dpre, dx1, low, d_mixed, full_down, _, _, *other = ffn_both(
        fast, order, mixed, tokens, gy, parts, f
    )

    def shared(value):
        return (value, over_core(value)) if fast else (value,)

    if fast:
        m_both = (m, over_core(other[1]))
        theirs = over_core(other[0])
        a_both, h2_both = (a, (theirs, 0)), (h2, (theirs, 1))
    else:
        gy_both, m_both, a_both, h2_both = (gy,), (m,), (a,), (h2,)
    low, dpre = shared(low), shared(dpre)

    def attend(group, groups, lse, so_far):
        return attention_backward(
            reach, qkv, d_mixed, mixed, lse, start_row, cos, sin, row_count, wide, group, groups, so_far
        )

    f = w_up.shape[1]
    d_qkv = attend(0, 1, lse, None)
    if fast:
        low = tie(low, d_qkv)
    grads = weight_grads(
        fast, back,
        [(m_both, gy_both, f // 384, True), (a_both, low, d // LANES, False), (h2_both, dpre, f // LANES, False)],
    )
    if fast:
        red = Reduce(*grads)
        first = red.first()
        h1 = tie(h1, grads[-1])
    d_qkv = attend(1, 2, tie(lse, grads[-1]), d_qkv)
    if fast:
        h1 = (h1[0], over_core(h1[1]))
        d_both = (d_qkv, over_core(tie(d_qkv, (first, h1[1]))))
        second = red.second(d_qkv)
        dx1 = tie(dx1, (d_qkv, first))
    else:
        d_both = (d_qkv,)
    grad_tokens = qkv_backward(d_qkv, tokens, dx1, full_qkv, g_attn)
    if fast:
        near = red.near_z(grad_tokens)
        h1 = tie(h1, (grad_tokens, second))
    grad_qkv = weight_grads(fast, back, [(h1, d_both, 3 * d // LANES, False)])
    if fast:
        red_qkv = Reduce(*grad_qkv)
        first = red_qkv.first()
        far = red.far_z(grad_qkv[-1])
        m = tie(m, (grad_qkv[-1], near))
    result = down_forward(m, x1, full_down)
    if fast:
        red_qkv.second((result, far))
        own = red.own()
        red_qkv.near_z()
        red_qkv.far_z()
        g_qkv = red_qkv.own()
        cuts = (w_down.shape[0], w_down.shape[0] + w_out.shape[0])
        own_down, grad_out, grad_up = own[: cuts[0]], own[cuts[0] : cuts[1]], unslab(own[cuts[1] :], f)
    else:
        own_down, grad_out, grad_up, g_qkv = (scatter(g.astype(BF)).astype(F32) for g in (*grads, *grad_qkv))
        g_qkv = jnp.concatenate(slab(g_qkv))
    size = w_qkv.shape[0]
    span = LANES // 3
    g_qkv = jnp.concatenate(
        [g_qkv[g * size : (g + 1) * size, p * span : (p + 1) * span] for p in range(3) for g in range(GRAD_GROUPS)], axis=1
    )
    raw = (g_qkv, grad_out, grad_up, own_down)
    row_sums = [jnp.sum(g * w.astype(F32), axis=1) for g, w in zip(raw, (w_qkv, w_out, w_up, w_down))]
    row_sums[0] = row_sums[0] / gain_attn.astype(F32)
    scaled_grads = [g * v.astype(F32)[:, None] for g, v in zip(raw[1:], shards[1:])]
    return (result, grad_tokens, g_qkv, *scaled_grads, *row_sums)


def solution(mesh):
    matrix, vector = P(AXES, None), P(AXES)
    fast = mesh.shape["dp"] == 4 and mesh.shape["fsdp"] == 2 * Z
    return jax.shard_map(
        functools.partial(local, fast),
        mesh=mesh,
        in_specs=(matrix,) * 7 + (vector,) * 4,
        out_specs=(matrix,) * 6 + (vector,) * 4,
        check_vma=False,
    )
```

```python
import functools
import math

import jax
import jax.numpy as jnp
import numpy as np
from jax import lax
from jax.experimental import pallas as pl
from jax.experimental.pallas import tpu as pltpu
from jax.sharding import PartitionSpec as P

HEADS = 12
HEAD_DIM = 64
PAIR = 2 * HEAD_DIM
PAIRS = HEADS // 2
EPSILON = 1e-05
MASKED_SCORE = -1e30
ROOT_HALF = 0.7071067811865476
INV_ROOT_TAU = 0.3989422804014327
BF = jnp.bfloat16
F32 = jnp.float32
MIB = 1 << 20
AXES = ("dp", "fsdp")
BLOCK = 256
ROWS = 256
LANES = 768
VMEM_MIB = 54
GRAD_GROUPS = 3


def dot(a, b, dims=((1,), (0,))):
    return lax.dot_general(a, b, (dims, ((), ())), preferred_element_type=F32)


def params(mib):
    return pltpu.CompilerParams(vmem_limit_bytes=max(mib, VMEM_MIB) * MIB)


def swap_halves(x):
    lane = lax.broadcasted_iota(jnp.int32, x.shape, 1)
    low = lax.rem(lane, HEAD_DIM) < HEAD_DIM // 2
    half = HEAD_DIM // 2
    return jnp.where(low, pltpu.roll(x, PAIR - half, 1), pltpu.roll(x, half, 1))


def unit_norm(x):
    mean = jnp.mean(x, axis=-1, keepdims=True)
    centred = x - mean
    inv = lax.rsqrt(jnp.mean(centred * centred, axis=-1, keepdims=True) + EPSILON)
    return centred * inv, inv


def norm_back(d_unit, unit, inv):
    return inv * (
        d_unit
        - jnp.mean(d_unit, axis=-1, keepdims=True)
        - unit * jnp.mean(d_unit * unit, axis=-1, keepdims=True)
    )


def whole(shape):
    return pl.BlockSpec(shape, lambda *_: (0,) * len(shape), pipeline_mode=pl.Buffered(1))


def rows(width, block=ROWS):
    return pl.BlockSpec((block, width), lambda i: (i, 0))


def shaped(shape, dtype):
    return jax.ShapeDtypeStruct(shape, dtype)


def hbm():
    return pl.BlockSpec(memory_space=pl.ANY)


def fetch(order, parts, places, sem):
    if len(parts) < 8 and parts[0].ndim == 2:
        for part, (_, _, buffer, _) in zip(parts, places):
            pltpu.make_async_copy(part, buffer, sem).start()
        return
    count = parts[0].shape[0]
    for p, part in enumerate(parts):
        for b in range(count):
            owner = b if order is None else order[p * count + b]
            for first, size, buffer, column in places:
                row = owner * size if order is None else pl.multiple_of(owner * size, 8)
                pltpu.make_async_copy(
                    part.at[b, pl.ds(first, size), :],
                    buffer.at[pl.ds(row, size), pl.ds(column, LANES)],
                    sem,
                ).start()


def arrive(buffers, sem):
    for buffer in buffers:
        pltpu.make_async_copy(buffer, buffer, sem).wait()


def deal(back, tile, outs, row, size):
    quarter = outs[0].shape[0]
    for q, out in enumerate(outs):

        @pl.loop(0, quarter)
        def _(j):
            block = tile[pl.ds(pl.multiple_of(back[q * quarter + j] * size, 8), size), :]
            out[j, pl.ds(row, size), :] = block.astype(out.dtype)


def slabs(first, size, buffer, width):
    return [(first + s * size, size, buffer, s * LANES) for s in range(width // LANES)]


def scale_rows(w, gain):
    n = w.shape[0]
    square = lax.broadcasted_iota(jnp.int32, (n, n), 0) == lax.broadcasted_iota(jnp.int32, (n, n), 1)
    return dot(jnp.where(square, gain.astype(F32), 0.0).astype(BF), w).astype(BF)


def pack_kernel(wq_ref, wo_ref, wu_ref, wd_ref, ga_ref, gi_ref, gf_ref, gm_ref, one_ref, two_ref):
    row = 0
    for c in range(wq_ref.shape[1] // LANES):
        one_ref[row : row + wq_ref.shape[0], :] = wq_ref[:, c * LANES : (c + 1) * LANES]
        row += wq_ref.shape[0]
    one_ref[row:, :] = ga_ref[...]
    row = 0
    for ref, gain in ((wd_ref, gm_ref), (wo_ref, gi_ref), (wu_ref, gf_ref)):
        for c in range(ref.shape[1] // LANES):
            two_ref[row : row + ref.shape[0], :] = scale_rows(ref[:, c * LANES : (c + 1) * LANES], gain[...])
            row += ref.shape[0]


def pack(w_qkv, w_out, w_up, w_down, gains):
    first = w_qkv.size // LANES + 8
    second = (w_out.size + w_up.size + w_down.size) // LANES
    row = jnp.pad(gains[0].reshape(1, -1), ((0, 7), (0, LANES - gains[0].shape[0])))
    return pl.pallas_call(
        pack_kernel, out_shape=[shaped((first, LANES), BF), shaped((second, LANES), BF)], name="pack"
    )(w_qkv, w_out, w_up, w_down, row, *(g.reshape(1, -1) for g in gains[1:]))


def spread(rows_in, offset, count, owners):
    lanes = rows_in.shape[1]
    wide = owners * count
    lane = lax.broadcasted_iota(jnp.int32, (lanes, wide), 0)
    column = lax.broadcasted_iota(jnp.int32, (lanes, wide), 1)
    pick = (lane - offset == lax.rem(column, count)).astype(F32).astype(BF)
    full = dot(rows_in, pick)
    owner = lax.broadcasted_iota(jnp.int32, (owners, wide), 0)
    column = lax.broadcasted_iota(jnp.int32, (owners, wide), 1)
    own = (column >= owner * count) & (column < owner * count + count)
    return jnp.sum(jnp.where(own, full, 0.0), axis=0, keepdims=True)


def qkv_kernel(split, *refs):
    if split:
        order, x_ref, cos_ref, sin_ref, *refs = refs
        parts, refs = refs[:8], refs[8:]
        h_ref, other_ref, qkv_ref, w_ref, ga_ref, gains, sem, gain_sem = refs
        h_refs = (h_ref, other_ref)
    else:
        order, x_ref, cos_ref, sin_ref, ga_ref, *refs = refs
        parts, refs = refs[:1], refs[1:]
        h_ref, qkv_ref, w_ref, sem = refs
        h_refs = (h_ref,)
    width = x_ref.shape[1]
    step = pl.program_id(0)
    if split:
        size = width // 32
        weight = slabs(0, size, w_ref, 3 * width)

        @pl.when(step == 0)
        def _():
            fetch(order, parts, [(3 * size, 8, gains, 0)], gain_sem)
            fetch(order, parts, weight, sem)
            arrive([gains], gain_sem)
            owner = lax.broadcasted_iota(jnp.int32, (32, 256), 0)
            lane = lax.broadcasted_iota(jnp.int32, (32, 256), 1)
            pick = (lane == owner * 8).astype(F32).astype(BF)
            per_owner = dot(pick, gains[:, :PAIR]).astype(BF)
            ga_ref[...] = spread(per_owner, 0, size, 32)
            arrive([w_ref], sem)
    else:

        @pl.when(step == 0)
        def _():
            fetch(None, parts, [(0, 0, w_ref, 0)], sem)
            arrive([w_ref], sem)

    unit, _ = unit_norm(x_ref[...].astype(F32))
    h = (unit * ga_ref[...]).astype(BF)
    store_low(split, order[32] if split else 0, h, h_refs)
    cos, sin = cos_ref[...], sin_ref[...]
    for part in range(3):
        y = dot(h, w_ref[:, part * width : (part + 1) * width])
        for c in range(width // PAIR):
            z = y[:, c * PAIR : (c + 1) * PAIR]
            if part < 2:
                z = z * cos + swap_halves(z) * sin
            if part == 0:
                z = z * (1.0 / math.sqrt(HEAD_DIM))
            at = part * width + c * PAIR
            qkv_ref[:, at : at + PAIR] = z.astype(BF)


def prefetched(kernel, order, inputs, in_specs, out_specs, out_shape, scratch, grid, mib, name, flops, data):
    return pl.pallas_call(
        kernel,
        grid_spec=pltpu.PrefetchScalarGridSpec(
            num_scalar_prefetch=1,
            grid=grid,
            in_specs=in_specs,
            out_specs=out_specs,
            scratch_shapes=scratch,
        ),
        out_shape=out_shape,
        compiler_params=params(mib),
        cost_estimate=pl.CostEstimate(flops=flops, transcendentals=0, bytes_accessed=data),
        name=name,
    )(order, *inputs)


def rows(width, block=ROWS):
    return pl.BlockSpec((block, width), lambda i, *_: (i, 0))


def whole(shape):
    return pl.BlockSpec(shape, lambda *_: (0,) * len(shape), pipeline_mode=pl.Buffered(1))


def qkv_forward(split, order, tokens, cos, sin, parts, gain):
    t, d = tokens.shape
    n = 3 * d
    inputs = [tokens, cos, sin]
    in_specs = [rows(d), rows(PAIR), rows(PAIR)]
    out_specs, out_shape = low_specs(split, t, d)
    lows = len(out_specs)
    out_specs = out_specs + [rows(n), whole((d, n))]
    out_shape = out_shape + [shaped((t, n), BF), shaped((d, n), BF)]
    scratch = [pltpu.SemaphoreType.DMA]
    if split:
        out_specs += [whole((1, d))]
        out_shape += [shaped((1, d), F32)]
        scratch = [pltpu.VMEM((32 * 8, LANES), BF), pltpu.SemaphoreType.DMA, pltpu.SemaphoreType.DMA]
    else:
        inputs.append(gain)
        in_specs.append(whole((1, d)))
    outs = prefetched(
        functools.partial(qkv_kernel, split), order, inputs + list(parts), in_specs + [hbm()] * len(parts),
        out_specs, out_shape, scratch, (t // ROWS,), 40, "qkv_forward",
        2 * t * d * n, 4 * d * n + 12 * t * d,
    )
    return (outs[:lows], *outs[lows:])


def window(i, n):
    return slice((i - n + 1) * BLOCK, (i + 1) * BLOCK)


def head_masks(shape):
    lane = lax.broadcasted_iota(jnp.int32, shape, 1)
    return lane < HEAD_DIM


def attention_forward_kernel(wide, reach, q_ref, k_ref, v_ref, start_ref, o_ref, lse_ref, bias):
    row, pair = pl.program_id(0), pl.program_id(1)
    seq = q_ref.shape[0]
    blocks = seq // BLOCK

    @pl.when(pair == 0)
    def _():
        for i in range(blocks):
            at = slice(i * BLOCK, (i + 1) * BLOCK)
            shape = (BLOCK, wide * BLOCK)
            key = (i - wide + 1) * BLOCK + lax.broadcasted_iota(jnp.int32, shape, 1)
            query = i * BLOCK + lax.broadcasted_iota(jnp.int32, shape, 0)
            row_of = start_ref[0:1, at].astype(F32)
            start = jnp.broadcast_to(row_of, (PAIR, BLOCK)).T[:, 0:1].astype(jnp.int32)
            keep = (key >= start) & (key <= query)
            bias[at, :] = jnp.where(keep, 0.0, MASKED_SCORE)

    first = head_masks((BLOCK, PAIR))
    for i in range(blocks):
        at = slice(i * BLOCK, (i + 1) * BLOCK)
        most = min(wide, i + 1)
        for n in range(1, most + 1):

            @pl.when(reach[row * blocks + i] == n)
            def _():
                q = q_ref[at, :]
                w = window(i, n)
                k, v = k_ref[w, :], v_ref[w, :]
                b = bias[at, (wide - n) * BLOCK :]
                mask = head_masks(k.shape)
                zero = jnp.zeros_like(k)
                masks = (mask, jnp.logical_not(mask))
                scores = [dot(q, jnp.where(pick, k, zero), ((1,), (1,))) for pick in masks]
                total, lses = None, []
                for s, pick in zip(scores, masks):
                    s = s + b
                    top = jnp.max(s, axis=-1, keepdims=True)
                    p = jnp.exp(s - top)
                    den = jnp.sum(p, axis=-1, keepdims=True)
                    part = dot((p * (1.0 / den)).astype(BF), jnp.where(pick, v, zero))
                    total = part if total is None else total + part
                    lses.append(top + jnp.log(den))
                o_ref[at, :] = total
                both = jnp.where(first, lses[0], lses[1]).T
                lse_ref[0, 0:1, at] = both[0:1, :]
                lse_ref[0, 1:2, at] = both[HEAD_DIM : HEAD_DIM + 1, :]


def attention_forward(reach, qkv, start, row_count, wide):
    t = qkv.shape[0]
    seq = t // row_count
    d = qkv.shape[1] // 3

    def columns(part):
        return pl.BlockSpec((seq, PAIR), lambda r, p, *_: (r, part * PAIRS + p))

    return pl.pallas_call(
        functools.partial(attention_forward_kernel, wide),
        grid_spec=pltpu.PrefetchScalarGridSpec(
            num_scalar_prefetch=1,
            grid=(row_count, PAIRS),
            in_specs=[
                columns(0),
                columns(1),
                columns(2),
                pl.BlockSpec((8, seq), lambda r, p, *_: (r, 0)),
            ],
            out_specs=[
                pl.BlockSpec((seq, PAIR), lambda r, p, *_: (r, p)),
                pl.BlockSpec((1, 8, seq), lambda r, p, *_: (r * PAIRS + p, 0, 0)),
            ],
            scratch_shapes=[pltpu.VMEM((seq, wide * BLOCK), F32)],
        ),
        out_shape=[shaped((t, d), F32), shaped((row_count * PAIRS, 8, seq), F32)],
        compiler_params=params(32),
        cost_estimate=pl.CostEstimate(
            flops=8 * t * d * BLOCK, transcendentals=t * HEADS * 512, bytes_accessed=12 * t * d
        ),
        name="attention_forward",
    )(reach, qkv, qkv, qkv, start)


def attention_backward_kernel(wide, reach, q_ref, k_ref, v_ref, do_ref, o_ref, lse_ref, start_ref, cos_ref, sin_ref, *refs):
    grad_ref, bias, ks, vs, qs, dos, dk_acc, dv_acc, dq_acc = refs[-9:]
    row, pair = pl.program_id(0), pl.program_id(1)
    seq = q_ref.shape[0]
    blocks = seq // BLOCK

    @pl.when(pair == 0)
    def _():
        for i in range(blocks):
            at = slice(i * BLOCK, (i + 1) * BLOCK)
            shape = (wide * BLOCK, BLOCK)
            key = (i - wide + 1) * BLOCK + lax.broadcasted_iota(jnp.int32, shape, 0)
            query = i * BLOCK + lax.broadcasted_iota(jnp.int32, shape, 1)
            keep = (key >= start_ref[0:1, at]) & (key <= query)
            bias[:, at] = jnp.where(keep, 0.0, MASKED_SCORE)

    mask = head_masks((seq, PAIR))
    for src, dst in ((k_ref, ks), (v_ref, vs), (q_ref, qs), (do_ref, dos)):
        x = src[...]
        zero = jnp.zeros_like(x)
        dst[0] = jnp.where(mask, x, zero)
        dst[1] = jnp.where(mask, zero, x)
    dk_acc[...] = jnp.zeros_like(dk_acc)
    dv_acc[...] = jnp.zeros_like(dv_acc)
    lane8 = lax.broadcasted_iota(jnp.int32, (8, PAIR), 1) // HEAD_DIM
    row8 = lax.broadcasted_iota(jnp.int32, (8, PAIR), 0)
    picks = (lane8 == row8).astype(F32)
    delta = lax.dot_general(
        picks, do_ref[...].astype(F32) * o_ref[...], (((1,), (1,)), ((), ())),
        precision=lax.Precision.HIGHEST, preferred_element_type=F32,
    )
    for i in range(blocks):
        at = slice(i * BLOCK, (i + 1) * BLOCK)
        most = min(wide, i + 1)
        for n in range(1, most + 1):

            @pl.when(reach[row * blocks + i] == n)
            def _():
                w = window(i, n)
                b = bias[(wide - n) * BLOCK :, at]
                q, do = q_ref[at, :], do_ref[at, :]
                ps, dss = [], []
                for h in range(2):
                    s = dot(ks[h, w, :], q, ((1,), (1,))) + b
                    p = jnp.exp(s - lse_ref[0, h : h + 1, at])
                    dp = dot(vs[h, w, :], do, ((1,), (1,)))
                    ds = (p * (dp - delta[h : h + 1, at])).astype(BF)
                    ps.append(p.astype(BF))
                    dss.append(ds)
                dv_acc[w, :] += dot(ps[0], dos[0, at, :]) + dot(ps[1], dos[1, at, :])
                dk_acc[w, :] += dot(dss[0], qs[0, at, :]) + dot(dss[1], qs[1, at, :])
                dq_acc[at, :] = dot(dss[0], ks[0, w, :], ((0,), (0,))) + dot(
                    dss[1], ks[1, w, :], ((0,), (0,))
                )

    cos, sin = cos_ref[...], sin_ref[...]
    dq = dq_acc[...] * (1.0 / math.sqrt(HEAD_DIM))
    dk = dk_acc[...]
    span = grad_ref.shape[2] // 3
    slot = lax.rem(pair, span // PAIR)
    grads = (dq * cos - swap_halves(dq) * sin, dk * cos - swap_halves(dk) * sin, dv_acc[...])
    for part, value in enumerate(grads):
        grad_ref[0, :, pl.ds(pl.multiple_of(part * span + slot * PAIR, PAIR), PAIR)] = value.astype(BF)


def attention_backward(reach, qkv, d_mixed, mixed, lse, start_row, cos, sin, row_count, wide, group, groups, so_far):
    pairs = PAIRS // GRAD_GROUPS
    t = qkv.shape[0]
    seq = t // row_count
    base = group * pairs
    span = 3 * pairs * PAIR

    def columns(part):
        return pl.BlockSpec((seq, PAIR), lambda r, p, *_: (r, part * PAIRS + base + p))

    table = pl.BlockSpec((seq, PAIR), lambda r, p, *_: (r, 0))
    inputs = [reach, qkv, qkv, qkv, d_mixed, mixed, lse, start_row, cos, sin]
    in_specs = [
        columns(0), columns(1), columns(2), columns(0), columns(0),
        pl.BlockSpec((1, 8, seq), lambda r, p, *_: (r * PAIRS + base + p, 0, 0)),
        pl.BlockSpec((8, seq), lambda r, p, *_: (r, 0)),
        table, table,
    ]
    aliases = {}
    if so_far is not None:
        aliases = {len(inputs): 0}
        inputs.append(so_far)
        in_specs.append(hbm())
    return pl.pallas_call(
        functools.partial(attention_backward_kernel, wide),
        grid_spec=pltpu.PrefetchScalarGridSpec(
            num_scalar_prefetch=1,
            grid=(row_count, pairs * groups),
            in_specs=in_specs,
            out_specs=pl.BlockSpec((1, seq, span), lambda r, p, *_: (group + p // pairs, r, 0)),
            scratch_shapes=[
                pltpu.VMEM((wide * BLOCK, seq), F32),
                pltpu.VMEM((2, seq, PAIR), BF),
                pltpu.VMEM((2, seq, PAIR), BF),
                pltpu.VMEM((2, seq, PAIR), BF),
                pltpu.VMEM((2, seq, PAIR), BF),
                pltpu.VMEM((seq, PAIR), F32),
                pltpu.VMEM((seq, PAIR), F32),
                pltpu.VMEM((seq, PAIR), F32),
            ],
        ),
        out_shape=shaped((GRAD_GROUPS, t, span), BF),
        input_output_aliases=aliases,
        compiler_params=params(40),
        cost_estimate=pl.CostEstimate(
            flops=20 * t * span * BLOCK // 3 * groups, transcendentals=t * HEADS * 128 * groups,
            bytes_accessed=20 * t * span // 3 * groups
        ),
        name="attention_backward",
    )(*inputs)


def halves(x):
    quarter = x.shape[1] // 4
    piece = [x[:, i * quarter : (i + 1) * quarter] for i in range(4)]
    return jnp.concatenate(piece[0::2], axis=1), jnp.concatenate(piece[1::2], axis=1)


def store_low(split, core, x, refs):
    if not split:
        refs[0][...] = x
        return
    pair = halves(x)
    for c in range(2):

        @pl.when(core == c)
        def _():
            refs[0][...] = pair[c]
            refs[1][...] = pair[1 - c]


def low_specs(split, t, d):
    if split:
        return [rows(d // 2)] * 2, [shaped((t, d // 2), BF)] * 2
    return [rows(d)], [shaped((t, d), BF)]


def ffn_kernel(split, *refs):
    order, o_ref, x_ref, gy_ref, *refs = refs
    count = 8 if split else 3
    parts, refs = refs[:count], refs[count:]
    a_ref, h2_ref, x1_ref, m_ref, dpre_ref, dx1_ref, low_ref, do_ref, wd_ref, wo_ref, wu_ref, *refs = refs
    theirs_ref, other_ref, *refs = refs if split else (None, None, *refs)
    act, slope, dm, out_sem, up_sem, down_sem = refs
    d, f = wu_ref.shape
    size, skip = d // 32, f // 32
    step = pl.program_id(0)
    core = order[32] if split else 0
    chunks = [slice(c, c + LANES) for c in range(0, f, LANES)]

    @pl.when(step == 0)
    def _():
        if split:
            fetch(order, parts, [(skip, size, wo_ref, 0)], out_sem)
            fetch(order, parts, slabs(skip + size, size, wu_ref, f), up_sem)
            fetch(order, parts, [(0, skip, wd_ref, 0)], down_sem)
        else:
            fetch(order, parts[:1], [(0, 0, wo_ref, 0)], out_sem)
            fetch(order, parts[1:2], [(0, 0, wu_ref, 0)], up_sem)
            fetch(order, parts[2:], [(0, 0, wd_ref, 0)], down_sem)

    mixed = o_ref[...]
    unit_in, inv_in = unit_norm(mixed)
    a = unit_in.astype(BF)
    store_low(split, core, a, (a_ref, theirs_ref.at[0] if split else None))

    @pl.when(step == 0)
    def _():
        arrive([wo_ref], out_sem)

    x1 = x_ref[...].astype(F32) + dot(a, wo_ref[...])
    x1_ref[...] = x1
    unit_two, inv_two = unit_norm(x1)
    h2 = unit_two.astype(BF)
    store_low(split, core, h2, (h2_ref, theirs_ref.at[1] if split else None))
    gy = gy_ref[...]

    @pl.when(step == 0)
    def _():
        arrive([wu_ref], up_sem)
        arrive([wd_ref], down_sem)

    total = None
    for at in chunks:
        hidden = dot(h2, wu_ref[:, at])
        dm[:, at] = dot(gy, wd_ref[at, :], ((1,), (1,)))
        cdf = 0.5 + 0.5 * lax.erf(hidden * ROOT_HALF)
        slope[:, at] = cdf + hidden * (jnp.exp(-0.5 * hidden * hidden) * INV_ROOT_TAU)
        value = hidden * cdf
        act[:, at] = value
        part = jnp.sum(value, axis=-1, keepdims=True)
        total = part if total is None else total + part
    mean = total * (1.0 / f)
    total = None
    for at in chunks:
        centred = act[:, at] - mean
        part = jnp.sum(centred * centred, axis=-1, keepdims=True)
        total = part if total is None else total + part
    inv = lax.rsqrt(total * (1.0 / f) + EPSILON)
    first = second = None
    for at in chunks:
        unit = (act[:, at] - mean) * inv
        act[:, at] = unit
        m_ref[:, at] = unit.astype(BF)
        d_unit = dm[:, at]
        part = jnp.sum(d_unit, axis=-1, keepdims=True)
        first = part if first is None else first + part
        part = jnp.sum(d_unit * unit, axis=-1, keepdims=True)
        second = part if second is None else second + part
    first, second = first * (1.0 / f), second * (1.0 / f)
    dh2 = None
    for at in chunks:
        d_act = inv * (dm[:, at] - first - act[:, at] * second)
        dpre = (d_act * slope[:, at]).astype(BF)
        dpre_ref[:, at] = dpre
        part = dot(dpre, wu_ref[:, at], ((1,), (1,)))
        dh2 = part if dh2 is None else dh2 + part
    dx1 = gy.astype(F32) + norm_back(dh2, unit_two, inv_two)
    dx1_ref[...] = dx1
    low = dx1.astype(BF)
    low_ref[...] = low
    da = dot(low, wo_ref[...], ((1,), (1,)))
    do_ref[...] = norm_back(da, unit_in, inv_in).astype(BF)

    if split:
        quarter = f // 4
        for j in range(2):
            at = pl.multiple_of((2 * j + 1 - core) * quarter, PAIR)
            other_ref[:, j * quarter : (j + 1) * quarter] = m_ref[:, pl.ds(at, quarter)]


def ffn_both(split, order, mixed, tokens, gy, parts, f):
    t, d = tokens.shape
    width = d // 2 if split else d
    more = [(rows(f // 2), shaped((t, f // 2), BF))] * split
    if split:
        theirs = pl.BlockSpec((2, ROWS, width), lambda i, *_: (0, i, 0))
        more.insert(0, (theirs, shaped((2, t, width), BF)))
    return prefetched(
        functools.partial(ffn_kernel, split), order, [mixed, tokens, gy, *parts],
        [rows(d), rows(d), rows(d)] + [hbm()] * len(parts),
        [rows(width), rows(width), rows(d), rows(f), rows(f), rows(d), rows(d), rows(d), whole((f, d)), whole((d, d)),
         whole((d, f))] + [m[0] for m in more],
        [
            shaped((t, width), BF), shaped((t, width), BF), shaped((t, d), F32), shaped((t, f), BF), shaped((t, f), BF),
            shaped((t, d), F32), shaped((t, d), BF), shaped((t, d), BF), shaped((f, d), BF), shaped((d, d), BF),
            shaped((d, f), BF),
        ] + [m[1] for m in more],
        [
            pltpu.VMEM((ROWS, f), F32), pltpu.VMEM((ROWS, f), F32), pltpu.VMEM((ROWS, f), F32), pltpu.SemaphoreType.DMA,
            pltpu.SemaphoreType.DMA, pltpu.SemaphoreType.DMA,
        ],
        (t // ROWS,), 60, "ffn_both", 2 * t * d * (2 * d + 3 * f), 6 * d * f + 4 * t * f + 30 * t * d,
    )


def result_kernel(m_ref, x1_ref, wd_ref, y_ref):
    y_ref[...] = (x1_ref[...] + dot(m_ref[...], wd_ref[...])).astype(BF)


def down_forward(m, x1, w_down):
    t, d = x1.shape
    f = m.shape[1]
    return pl.pallas_call(
        result_kernel,
        grid=(t // ROWS,),
        in_specs=[rows(f), rows(d), whole((f, d))],
        out_specs=rows(d),
        out_shape=shaped((t, d), BF),
        compiler_params=params(48),
        cost_estimate=pl.CostEstimate(flops=2 * t * d * f, transcendentals=0, bytes_accessed=2 * d * f + 2 * t * f + 6 * t * d),
        name="down_forward",
    )(m, x1, w_down)


def grads_kernel(split, products, *refs):
    back, *refs = refs
    count = 2 if split else 1
    left, refs = refs[: len(products) * count], refs[len(products) * count :]
    right, refs = refs[: len(products) * count], refs[len(products) * count :]
    outs, refs = refs[: 4 if split else len(products)], refs[4 if split else len(products) :]
    tile, turned = refs[0], refs[1:]
    step = pl.program_id(0)
    first, row = 0, 0
    for n, (by_left, tiles, size) in enumerate(products):
        mine = [left[n * count + c] for c in range(count)]
        value = [right[n * count + c] for c in range(count)]

        if not by_left:

            @pl.when(step == first)
            def _():
                t = mine[0].shape[0]
                for c in range(count):
                    flat = mine[c][...] if len(mine[c].shape) == 2 else mine[c][0]
                    turned[0][:, c * t : (c + 1) * t] = flat.T

        @pl.when((step >= first) & (step < first + tiles))
        def _():
            total = None
            for c in range(count):
                v = value[c][...] if len(value[c].shape) == 2 else value[c][0]
                t = v.shape[0]
                if by_left:
                    part = dot(mine[c][...], v, ((0,), (0,)))
                else:
                    part = dot(turned[0][:, c * t : (c + 1) * t], v)
                total = part if total is None else total + part
            if not split:
                outs[n][...] = total
            else:
                tile[...] = total
                if by_left:
                    owners = tile.shape[0] // size
                    for e in range(owners):
                        at = back[16 + (step - first) * owners + e]
                        for q in range(4):

                            @pl.when(at // 4 == q)
                            def _():
                                block = tile[e * size : (e + 1) * size, :]
                                outs[q][at - 4 * q, row : row + size, :] = block.astype(outs[q].dtype)
                else:
                    deal(back, tile, outs, row + pl.multiple_of((step - first) * size, 8), size)

        first += tiles
        row += size if by_left else tiles * size


def weight_grads(split, back, products):
    count = 2 if split else 1
    t = products[0][0][0].shape[0]
    left_specs, right_specs, lefts, rights, plan = [], [], [], [], []
    out_specs, out_shape = [], []
    at = row = 0
    for left, right, tiles, by_left in products:
        width = 0
        for c in range(count):
            a, b = left[c], right[c]
            a, part = a if isinstance(a, tuple) else (a, None)

            if by_left and c == 0:
                tiles = tiles // count
                width = a.shape[1] // (tiles * count)

            def step(i, at=at, tiles=tiles):
                return jnp.clip(i - at, 0, tiles - 1)

            if by_left:
                per = tiles // 2
                if split and c == 0:
                    left_specs.append(pl.BlockSpec(
                        (t, width), lambda i, back, step=step, per=per: (0, (2 * (step(i) // per) + back[32]) * per + step(i) % per)
                    ))
                else:
                    left_specs.append(pl.BlockSpec((t, width), lambda i, *_, step=step: (0, step(i))))
                right_specs.append(whole(b.shape))
            else:
                width = a.shape[-1]
                if part is None:
                    left_specs.append(whole(a.shape))
                else:
                    left_specs.append(pl.BlockSpec(
                        (1, t, width), lambda *_, part=part: (part, 0, 0), pipeline_mode=pl.Buffered(1)
                    ))
                if b.ndim == 3:
                    right_specs.append(pl.BlockSpec((1, t, LANES), lambda i, *_, step=step: (step(i), 0, 0)))
                else:
                    right_specs.append(pl.BlockSpec((t, LANES), lambda i, *_, step=step: (0, step(i))))
            lefts.append(a)
            rights.append(b)
        size = (width * tiles if by_left else width) // 16
        if not split:
            shape = (width * tiles, LANES) if by_left else (width, tiles * LANES)
            block = (width, LANES)
            out_specs.append(pl.BlockSpec(
                block, (lambda i, *_, step=step: (step(i), 0)) if by_left else (lambda i, *_, step=step: (0, step(i)))
            ))
            out_shape.append(shaped(shape, F32))
        plan.append((by_left, tiles, size))
        at += tiles
        row += size if by_left else tiles * size
    narrow = next(p[0][0].shape[1] for p in products if not p[3])
    if split:
        out_specs = [whole((4, row, LANES))] * 4
        out_shape = [shaped((4, row, LANES), BF)] * 4
    flops = 2 * count * t * narrow * at * LANES
    return prefetched(
        functools.partial(grads_kernel, split, tuple(plan)), back, lefts + rights, left_specs + right_specs,
        out_specs, out_shape, [pltpu.VMEM((narrow, LANES), F32), pltpu.VMEM((narrow, count * t), BF)],
        (at,), 60, "weight_grads", flops, flops // 256,
    )


def qkv_back_kernel(d_ref, x_ref, dx1_ref, w_ref, gain_ref, dx_ref):
    d = x_ref.shape[1]
    groups, _, span = d_ref.shape
    span //= 3
    dh = None
    for part in range(3):
        for g in range(groups):
            at = part * d + g * span
            piece = dot(d_ref[g, :, part * span : (part + 1) * span], w_ref[:, at : at + span], ((1,), (1,)))
            dh = piece if dh is None else dh + piece
    unit, inv = unit_norm(x_ref[...].astype(F32))
    dx_ref[...] = dx1_ref[...] + norm_back(dh * gain_ref[...], unit, inv)


def qkv_backward(d_qkv, tokens, dx1, w_qkv, gain):
    t, d = tokens.shape
    groups, _, span = d_qkv.shape
    return pl.pallas_call(
        qkv_back_kernel,
        grid=(t // ROWS,),
        in_specs=[pl.BlockSpec((groups, ROWS, span), lambda i: (0, i, 0))] + [rows(d)] * 2
        + [whole((d, 3 * d)), whole((1, d))],
        out_specs=rows(d),
        out_shape=shaped((t, d), F32),
        compiler_params=params(48),
        cost_estimate=pl.CostEstimate(flops=6 * t * d * d, transcendentals=0, bytes_accessed=6 * d * d + 16 * t * d),
        name="qkv_backward",
    )(d_qkv, tokens, dx1, w_qkv, gain)


def layout(doc_lengths, seq):
    docs = doc_lengths.shape[-1]
    upto = jnp.arange(docs)[:, None] <= jnp.arange(docs)[None, :]
    ends = jnp.sum(jnp.where(upto[None], doc_lengths[:, :, None], 0), axis=1)
    places = jnp.arange(seq, dtype=jnp.int32)
    passed = places[None, :, None] >= ends[:, None, :]
    start = jnp.sum(jnp.where(passed, doc_lengths[:, None, :], 0), axis=-1)
    valid = places[None, :] < ends[:, docs - 2 : docs - 1]
    return start.astype(jnp.int32), places[None, :] - start, valid


def tables(position):
    half = HEAD_DIM // 2
    lane = jnp.arange(PAIR)
    frequency = jnp.exp((lane % half).astype(F32) * (-2.0 * math.log(10000.0) / HEAD_DIM))
    angles = position.reshape(-1, 1).astype(F32) * frequency[None, :]
    sign = jnp.where(lane % HEAD_DIM < half, -1.0, 1.0)
    return jnp.cos(angles), jnp.sin(angles) * sign[None, :]


Z = 4
GROUPS = ((0, 2), (1, 3))


def index(x, core, z, y):
    return ((x * 2 + core) * Z + z) * 2 + y


def permute(value, move):
    places = [(x, c, z, y) for x in range(2) for c in range(2) for z in range(Z) for y in range(2)]
    return lax.ppermute(value, AXES, [(index(*p), index(*move(*p))) for p in places])


def over_x(v):
    return permute(v, lambda x, c, z, y: (1 - x, c, z, y))


def over_y(v):
    return permute(v, lambda x, c, z, y: (x, c, z, 1 - y))


def over_core(v):
    return permute(v, lambda x, c, z, y: (x, 1 - c, z, y))


def over_z(v, bits):
    return permute(v, lambda x, c, z, y: (x, c, z ^ bits, y))


def place():
    dp, fs = lax.axis_index("dp"), lax.axis_index("fsdp")
    return dp >> 1, dp & 1, fs >> 1, fs & 1


def gather_order():
    rows_of = []
    for core in range(2):
        for group, first in zip(GROUPS, ("x", "y")):
            for second in range(2):
                for one in range(2):
                    dx, dy = (one, second) if first == "x" else (second, one)
                    rows_of += [(dx, core, dz, dy) for dz in group]
    dx, dc, dz, dy = np.array(rows_of, np.int32).T
    x, c, z, y = place()
    order = index(x ^ dx, c ^ dc, z ^ dz, y ^ dy)
    return jnp.concatenate([order, c[None]]).astype(jnp.int32)


def scatter_order():
    rows_of = []
    for group, first in zip(GROUPS, ("y", "x")):
        for one in (1, 0):
            for second in (1, 0):
                dx, dy = (second, one) if first == "y" else (one, second)
                rows_of += [(dx, dz, dy) for dz in group]
    dx, dz, dy = np.array(rows_of, np.int32).T
    x, c, z, y = place()
    order = ((x ^ dx) * Z + (z ^ dz)) * 2 + (y ^ dy)
    spots = jnp.arange(len(rows_of), dtype=jnp.int32)
    where = jnp.sum(jnp.where(order[None, :] == spots[:, None], spots[None, :], 0), axis=1)
    return jnp.concatenate([order, where, c[None]]).astype(jnp.int32)


def tie(value, other):
    return lax.optimization_barrier((value, other))[0]


class Gather:
    def __init__(self, block):
        self.block = block

    def far_z(self, after=None):
        block = self.block if after is None else tie(self.block, after)
        self.even = jnp.stack([block, over_z(block, 2)])
        return self.even

    def near_z(self, after=None):
        if after is not None:
            self.even = tie(self.even, after)
        self.odd = over_z(self.even, 1)
        return self.odd

    def first(self):
        self.got = (over_x(self.even), over_y(self.odd))
        return self.got

    def second(self, after=None):
        got = self.got if after is None else tie(self.got, after)
        even, odd = jnp.concatenate([self.even, got[0]]), jnp.concatenate([self.odd, got[1]])
        self.near = [even, odd, over_core(even), over_core(odd)]
        self.far = [over_y(even), over_x(odd)]
        return self.far

    def core(self, after=None):
        far = self.far if after is None else tie(self.far, after)
        even, odd, even_core, odd_core = self.near
        return [even, far[0], odd, far[1], even_core, over_core(far[0]), odd_core, over_core(far[1])]


class Reduce:
    def __init__(self, send_a, keep_a, send_b, keep_b):
        self.sends, self.a, self.b = (send_a, send_b), keep_a.astype(F32), keep_b.astype(F32)

    def first(self, after=None):
        sends = self.sends if after is None else tie(self.sends, after)
        self.got = (over_y(sends[0]), over_x(sends[1]))
        return self.got

    def wait_for(self, after):
        if after is not None:
            self.got = tie(self.got, after)

    def second(self, after=None):
        self.wait_for(after)
        self.a = self.a + self.got[0].astype(F32)
        self.b = self.b + self.got[1].astype(F32)
        self.got = (over_x(self.a[:2].astype(BF)), over_y(self.b[:2].astype(BF)))
        return self.got

    def near_z(self, after=None):
        self.wait_for(after)
        self.a = self.a[2:] + self.got[0].astype(F32)
        self.got = over_z((self.b[2:] + self.got[1].astype(F32)).astype(BF), 1)
        return self.got

    def far_z(self, after=None):
        self.wait_for(after)
        self.a = self.a + self.got.astype(F32)
        self.got = over_z(self.a[1].astype(BF), 2)
        return self.got

    def own(self):
        return self.a[0] + self.got.astype(F32)


def unslab(block, width):
    size = block.shape[0] * LANES // width
    return jnp.concatenate([block[s * size : (s + 1) * size] for s in range(width // LANES)], axis=1)


def slab(block):
    return [block[:, s * LANES : (s + 1) * LANES] for s in range(block.shape[1] // LANES)]


def local(fast, tokens, doc_lengths, cotangent, w_qkv, w_out, w_up, w_down,
          gain_attn, gain_inner, gain_ffn, gain_mid):
    row_count = doc_lengths.shape[0]
    seq = tokens.shape[0] // row_count
    d, f = tokens.shape[1], w_up.shape[1]
    wide = min(seq, 512) // BLOCK + 1
    blocks = seq // BLOCK
    shards = (gain_attn, gain_inner, gain_ffn, gain_mid)

    start, position, valid = layout(doc_lengths, seq)
    cos, sin = tables(position)
    firsts = start[:, ::BLOCK] // BLOCK
    reach = (jnp.arange(blocks, dtype=jnp.int32)[None, :] - firsts + 1).reshape(-1)
    start_row = jnp.repeat(start, 8, axis=0)
    gy = jnp.where(valid.reshape(-1, 1), cotangent, jnp.zeros_like(cotangent))

    def scatter(g):
        return lax.psum_scatter(g, AXES, scatter_dimension=0, tiled=True)

    def gather(v):
        return lax.all_gather(v, AXES, axis=0, tiled=True)

    if fast:
        order, back = gather_order(), scatter_order()
        one, two = (Gather(b) for b in pack(w_qkv, w_out, w_up, w_down, shards))
        seen = one.far_z()
        two.far_z(seen)
        one.even = tie(one.even, (cos, sin))
        one.near_z()
        one.first()
        one.second(two.even)
        two.near_z()
        two.first()
        parts_qkv = one.core()
        gy_both = (gy, over_core(gy))
        cos, sin = tie((cos, sin), (gy, start_row, reach, order, back))
    else:
        order = back = jnp.zeros((8,), jnp.int32)

        def scaled(w, gain):
            return gather((w.astype(F32) * gain.astype(F32)[:, None]).astype(BF))

        parts_qkv, parts_down = [gather(w_qkv)], [scaled(w_down, gain_mid)]
        parts_up = [scaled(w_out, gain_inner), scaled(w_up, gain_ffn)]

    whole_gain = None if fast else gather(gain_attn).astype(F32).reshape(1, -1)
    h1, qkv, full_qkv, *rest = qkv_forward(fast, order, tokens, cos, sin, parts_qkv, whole_gain)
    g_attn = rest[0] if fast else whole_gain
    if fast:
        two.second(g_attn)
        start_row = tie(start_row, (gy_both[1], two.near[2:]))
    mixed, lse = attention_forward(reach, qkv, start_row, row_count, wide)
    parts = two.core(lse) if fast else parts_up + parts_down
    a, h2, x1, m, dpre, dx1, low, d_mixed, full_down, _, _, *other = ffn_both(
        fast, order, mixed, tokens, gy, parts, f
    )

    def shared(value):
        return (value, over_core(value)) if fast else (value,)

    if fast:
        m_both = (m, over_core(other[1]))
        theirs = over_core(other[0])
        a_both, h2_both = (a, (theirs, 0)), (h2, (theirs, 1))
    else:
        gy_both, m_both, a_both, h2_both = (gy,), (m,), (a,), (h2,)
    low, dpre = shared(low), shared(dpre)

    def attend(group, groups, lse, so_far):
        return attention_backward(
            reach, qkv, d_mixed, mixed, lse, start_row, cos, sin, row_count, wide, group, groups, so_far
        )

    f = w_up.shape[1]
    d_qkv = attend(0, 1, lse, None)
    if fast:
        low = tie(low, d_qkv)
    grads = weight_grads(
        fast, back,
        [(m_both, gy_both, f // 384, True), (a_both, low, d // LANES, False), (h2_both, dpre, f // LANES, False)],
    )
    if fast:
        red = Reduce(*grads)
        first = red.first()
        h1 = tie(h1, grads[-1])
    d_qkv = attend(1, 2, tie(lse, grads[-1]), d_qkv)
    if fast:
        h1 = (h1[0], over_core(h1[1]))
        d_both = (d_qkv, over_core(tie(d_qkv, (first, h1[1]))))
        second = red.second(d_qkv)
        dx1 = tie(dx1, (d_qkv, first))
    else:
        d_both = (d_qkv,)
    grad_tokens = qkv_backward(d_qkv, tokens, dx1, full_qkv, g_attn)
    if fast:
        near = red.near_z(grad_tokens)
        h1 = tie(h1, (grad_tokens, second))
    grad_qkv = weight_grads(fast, back, [(h1, d_both, 3 * d // LANES, False)])
    if fast:
        red_qkv = Reduce(*grad_qkv)
        first = red_qkv.first()
        far = red.far_z(grad_qkv[-1])
        m = tie(m, (grad_qkv[-1], near))
    result = down_forward(m, x1, full_down)
    if fast:
        red_qkv.second((result, far))
        own = red.own()
        red_qkv.near_z()
        red_qkv.far_z()
        g_qkv = red_qkv.own()
        cuts = (w_down.shape[0], w_down.shape[0] + w_out.shape[0])
        own_down, grad_out, grad_up = own[: cuts[0]], own[cuts[0] : cuts[1]], unslab(own[cuts[1] :], f)
    else:
        own_down, grad_out, grad_up, g_qkv = (scatter(g.astype(BF)).astype(F32) for g in (*grads, *grad_qkv))
        g_qkv = jnp.concatenate(slab(g_qkv))
    size = w_qkv.shape[0]
    span = LANES // 3
    g_qkv = jnp.concatenate(
        [g_qkv[g * size : (g + 1) * size, p * span : (p + 1) * span] for p in range(3) for g in range(GRAD_GROUPS)], axis=1
    )
    raw = (g_qkv, grad_out, grad_up, own_down)
    row_sums = [jnp.sum(g * w.astype(F32), axis=1) for g, w in zip(raw, (w_qkv, w_out, w_up, w_down))]
    row_sums[0] = row_sums[0] / gain_attn.astype(F32)
    scaled_grads = [g * v.astype(F32)[:, None] for g, v in zip(raw[1:], shards[1:])]
    return (result, grad_tokens, g_qkv, *scaled_grads, *row_sums)


def solution(mesh):
    matrix, vector = P(AXES, None), P(AXES)
    fast = mesh.shape["dp"] == 4 and mesh.shape["fsdp"] == 2 * Z
    return jax.shard_map(
        functools.partial(local, fast),
        mesh=mesh,
        in_specs=(matrix,) * 7 + (vector,) * 4,
        out_specs=(matrix,) * 6 + (vector,) * 4,
        check_vma=False,
    )
```
